32 devices in a mesh: seq: 2 (over core), dp: 16 (over z, y, x).
Axes of the slice: x: 2, y: 2, z: 4, core: 2. Of those that a mesh axis runs over, the one named last changes fastest.
Arguments:
- visible: bfloat16 [16, 512, 768], P('dp', 'seq'), may hold values from -6 to 6
- segments: int32 [16, 512], P('dp'), may hold values from 0 to 10, as said below
- patch_ids: int32 [16, 512], P('dp'), may hold values from 0 to 195, as said below
- targets: bfloat16 [16, 10, 196, 768], P('dp', 'seq'), may hold values from -6 to 6
- master: float32 [11608064], P(('seq', 'dp'))
- moment_one: float32 [11608064], P(('seq', 'dp')), may hold values from -4.172325e-07 to 4.172325e-07
- moment_two: float32 [11608064], P(('seq', 'dp')), may hold values from 8.614701e-16 to 3.4458804e-15
- step_count: int32 [1], replicated, may hold values from 2 to 20
Outputs:
- new_moment_one: float32 [11608064], P(('seq', 'dp'))
- new_moment_two: float32 [11608064], P(('seq', 'dp'))
- new_master: float32 [11608064], P(('seq', 'dp'))
- new_copy: bfloat16 [11608064], P(('seq', 'dp'))
- grad_norm: float32 [], replicated
- loss: float32 [], replicated
The draws below stay inside these ranges and needn't reach their ends.
Inputs may be any that keep to these rules, and one draw needn't show every extreme that they name: `segments`: in each sequence each image 0 to 9 holds exactly 49 rows, placed at drawn positions anywhere in the sequence; the other 22 rows are padding and hold 10. `patch_ids`: the 49 rows of one image hold distinct values; padding rows hold 0.
All inputs are finite; a program needn't handle non-finite values.
Results may differ from the reference program's by a relative error of at most 0.0066.
The reference program's roundings to bfloat16 on the way count: a program that leaves them out, or rounds other values in their place, can miss the bound.
Values may be sent and summed in bfloat16 or wider, within the bound.
A program may use at most 256 MiB of HBM per device.

```python
import math
import jax
import jax.numpy as jnp
from jax import lax

D = 768
HEADS = 12
FF = 3072
DD = 512
DHEADS = 16
DFF = 2048
PIX = 768
PATCHES = 196
VIS = 49
IMG_SEQ = 10
SEQ_LEN = 512
SEQUENCES = 16
MTOT = 23520
P_SIZE = 11608064


def layout_drawn():
    return [('embed', (PIX, D)), ('enc_qkv', (D, 3 * D)), ('enc_out', (D, D)), ('enc_up', (D, FF)), ('enc_down', (FF, D)), ('project', (D, DD)), ('dec_qkv', (DD, 3 * DD)), ('dec_out', (DD, DD)), ('dec_up', (DD, DFF)), ('dec_down', (DFF, DD)), ('pixel', (DD, PIX)), ('enc_vecs', (6, D)), ('dec_vecs', (7, DD))]


def matrix_scale(entry_name):
    scales = {'embed': PIX ** (-0.5), 'enc_qkv': D ** (-0.5), 'enc_out': (VIS / D) ** 0.5, 'enc_up': D ** (-0.5), 'enc_down': FF ** (-0.5), 'project': D ** (-0.5), 'dec_qkv': DD ** (-0.5), 'dec_out': (PATCHES / DD) ** 0.5, 'dec_up': DD ** (-0.5), 'dec_down': DFF ** (-0.5), 'pixel': DD ** (-0.5)}
    return scales[entry_name]


def draw_master(key, part):
    pieces = []
    for position, (entry_name, entry_shape) in enumerate(layout_drawn()):
        sub_key = jax.random.fold_in(key, position + 11)
        noise = jax.random.normal(sub_key, entry_shape, jnp.float32)
        if entry_name in ('enc_vecs', 'dec_vecs'):
            rows = entry_shape[0]
            centers = jnp.array([1.0, 0.0, 1.0, 0.0, 1.0, 0.0, 0.0][:rows], jnp.float32)[:, None]
            spreads = jnp.array([0.1, 0.2, 0.1, 0.2, 0.1, 0.2, 1.0][:rows], jnp.float32)[:, None]
            values = centers + spreads * noise
        else:
            values = noise * matrix_scale(entry_name)
        pieces.append(values.reshape(-1))
    return jnp.concatenate(pieces)


def packing_common(key):
    seq_keys = jax.random.split(jax.random.fold_in(key, 3), SEQUENCES)

    def one_sequence(seq_key):
        order = jax.random.permutation(jax.random.fold_in(seq_key, 1), SEQ_LEN)
        image_keys = jax.random.split(jax.random.fold_in(seq_key, 2), IMG_SEQ)

        def one_image(image_key):
            return jax.random.permutation(image_key, PATCHES)[:VIS].astype(jnp.int32)
        base_patches = jnp.concatenate([jax.vmap(one_image)(image_keys).reshape(-1), jnp.zeros((SEQ_LEN - VIS * IMG_SEQ,), jnp.int32)])
        base_segments = jnp.concatenate([jnp.repeat(jnp.arange(IMG_SEQ, dtype=jnp.int32), VIS), jnp.full((SEQ_LEN - VIS * IMG_SEQ,), IMG_SEQ, jnp.int32)])
        return (base_segments[order], base_patches[order])
    return jax.vmap(one_sequence)(seq_keys)


def draw_segments(key, part):
    return packing_common(key)[0]


def draw_patch_ids(key, part):
    return packing_common(key)[1]


def levels(key, shape, cuts, smallest, high):
    loudness = 1.0
    for dim, blocks in cuts:
        draws = jax.random.uniform(jax.random.fold_in(jax.random.fold_in(key, 6), dim), (blocks,), jnp.float32, smallest / len(cuts), high / len(cuts))
        loudness = loudness * jnp.repeat(jnp.exp(draws), shape[dim] // blocks).reshape((-1,) + (1,) * (len(shape) - 1 - dim))
    return loudness


def bell_draw(key, dims, deviation, reach, shards=(), held_as=jnp.bfloat16):
    level = levels(key, dims, shards, -0.22, 0.18) if shards else 1.0
    drawn = jax.random.normal(key, dims, jnp.float32) * deviation * level
    return jnp.minimum(jnp.maximum(drawn, -reach), reach).astype(held_as)


def setup_inputs(seed: int = 0) -> dict:
    keys = jax.random.split(jax.random.key(seed), 9)
    visible = bell_draw(keys[0], (SEQUENCES, SEQ_LEN, PIX), 1.0, 6.0, ((0, 16), (1, 2)))
    segments = draw_segments(jax.random.fold_in(keys[8], 71), 0)
    patch_ids = draw_patch_ids(jax.random.fold_in(keys[8], 71), 0)
    targets = bell_draw(keys[3], (SEQUENCES, IMG_SEQ, PATCHES, PIX), 1.0, 6.0, ((0, 16), (1, 2)))
    master = draw_master(jax.random.fold_in(keys[8], 71), 0)
    moment_one = bell_draw(keys[5], (P_SIZE,), (0.0001 * P_SIZE ** -0.5), 4.172325134277344e-07, ((0, 32),), jnp.float32)
    moment_two = jnp.clip(jnp.exp(math.log(3.4458803777786314e-15) - 1.3862944 * jax.random.uniform(keys[6], (P_SIZE,), jnp.float32) ** levels(keys[6], (P_SIZE,), ((0, 32),), -0.2, 0.2)), 8.614700944446579e-16, 3.4458803777786314e-15)
    step_count = jax.random.randint(keys[7], (1,), 2, 21).astype(jnp.int32)
    return {"visible": visible, "segments": segments, "patch_ids": patch_ids, "targets": targets, "master": master, "moment_one": moment_one, "moment_two": moment_two, "step_count": step_count}


@jax.custom_vjp
def low(v):
    return lax.optimization_barrier(v.astype(jnp.bfloat16)).astype(jnp.float32)

@jax.custom_vjp
def low_back(v):
    return v

def low_keep(v):
    return (low(v), None)

def low_pass(kept, grad):
    return (grad,)

def back_keep(v):
    return (v, None)

def back_low(kept, grad):
    return (low(grad),)
low.defvjp(low_keep, low_pass)
low_back.defvjp(back_keep, back_low)
norm_eps = 1e-06
neg_big = -1000000000.0
clip_limit = 0.0001
learn_rate = 0.03
decay_rate = 0.05
adam_eps = 1e-08
beta_mom = 0.5
top_precision = lax.Precision.HIGHEST

def layout():
    return [('embed', (PIX, D)), ('enc_qkv', (D, 3 * D)), ('enc_out', (D, D)), ('enc_up', (D, FF)), ('enc_down', (FF, D)), ('project', (D, DD)), ('dec_qkv', (DD, 3 * DD)), ('dec_out', (DD, DD)), ('dec_up', (DD, DFF)), ('dec_down', (DFF, DD)), ('pixel', (DD, PIX)), ('enc_vecs', (6, D)), ('dec_vecs', (7, DD))]

def unflatten(flat_vec):
    params = {}
    offset = 0
    for entry_name, entry_shape in layout():
        entry_size = entry_shape[0] * entry_shape[1]
        params[entry_name] = flat_vec[offset:offset + entry_size].reshape(entry_shape)
        offset += entry_size
    return params

def sincos(positions, columns):
    half_cols = columns // 2
    frequency = jnp.exp(-math.log(10000.0) * jnp.arange(half_cols, dtype=jnp.float32) / half_cols)
    angles = positions.astype(jnp.float32)[..., None] * frequency
    return jnp.concatenate([jnp.sin(angles), jnp.cos(angles)], axis=-1)

def layer_norm(inputs, norm_gain, norm_shift):
    average = lax.optimization_barrier(jnp.mean(inputs, axis=-1, keepdims=True))
    centered = inputs - average
    spread = lax.optimization_barrier(jnp.mean(centered * centered, axis=-1, keepdims=True))
    return centered * lax.rsqrt(spread + norm_eps) * norm_gain + norm_shift

def matmul(left, right):
    return jnp.einsum('...i,ij->...j', left, right, precision=top_precision)

def attention(qkv_rows, heads, allowed):
    columns = qkv_rows.shape[-1] // 3
    head_size = columns // heads
    shaped = qkv_rows.reshape(qkv_rows.shape[:-1] + (3, heads, head_size))
    queries, keys_all, values_all = (shaped[:, :, 0], shaped[:, :, 1], shaped[:, :, 2])
    scores = low_back(jnp.einsum('bqhd,bkhd->bhqk', queries, keys_all, precision=top_precision) * head_size ** (-0.5))
    if allowed is not None:
        scores = jnp.where(allowed, scores, neg_big)
    probs = low(jax.nn.softmax(scores, axis=-1))
    outputs = jnp.einsum('bhqk,bkhd->bqhd', probs, values_all, precision=top_precision)
    return low_back(low(outputs.reshape(qkv_rows.shape[:-1] + (columns,))))

def block(inputs, vecs, w_qkv, w_out, w_up, w_down, heads, allowed):
    normed_a = low(layer_norm(inputs, vecs[0], vecs[1]))
    qkv_rows = low_back(low(matmul(normed_a, w_qkv)))
    after_attn = inputs + low_back(matmul(attention(qkv_rows, heads, allowed), w_out))
    normed_b = low(layer_norm(after_attn, vecs[2], vecs[3]))
    hidden_act = low(jax.nn.gelu(low_back(matmul(normed_b, w_up)), approximate=False))
    return after_attn + low_back(matmul(hidden_act, w_down))

def normalize(pixels):
    average = lax.optimization_barrier(jnp.mean(pixels, axis=-1, keepdims=True))
    centered = pixels - average
    return centered * lax.rsqrt(lax.optimization_barrier(jnp.mean(centered * centered, axis=-1, keepdims=True)) + norm_eps)

def sequence_loss(params, visible_seq, segments_seq, patches_seq, targets_seq):
    enc_vecs, decoder_vectors = (params['enc_vecs'], params['dec_vecs'])
    embedded = low_back(matmul(visible_seq, params['embed'])) + sincos(patches_seq, D)
    allowed = segments_seq[:, None] == segments_seq[None, :]
    encoded = block(embedded[None], enc_vecs, params['enc_qkv'], params['enc_out'], params['enc_up'], params['enc_down'], HEADS, allowed)[0]
    final_enc = low(layer_norm(encoded, enc_vecs[4], enc_vecs[5]))
    projected = low_back(low(matmul(final_enc, params['project'])))
    target_row = jnp.where(segments_seq < IMG_SEQ, segments_seq * PATCHES + patches_seq, -1)
    selector = (target_row[None, :] == jnp.arange(IMG_SEQ * PATCHES)[:, None]).astype(jnp.float32)
    placed = jnp.dot(selector, projected, precision=top_precision)
    masked_rows = 1.0 - lax.optimization_barrier(jnp.sum(selector, axis=1))
    dec_in = placed + masked_rows[:, None] * decoder_vectors[6] + sincos(jnp.arange(IMG_SEQ * PATCHES) % PATCHES, DD)
    decoder_result = block(dec_in.reshape(IMG_SEQ, PATCHES, DD), decoder_vectors, params['dec_qkv'], params['dec_out'], params['dec_up'], params['dec_down'], DHEADS, None)
    final_dec = low(layer_norm(decoder_result, decoder_vectors[4], decoder_vectors[5]))
    predicted = low_back(matmul(final_dec, params['pixel']))
    error = predicted - normalize(targets_seq)
    return jnp.sum(masked_rows.reshape(IMG_SEQ, PATCHES) * lax.optimization_barrier(jnp.mean(error * error, axis=-1)))

def total_loss(master_vec, visible, segments, patch_ids, targets):
    params = unflatten(low(master_vec))
    checked = jax.checkpoint(sequence_loss)

    def one_sequence(carry, inputs_seq):
        return (carry + checked(params, *inputs_seq), None)
    total, _ = lax.scan(one_sequence, jnp.zeros((), jnp.float32), (visible, segments, patch_ids, targets))
    return total / MTOT

def reference(visible, segments, patch_ids, targets, master, moment_one, moment_two, step_count):
    visible_f = visible.astype(jnp.float32)
    targets_f = targets.astype(jnp.float32)

    def loss_of(master_vec):
        return total_loss(master_vec, visible_f, segments, patch_ids, targets_f)
    loss, pullback = jax.vjp(loss_of, master)
    gradient, = pullback(jnp.ones((), jnp.float32))
    grad_norm = jnp.sqrt(jnp.sum(gradient * gradient))
    clipped = gradient * jnp.minimum(1.0, clip_limit / (grad_norm + 1e-06))
    new_one = beta_mom * moment_one + (1.0 - beta_mom) * clipped
    new_two = beta_mom * moment_two + (1.0 - beta_mom) * clipped * clipped
    correction = 1.0 - jnp.power(jnp.float32(beta_mom), step_count[0].astype(jnp.float32))
    new_master = master - learn_rate * (new_one / correction / (jnp.sqrt(new_two / correction) + adam_eps) + decay_rate * master)
    return (new_one, new_two, new_master, new_master.astype(jnp.bfloat16), grad_norm, loss)
```

```python
from functools import partial
import math

import jax
import jax.numpy as jnp
import ml_dtypes
import numpy as np
from jax import lax
from jax.experimental import pallas as pl
from jax.experimental.pallas import tpu as pltpu
from jax.sharding import PartitionSpec as P

D = 768
HEADS = 12
FF = 3072
DD = 512
DHEADS = 16
DFF = 2048
PIX = 768
PATCHES = 196
VIS = 49
IMG_SEQ = 10


norm_eps = 1e-06
neg_big = -1000000000.0
clip_limit = 0.0001
learn_rate = 0.03
decay_rate = 0.05
adam_eps = 1e-08
beta_mom = 0.5


def layout():
    return [
        ("embed", (PIX, D)),
        ("enc_qkv", (D, 3 * D)),
        ("enc_out", (D, D)),
        ("enc_up", (D, FF)),
        ("enc_down", (FF, D)),
        ("project", (D, DD)),
        ("dec_qkv", (DD, 3 * DD)),
        ("dec_out", (DD, DD)),
        ("dec_up", (DD, DFF)),
        ("dec_down", (DFF, DD)),
        ("pixel", (DD, PIX)),
        ("enc_vecs", (6, D)),
        ("dec_vecs", (7, DD)),
    ]


def unflatten(flat_vec):
    params = {}
    offset = 0
    for entry_name, entry_shape in layout():
        entry_size = entry_shape[0] * entry_shape[1]
        params[entry_name] = flat_vec[offset : offset + entry_size].reshape(entry_shape)
        offset += entry_size
    return params


MESH = pl.DeviceIdType.MESH
LANES = 128
A_HALF = 1104
A_ROWS = 2 * A_HALF
B_HALF = 320
B_ROWS = 2 * B_HALF
SHARD_ROWS = 2834
PAD_ROWS = A_ROWS + B_ROWS
STAGE_ROWS = 64
PARTS = {
    "a": (0, A_ROWS),
    "a1": (0, A_HALF),
    "a2": (A_HALF, A_HALF),
    "b": (A_ROWS, B_ROWS),
    "b1": (A_ROWS, B_HALF),
    "b2": (A_ROWS + B_HALF, B_HALF),
}


def rows_of(part):
    return pl.ds(*PARTS[part])


class Place:
    def __init__(self):
        self.core = lax.axis_index("seq")
        self.chip = lax.axis_index("dp")
        chip = self.chip
        self.z = chip // 4
        y, x = (chip // 2) % 2, chip % 2
        self.col = chip % 4
        self.col_x = self.col + 1 - 2 * x
        self.col_y = self.col + 2 - 4 * y
        self.col_d = self.col_x + 2 - 4 * y
        self.side = self.z // 2
        sign = 1 - 2 * self.side
        self.inner = self.z + self.side * (3 - 2 * self.z)
        self.outer_chip, self.middle_chip = self.inner == 0, self.inner == 1
        self.to_x = (self.core, 4 * self.z + self.col_x)
        self.to_y = (self.core, 4 * self.z + self.col_y)
        self.to_far = (self.core, chip + 4 * sign)
        self.to_near = (self.core, chip - 4 * sign * self.inner)
        self.to_core = (1 - self.core, chip)

    def plane(self, mirrored):
        return mirrored + self.side * (3 - 2 * mirrored)

    def greet(self):
        barrier = pltpu.get_barrier_semaphore()
        for device in (self.to_x, self.to_y, self.to_far, self.to_core):
            pl.semaphore_signal(barrier, inc=1, device_id=device, device_id_type=MESH)

        @pl.when(self.middle_chip)
        def _():
            pl.semaphore_signal(barrier, inc=1, device_id=self.to_near, device_id_type=MESH)

        pl.semaphore_wait(barrier, 4 + self.inner)


def maybe(when, action):
    if when is None:
        action()
    else:
        pl.when(when)(action)


class Outbox:
    def __init__(self):
        self.sent = []

    def send(self, src, dst, send_sem, recv_sem, device, when=None):
        def build():
            return pltpu.make_async_remote_copy(
                src_ref=src,
                dst_ref=dst,
                send_sem=send_sem,
                recv_sem=recv_sem,
                device_id=device,
                device_id_type=MESH,
            )

        maybe(when, lambda: build().start())
        self.sent.append((when, build))

    def finish(self):
        for when, build in self.sent:
            maybe(when, lambda: build().wait_send())


def arrived(ref, sem, device, when=None):
    def wait():
        pltpu.make_async_remote_copy(
            src_ref=ref,
            dst_ref=ref,
            send_sem=sem,
            recv_sem=sem,
            device_id=device,
            device_id_type=MESH,
        ).wait_recv()

    maybe(when, wait)


def gather_exchange(held, recv, core_recv, send_x, send_y, send_far, send_near, core_send):
    at = Place()
    at.greet()
    out = Outbox()
    middle = at.middle_chip

    def block(chip, part):
        return held.at[at.core * 16 + chip, rows_of(part)]

    def move(chip, part, slot, sems_out, device, when=None):
        ref = block(chip, part)
        out.send(ref, ref, sems_out.at[chip, slot], recv.at[chip, slot], device, when)

    def to_partner(chip):
        ref = block(chip, "a")
        out.send(ref, ref, core_send.at[chip, 0], core_recv.at[chip, 0], at.to_core)

    def got(chip, part, slot):
        arrived(block(chip, part), recv.at[chip, slot], at.to_x)

    def b_plane(mirrored, core=None):
        first = 4 * at.plane(mirrored)
        core = at.core if core is None else core
        return held.at[pl.ds(core * 16 + first, 4), rows_of("b")], first

    def move_b(mirrored, sems_out, device, when=None):
        ref, first = b_plane(mirrored)
        out.send(ref, ref, sems_out.at[first, 2], recv.at[first, 2], device, when)

    def got_b(mirrored):
        ref, first = b_plane(mirrored)
        arrived(ref, recv.at[first, 2], at.to_x)

    def partner_b(mirrored):
        ref, first = b_plane(mirrored)
        out.send(ref, ref, core_send.at[first, 1], core_recv.at[first, 1], at.to_core)

    def relay(mirrored):
        first = 4 * at.plane(mirrored)
        got(first + at.col_x, "a1", 0)
        move(first + at.col_x, "a1", 0, send_y, at.to_y)
        got(first + at.col_y, "a2", 1)
        move(first + at.col_y, "a2", 1, send_x, at.to_x)

    def settle(mirrored):
        first = 4 * at.plane(mirrored)
        got(first + at.col_x, "a2", 1)
        to_partner(first + at.col_x)
        got(first + at.col_y, "a1", 0)
        to_partner(first + at.col_y)
        got(first + at.col_d, "a1", 0)
        got(first + at.col_d, "a2", 1)
        to_partner(first + at.col_d)

    def spread(mirrored, sems_on, device_on):
        chip = 4 * at.plane(mirrored) + at.col
        for slot, part in enumerate(("a1", "a2")):
            got(chip, part, slot)
            move(chip, part, slot, sems_on, device_on, middle)
            move(chip, part, slot, send_x, at.to_x)
            move(chip, part, slot, send_y, at.to_y)
        to_partner(chip)

    own = at.chip
    own_plane = 4 * at.z
    chip_x, chip_y, chip_d = own_plane + at.col_x, own_plane + at.col_y, own_plane + at.col_d
    for slot, part in enumerate(("a1", "a2")):
        move(own, part, slot, send_far, at.to_far)
        move(own, part, slot, send_near, at.to_near, middle)
    move(own, "b", 2, send_x, at.to_x)
    move(own, "b", 2, send_y, at.to_y)
    move(own, "a1", 0, send_x, at.to_x)
    move(own, "a2", 1, send_y, at.to_y)
    move(own, "a2", 1, send_x, at.to_x)
    move(own, "a1", 0, send_y, at.to_y)
    to_partner(own)

    got(chip_x, "b", 2)
    move(chip_x, "b1", 2, send_y, at.to_y)
    got(chip_y, "b", 2)
    move(chip_y, "b2", 3, send_x, at.to_x)
    relay(at.inner)
    got(chip_d, "b1", 2)
    got(chip_d, "b2", 3)
    first, second, third = 1 - at.inner, 2, 3
    spread(first, send_far, at.to_far)
    move_b(at.inner, send_far, at.to_far)
    move_b(at.inner, send_near, at.to_near, middle)
    partner_b(at.inner)
    settle(at.inner)
    relay(first)
    spread(second, send_near, at.to_near)
    got_b(first)
    move_b(first, send_far, at.to_far, middle)
    partner_b(first)
    settle(first)
    relay(second)
    spread(third, send_near, at.to_near)
    got_b(second)
    move_b(second, send_near, at.to_near, middle)
    partner_b(second)
    settle(second)
    relay(third)
    got_b(third)
    move_b(third, send_near, at.to_near, middle)
    partner_b(third)
    settle(third)
    other = 1 - at.core
    for chip in range(16):
        arrived(held.at[other * 16 + chip, rows_of("a")], core_recv.at[chip, 0], at.to_core)
    for plane in range(4):
        ref = held.at[pl.ds(other * 16 + 4 * plane, 4), rows_of("b")]
        arrived(ref, core_recv.at[4 * plane, 1], at.to_core)
    out.finish()


def matrix_entries():
    entries, offset = [], 0
    for entry_name, entry_shape in layout():
        entries.append((offset // LANES, entry_shape[0], entry_shape[1] // LANES))
        offset += entry_shape[0] * entry_shape[1]
    return entries


SPLIT_ENTRY, SPLIT_ROW = 4, 704


def gather_kernel(master_ref, *refs):
    outs, (held, flat, stage, out_sem, *sems) = refs[:13], refs[13:]
    me = lax.axis_index("seq") * 16 + lax.axis_index("dp")
    held[me, pl.ds(SHARD_ROWS - 2, 16), :] = jnp.zeros((16, LANES), jnp.bfloat16)
    held[me, pl.ds(0, SHARD_ROWS), :] = master_ref[...].astype(jnp.bfloat16)
    gather_exchange(held, *sems)
    entries = matrix_entries()

    def unpack(first, count):
        def one(index, _):
            shard, piece = index // (PAD_ROWS // 32), index % (PAD_ROWS // 32)
            start = pl.multiple_of(piece * 32, 32)
            flat[pl.ds(shard * SHARD_ROWS + piece * 32, 32), :] = held[
                first + shard, pl.ds(start, 32), :
            ].astype(jnp.float32)
            return 0

        lax.fori_loop(0, count * (PAD_ROWS // 32), one, 0)

    def place(entry, row_start, row_stop, base):
        offset, _, groups = entries[entry]
        out = outs[entry]
        count = (row_stop - row_start) // STAGE_ROWS
        local = offset + row_start * groups - base

        def copy(slot, step):
            row = pl.multiple_of(row_start + step * STAGE_ROWS, 16)
            return pltpu.make_async_copy(
                stage.at[slot, :, pl.ds(0, groups * LANES)],
                out.at[pl.ds(row, STAGE_ROWS), :],
                out_sem.at[slot],
            )

        def one(step, _):
            slot = step % 2

            @pl.when(step >= 2)
            def _():
                copy(slot, step - 2).wait()

            for group in range(groups):
                stage[slot, :, pl.ds(group * LANES, LANES)] = flat[
                    pl.ds(local + step * (STAGE_ROWS * groups) + group, STAGE_ROWS, stride=groups), :
                ].astype(jnp.bfloat16)
            copy(slot, step).start()
            return 0

        lax.fori_loop(0, count, one, 0)
        for step in range(max(count - 2, 0), count):
            copy(step % 2, step).wait()

    unpack(0, 17)
    for entry in range(SPLIT_ENTRY):
        place(entry, 0, entries[entry][1], 0)
    place(SPLIT_ENTRY, 0, SPLIT_ROW, 0)
    base = 16 * SHARD_ROWS
    unpack(16, 16)
    place(SPLIT_ENTRY, SPLIT_ROW, entries[SPLIT_ENTRY][1], base)
    for entry in range(SPLIT_ENTRY + 1, 11):
        place(entry, 0, entries[entry][1], base)
    for entry in (11, 12):
        offset, rows, groups = entries[entry]
        for group in range(groups):
            outs[entry][:, pl.ds(group * LANES, LANES)] = flat[
                pl.ds(offset - base + group, rows, stride=groups), :
            ]


def gather_weights(master_rows):
    shapes = [entry_shape for _, entry_shape in layout()]
    hbm = pl.BlockSpec(memory_space=pl.ANY)
    vmem = pl.BlockSpec(memory_space=pltpu.VMEM)
    widest = max(shape[1] for shape in shapes)
    sixteen = pltpu.SemaphoreType.DMA((16, 4))
    return pl.pallas_call(
        gather_kernel,
        out_shape=[jax.ShapeDtypeStruct(s, jnp.bfloat16) for s in shapes[:11]]
        + [jax.ShapeDtypeStruct(s, jnp.float32) for s in shapes[11:]],
        in_specs=[vmem],
        out_specs=[hbm] * 11 + [vmem] * 2,
        scratch_shapes=[
            pltpu.VMEM((32, PAD_ROWS, LANES), jnp.bfloat16),
            pltpu.VMEM((17 * SHARD_ROWS + 30, LANES), jnp.float32),
            pltpu.VMEM((2, STAGE_ROWS, widest), jnp.bfloat16),
            pltpu.SemaphoreType.DMA((2,)),
            sixteen,
            pltpu.SemaphoreType.DMA((16, 2)),
            sixteen,
            sixteen,
            sixteen,
            sixteen,
            pltpu.SemaphoreType.DMA((16, 2)),
        ],
        compiler_params=pltpu.CompilerParams(
            collective_id=0, has_side_effects=True, vmem_limit_bytes=60 * 1024 * 1024
        ),
        name="gather_weights",
    )(master_rows)


def reduce_kernel(
    grad_ref,
    loss_ref,
    shard_ref,
    total_ref,
    own,
    theirs,
    from_x,
    from_y,
    pass_x,
    pass_y,
    far_a,
    near_a,
    far_b,
    near_b,
    scalars,
    load_sem,
    core_send,
    core_recv,
    send_x,
    send_y,
    send_z,
    recv_x,
    recv_y,
    recv_z,
    tiny_send,
    tiny_recv,
):
    at = Place()
    far, near = at.to_far, at.to_near
    outer, middle = at.outer_chip, at.middle_chip
    tail = pl.ds(SHARD_ROWS - 2, 16)
    for index in range(16):
        own[index, tail, :] = jnp.zeros((16, LANES), jnp.bfloat16)
        theirs[index, tail, :] = jnp.zeros((16, LANES), jnp.bfloat16)
    at.greet()
    out = Outbox()
    order = (3, 2, 1 - at.inner, at.inner)
    body = pl.ds(0, SHARD_ROWS)

    def shard_rows(core, chip):
        return grad_ref.at[pl.ds((core * 16 + chip) * SHARD_ROWS, SHARD_ROWS)]

    def load(chip):
        return pltpu.make_async_copy(
            shard_rows(at.core, chip), own.at[chip, body], load_sem.at[chip]
        )

    for mirrored in order:
        for column in range(4):
            chip = 4 * at.plane(mirrored) + column
            out.send(
                shard_rows(1 - at.core, chip),
                theirs.at[chip, body],
                core_send.at[chip],
                core_recv.at[chip],
                at.to_core,
            )
            load(chip).start()

    def combine(dst, start, terms, size, chunk):
        def one(step, _):
            row = pl.multiple_of(step * chunk, 16)
            total = None
            for ref, first in terms:
                piece = ref[pl.ds(pl.multiple_of(first + row, 16), chunk), :].astype(jnp.float32)
                total = piece if total is None else total + piece
            dst[pl.ds(pl.multiple_of(start + row, 16), chunk), :] = total.astype(dst.dtype)
            return 0

        lax.fori_loop(0, size // chunk, one, 0)

    def pair(mirrored):
        for column in range(4):
            chip = 4 * at.plane(mirrored) + column
            load(chip).wait()
            arrived(theirs.at[chip, body], core_recv.at[chip], at.to_core)
            combine(
                own.at[chip], 0, [(own.at[chip], 0), (theirs.at[chip], 0)], PAD_ROWS, 32
            )

    def chips(mirrored):
        first = 4 * at.plane(mirrored)
        return (
            first // 4,
            first + at.col,
            first + at.col_x,
            first + at.col_y,
            first + at.col_d,
        )

    def part(chip, name):
        return own.at[chip, rows_of(name)]

    halves = {"a": ("a1", "a2", A_HALF, 0), "b": ("b1", "b2", B_HALF, A_ROWS)}

    def open_plane(plane, ids, kind, slot):
        _, chip_x, chip_y, chip_d = ids
        one, two, half, begin = halves[kind]
        rows = pl.ds(begin, half)
        more = pl.ds(begin + half, half)
        out.send(part(chip_d, one), pass_y.at[plane, rows], send_y.at[plane, slot], recv_y.at[plane, slot], at.to_y)
        out.send(part(chip_d, two), pass_x.at[plane, rows], send_x.at[plane, slot], recv_x.at[plane, slot], at.to_x)
        out.send(part(chip_x, two), from_x.at[plane, more], send_x.at[plane, slot + 1], recv_x.at[plane, slot + 1], at.to_x)
        out.send(part(chip_y, one), from_y.at[plane, rows], send_y.at[plane, slot + 1], recv_y.at[plane, slot + 1], at.to_y)

    def relay_plane(plane, ids, kind, slot):
        _, chip_x, chip_y, _ = ids
        one, two, half, begin = halves[kind]
        rows = pl.ds(begin, half)
        more = pl.ds(begin + half, half)
        chunk = half // 4 if kind == "b" else half // 3
        arrived(pass_y.at[plane, rows], recv_y.at[plane, slot], at.to_y)
        combine(
            own.at[chip_x], begin, [(own.at[chip_x], begin), (pass_y.at[plane], begin)], half, chunk
        )
        out.send(part(chip_x, one), from_x.at[plane, rows], send_x.at[plane, slot + 2], recv_x.at[plane, slot + 2], at.to_x)
        arrived(pass_x.at[plane, rows], recv_x.at[plane, slot], at.to_x)
        combine(
            own.at[chip_y],
            begin + half,
            [(own.at[chip_y], begin + half), (pass_x.at[plane], begin)],
            half,
            chunk,
        )
        out.send(part(chip_y, two), from_y.at[plane, more], send_y.at[plane, slot + 2], recv_y.at[plane, slot + 2], at.to_y)

    def close_plane(plane, kind, slot):
        _, _, half, begin = halves[kind]
        rows = pl.ds(begin, half)
        more = pl.ds(begin + half, half)
        arrived(from_x.at[plane, more], recv_x.at[plane, slot + 1], at.to_x)
        arrived(from_y.at[plane, rows], recv_y.at[plane, slot + 1], at.to_y)
        arrived(from_x.at[plane, rows], recv_x.at[plane, slot + 2], at.to_x)
        arrived(from_y.at[plane, more], recv_y.at[plane, slot + 2], at.to_y)

    def begin_a(mirrored):
        plane, *ids = chips(mirrored)
        open_plane(plane, ids, "a", 0)

    def relay_a(mirrored):
        plane, *ids = chips(mirrored)
        relay_plane(plane, ids, "a", 0)

    def close_a(mirrored):
        close_plane(chips(mirrored)[0], "a", 0)

    def plane_terms(plane, chip):
        return [(own.at[chip], 0), (from_x.at[plane], 0), (from_y.at[plane], 0)]

    def start_line_a(mirrored, when):
        plane, chip, *_ = chips(mirrored)

        def add():
            combine(own.at[chip], 0, plane_terms(plane, chip), A_ROWS, A_HALF // 3)

        maybe(when, add)
        out.send(part(chip, "a"), near_a.at[plane], send_z.at[plane, 0], recv_z.at[plane, 0], far, when)

    def pass_line_a(mirrored, source, slot, target, target_buffer, target_slot):
        plane, chip, *_ = chips(mirrored)
        arrived(source.at[plane], recv_z.at[plane, slot], at.to_x, middle)

        def add():
            terms = plane_terms(plane, chip) + [(source.at[plane], 0)]
            combine(own.at[chip], 0, terms, A_ROWS, A_HALF // 3)

        maybe(middle, add)
        out.send(
            part(chip, "a"),
            target_buffer.at[plane],
            send_z.at[plane, 0],
            recv_z.at[plane, target_slot],
            target,
            middle,
        )

    def b_rows(plane):
        return own.at[pl.ds(4 * plane, 4), rows_of("b")]

    def start_line_b(mirrored):
        plane = at.plane(mirrored)
        out.send(b_rows(plane), near_b.at[plane], send_z.at[plane, 2], recv_z.at[plane, 2], far, outer)

    def add_b(plane, source):
        for column in range(4):
            chip = 4 * plane + column
            combine(
                own.at[chip],
                A_ROWS,
                [(own.at[chip], A_ROWS), (source.at[plane, column], 0)],
                B_ROWS,
                B_ROWS // 4,
            )

    def pass_line_b(mirrored, source, slot, target, target_buffer, target_slot):
        plane = at.plane(mirrored)
        arrived(source.at[plane], recv_z.at[plane, slot], at.to_x, middle)
        maybe(middle, lambda: add_b(plane, source))
        out.send(
            b_rows(plane),
            target_buffer.at[plane],
            send_z.at[plane, 2],
            recv_z.at[plane, target_slot],
            target,
            middle,
        )

    for step in range(3):
        pair(order[step])
        begin_a(order[step])
        start_line_b(order[step])
        if step >= 1:
            relay_a(order[step - 1])
        if step == 2:
            close_a(order[0])
            start_line_a(order[0], outer)
    pair(order[3])
    begin_a(order[3])
    relay_a(order[2])
    close_a(order[1])
    start_line_a(order[1], outer)
    pass_line_b(order[0], near_b, 2, far, far_b, 3)
    pass_line_b(order[1], near_b, 2, far, far_b, 3)
    pass_line_a(order[0], near_a, 0, far, far_a, 1)
    relay_a(order[3])
    pass_line_b(order[2], far_b, 3, near, far_b, 3)
    own_plane, chip, chip_x, chip_y, chip_d = chips(at.inner)
    arrived(far_b.at[own_plane], recv_z.at[own_plane, 3], at.to_x)
    add_b(own_plane, far_b)
    arrived(near_b.at[own_plane], recv_z.at[own_plane, 2], at.to_x, middle)
    maybe(middle, lambda: add_b(own_plane, near_b))
    ids = (chip, chip_x, chip_y, chip_d)
    open_plane(own_plane, ids, "b", 3)
    close_a(order[2])
    start_line_a(order[2], outer)
    pass_line_a(order[1], near_a, 0, far, far_a, 1)
    pass_line_a(order[2], far_a, 1, near, far_a, 1)
    relay_plane(own_plane, ids, "b", 3)
    close_a(order[3])
    terms = plane_terms(own_plane, chip)
    arrived(near_a.at[own_plane], recv_z.at[own_plane, 0], at.to_x, middle)

    @pl.when(outer)
    def _():
        near_a[own_plane] = jnp.zeros((A_ROWS, LANES), jnp.bfloat16)

    arrived(far_a.at[own_plane], recv_z.at[own_plane, 1], at.to_x)
    terms_line = terms + [(near_a.at[own_plane], 0), (far_a.at[own_plane], 0)]
    combine(shard_ref, 0, terms_line, A_ROWS, A_HALF // 3)
    close_plane(own_plane, "b", 3)
    terms_b = [(ref, A_ROWS) for ref, _ in terms]
    combine(shard_ref, A_ROWS, terms_b, B_ROWS, B_ROWS // 4)

    def squares(step, carry):
        piece = shard_ref[pl.ds(pl.multiple_of(step * 32, 32), 32), :]
        piece = piece * piece
        return carry + jnp.sum(piece.reshape(4, 8, LANES), axis=0)

    square = lax.fori_loop(0, PAD_ROWS // 32, squares, jnp.zeros((8, LANES), jnp.float32))
    me = at.core * 16 + at.chip
    scalars[me, 0] = square
    scalars[me, 1] = jnp.broadcast_to(loss_ref[...], (8, LANES))
    barrier_free_devices = []
    for step in range(1, 32):
        peer = (me + step) % 32
        barrier_free_devices.append(peer)
        out.send(
            scalars.at[me],
            scalars.at[me],
            tiny_send.at[step],
            tiny_recv.at[me],
            (peer // 16, peer % 16),
        )
    for step in range(1, 32):
        peer = (me + step) % 32
        arrived(scalars.at[peer], tiny_recv.at[peer], at.to_x)
    total_ref[...] = jnp.sum(scalars[...], axis=0)
    out.finish()


def reduce_gradients(grad_rows, loss_row):
    hbm = pl.BlockSpec(memory_space=pl.ANY)
    vmem = pl.BlockSpec(memory_space=pltpu.VMEM)
    low = jnp.bfloat16
    shard_total, totals = pl.pallas_call(
        reduce_kernel,
        out_shape=[
            jax.ShapeDtypeStruct((PAD_ROWS, LANES), jnp.float32),
            jax.ShapeDtypeStruct((2, 8, LANES), jnp.float32),
        ],
        in_specs=[hbm, vmem],
        out_specs=[vmem, vmem],
        scratch_shapes=[pltpu.VMEM((16, PAD_ROWS, LANES), low)] * 2
        + [pltpu.VMEM((4, PAD_ROWS, LANES), low)] * 4
        + [pltpu.VMEM((4, A_ROWS, LANES), low)] * 2
        + [pltpu.VMEM((4, 4, B_ROWS, LANES), low)] * 2
        + [pltpu.VMEM((32, 2, 8, LANES), jnp.float32)]
        + [pltpu.SemaphoreType.DMA((16,))] * 3
        + [pltpu.SemaphoreType.DMA((4, 6))] * 2
        + [pltpu.SemaphoreType.DMA((4, 3))]
        + [pltpu.SemaphoreType.DMA((4, 6))] * 2
        + [pltpu.SemaphoreType.DMA((4, 4))]
        + [pltpu.SemaphoreType.DMA((32,))] * 2,
        compiler_params=pltpu.CompilerParams(
            collective_id=1, has_side_effects=True, vmem_limit_bytes=56 * 1024 * 1024
        ),
        name="reduce_gradients",
    )(grad_rows, loss_row)
    return shard_total[:SHARD_ROWS].reshape(-1), jnp.sum(totals[0]), totals[1, 0, 0]


LOW = jnp.bfloat16
FULL = jnp.float32
TILE = 256
NEG = neg_big
ROOT_HALF = math.sqrt(0.5)
BELL = 1.0 / math.sqrt(2.0 * math.pi)


def dot_nn(left, right):
    return lax.dot_general(left, right, (((1,), (0,)), ((), ())), preferred_element_type=FULL)


def dot_nt(left, right):
    return lax.dot_general(left, right, (((1,), (1,)), ((), ())), preferred_element_type=FULL)


def dot_tn(left, right):
    return lax.dot_general(left, right, (((0,), (0,)), ((), ())), preferred_element_type=FULL)


def loop(count, body):
    def one(step, carry):
        body(step)
        return carry

    lax.fori_loop(0, count, one, 0)


def span(step, size):
    return pl.ds(pl.multiple_of(step * size, size), size)


def norm_parts(rows):
    average = jnp.mean(rows, axis=-1, keepdims=True)
    centered = rows - average
    scale = lax.rsqrt(jnp.mean(centered * centered, axis=-1, keepdims=True) + norm_eps)
    return centered * scale, scale


def norm_into(dst, src, gain, shift, rows, chunk):
    def one(step):
        at = span(step, chunk)
        unit, _ = norm_parts(src[at, :])
        dst[at, :] = (unit * gain + shift).astype(LOW)

    loop(rows // chunk, one)


def norm_back(dst, src, grad, residual, gain, gain_grad, shift_grad, rows, chunk):
    width = src.shape[1]

    def one(step, carry):
        at = span(step, chunk)
        unit, scale = norm_parts(src[at, :])
        upper = grad[at, :]
        gains = carry[0] + jnp.sum((upper * unit).reshape(chunk // 8, 8, width), axis=0)
        shifts = carry[1] + jnp.sum(upper.reshape(chunk // 8, 8, width), axis=0)
        upper = upper * gain
        lower = scale * (
            upper
            - jnp.mean(upper, axis=-1, keepdims=True)
            - unit * jnp.mean(upper * unit, axis=-1, keepdims=True)
        )
        if residual is not None:
            lower = lower + residual[at, :]
        dst[at, :] = lower
        return gains, shifts

    zero = jnp.zeros((8, width), FULL)
    gains, shifts = lax.fori_loop(0, rows // chunk, one, (zero, zero))
    gain_grad[...] = jnp.sum(gains, axis=0, keepdims=True)
    shift_grad[...] = jnp.sum(shifts, axis=0, keepdims=True)


def product_into(dst, left, right, columns, tile=TILE, residual=None):
    def one(step):
        at = span(step, tile)
        value = dot_nn(left[...], right[:, at])
        if residual is not None:
            value = value + residual[:, at]
        dst[:, at] = value.astype(dst.dtype)

    loop(columns // tile, one)


def product_t_into(dst, left, right, columns, tile=TILE):
    def one(step):
        at = span(step, tile)
        dst[:, at] = dot_nt(left[...], right[at, :]).astype(dst.dtype)

    loop(columns // tile, one)


def up_into(act, slope, left, w_up, columns, tile):
    def one(step):
        at = span(step, tile)
        hidden = dot_nn(left[...], w_up[:, at])
        share = 0.5 * (1.0 + lax.erf(hidden * ROOT_HALF))
        act[:, at] = (hidden * share).astype(LOW)
        slope[:, at] = share + hidden * (BELL * jnp.exp(-0.5 * hidden * hidden))

    loop(columns // tile, one)


def down_back_into(grad_pre, branch, w_down, slope, columns, tile):
    def one(step):
        at = span(step, tile)
        grad_pre[:, at] = (dot_nt(branch[...], w_down[at, :]) * slope[:, at]).astype(LOW)

    loop(columns // tile, one)


def weight_grad(out, out_row, left, right, turned, piled, stage, stage_sem):
    rows, columns = left.shape[1], right.shape[1]
    groups = columns // LANES
    steps = rows // TILE
    count = TILE * groups
    depth = left.shape[0]

    def copy(slot, step):
        return pltpu.make_async_copy(
            stage.at[slot, pl.ds(0, count)],
            out.at[pl.ds(pl.multiple_of(out_row + step * count, 512), count)],
            stage_sem.at[slot],
        )

    def one(step):
        slot = step % 2
        turned[:, pl.ds(0, depth)] = left[:, span(step, TILE)].T

        def across(tile):
            value = dot_nn(turned[:, pl.ds(0, depth)], right[:, span(tile, TILE)])
            for half in range(2):
                piled[pl.ds(tile * 2 + half, TILE, stride=groups), :] = value[
                    :, half * LANES : (half + 1) * LANES
                ]

        loop(columns // TILE, across)

        @pl.when(step >= 2)
        def _():
            copy(slot, step - 2).wait()

        def shrink(piece):
            at = span(piece, TILE)
            stage[slot, at, :] = piled[at, :].astype(LOW)

        loop(groups, shrink)
        copy(slot, step).start()

    loop(steps, one)
    for step in range(max(steps - 2, 0), steps):
        copy(step % 2, step).wait()


def head_masks(head_size, dtype):
    lane = lax.broadcasted_iota(jnp.int32, (1, LANES), 1) // head_size
    return [(lane == head).astype(dtype) for head in range(LANES // head_size)]


def stacked(rows, masks):
    return jnp.concatenate([rows * mask for mask in masks], axis=0)


def unstacked(rows, masks, size):
    total = None
    for index, mask in enumerate(masks):
        piece = rows[index * size : (index + 1) * size] * mask
        total = piece if total is None else total + piece
    return total


def soft_rows(queries, keys, allowed, scale):
    scores = jnp.where(allowed, dot_nt(queries, keys) * scale, NEG)
    scores = scores - jnp.max(scores, axis=-1, keepdims=True)
    powers = jnp.exp(scores)
    return powers / jnp.sum(powers, axis=-1, keepdims=True)


def attend_into(dst, qkv, rows, at, width, allowed, head_size):
    masks = head_masks(head_size, LOW)
    size = rows.size
    column = lambda part: pl.ds(pl.multiple_of(part * width + at * LANES, LANES), LANES)
    queries = stacked(qkv[rows, column(0)], masks)
    probs = soft_rows(queries, qkv[rows, column(1)], allowed, head_size**-0.5).astype(LOW)
    values = dot_nn(probs, qkv[rows, column(2)])
    dst[rows, column(0)] = unstacked(values, head_masks(head_size, FULL), size).astype(LOW)


def attend_back_into(dst, grad, qkv, rows, at, width, allowed, head_size):
    masks = head_masks(head_size, LOW)
    lanes = head_masks(head_size, FULL)
    size = rows.size
    scale = head_size**-0.5
    column = lambda part: pl.ds(pl.multiple_of(part * width + at * LANES, LANES), LANES)
    queries = stacked(qkv[rows, column(0)], masks)
    keys = qkv[rows, column(1)]
    probs = soft_rows(queries, keys, allowed, scale)
    grads = stacked(grad[rows, column(0)], masks)
    slopes = dot_nt(grads, qkv[rows, column(2)])
    slopes = probs * (slopes - jnp.sum(slopes * probs, axis=-1, keepdims=True))
    slopes = slopes.astype(LOW)
    dst[rows, column(0)] = (unstacked(dot_nn(slopes, keys), lanes, size) * scale).astype(LOW)
    dst[rows, column(1)] = (dot_tn(slopes, queries) * scale).astype(LOW)
    dst[rows, column(2)] = dot_tn(probs.astype(LOW), grads).astype(LOW)


def fetch(pairs, sems):
    for index, (src, dst) in enumerate(pairs):
        pltpu.make_async_copy(src, dst, sems.at[index]).start()

    def ready(index):
        src, dst = pairs[index]
        pltpu.make_async_copy(src, dst, sems.at[index]).wait()

    return ready


def position_table(columns, padded):
    half = columns // 2
    frequency = np.exp(
        np.float32(-math.log(10000.0)) * np.arange(half, dtype=np.float32) / np.float32(half)
    ).astype(np.float32)
    angles = np.arange(PATCHES, dtype=np.float32)[:, None] * frequency
    table = np.zeros((padded, columns), np.float32)
    table[:PATCHES] = np.concatenate(
        [np.sin(angles.astype(np.float64)), np.cos(angles.astype(np.float64))], axis=-1
    )
    return table


def split_low(table):
    parts, rest = [], table.astype(np.float64)
    for _ in range(3):
        part = rest.astype(ml_dtypes.bfloat16)
        parts.append(part)
        rest = rest - part.astype(np.float64)
    return np.stack(parts)


ROWS = 256
ENC_CHUNK = 64
FETCHED = ("embed", "enc_qkv", "enc_out", "enc_up", "enc_down", "project")


def encoder_forward_kernel(
    part_ref,
    visible_ref,
    segments_ref,
    patches_ref,
    table_ref,
    vecs_ref,
    w_embed_hbm,
    w_qkv_hbm,
    w_out_hbm,
    w_up_hbm,
    w_down_hbm,
    w_proj_hbm,
    vis_rows,
    embedded,
    normed_a,
    qkv_rows,
    attn_out,
    after_attn,
    normed_b,
    slope,
    hidden_act,
    encoded,
    final_enc,
    projected,
    row_facts,
    column_facts,
    w_embed,
    w_qkv,
    w_out,
    w_up,
    w_down,
    w_proj,
    sems,
):
    ready = fetch(
        [
            (w_embed_hbm, w_embed),
            (w_qkv_hbm, w_qkv),
            (w_out_hbm, w_out),
            (w_up_hbm, w_up),
            (w_down_hbm, w_down),
            (w_proj_hbm, w_proj),
        ],
        sems,
    )
    part = part_ref[0]
    total = segments_ref.shape[1]
    images = IMG_SEQ // 2
    spare = ROWS - images * VIS
    segments = segments_ref[...]
    image = segments - part * images
    inside = (image >= 0) & (image < images)
    padding = segments == IMG_SEQ
    flags = jnp.concatenate(
        [
            inside.astype(FULL),
            padding.astype(FULL),
            jnp.zeros((6, total), FULL),
        ],
        axis=0,
    ).astype(LOW)
    row = lax.broadcasted_iota(jnp.int32, (total, total), 0)
    column = lax.broadcasted_iota(jnp.int32, (total, total), 1)
    counts = dot_nn(flags, (row <= column).astype(FULL).astype(LOW)).astype(jnp.int32)
    inside_count, padding_count = counts[0:1], counts[1:2]
    padding_slot = padding_count - part * spare
    chosen = inside | (padding & (padding_slot >= 1) & (padding_slot <= spare))
    slot = inside_count + jnp.clip(padding_slot, 0, spare) - 1
    slot = jnp.where(chosen, slot, -1)
    select = (lax.broadcasted_iota(jnp.int32, (ROWS, total), 0) == slot).astype(FULL).astype(LOW)
    facts = jnp.concatenate(
        [segments.astype(FULL), patches_ref[...].astype(FULL), jnp.zeros((LANES - 2, total), FULL)],
        axis=0,
    ).astype(LOW)
    row_facts[...] = dot_nt(facts[0:16], select)
    column_facts[...] = dot_nt(select, facts)
    vis_rows[...] = dot_nn(select, visible_ref[...]).astype(LOW)
    patch = column_facts[:, 1:2].astype(jnp.int32)
    spot = (lax.broadcasted_iota(jnp.int32, (ROWS, table_ref.shape[1]), 1) == patch).astype(FULL).astype(LOW)
    embedded[...] = dot_nn(spot, table_ref[0]) + dot_nn(spot, table_ref[1]) + dot_nn(spot, table_ref[2])
    ready(0)
    product_into(embedded, vis_rows, w_embed, D, residual=embedded)
    vec = lambda index: vecs_ref[index : index + 1, :]
    norm_into(normed_a, embedded, vec(0), vec(1), ROWS, ENC_CHUNK)
    ready(1)
    product_into(qkv_rows, normed_a, w_qkv, 3 * D)
    allowed = column_facts[:, 0:1] == row_facts[0:1, :]
    allowed = jnp.concatenate([allowed.astype(FULL)] * 2, axis=0) > 0.5
    loop(
        D // LANES,
        lambda at: attend_into(attn_out, qkv_rows, pl.ds(0, ROWS), at, D, allowed, D // HEADS),
    )
    ready(2)
    product_into(after_attn, attn_out, w_out, D, residual=embedded)
    norm_into(normed_b, after_attn, vec(2), vec(3), ROWS, ENC_CHUNK)
    ready(3)
    up_into(hidden_act, slope, normed_b, w_up, FF, 512)
    ready(4)
    product_into(encoded, hidden_act, w_down, D, residual=after_attn)
    norm_into(final_enc, encoded, vec(4), vec(5), ROWS, ENC_CHUNK)
    ready(5)
    product_into(projected, final_enc, w_proj, DD)


def encoder_forward(part, visible_rows, segments, patch_ids, weights):
    hbm = pl.BlockSpec(memory_space=pl.ANY)
    vmem = pl.BlockSpec(memory_space=pltpu.VMEM)
    smem = pl.BlockSpec(memory_space=pltpu.SMEM)
    table = jnp.asarray(split_low(position_table(D, 256)))
    low, full = (lambda *s: jax.ShapeDtypeStruct(s, LOW)), (lambda *s: jax.ShapeDtypeStruct(s, FULL))
    mats = [weights[entry] for entry in FETCHED]
    return pl.pallas_call(
        encoder_forward_kernel,
        out_shape=[
            low(ROWS, PIX),
            full(ROWS, D),
            low(ROWS, D),
            low(ROWS, 3 * D),
            low(ROWS, D),
            full(ROWS, D),
            low(ROWS, D),
            full(ROWS, FF),
            low(ROWS, FF),
            full(ROWS, D),
            low(ROWS, D),
            low(ROWS, DD),
            full(16, ROWS),
            full(ROWS, LANES),
        ],
        in_specs=[smem] + [vmem] * 5 + [hbm] * 6,
        out_specs=[vmem] * 14,
        scratch_shapes=[pltpu.VMEM(mat.shape, LOW) for mat in mats] + [pltpu.SemaphoreType.DMA((6,))],
        compiler_params=pltpu.CompilerParams(vmem_limit_bytes=56 * 1024 * 1024),
        name="encoder_forward",
    )(part, visible_rows, segments, patch_ids, table, weights["enc_vecs"], *mats)


def encoder_backward_kernel(
    vis_rows,
    embedded,
    normed_a,
    qkv_rows,
    attn_out,
    after_attn,
    normed_b,
    slope,
    hidden_act,
    encoded,
    final_enc,
    row_facts,
    column_facts,
    grad_projected,
    vecs_ref,
    decoder_vecs,
    w_qkv_hbm,
    w_out_hbm,
    w_up_hbm,
    w_down_hbm,
    w_proj_hbm,
    partial_ref,
    flat_ref,
    w_qkv,
    w_out,
    w_up,
    w_down,
    w_proj,
    grad_rows,
    upper,
    branch,
    grad_pre,
    middle,
    grad_attn,
    grad_qkv,
    vec_grads,
    turned,
    piled,
    stage,
    vec_stage,
    stage_sem,
    sems,
):
    del partial_ref
    ready = fetch(
        [
            (w_proj_hbm, w_proj),
            (w_down_hbm, w_down),
            (w_up_hbm, w_up),
            (w_out_hbm, w_out),
            (w_qkv_hbm, w_qkv),
        ],
        sems,
    )
    entries = matrix_entries()
    vec = lambda index: vecs_ref[index : index + 1, :]
    grad_of = lambda index: vec_grads.at[pl.ds(index, 1), :]

    def emit(entry, left, right):
        weight_grad(flat_ref, entries[entry][0], left, right, turned, piled, stage, stage_sem)

    emit(5, final_enc, grad_projected)
    ready(0)
    product_t_into(upper, grad_projected, w_proj, D)
    norm_back(grad_rows, encoded, upper, None, vec(4), grad_of(4), grad_of(5), ROWS, ENC_CHUNK)
    branch[...] = grad_rows[...].astype(LOW)
    emit(4, hidden_act, branch)
    ready(1)
    down_back_into(grad_pre, branch, w_down, slope, FF, 512)
    emit(3, normed_b, grad_pre)
    ready(2)
    product_t_into(upper, grad_pre, w_up, D)
    norm_back(grad_rows, after_attn, upper, grad_rows, vec(2), grad_of(2), grad_of(3), ROWS, ENC_CHUNK)
    middle[...] = grad_rows[...].astype(LOW)
    emit(2, attn_out, middle)
    ready(3)
    product_t_into(grad_attn, middle, w_out, D)
    allowed = column_facts[:, 0:1] == row_facts[0:1, :]
    allowed = jnp.concatenate([allowed.astype(FULL)] * 2, axis=0) > 0.5
    loop(
        D // LANES,
        lambda at: attend_back_into(
            grad_qkv, grad_attn, qkv_rows, pl.ds(0, ROWS), at, D, allowed, D // HEADS
        ),
    )
    emit(1, normed_a, grad_qkv)
    ready(4)
    product_t_into(upper, grad_qkv, w_qkv, D)
    norm_back(grad_rows, embedded, upper, grad_rows, vec(0), grad_of(0), grad_of(1), ROWS, ENC_CHUNK)
    branch[...] = grad_rows[...].astype(LOW)
    emit(0, vis_rows, branch)
    groups = D // LANES
    for index in range(6):
        for group in range(groups):
            piled[pl.ds(index * groups + group, 1), :] = vec_grads[
                pl.ds(index, 1), pl.ds(group * LANES, LANES)
            ]
    base, groups = 6 * groups, DD // LANES
    for index in range(7):
        for group in range(groups):
            piled[pl.ds(base + index * groups + group, 1), :] = decoder_vecs[
                pl.ds(index, 1), pl.ds(group * LANES, LANES)
            ]
    vec_stage[...] = piled[pl.ds(0, 64), :].astype(LOW)
    copy = pltpu.make_async_copy(vec_stage, flat_ref.at[pl.ds(entries[11][0], 64)], stage_sem.at[0])
    copy.start()
    copy.wait()


def encoder_backward(saved, grad_projected, weights, decoder_vec_grads, flat):
    hbm = pl.BlockSpec(memory_space=pl.ANY)
    vmem = pl.BlockSpec(memory_space=pltpu.VMEM)
    mats = [weights[entry] for entry in FETCHED[1:]]
    inputs = [*saved, grad_projected, weights["enc_vecs"], decoder_vec_grads, *mats, flat]
    low, full = (lambda *s: pltpu.VMEM(s, LOW)), (lambda *s: pltpu.VMEM(s, FULL))
    return pl.pallas_call(
        encoder_backward_kernel,
        out_shape=jax.ShapeDtypeStruct(flat.shape, LOW),
        in_specs=[vmem] * 16 + [hbm] * 6,
        out_specs=hbm,
        input_output_aliases={len(inputs) - 1: 0},
        scratch_shapes=[low(*mat.shape) for mat in mats]
        + [
            full(ROWS, D),
            full(ROWS, D),
            low(ROWS, D),
            low(ROWS, FF),
            low(ROWS, D),
            low(ROWS, D),
            low(ROWS, 3 * D),
            full(8, D),
            low(TILE, ROWS),
            full(TILE * FF // LANES, LANES),
            low(2, TILE * FF // LANES, LANES),
            low(64, LANES),
            pltpu.SemaphoreType.DMA((2,)),
            pltpu.SemaphoreType.DMA((5,)),
        ],
        compiler_params=pltpu.CompilerParams(vmem_limit_bytes=60 * 1024 * 1024),
        name="encoder_backward",
    )(*inputs)


IMAGES = 5
IMG_ROWS = 208
DEC_ROWS = IMAGES * IMG_ROWS


def decoder_kernel(
    part_ref,
    projected,
    row_facts,
    targets_ref,
    table_ref,
    vecs_ref,
    w_qkv_hbm,
    w_out_hbm,
    w_up_hbm,
    w_down_hbm,
    w_pix_hbm,
    flat_ref,
    grad_projected,
    vec_grads,
    loss_ref,
    w_qkv,
    w_out,
    w_up,
    w_down,
    w_pix,
    dec_in,
    low_rows,
    qkv_rows,
    attn_out,
    after_attn,
    normed_b,
    slope,
    hidden_act,
    decoded,
    final_dec,
    grad_pred,
    upper,
    masked,
    turned,
    piled,
    stage,
    stage_sem,
    sems,
    *,
    mask_total,
):
    ready = fetch(
        [
            (w_qkv_hbm, w_qkv),
            (w_out_hbm, w_out),
            (w_up_hbm, w_up),
            (w_down_hbm, w_down),
            (w_pix_hbm, w_pix),
        ],
        sems,
    )
    entries = matrix_entries()
    vec = lambda index: vecs_ref[index : index + 1, :]
    grad_of = lambda index: vec_grads.at[pl.ds(index, 1), :]
    part = part_ref[0]
    image_of = row_facts[0:1, :].astype(jnp.int32) - part * IMAGES
    patch_of = row_facts[1:2, :].astype(jnp.int32)
    patch = lax.broadcasted_iota(jnp.int32, (IMG_ROWS, ROWS), 0)

    def selector(index):
        return ((patch_of == patch) & (image_of == index)).astype(FULL)

    def place(index):
        at = span(index, IMG_ROWS)
        select = selector(index)
        real = (patch[:, 0:1] < PATCHES).astype(FULL)
        hidden = real * (1.0 - jnp.sum(select, axis=-1, keepdims=True))
        masked[at, :] = jnp.broadcast_to(hidden, (IMG_ROWS, LANES))
        dec_in[at, :] = dot_nn(select.astype(LOW), projected[...]) + hidden * vec(6) + table_ref[...]

    loop(IMAGES, place)
    norm_into(low_rows, dec_in, vec(0), vec(1), DEC_ROWS, IMG_ROWS)
    ready(0)
    product_into(qkv_rows, low_rows, w_qkv, 3 * DD)
    head_size = DD // DHEADS
    heads = LANES // head_size
    allowed = lax.broadcasted_iota(jnp.int32, (heads * IMG_ROWS, IMG_ROWS), 1) < PATCHES
    groups = DD // LANES

    def attend(step):
        rows = span(step // groups, IMG_ROWS)
        attend_into(attn_out, qkv_rows, rows, step % groups, DD, allowed, head_size)

    loop(IMAGES * groups, attend)
    ready(1)
    product_into(after_attn, attn_out, w_out, DD, residual=dec_in)
    norm_into(normed_b, after_attn, vec(2), vec(3), DEC_ROWS, IMG_ROWS)
    ready(2)
    up_into(hidden_act, slope, normed_b, w_up, DFF, TILE)
    ready(3)
    product_into(decoded, hidden_act, w_down, DD, residual=after_attn)
    norm_into(final_dec, decoded, vec(4), vec(5), DEC_ROWS, IMG_ROWS)
    ready(4)
    loss_ref[...] = jnp.zeros_like(loss_ref)

    def compare(index):
        at = span(index, IMG_ROWS)
        image = pl.ds(0, PATCHES)
        goal, _ = norm_parts(targets_ref[index].astype(FULL))
        goal = jnp.concatenate([goal, jnp.zeros((IMG_ROWS - PATCHES, PIX), FULL)], axis=0)
        error = dot_nn(final_dec[at, :], w_pix[...]) - goal
        weight = masked[at, 0:1]
        rows = jnp.mean(error * error, axis=-1, keepdims=True) * weight
        loss_ref[...] = loss_ref[...] + jnp.sum(rows) * (1.0 / mask_total)
        grad_pred[at, :] = (weight * error * (2.0 / (PIX * mask_total))).astype(LOW)

    loop(IMAGES, compare)

    def emit(entry, left, right):
        weight_grad(flat_ref, entries[entry][0], left, right, turned, piled, stage, stage_sem)

    emit(10, final_dec, grad_pred)
    product_t_into(upper, grad_pred, w_pix, DD)
    grad_rows, branch = decoded, final_dec
    norm_back(grad_rows, decoded, upper, None, vec(4), grad_of(4), grad_of(5), DEC_ROWS, IMG_ROWS)
    branch[...] = grad_rows[...].astype(LOW)
    emit(9, hidden_act, branch)
    grad_pre = hidden_act
    down_back_into(grad_pre, branch, w_down, slope, DFF, TILE)
    emit(8, normed_b, grad_pre)
    product_t_into(upper, grad_pre, w_up, DD)
    norm_back(grad_rows, after_attn, upper, grad_rows, vec(2), grad_of(2), grad_of(3), DEC_ROWS, IMG_ROWS)
    branch[...] = grad_rows[...].astype(LOW)
    emit(7, attn_out, branch)
    grad_attn, grad_qkv = normed_b, grad_pre.at[:, pl.ds(0, 3 * DD)]
    product_t_into(grad_attn, branch, w_out, DD)

    def attend_back(step):
        rows = span(step // groups, IMG_ROWS)
        attend_back_into(grad_qkv, grad_attn, qkv_rows, rows, step % groups, DD, allowed, head_size)

    loop(IMAGES * groups, attend_back)
    emit(6, low_rows, grad_qkv)
    product_t_into(upper, grad_qkv, w_qkv, DD)
    norm_back(grad_rows, dec_in, upper, grad_rows, vec(0), grad_of(0), grad_of(1), DEC_ROWS, IMG_ROWS)
    upper[pl.ds(0, ROWS), :] = jnp.zeros((ROWS, DD), FULL)

    def collect(index, token):
        at = span(index, IMG_ROWS)
        rows = grad_rows[at, :]
        token = token + jnp.sum((rows * masked[at, 0:1]).reshape(IMG_ROWS // 8, 8, DD), axis=0)
        upper[pl.ds(0, ROWS), :] = upper[pl.ds(0, ROWS), :] + dot_tn(
            selector(index).astype(LOW), rows.astype(LOW)
        )
        return token

    token = lax.fori_loop(0, IMAGES, collect, jnp.zeros((8, DD), FULL))
    grad_of(6)[...] = jnp.sum(token, axis=0, keepdims=True)
    grad_projected[...] = upper[pl.ds(0, ROWS), :].astype(LOW)


def decoder_step(part, projected, row_facts, targets, weights, mask_total, flat_rows):
    hbm = pl.BlockSpec(memory_space=pl.ANY)
    vmem = pl.BlockSpec(memory_space=pltpu.VMEM)
    smem = pl.BlockSpec(memory_space=pltpu.SMEM)
    table = jnp.asarray(position_table(DD, IMG_ROWS))
    mats = [weights[entry] for entry in ("dec_qkv", "dec_out", "dec_up", "dec_down", "pixel")]
    low, full = (lambda *s: pltpu.VMEM(s, LOW)), (lambda *s: pltpu.VMEM(s, FULL))
    return pl.pallas_call(
        partial(decoder_kernel, mask_total=mask_total),
        out_shape=[
            jax.ShapeDtypeStruct((flat_rows, LANES), LOW),
            jax.ShapeDtypeStruct((ROWS, DD), LOW),
            jax.ShapeDtypeStruct((8, DD), FULL),
            jax.ShapeDtypeStruct((1, LANES), FULL),
        ],
        in_specs=[smem] + [vmem] * 5 + [hbm] * 5,
        out_specs=[hbm] + [vmem] * 3,
        scratch_shapes=[low(*mat.shape) for mat in mats]
        + [
            full(DEC_ROWS, DD),
            low(DEC_ROWS, DD),
            low(DEC_ROWS, 3 * DD),
            low(DEC_ROWS, DD),
            full(DEC_ROWS, DD),
            low(DEC_ROWS, DD),
            full(DEC_ROWS, DFF),
            low(DEC_ROWS, DFF),
            full(DEC_ROWS, DD),
            low(DEC_ROWS, DD),
            low(DEC_ROWS, PIX),
            full(DEC_ROWS, DD),
            full(DEC_ROWS, LANES),
            low(TILE, DEC_ROWS),
            full(TILE * DFF // LANES, LANES),
            low(2, TILE * DFF // LANES, LANES),
            pltpu.SemaphoreType.DMA((2,)),
            pltpu.SemaphoreType.DMA((5,)),
        ],
        compiler_params=pltpu.CompilerParams(vmem_limit_bytes=62 * 1024 * 1024),
        name="decoder_step",
    )(part, projected, row_facts, targets, table, weights["dec_vecs"], *mats)


def shards(visible, segments, patch_ids, targets, master, moment_one, moment_two, step_count):
    part = lax.axis_index("seq")
    in_kernels = master.shape[0] == SHARD_ROWS * LANES and lax.axis_size("dp") == 16
    if in_kernels:
        gathered = gather_weights(master.reshape(SHARD_ROWS, LANES))
        weights = {entry[0]: array for entry, array in zip(layout(), gathered)}
    else:
        full_flat = lax.all_gather(master.astype(LOW), ("seq", "dp"), axis=0, tiled=True)
        weights = unflatten(full_flat)
        weights["enc_vecs"] = weights["enc_vecs"].astype(FULL)
        weights["dec_vecs"] = weights["dec_vecs"].astype(FULL)
    visible_rows = lax.all_gather(visible[0], "seq", axis=0, tiled=True)
    part_row = part.reshape(1).astype(jnp.int32)
    mask_total = (PATCHES - VIS) * IMG_SEQ * visible.shape[0] * lax.axis_size("dp")
    *saved, projected, row_facts, column_facts = encoder_forward(
        part_row, visible_rows, segments, patch_ids, weights
    )
    flat_rows = master.shape[0] * lax.axis_size("dp") * lax.axis_size("seq") // LANES
    flat, grad_projected, decoder_vec_grads, loss_row = decoder_step(
        part_row, projected, row_facts, targets[0], weights, mask_total, flat_rows
    )
    flat = encoder_backward(
        [*saved, row_facts, column_facts], grad_projected, weights, decoder_vec_grads, flat
    )
    if in_kernels:
        grad_shard, square_sum, loss_sum = reduce_gradients(flat, loss_row)
    else:
        grad_flat = flat.astype(FULL).reshape(-1)
        grad_shard = lax.psum_scatter(grad_flat, ("seq", "dp"), scatter_dimension=0, tiled=True)
        square_sum, loss_sum = lax.psum(
            (jnp.sum(grad_shard * grad_shard), loss_row[0, 0]), ("seq", "dp")
        )
    grad_norm = jnp.sqrt(square_sum)
    clipped = grad_shard * jnp.minimum(1.0, clip_limit / (grad_norm + 1e-06))
    new_one = beta_mom * moment_one + (1.0 - beta_mom) * clipped
    new_two = beta_mom * moment_two + (1.0 - beta_mom) * clipped * clipped
    correction = 1.0 - jnp.power(jnp.float32(beta_mom), step_count[0].astype(jnp.float32))
    new_master = master - learn_rate * (
        new_one / correction / (jnp.sqrt(new_two / correction) + adam_eps) + decay_rate * master
    )
    return (new_one, new_two, new_master, new_master.astype(jnp.bfloat16), grad_norm, loss_sum)


def solution(mesh):
    in_specs = (
        P("dp", "seq", None),
        P("dp", None),
        P("dp", None),
        P("dp", "seq", None, None),
        P(("seq", "dp")),
        P(("seq", "dp")),
        P(("seq", "dp")),
        P(),
    )
    out_specs = (P(("seq", "dp")), P(("seq", "dp")), P(("seq", "dp")), P(("seq", "dp")), P(), P())
    return jax.shard_map(shards, mesh=mesh, in_specs=in_specs, out_specs=out_specs, check_vma=False)
```

```python
from functools import partial
import math

import jax
import jax.numpy as jnp
import ml_dtypes
import numpy as np
from jax import lax
from jax.experimental import pallas as pl
from jax.experimental.pallas import tpu as pltpu
from jax.sharding import PartitionSpec as P

D = 768
HEADS = 12
FF = 3072
DD = 512
DHEADS = 16
DFF = 2048
PIX = 768
PATCHES = 196
VIS = 49
IMG_SEQ = 10


norm_eps = 1e-06
neg_big = -1000000000.0
clip_limit = 0.0001
learn_rate = 0.03
decay_rate = 0.05
adam_eps = 1e-08
beta_mom = 0.5


def layout():
    return [
        ("embed", (PIX, D)),
        ("enc_qkv", (D, 3 * D)),
        ("enc_out", (D, D)),
        ("enc_up", (D, FF)),
        ("enc_down", (FF, D)),
        ("project", (D, DD)),
        ("dec_qkv", (DD, 3 * DD)),
        ("dec_out", (DD, DD)),
        ("dec_up", (DD, DFF)),
        ("dec_down", (DFF, DD)),
        ("pixel", (DD, PIX)),
        ("enc_vecs", (6, D)),
        ("dec_vecs", (7, DD)),
    ]


def unflatten(flat_vec):
    params = {}
    offset = 0
    for entry_name, entry_shape in layout():
        entry_size = entry_shape[0] * entry_shape[1]
        params[entry_name] = flat_vec[offset : offset + entry_size].reshape(entry_shape)
        offset += entry_size
    return params


LOW = jnp.bfloat16
FULL = jnp.float32
TILE = 256
TALL = 16
LANES = 128
NEG = neg_big
ROOT_HALF = math.sqrt(0.5)
BELL = 1.0 / math.sqrt(2.0 * math.pi)


def dot_nn(left, right):
    return lax.dot_general(left, right, (((1,), (0,)), ((), ())), preferred_element_type=FULL)


def dot_nt(left, right):
    return lax.dot_general(left, right, (((1,), (1,)), ((), ())), preferred_element_type=FULL)


def dot_tn(left, right):
    return lax.dot_general(left, right, (((0,), (0,)), ((), ())), preferred_element_type=FULL)


def loop(count, body):
    def one(step, carry):
        body(step)
        return carry

    lax.fori_loop(0, count, one, 0)


def span(step, size):
    return pl.ds(pl.multiple_of(step * size, size), size)


def norm_parts(rows):
    average = jnp.mean(rows, axis=-1, keepdims=True)
    centered = rows - average
    scale = lax.rsqrt(jnp.mean(centered * centered, axis=-1, keepdims=True) + norm_eps)
    return centered * scale, scale


def norm_into(dst, src, gain, shift, rows, chunk):
    def one(step):
        at = span(step, chunk)
        unit, _ = norm_parts(src[at, :])
        dst[at, :] = (unit * gain + shift).astype(LOW)

    loop(rows // chunk, one)


def norm_back(dst, src, grad, residual, gain, gain_grad, shift_grad, rows, chunk):
    width = src.shape[1]

    def one(step, carry):
        at = span(step, chunk)
        unit, scale = norm_parts(src[at, :])
        upper = grad[at, :]
        gains = carry[0] + jnp.sum((upper * unit).reshape(chunk // 8, 8, width), axis=0)
        shifts = carry[1] + jnp.sum(upper.reshape(chunk // 8, 8, width), axis=0)
        upper = upper * gain
        lower = scale * (
            upper
            - jnp.mean(upper, axis=-1, keepdims=True)
            - unit * jnp.mean(upper * unit, axis=-1, keepdims=True)
        )
        if residual is not None:
            lower = lower + residual[at, :]
        dst[at, :] = lower
        return gains, shifts

    zero = jnp.zeros((8, width), FULL)
    gains, shifts = lax.fori_loop(0, rows // chunk, one, (zero, zero))
    gain_grad[...] = jnp.sum(gains, axis=0, keepdims=True)
    shift_grad[...] = jnp.sum(shifts, axis=0, keepdims=True)


class Blocked:
    def __init__(self, ref, rows, columns):
        self.rows, self.groups = rows, columns // LANES
        self.ref = ref.reshape(rows // TALL, self.groups, TALL, LANES)

    def piece(self, first_row, rows, first_group, groups):
        tall = pl.ds(first_row // TALL, rows // TALL)
        parts = [
            self.ref[tall, first_group + index].reshape(rows, LANES) for index in range(groups)
        ]
        return parts[0] if groups == 1 else jnp.concatenate(parts, axis=1)

    def column_tile(self, step, tile):
        count = tile // LANES
        return self.piece(0, self.rows, step * count, count)

    def row_tile(self, step, tile):
        return self.piece(step * tile, tile, 0, self.groups)


def product_into(dst, left, right, columns, tile=TILE, residual=None):
    def one(step):
        at = span(step, tile)
        value = dot_nn(left[...], right.column_tile(step, tile))
        if residual is not None:
            value = value + residual[:, at]
        dst[:, at] = value.astype(dst.dtype)

    loop(columns // tile, one)


def product_t_into(dst, left, right, columns, tile=TILE):
    def one(step):
        dst[:, span(step, tile)] = dot_nt(left[...], right.row_tile(step, tile)).astype(dst.dtype)

    loop(columns // tile, one)


def up_into(act, slope, left, w_up, columns, tile):
    def one(step):
        at = span(step, tile)
        hidden = dot_nn(left[...], w_up.column_tile(step, tile))
        share = 0.5 * (1.0 + lax.erf(hidden * ROOT_HALF))
        act[:, at] = (hidden * share).astype(LOW)
        slope[:, at] = share + hidden * (BELL * jnp.exp(-0.5 * hidden * hidden))

    loop(columns // tile, one)


def down_back_into(grad_pre, branch, w_down, slope, columns, tile):
    def one(step):
        at = span(step, tile)
        grad_pre[:, at] = (dot_nt(branch[...], w_down.row_tile(step, tile)) * slope[:, at]).astype(LOW)

    loop(columns // tile, one)


def weight_grad(out, out_tile, left, right, turned, stage, stage_sem):
    rows, columns = left.shape[1], right.shape[1]
    groups = columns // LANES
    steps = rows // TILE
    high = TILE // TALL
    count = high * groups

    def copy(slot, step):
        return pltpu.make_async_copy(
            stage.at[slot, pl.ds(0, count)],
            out.at[pl.ds(out_tile + step * count, count)],
            stage_sem.at[slot],
        )

    def one(step):
        slot = step % 2
        turned[...] = left[:, span(step, TILE)].T

        @pl.when(step >= 2)
        def _():
            copy(slot, step - 2).wait()

        tiles = stage.at[slot, pl.ds(0, count)].reshape(high, groups, TALL, LANES)

        def across(tile):
            value = dot_nn(turned[...], right[:, span(tile, TILE)]).astype(LOW)
            for half in range(2):
                tiles[:, tile * 2 + half] = value[:, half * LANES : (half + 1) * LANES].reshape(
                    high, TALL, LANES
                )

        loop(columns // TILE, across)
        copy(slot, step).start()

    loop(steps, one)
    for step in range(max(steps - 2, 0), steps):
        copy(step % 2, step).wait()


def head_masks(head_size, dtype):
    lane = lax.broadcasted_iota(jnp.int32, (1, LANES), 1) // head_size
    return [(lane == head).astype(dtype) for head in range(LANES // head_size)]


def stacked(rows, masks):
    return jnp.concatenate([rows * mask for mask in masks], axis=0)


def unstacked(rows, masks, size):
    total = None
    for index, mask in enumerate(masks):
        piece = rows[index * size : (index + 1) * size] * mask
        total = piece if total is None else total + piece
    return total


def soft_rows(queries, keys, allowed, scale):
    scores = jnp.where(allowed, dot_nt(queries, keys) * scale, NEG)
    scores = scores - jnp.max(scores, axis=-1, keepdims=True)
    powers = jnp.exp(scores)
    return powers / jnp.sum(powers, axis=-1, keepdims=True)


def attend_into(dst, qkv, rows, at, width, allowed, head_size):
    masks = head_masks(head_size, LOW)
    size = rows.size
    column = lambda part: pl.ds(pl.multiple_of(part * width + at * LANES, LANES), LANES)
    queries = stacked(qkv[rows, column(0)], masks)
    probs = soft_rows(queries, qkv[rows, column(1)], allowed, head_size**-0.5).astype(LOW)
    values = dot_nn(probs, qkv[rows, column(2)])
    dst[rows, column(0)] = unstacked(values, head_masks(head_size, FULL), size).astype(LOW)


def attend_back_into(dst, grad, qkv, rows, at, width, allowed, head_size):
    masks = head_masks(head_size, LOW)
    lanes = head_masks(head_size, FULL)
    size = rows.size
    scale = head_size**-0.5
    column = lambda part: pl.ds(pl.multiple_of(part * width + at * LANES, LANES), LANES)
    queries = stacked(qkv[rows, column(0)], masks)
    keys = qkv[rows, column(1)]
    probs = soft_rows(queries, keys, allowed, scale)
    grads = stacked(grad[rows, column(0)], masks)
    slopes = dot_nt(grads, qkv[rows, column(2)])
    slopes = probs * (slopes - jnp.sum(slopes * probs, axis=-1, keepdims=True))
    slopes = slopes.astype(LOW)
    dst[rows, column(0)] = (unstacked(dot_nn(slopes, keys), lanes, size) * scale).astype(LOW)
    dst[rows, column(1)] = (dot_tn(slopes, queries) * scale).astype(LOW)
    dst[rows, column(2)] = dot_tn(probs.astype(LOW), grads).astype(LOW)


def entry_tiles():
    tiles, offset = {}, 0
    for entry_name, (rows, columns) in layout():
        tiles[entry_name] = (offset // (TALL * LANES), rows, columns)
        offset += rows * columns
    tiles["vecs"] = (tiles["enc_vecs"][0], 4 * TALL, LANES)
    return tiles


def vec_reader(buffer, first, groups):
    rows = buffer[...].reshape(4 * TALL, LANES).astype(FULL)

    def vec(index):
        start = first + index * groups
        return jnp.concatenate([rows[start + g : start + g + 1] for g in range(groups)], axis=1)

    return vec


def fetch(flat, names, buffers, sems):
    tiles = entry_tiles()

    def build(index):
        start, rows, columns = tiles[names[index]]
        count = rows * columns // (TALL * LANES)
        return pltpu.make_async_copy(flat.at[pl.ds(start, count)], buffers[index], sems.at[index])

    for index in range(len(names)):
        build(index).start()

    def ready(index):
        build(index).wait()
        _, rows, columns = tiles[names[index]]
        return Blocked(buffers[index], rows, columns)

    return ready


def tile_buffers(names):
    tiles = entry_tiles()
    return [
        pltpu.VMEM((tiles[entry][1] * tiles[entry][2] // (TALL * LANES), TALL, LANES), LOW)
        for entry in names
    ]


def position_table(columns, padded):
    half = columns // 2
    frequency = np.exp(
        np.float32(-math.log(10000.0)) * np.arange(half, dtype=np.float32) / np.float32(half)
    ).astype(np.float32)
    angles = np.arange(PATCHES, dtype=np.float32)[:, None] * frequency
    table = np.zeros((padded, columns), np.float32)
    table[:PATCHES] = np.concatenate(
        [np.sin(angles.astype(np.float64)), np.cos(angles.astype(np.float64))], axis=-1
    )
    return table


def split_low(table):
    parts, rest = [], table.astype(np.float64)
    for _ in range(3):
        part = rest.astype(ml_dtypes.bfloat16)
        parts.append(part)
        rest = rest - part.astype(np.float64)
    return np.stack(parts)


MESH = pl.DeviceIdType.MESH
A_HALF = 1104
A_ROWS = 2 * A_HALF
B_HALF = 320
B_ROWS = 2 * B_HALF
SHARD_ROWS = 2834
PAD_ROWS = A_ROWS + B_ROWS
B_TRUE = SHARD_ROWS - A_ROWS
HALO = 384
WIDE_ROWS = SHARD_ROWS + 2 * HALO
PARTS = {
    "a1": (0, A_HALF),
    "a2": (A_HALF, A_HALF),
    "b": (A_ROWS, B_ROWS),
    "b1": (A_ROWS, B_HALF),
    "b2": (A_ROWS + B_HALF, B_HALF),
}
TRUE_PARTS = {**PARTS, "b": (A_ROWS, B_TRUE), "b2": (A_ROWS + B_HALF, B_TRUE - B_HALF)}
SLOTS = {"a1": 0, "a2": 1, "b": 2, "b1": 2, "b2": 3}
COLUMNS = "oxyd"
ARRIVALS = {
    0: (
        12, 22, 102, 10, 20, 100, 11, 21, 101, 33, 34, 112, 122, 30, 110, 202, 120, 31, 200, 121,
        111, 201, 132, 130, 210, 212, 220, 131, 222, 302, 221, 211, 300, 230, 231, 301, 320, 310,
        232, 312, 321, 311, 322, 332, 330, 331,
    ),
    1: (
        2, 112, 122, 202, 0, 110, 120, 200, 1, 111, 121, 201, 133, 134, 12, 212, 22, 222, 20, 10,
        32, 302, 130, 210, 300, 220, 11, 301, 232, 21, 131, 312, 221, 211, 322, 332, 30, 310,
        230, 311, 320, 31, 321, 231, 330, 331,
    ),
}


def item_of(code):
    return code // 100, COLUMNS[code // 10 % 10], list(PARTS)[code % 10]


def own_item(inner, part):
    return 100 * inner + list(PARTS).index(part)


class Place:
    def __init__(self):
        self.core = lax.axis_index("seq")
        self.chip = lax.axis_index("dp")
        chip = self.chip
        self.z = chip // 4
        y, x = (chip // 2) % 2, chip % 2
        self.col = chip % 4
        self.col_x = self.col + 1 - 2 * x
        self.col_y = self.col + 2 - 4 * y
        self.col_d = self.col_x + 2 - 4 * y
        self.columns = {"o": self.col, "x": self.col_x, "y": self.col_y, "d": self.col_d}
        self.side = self.z // 2
        sign = 1 - 2 * self.side
        self.inner = self.z + self.side * (3 - 2 * self.z)
        self.me = 16 * self.core + chip
        self.devices = {
            "x": (self.core, 4 * self.z + self.col_x),
            "y": (self.core, 4 * self.z + self.col_y),
            "far": (self.core, chip + 4 * sign),
            "near": (self.core, chip - 4 * sign * self.inner),
            "core": (1 - self.core, chip),
            "next": self.ring(1),
            "back": self.ring(31),
        }

    def ring(self, step):
        peer = (self.me + step) % 32
        return (peer // 16, peer % 16)

    def plane(self, mirrored):
        return mirrored + self.side * (3 - 2 * mirrored)

    def greet(self):
        barrier = pltpu.get_barrier_semaphore()
        for link in ("x", "y", "far", "core", "next", "back"):
            pl.semaphore_signal(
                barrier, inc=1, device_id=self.devices[link], device_id_type=MESH
            )

        @pl.when(self.inner == 1)
        def _():
            pl.semaphore_signal(
                barrier, inc=1, device_id=self.devices["near"], device_id_type=MESH
            )

        pl.semaphore_wait(barrier, 6 + self.inner)


class Outbox:
    def __init__(self):
        self.sent = []

    def send(self, src, dst, send_sem, recv_sem, device):
        def build():
            return pltpu.make_async_remote_copy(
                src_ref=src,
                dst_ref=dst,
                send_sem=send_sem,
                recv_sem=recv_sem,
                device_id=device,
                device_id_type=MESH,
            )

        build().start()
        self.sent.append(build)

    def finish(self):
        for build in self.sent:
            build().wait_send()


def arrived(ref, sem, device):
    pltpu.make_async_remote_copy(
        src_ref=ref, dst_ref=ref, send_sem=sem, recv_sem=sem, device_id=device, device_id_type=MESH
    ).wait_recv()


def by_place(at, body):
    for inner in (0, 1):
        pl.when(at.inner == inner)(partial(body, inner))


def onward(inner, item):
    mirrored, column, part = item_of(item)
    line = ["far", "near"][: 1 + inner]
    if mirrored != inner:
        line = [] if inner == 0 else ["far" if mirrored == 0 else "near"]
    if part[0] == "a":
        if column == "o":
            return [(link, part) for link in [*line, "x", "y"]]
        if (column, part) in (("x", "a1"), ("y", "a2")):
            return [("y" if column == "x" else "x", part)]
        return []
    links = [(link, "b") for link in line]
    if mirrored == inner:
        links = {
            "o": [("x", "b"), ("y", "b")],
            "x": [("y", "b1")],
            "y": [("x", "b2")],
            "d": [],
        }[column] + links
    return links


def gather_exchange(at, flat, source, recv, core_recv, sends, core_send):
    def block(chip, part, core):
        first, size = TRUE_PARTS[part]
        return flat.at[pl.ds((core * 16 + chip) * SHARD_ROWS + first, size)]

    def body(inner):
        out = Outbox()
        diagonal = []

        def pass_on(item):
            mirrored, column, part = item_of(item)
            chip = 4 * at.plane(mirrored) + at.columns[column]
            own = mirrored == inner and column == "o"
            links = onward(inner, item)
            if mirrored == inner and column == "d" and part[0] == "b":
                diagonal.append(part)
                links = links if len(diagonal) == 2 else []
            for link, piece in [*links, ("core", part)]:
                slot = SLOTS[piece]
                ref = block(chip, piece, at.core)
                sent, got = (core_send, core_recv) if link == "core" else (sends[link], recv)
                out.send(
                    source(piece) if own else ref,
                    ref,
                    sent.at[chip, slot],
                    got.at[chip, slot],
                    at.devices[link],
                )

        for part in ("b", "a1", "a2"):
            pass_on(own_item(inner, part))
        for item in ARRIVALS[inner]:
            mirrored, column, part = item_of(item)
            chip = 4 * at.plane(mirrored) + at.columns[column]
            arrived(block(chip, part, at.core), recv.at[chip, SLOTS[part]], at.devices["x"])
            pass_on(item)
        for part in ("b", "a1", "a2"):
            arrived(
                block(at.chip, part, 1 - at.core),
                core_recv.at[at.chip, SLOTS[part]],
                at.devices["x"],
            )
        for item in ARRIVALS[inner]:
            mirrored, column, part = item_of(item)
            chip = 4 * at.plane(mirrored) + at.columns[column]
            ref = block(chip, part, 1 - at.core)
            arrived(ref, core_recv.at[chip, SLOTS[part]], at.devices["x"])
        out.finish()

    by_place(at, body)


def entry_blocks(me, body):
    first = me * SHARD_ROWS
    offset = 0
    for _, (rows, columns) in layout()[:11]:
        groups, blocks = columns // LANES, rows // TALL
        unit = TALL * groups
        low = jnp.minimum(jnp.maximum(first - offset, 0) // unit, blocks)
        high = jnp.minimum(
            (jnp.maximum(first + SHARD_ROWS - offset, 0) + unit - 1) // unit, blocks
        )

        def one(block, carry, offset=offset, unit=unit, groups=groups):
            body(offset + block * unit, groups)
            return carry

        lax.fori_loop(low, high, one, 0)
        offset += unit * blocks
    return offset


VEC_ROWS = 64


def gather_kernel(master_ref, flat_ref, wide, turned, own_sem, halo_send, halo_recv, *sems):
    recv, core_recv, send_x, send_y, send_far, send_near, core_send = sems
    at = Place()
    first = at.me * SHARD_ROWS
    skew = (at.me * 2) % TALL
    own = pltpu.make_async_copy(master_ref, wide.at[pl.ds(HALO, SHARD_ROWS)], own_sem.at[0])
    own.start()
    at.greet()
    out = Outbox()
    tail = wide.at[pl.ds(HALO + SHARD_ROWS, HALO)]
    head = wide.at[pl.ds(0, HALO)]
    out.send(
        master_ref.at[pl.ds(0, HALO)],
        tail,
        halo_send.at[0],
        halo_recv.at[0],
        at.devices["back"],
    )
    out.send(
        master_ref.at[pl.ds(SHARD_ROWS - HALO, HALO)],
        head,
        halo_send.at[1],
        halo_recv.at[1],
        at.devices["next"],
    )
    own.wait()
    arrived(tail, halo_recv.at[0], at.devices["x"])
    arrived(head, halo_recv.at[1], at.devices["x"])

    def turn(row, groups):
        start = row - first + HALO
        spot = row - (first - skew) + HALO
        for group in range(groups):
            turned[pl.ds(pl.multiple_of(spot + group * TALL, TALL), TALL), :] = wide[
                pl.ds(start + group, TALL, stride=groups), :
            ].astype(LOW)

    vec_start = entry_blocks(at.me, turn)

    @pl.when(at.me == 31)
    def _():
        start = vec_start - 31 * SHARD_ROWS + HALO
        spot = start + (31 * 2) % TALL
        turned[pl.ds(spot, VEC_ROWS), :] = wide[pl.ds(start, VEC_ROWS), :].astype(LOW)

    mine = pltpu.make_async_copy(
        turned.at[pl.ds(HALO + skew, SHARD_ROWS)],
        flat_ref.at[pl.ds(first, SHARD_ROWS)],
        own_sem.at[1],
    )
    mine.start()

    def source(part):
        start, size = TRUE_PARTS[part]
        return turned.at[pl.ds(HALO + skew + start, size)]

    sends = {"x": send_x, "y": send_y, "far": send_far, "near": send_near}
    gather_exchange(at, flat_ref, source, recv, core_recv, sends, core_send)
    mine.wait()
    out.finish()


def gather_weights(master_rows):
    hbm = pl.BlockSpec(memory_space=pl.ANY)
    pairs = pltpu.SemaphoreType.DMA((2,))
    return pl.pallas_call(
        gather_kernel,
        out_shape=jax.ShapeDtypeStruct((32 * SHARD_ROWS, LANES), LOW),
        in_specs=[hbm],
        out_specs=hbm,
        scratch_shapes=[
            pltpu.VMEM((WIDE_ROWS + 6, LANES), FULL),
            pltpu.VMEM((WIDE_ROWS + 30, LANES), LOW),
            pairs,
            pairs,
            pairs,
        ]
        + [pltpu.SemaphoreType.DMA((16, 4))] * 7,
        compiler_params=pltpu.CompilerParams(
            collective_id=0, has_side_effects=True, vmem_limit_bytes=16 * 1024 * 1024
        ),
        name="gather_weights",
    )(master_rows)


def add_into(dst, start, terms, size, chunk):
    def one(step):
        row = step * chunk
        total = None
        for ref, first in terms:
            piece = ref[pl.ds(pl.multiple_of(first + row, TALL), chunk), :].astype(FULL)
            total = piece if total is None else total + piece
        dst[pl.ds(pl.multiple_of(start + row, TALL), chunk), :] = total.astype(dst.dtype)

    loop(size // chunk, one)


def reduce_kernel(
    grad_ref,
    loss_ref,
    shard_ref,
    total_ref,
    own,
    theirs,
    from_x,
    from_y,
    pass_x,
    pass_y,
    far_a,
    near_a,
    far_b,
    near_b,
    wide,
    plain,
    scalars,
    load_sem,
    core_send,
    core_recv,
    send_x,
    send_y,
    send_far,
    send_near,
    recv_x,
    recv_y,
    recv_far,
    recv_near,
    halo_send,
    halo_recv,
    tiny_send,
    tiny_recv,
):
    at = Place()
    tail = pl.ds(SHARD_ROWS - 2, TALL)
    for index in range(16):
        own[index, tail, :] = jnp.zeros((TALL, LANES), LOW)
        theirs[index, tail, :] = jnp.zeros((TALL, LANES), LOW)
    body = pl.ds(0, SHARD_ROWS)

    def shard_rows(core, chip):
        return grad_ref.at[pl.ds((core * 16 + chip) * SHARD_ROWS, SHARD_ROWS)]

    def load(chip):
        return pltpu.make_async_copy(
            shard_rows(at.core, chip), own.at[chip, body], load_sem.at[chip]
        )

    at.greet()
    pairs = Outbox()
    for mirrored in (3, 2, 1 - at.inner, at.inner):
        for column in ("d", "y", "x", "o"):
            chip = 4 * at.plane(mirrored) + at.columns[column]
            pairs.send(
                shard_rows(1 - at.core, chip),
                theirs.at[chip, body],
                core_send.at[chip],
                core_recv.at[chip],
                at.devices["core"],
            )
            load(chip).start()
    sends = {"x": send_x, "y": send_y, "far": send_far, "near": send_near}
    recvs = {"x": recv_x, "y": recv_y, "far": recv_far, "near": recv_near}
    relayed = {"x": pass_x, "y": pass_y}
    direct = {"x": from_x, "y": from_y}
    lines = {"far": (far_a, far_b), "near": (near_a, near_b)}

    def reduce_parts(inner):
        out = Outbox()
        paired, joined = set(), set()

        def pair(chip, key):
            if key in paired:
                return
            paired.add(key)
            load(chip).wait()
            arrived(theirs.at[chip, body], core_recv.at[chip], at.devices["x"])
            add_into(own.at[chip], 0, [(own.at[chip], 0), (theirs.at[chip], 0)], PAD_ROWS, 32)

        def landing(link, plane, chip, part, relay):
            first, size = PARTS[part]
            if link in lines and part == "b":
                return lines[link][1].at[chip], 0, size, (chip, SLOTS[part])
            if link in lines:
                return lines[link][0].at[plane], first, size, (chip, SLOTS[part])
            if relay:
                return relayed[link].at[plane], first, size, (plane, 3 + (part[0] == "b"))
            return direct[link].at[plane], first, size, (plane, SLOTS[part])

        def step(item):
            mirrored, column, part = item_of(item)
            plane = at.plane(mirrored)
            chip = 4 * plane + at.columns[column]
            pair(chip, (mirrored, column))
            first, size = PARTS[part]
            terms = []
            links = onward(inner, item)
            if mirrored == inner and column == "d" and part[0] == "b":
                links = [] if joined else links
                joined.add(part)
            own_item = mirrored == inner and column == "o"
            for link, piece in links:
                relay = column in ("x", "y")
                buffer, start, count, index = landing(link, plane, chip, piece, relay)
                arrived(buffer.at[pl.ds(start, count)], recvs[link].at[*index], at.devices["x"])
                terms.append((buffer, start, count))
            if own_item:
                whole = [(own.at[chip], first)] + [(buffer, start) for buffer, start, _ in terms]
                if part == "b":
                    add_into(plain, 0, whole, size, size // 4)
                    wide[pl.ds(HALO + A_ROWS, B_TRUE), :] = plain[pl.ds(0, B_TRUE), :]
                else:
                    add_into(wide, HALO + first, whole, size, size // 3)
                return
            full_size = B_ROWS if part[0] == "b" else size
            full_first = PARTS["b"][0] if part[0] == "b" else first
            whole = [(buffer, start) for buffer, start, count in terms if count == full_size]
            halves = [(buffer, start, count) for buffer, start, count in terms if count != full_size]
            if whole:
                add_into(
                    own.at[chip],
                    full_first,
                    [(own.at[chip], full_first), *whole],
                    full_size,
                    full_size // (4 if part[0] == "b" else 3),
                )
            for buffer, start, count in halves:
                add_into(
                    own.at[chip], start, [(own.at[chip], start), (buffer, start)], count, count // 2
                )
            if column == "o" or (part == "b" and mirrored != inner):
                link = "near" if inner == 1 and mirrored == 0 else "far"
                target = "near" if inner == 0 else "far"
                buffer, start, _, index = landing(target, plane, chip, part, False)
                arrive_sem = recvs[target]
            else:
                link = {"x": "x", "y": "y", "d": "y" if part in ("a1", "b1") else "x"}[column]
                buffer, start, _, index = landing(link, plane, chip, part, column == "d")
                arrive_sem = recvs[link]
            out.send(
                own.at[chip, pl.ds(first, size)],
                buffer.at[pl.ds(start, size)],
                sends[link].at[*index],
                arrive_sem.at[*index],
                at.devices[link],
            )

        for item in reversed(ARRIVALS[inner]):
            step(item)
        for part in ("a2", "a1", "b"):
            step(own_item(inner, part))
        out.finish()

    by_place(at, reduce_parts)
    pairs.finish()

    halo = Outbox()
    head, after = wide.at[pl.ds(0, HALO)], wide.at[pl.ds(HALO + SHARD_ROWS, HALO)]
    halo.send(
        wide.at[pl.ds(HALO, HALO)], after, halo_send.at[0], halo_recv.at[0], at.devices["back"]
    )
    halo.send(
        wide.at[pl.ds(SHARD_ROWS, HALO)], head, halo_send.at[1], halo_recv.at[1], at.devices["next"]
    )
    whole_steps = SHARD_ROWS // 32

    def squares(index, carry):
        piece = wide[pl.ds(pl.multiple_of(HALO + index * 32, 8), 32), :]
        piece = piece * piece
        return carry + jnp.sum(piece.reshape(4, 8, LANES), axis=0)

    square = lax.fori_loop(0, whole_steps, squares, jnp.zeros((8, LANES), FULL))
    rest = wide[pl.ds(HALO + whole_steps * 32, SHARD_ROWS - whole_steps * 32), :]
    square = square + 0.125 * jnp.sum(rest * rest, axis=0, keepdims=True)
    scalars[at.me, 0] = square
    scalars[at.me, 1] = jnp.broadcast_to(loss_ref[...], (8, LANES))
    for index in range(1, 32):
        halo.send(
            scalars.at[at.me],
            scalars.at[at.me],
            tiny_send.at[index],
            tiny_recv.at[at.me],
            at.ring(index),
        )
    arrived(after, halo_recv.at[0], at.devices["x"])
    arrived(head, halo_recv.at[1], at.devices["x"])

    def turn_back(row, groups):
        start = row - at.me * SHARD_ROWS + HALO
        for group in range(groups):
            plain[pl.ds(start + group, TALL, stride=groups), :] = wide[
                pl.ds(start + group * TALL, TALL), :
            ]

    vec_start = entry_blocks(at.me, turn_back)

    @pl.when(at.me == 31)
    def _():
        spot = pl.ds(vec_start - 31 * SHARD_ROWS + HALO, VEC_ROWS)
        plain[spot, :] = wide[spot, :]

    shard_ref[...] = plain[pl.ds(HALO, SHARD_ROWS), :]
    for index in range(1, 32):
        peer = (at.me + index) % 32
        arrived(scalars.at[peer], tiny_recv.at[peer], at.devices["x"])
    total_ref[...] = jnp.sum(scalars[...], axis=0)
    halo.finish()


def reduce_gradients(grad_rows, loss_row):
    hbm = pl.BlockSpec(memory_space=pl.ANY)
    vmem = pl.BlockSpec(memory_space=pltpu.VMEM)
    dma = pltpu.SemaphoreType.DMA
    shard_total, totals = pl.pallas_call(
        reduce_kernel,
        out_shape=[
            jax.ShapeDtypeStruct((SHARD_ROWS, LANES), FULL),
            jax.ShapeDtypeStruct((2, 8, LANES), FULL),
        ],
        in_specs=[hbm, vmem],
        out_specs=[vmem, vmem],
        scratch_shapes=[pltpu.VMEM((16, PAD_ROWS, LANES), LOW)] * 2
        + [pltpu.VMEM((4, PAD_ROWS, LANES), LOW)] * 4
        + [pltpu.VMEM((4, A_ROWS, LANES), LOW)] * 2
        + [pltpu.VMEM((16, B_ROWS, LANES), LOW)] * 2
        + [pltpu.VMEM((WIDE_ROWS + 6, LANES), FULL)] * 2
        + [pltpu.VMEM((32, 2, 8, LANES), FULL)]
        + [dma((16,))] * 3
        + [dma((4, 5))] * 2
        + [dma((16, 4))] * 2
        + [dma((4, 5))] * 2
        + [dma((16, 4))] * 2
        + [dma((2,))] * 2
        + [dma((32,))] * 2,
        compiler_params=pltpu.CompilerParams(
            collective_id=1, has_side_effects=True, vmem_limit_bytes=56 * 1024 * 1024
        ),
        name="reduce_gradients",
    )(grad_rows, loss_row)
    return shard_total.reshape(-1), jnp.sum(totals[0]), totals[1, 0, 0]


ROWS = 256
ENC_CHUNK = 64
FETCHED = ("vecs", "embed", "enc_qkv", "enc_out", "enc_up", "enc_down", "project")
BACKWARD_FETCHED = ("vecs", "project", "enc_down", "enc_up", "enc_out", "enc_qkv")


def encoder_forward_kernel(
    part_ref,
    visible_ref,
    segments_ref,
    patches_ref,
    table_ref,
    flat_ref,
    vis_rows,
    embedded,
    normed_a,
    qkv_rows,
    attn_out,
    after_attn,
    normed_b,
    slope,
    hidden_act,
    encoded,
    final_enc,
    projected,
    row_facts,
    column_facts,
    sems,
    *buffers,
):
    ready = fetch(flat_ref, FETCHED, buffers, sems)
    part = part_ref[0]
    total = segments_ref.shape[1]
    images = IMG_SEQ // 2
    spare = ROWS - images * VIS
    segments = segments_ref[...]
    image = segments - part * images
    inside = (image >= 0) & (image < images)
    padding = segments == IMG_SEQ
    flags = jnp.concatenate(
        [
            inside.astype(FULL),
            padding.astype(FULL),
            jnp.zeros((6, total), FULL),
        ],
        axis=0,
    ).astype(LOW)
    row = lax.broadcasted_iota(jnp.int32, (total, total), 0)
    column = lax.broadcasted_iota(jnp.int32, (total, total), 1)
    counts = dot_nn(flags, (row <= column).astype(FULL).astype(LOW)).astype(jnp.int32)
    inside_count, padding_count = counts[0:1], counts[1:2]
    padding_slot = padding_count - part * spare
    chosen = inside | (padding & (padding_slot >= 1) & (padding_slot <= spare))
    slot = inside_count + jnp.clip(padding_slot, 0, spare) - 1
    slot = jnp.where(chosen, slot, -1)
    select = (lax.broadcasted_iota(jnp.int32, (ROWS, total), 0) == slot).astype(FULL).astype(LOW)
    facts = jnp.concatenate(
        [segments.astype(FULL), patches_ref[...].astype(FULL), jnp.zeros((LANES - 2, total), FULL)],
        axis=0,
    ).astype(LOW)
    row_facts[...] = dot_nt(facts[0:16], select)
    column_facts[...] = dot_nt(select, facts)
    vis_rows[...] = dot_nn(select, visible_ref[...]).astype(LOW)
    patch = column_facts[:, 1:2].astype(jnp.int32)
    spot = (lax.broadcasted_iota(jnp.int32, (ROWS, table_ref.shape[1]), 1) == patch).astype(FULL).astype(LOW)
    embedded[...] = dot_nn(spot, table_ref[0]) + dot_nn(spot, table_ref[1]) + dot_nn(spot, table_ref[2])
    w_embed = ready(1)
    product_into(embedded, vis_rows, w_embed, D, residual=embedded)
    ready(0)
    vec = vec_reader(buffers[0], 0, D // LANES)
    norm_into(normed_a, embedded, vec(0), vec(1), ROWS, ENC_CHUNK)
    w_qkv = ready(2)
    product_into(qkv_rows, normed_a, w_qkv, 3 * D)
    allowed = column_facts[:, 0:1] == row_facts[0:1, :]
    allowed = jnp.concatenate([allowed.astype(FULL)] * 2, axis=0) > 0.5
    loop(
        D // LANES,
        lambda at: attend_into(attn_out, qkv_rows, pl.ds(0, ROWS), at, D, allowed, D // HEADS),
    )
    w_out = ready(3)
    product_into(after_attn, attn_out, w_out, D, residual=embedded)
    norm_into(normed_b, after_attn, vec(2), vec(3), ROWS, ENC_CHUNK)
    w_up = ready(4)
    up_into(hidden_act, slope, normed_b, w_up, FF, 512)
    w_down = ready(5)
    product_into(encoded, hidden_act, w_down, D, residual=after_attn)
    norm_into(final_enc, encoded, vec(4), vec(5), ROWS, ENC_CHUNK)
    w_proj = ready(6)
    product_into(projected, final_enc, w_proj, DD)


def encoder_forward(part, visible_rows, segments, patch_ids, flat_weights):
    hbm = pl.BlockSpec(memory_space=pl.ANY)
    vmem = pl.BlockSpec(memory_space=pltpu.VMEM)
    smem = pl.BlockSpec(memory_space=pltpu.SMEM)
    table = jnp.asarray(split_low(position_table(D, 256)))
    low, full = (lambda *s: jax.ShapeDtypeStruct(s, LOW)), (lambda *s: jax.ShapeDtypeStruct(s, FULL))
    return pl.pallas_call(
        encoder_forward_kernel,
        out_shape=[
            low(ROWS, PIX),
            full(ROWS, D),
            low(ROWS, D),
            low(ROWS, 3 * D),
            low(ROWS, D),
            full(ROWS, D),
            low(ROWS, D),
            full(ROWS, FF),
            low(ROWS, FF),
            full(ROWS, D),
            low(ROWS, D),
            low(ROWS, DD),
            full(16, ROWS),
            full(ROWS, LANES),
        ],
        in_specs=[smem] + [vmem] * 4 + [hbm],
        out_specs=[vmem] * 14,
        scratch_shapes=[pltpu.SemaphoreType.DMA((7,))] + tile_buffers(FETCHED),
        compiler_params=pltpu.CompilerParams(vmem_limit_bytes=56 * 1024 * 1024),
        name="encoder_forward",
    )(part, visible_rows, segments, patch_ids, table, flat_weights)


def encoder_backward_kernel(
    vis_rows,
    embedded,
    normed_a,
    qkv_rows,
    attn_out,
    after_attn,
    normed_b,
    slope,
    hidden_act,
    encoded,
    final_enc,
    row_facts,
    column_facts,
    grad_projected,
    decoder_vecs,
    weights_ref,
    partial_ref,
    flat_ref,
    grad_rows,
    upper,
    branch,
    grad_pre,
    middle,
    grad_attn,
    grad_qkv,
    vec_grads,
    turned,
    stage,
    vec_full,
    vec_stage,
    stage_sem,
    sems,
    *buffers,
):
    del partial_ref
    ready = fetch(weights_ref, BACKWARD_FETCHED, buffers, sems)
    tiles = entry_tiles()
    ready(0)
    vec = vec_reader(buffers[0], 0, D // LANES)
    grad_of = lambda index: vec_grads.at[pl.ds(index, 1), :]

    def emit(entry, left, right):
        weight_grad(flat_ref, tiles[entry][0], left, right, turned, stage, stage_sem)

    emit("project", final_enc, grad_projected)
    w_proj = ready(1)
    product_t_into(upper, grad_projected, w_proj, D)
    norm_back(grad_rows, encoded, upper, None, vec(4), grad_of(4), grad_of(5), ROWS, ENC_CHUNK)
    branch[...] = grad_rows[...].astype(LOW)
    emit("enc_down", hidden_act, branch)
    w_down = ready(2)
    down_back_into(grad_pre, branch, w_down, slope, FF, 512)
    emit("enc_up", normed_b, grad_pre)
    w_up = ready(3)
    product_t_into(upper, grad_pre, w_up, D)
    norm_back(grad_rows, after_attn, upper, grad_rows, vec(2), grad_of(2), grad_of(3), ROWS, ENC_CHUNK)
    middle[...] = grad_rows[...].astype(LOW)
    emit("enc_out", attn_out, middle)
    w_out = ready(4)
    product_t_into(grad_attn, middle, w_out, D)
    allowed = column_facts[:, 0:1] == row_facts[0:1, :]
    allowed = jnp.concatenate([allowed.astype(FULL)] * 2, axis=0) > 0.5
    loop(
        D // LANES,
        lambda at: attend_back_into(
            grad_qkv, grad_attn, qkv_rows, pl.ds(0, ROWS), at, D, allowed, D // HEADS
        ),
    )
    emit("enc_qkv", normed_a, grad_qkv)
    w_qkv = ready(5)
    product_t_into(upper, grad_qkv, w_qkv, D)
    norm_back(grad_rows, embedded, upper, grad_rows, vec(0), grad_of(0), grad_of(1), ROWS, ENC_CHUNK)
    branch[...] = grad_rows[...].astype(LOW)
    emit("embed", vis_rows, branch)
    groups = D // LANES
    for index in range(6):
        for group in range(groups):
            vec_full[pl.ds(index * groups + group, 1), :] = vec_grads[
                pl.ds(index, 1), pl.ds(group * LANES, LANES)
            ]
    base, groups = 6 * groups, DD // LANES
    for index in range(7):
        for group in range(groups):
            vec_full[pl.ds(base + index * groups + group, 1), :] = decoder_vecs[
                pl.ds(index, 1), pl.ds(group * LANES, LANES)
            ]
    vec_stage[...] = vec_full[...].astype(LOW).reshape(4, TALL, LANES)
    copy = pltpu.make_async_copy(vec_stage, flat_ref.at[pl.ds(tiles["enc_vecs"][0], 4)], stage_sem.at[0])
    copy.start()
    copy.wait()


def encoder_backward(saved, grad_projected, flat_weights, decoder_vec_grads, flat):
    hbm = pl.BlockSpec(memory_space=pl.ANY)
    vmem = pl.BlockSpec(memory_space=pltpu.VMEM)
    inputs = [*saved, grad_projected, decoder_vec_grads, flat_weights, flat]
    low, full = (lambda *s: pltpu.VMEM(s, LOW)), (lambda *s: pltpu.VMEM(s, FULL))
    return pl.pallas_call(
        encoder_backward_kernel,
        out_shape=jax.ShapeDtypeStruct(flat.shape, LOW),
        in_specs=[vmem] * 15 + [hbm] * 2,
        out_specs=hbm,
        input_output_aliases={len(inputs) - 1: 0},
        scratch_shapes=[
            full(ROWS, D),
            full(ROWS, D),
            low(ROWS, D),
            low(ROWS, FF),
            low(ROWS, D),
            low(ROWS, D),
            low(ROWS, 3 * D),
            full(8, D),
            low(TILE, ROWS),
            low(2, TILE // TALL * FF // LANES, TALL, LANES),
            full(64, LANES),
            low(4, TALL, LANES),
            pltpu.SemaphoreType.DMA((2,)),
            pltpu.SemaphoreType.DMA((6,)),
        ]
        + tile_buffers(BACKWARD_FETCHED),
        compiler_params=pltpu.CompilerParams(vmem_limit_bytes=60 * 1024 * 1024),
        name="encoder_backward",
    )(*inputs)


IMAGES = 5
DECODER_FETCHED = ("vecs", "dec_qkv", "dec_out", "dec_up", "dec_down", "pixel")
IMG_ROWS = 208
DEC_ROWS = IMAGES * IMG_ROWS


def decoder_kernel(
    part_ref,
    projected,
    row_facts,
    targets_ref,
    table_ref,
    weights_ref,
    flat_ref,
    grad_projected,
    vec_grads,
    loss_ref,
    dec_in,
    low_rows,
    qkv_rows,
    attn_out,
    after_attn,
    normed_b,
    slope,
    hidden_act,
    decoded,
    final_dec,
    grad_pred,
    upper,
    masked,
    turned,
    stage,
    stage_sem,
    sems,
    *buffers,
    mask_total,
):
    ready = fetch(weights_ref, DECODER_FETCHED, buffers, sems)
    tiles = entry_tiles()
    ready(0)
    vec = vec_reader(buffers[0], 6 * D // LANES, DD // LANES)
    grad_of = lambda index: vec_grads.at[pl.ds(index, 1), :]
    part = part_ref[0]
    image_of = row_facts[0:1, :].astype(jnp.int32) - part * IMAGES
    patch_of = row_facts[1:2, :].astype(jnp.int32)
    patch = lax.broadcasted_iota(jnp.int32, (IMG_ROWS, ROWS), 0)

    def selector(index):
        return ((patch_of == patch) & (image_of == index)).astype(FULL)

    def place(index):
        at = span(index, IMG_ROWS)
        select = selector(index)
        real = (patch[:, 0:1] < PATCHES).astype(FULL)
        hidden = real * (1.0 - jnp.sum(select, axis=-1, keepdims=True))
        masked[at, :] = jnp.broadcast_to(hidden, (IMG_ROWS, LANES))
        dec_in[at, :] = dot_nn(select.astype(LOW), projected[...]) + hidden * vec(6) + table_ref[...]

    loop(IMAGES, place)
    norm_into(low_rows, dec_in, vec(0), vec(1), DEC_ROWS, IMG_ROWS)
    w_qkv = ready(1)
    product_into(qkv_rows, low_rows, w_qkv, 3 * DD)
    head_size = DD // DHEADS
    heads = LANES // head_size
    allowed = lax.broadcasted_iota(jnp.int32, (heads * IMG_ROWS, IMG_ROWS), 1) < PATCHES
    groups = DD // LANES

    def attend(step):
        rows = span(step // groups, IMG_ROWS)
        attend_into(attn_out, qkv_rows, rows, step % groups, DD, allowed, head_size)

    loop(IMAGES * groups, attend)
    w_out = ready(2)
    product_into(after_attn, attn_out, w_out, DD, residual=dec_in)
    norm_into(normed_b, after_attn, vec(2), vec(3), DEC_ROWS, IMG_ROWS)
    w_up = ready(3)
    up_into(hidden_act, slope, normed_b, w_up, DFF, TILE)
    w_down = ready(4)
    product_into(decoded, hidden_act, w_down, DD, residual=after_attn)
    norm_into(final_dec, decoded, vec(4), vec(5), DEC_ROWS, IMG_ROWS)
    w_pix = ready(5)
    loss_ref[...] = jnp.zeros_like(loss_ref)

    def compare(index):
        at = span(index, IMG_ROWS)
        image = pl.ds(0, PATCHES)
        goal, _ = norm_parts(targets_ref[index].astype(FULL))
        goal = jnp.concatenate([goal, jnp.zeros((IMG_ROWS - PATCHES, PIX), FULL)], axis=0)
        error = dot_nn(final_dec[at, :], w_pix.column_tile(0, PIX)) - goal
        weight = masked[at, 0:1]
        rows = jnp.mean(error * error, axis=-1, keepdims=True) * weight
        loss_ref[...] = loss_ref[...] + jnp.sum(rows) * (1.0 / mask_total)
        grad_pred[at, :] = (weight * error * (2.0 / (PIX * mask_total))).astype(LOW)

    loop(IMAGES, compare)

    def emit(entry, left, right):
        weight_grad(flat_ref, tiles[entry][0], left, right, turned, stage, stage_sem)

    emit("pixel", final_dec, grad_pred)
    product_t_into(upper, grad_pred, w_pix, DD)
    grad_rows, branch = decoded, final_dec
    norm_back(grad_rows, decoded, upper, None, vec(4), grad_of(4), grad_of(5), DEC_ROWS, IMG_ROWS)
    branch[...] = grad_rows[...].astype(LOW)
    emit("dec_down", hidden_act, branch)
    grad_pre = hidden_act
    down_back_into(grad_pre, branch, w_down, slope, DFF, TILE)
    emit("dec_up", normed_b, grad_pre)
    product_t_into(upper, grad_pre, w_up, DD)
    norm_back(grad_rows, after_attn, upper, grad_rows, vec(2), grad_of(2), grad_of(3), DEC_ROWS, IMG_ROWS)
    branch[...] = grad_rows[...].astype(LOW)
    emit("dec_out", attn_out, branch)
    grad_attn, grad_qkv = normed_b, grad_pre.at[:, pl.ds(0, 3 * DD)]
    product_t_into(grad_attn, branch, w_out, DD)

    def attend_back(step):
        rows = span(step // groups, IMG_ROWS)
        attend_back_into(grad_qkv, grad_attn, qkv_rows, rows, step % groups, DD, allowed, head_size)

    loop(IMAGES * groups, attend_back)
    emit("dec_qkv", low_rows, grad_qkv)
    product_t_into(upper, grad_qkv, w_qkv, DD)
    norm_back(grad_rows, dec_in, upper, grad_rows, vec(0), grad_of(0), grad_of(1), DEC_ROWS, IMG_ROWS)
    upper[pl.ds(0, ROWS), :] = jnp.zeros((ROWS, DD), FULL)

    def collect(index, token):
        at = span(index, IMG_ROWS)
        rows = grad_rows[at, :]
        token = token + jnp.sum((rows * masked[at, 0:1]).reshape(IMG_ROWS // 8, 8, DD), axis=0)
        upper[pl.ds(0, ROWS), :] = upper[pl.ds(0, ROWS), :] + dot_tn(
            selector(index).astype(LOW), rows.astype(LOW)
        )
        return token

    token = lax.fori_loop(0, IMAGES, collect, jnp.zeros((8, DD), FULL))
    grad_of(6)[...] = jnp.sum(token, axis=0, keepdims=True)
    grad_projected[...] = upper[pl.ds(0, ROWS), :].astype(LOW)


def decoder_step(part, projected, row_facts, targets, flat_weights, mask_total):
    hbm = pl.BlockSpec(memory_space=pl.ANY)
    vmem = pl.BlockSpec(memory_space=pltpu.VMEM)
    smem = pl.BlockSpec(memory_space=pltpu.SMEM)
    table = jnp.asarray(position_table(DD, IMG_ROWS))
    low, full = (lambda *s: pltpu.VMEM(s, LOW)), (lambda *s: pltpu.VMEM(s, FULL))
    return pl.pallas_call(
        partial(decoder_kernel, mask_total=mask_total),
        out_shape=[
            jax.ShapeDtypeStruct(flat_weights.shape, LOW),
            jax.ShapeDtypeStruct((ROWS, DD), LOW),
            jax.ShapeDtypeStruct((8, DD), FULL),
            jax.ShapeDtypeStruct((1, LANES), FULL),
        ],
        in_specs=[smem] + [vmem] * 4 + [hbm],
        out_specs=[hbm] + [vmem] * 3,
        scratch_shapes=[
            full(DEC_ROWS, DD),
            low(DEC_ROWS, DD),
            low(DEC_ROWS, 3 * DD),
            low(DEC_ROWS, DD),
            full(DEC_ROWS, DD),
            low(DEC_ROWS, DD),
            full(DEC_ROWS, DFF),
            low(DEC_ROWS, DFF),
            full(DEC_ROWS, DD),
            low(DEC_ROWS, DD),
            low(DEC_ROWS, PIX),
            full(DEC_ROWS, DD),
            full(DEC_ROWS, LANES),
            low(TILE, DEC_ROWS),
            low(2, TILE // TALL * DFF // LANES, TALL, LANES),
            pltpu.SemaphoreType.DMA((2,)),
            pltpu.SemaphoreType.DMA((6,)),
        ]
        + tile_buffers(DECODER_FETCHED),
        compiler_params=pltpu.CompilerParams(vmem_limit_bytes=62 * 1024 * 1024),
        name="decoder_step",
    )(part, projected, row_facts, targets, table, flat_weights)


def to_tiles(full_flat):
    pieces, offset = [], 0
    for _, (rows, columns) in layout()[:11]:
        piece = full_flat[offset : offset + rows * columns]
        piece = piece.reshape(rows // TALL, TALL, columns // LANES, LANES)
        pieces.append(piece.transpose(0, 2, 1, 3).reshape(-1, LANES))
        offset += rows * columns
    return jnp.concatenate([*pieces, full_flat[offset:].reshape(-1, LANES)])


def from_tiles(rows_flat):
    pieces, offset = [], 0
    for _, (rows, columns) in layout()[:11]:
        count = rows * columns // LANES
        piece = rows_flat[offset : offset + count]
        piece = piece.reshape(rows // TALL, columns // LANES, TALL, LANES)
        pieces.append(piece.transpose(0, 2, 1, 3).reshape(-1))
        offset += count
    return jnp.concatenate([*pieces, rows_flat[offset:].reshape(-1)])


def shards(visible, segments, patch_ids, targets, master, moment_one, moment_two, step_count):
    part = lax.axis_index("seq")
    in_kernels = master.shape[0] == SHARD_ROWS * LANES and lax.axis_size("dp") == 16
    if in_kernels:
        flat_weights = gather_weights(master.reshape(SHARD_ROWS, LANES))
    else:
        full_flat = lax.all_gather(master.astype(LOW), ("seq", "dp"), axis=0, tiled=True)
        flat_weights = to_tiles(full_flat)
    flat_weights = flat_weights.reshape(-1, TALL, LANES)
    visible_rows = lax.all_gather(visible[0], "seq", axis=0, tiled=True)
    part_row = part.reshape(1).astype(jnp.int32)
    mask_total = (PATCHES - VIS) * IMG_SEQ * visible.shape[0] * lax.axis_size("dp")
    *saved, projected, row_facts, column_facts = encoder_forward(
        part_row, visible_rows, segments, patch_ids, flat_weights
    )
    flat_grads, grad_projected, decoder_vec_grads, loss_row = decoder_step(
        part_row, projected, row_facts, targets[0], flat_weights, mask_total
    )
    flat_grads = encoder_backward(
        [*saved, row_facts, column_facts],
        grad_projected,
        flat_weights,
        decoder_vec_grads,
        flat_grads,
    )
    flat_grads = flat_grads.reshape(-1, LANES)
    if in_kernels:
        grad_shard, square_sum, loss_sum = reduce_gradients(flat_grads, loss_row)
    else:
        grad_flat = from_tiles(flat_grads.astype(FULL))
        grad_shard = lax.psum_scatter(grad_flat, ("seq", "dp"), scatter_dimension=0, tiled=True)
        square_sum, loss_sum = lax.psum(
            (jnp.sum(grad_shard * grad_shard), loss_row[0, 0]), ("seq", "dp")
        )
    grad_norm = jnp.sqrt(square_sum)
    clipped = grad_shard * jnp.minimum(1.0, clip_limit / (grad_norm + 1e-06))
    new_one = beta_mom * moment_one + (1.0 - beta_mom) * clipped
    new_two = beta_mom * moment_two + (1.0 - beta_mom) * clipped * clipped
    correction = 1.0 - jnp.power(jnp.float32(beta_mom), step_count[0].astype(jnp.float32))
    new_master = master - learn_rate * (
        new_one / correction / (jnp.sqrt(new_two / correction) + adam_eps) + decay_rate * master
    )
    return (new_one, new_two, new_master, new_master.astype(jnp.bfloat16), grad_norm, loss_sum)


def solution(mesh):
    in_specs = (
        P("dp", "seq", None),
        P("dp", None),
        P("dp", None),
        P("dp", "seq", None, None),
        P(("seq", "dp")),
        P(("seq", "dp")),
        P(("seq", "dp")),
        P(),
    )
    out_specs = (P(("seq", "dp")), P(("seq", "dp")), P(("seq", "dp")), P(("seq", "dp")), P(), P())
    return jax.shard_map(shards, mesh=mesh, in_specs=in_specs, out_specs=out_specs, check_vma=False)
```

```python
from functools import partial
import math

import jax
import jax.numpy as jnp
import ml_dtypes
import numpy as np
from jax import lax
from jax.experimental import pallas as pl
from jax.experimental.pallas import tpu as pltpu
from jax.sharding import PartitionSpec as P

D = 768
HEADS = 12
FF = 3072
DD = 512
DHEADS = 16
DFF = 2048
PIX = 768
PATCHES = 196
VIS = 49
IMG_SEQ = 10


norm_eps = 1e-06
neg_big = -1000000000.0
clip_limit = 0.0001
learn_rate = 0.03
decay_rate = 0.05
adam_eps = 1e-08
beta_mom = 0.5


def layout():
    return [
        ("embed", (PIX, D)),
        ("enc_qkv", (D, 3 * D)),
        ("enc_out", (D, D)),
        ("enc_up", (D, FF)),
        ("enc_down", (FF, D)),
        ("project", (D, DD)),
        ("dec_qkv", (DD, 3 * DD)),
        ("dec_out", (DD, DD)),
        ("dec_up", (DD, DFF)),
        ("dec_down", (DFF, DD)),
        ("pixel", (DD, PIX)),
        ("enc_vecs", (6, D)),
        ("dec_vecs", (7, DD)),
    ]


def unflatten(flat_vec):
    params = {}
    offset = 0
    for entry_name, entry_shape in layout():
        entry_size = entry_shape[0] * entry_shape[1]
        params[entry_name] = flat_vec[offset : offset + entry_size].reshape(entry_shape)
        offset += entry_size
    return params


LOW = jnp.bfloat16
FULL = jnp.float32
TILE = 256
TALL = 16
LANES = 128
NEG = neg_big
ROOT_HALF = math.sqrt(0.5)
LOG2_E = 1.0 / math.log(2.0)
BELL = 1.0 / math.sqrt(2.0 * math.pi)


def dot_nn(left, right):
    return lax.dot_general(left, right, (((1,), (0,)), ((), ())), preferred_element_type=FULL)


def dot_nt(left, right):
    return lax.dot_general(left, right, (((1,), (1,)), ((), ())), preferred_element_type=FULL)


def dot_tn(left, right):
    return lax.dot_general(left, right, (((0,), (0,)), ((), ())), preferred_element_type=FULL)


def loop(count, body):
    def one(step, carry):
        body(step)
        return carry

    lax.fori_loop(0, count, one, 0)


def unrolled(count, body):
    size = next(size for size in (3, 2, 1) if count % size == 0)

    def one(step):
        for part in range(size):
            body(step * size + part)

    loop(count // size, one)


def span(step, size):
    return pl.ds(pl.multiple_of(step * size, size), size)


def norm_parts(rows):
    average = jnp.mean(rows, axis=-1, keepdims=True)
    centered = rows - average
    scale = lax.rsqrt(jnp.mean(centered * centered, axis=-1, keepdims=True) + norm_eps)
    return centered * scale, scale


def norm_into(dst, src, gain, shift, rows, chunk):
    def one(step):
        at = span(step, chunk)
        unit, _ = norm_parts(src[at, :])
        dst[at, :] = (unit * gain + shift).astype(LOW)

    loop(rows // chunk, one)


def norm_back(dst, src, grad, residual, gain, gain_grad, shift_grad, rows, chunk):
    width = src.shape[1]

    def one(step, carry):
        at = span(step, chunk)
        unit, scale = norm_parts(src[at, :])
        upper = grad[at, :]
        gains = carry[0] + jnp.sum((upper * unit).reshape(chunk // 8, 8, width), axis=0)
        shifts = carry[1] + jnp.sum(upper.reshape(chunk // 8, 8, width), axis=0)
        upper = upper * gain
        lower = scale * (
            upper
            - jnp.mean(upper, axis=-1, keepdims=True)
            - unit * jnp.mean(upper * unit, axis=-1, keepdims=True)
        )
        if residual is not None:
            lower = lower + residual[at, :]
        dst[at, :] = lower
        return gains, shifts

    zero = jnp.zeros((8, width), FULL)
    gains, shifts = lax.fori_loop(0, rows // chunk, one, (zero, zero))
    gain_grad[...] = jnp.sum(gains, axis=0, keepdims=True)
    shift_grad[...] = jnp.sum(shifts, axis=0, keepdims=True)


class Blocked:
    def __init__(self, ref, rows, columns):
        self.rows, self.groups = rows, columns // LANES
        self.ref = ref.reshape(rows // TALL, self.groups, TALL, LANES)

    def piece(self, first_row, rows, first_group, groups):
        tall = pl.ds(first_row // TALL, rows // TALL)
        parts = [
            self.ref[tall, first_group + index].reshape(rows, LANES) for index in range(groups)
        ]
        return parts[0] if groups == 1 else jnp.concatenate(parts, axis=1)

    def column_tile(self, step, tile):
        count = tile // LANES
        return self.piece(0, self.rows, step * count, count)

    def row_tile(self, step, tile):
        return self.piece(step * tile, tile, 0, self.groups)


def product_into(dst, left, right, columns, tile=TILE, residual=None):
    def one(step):
        at = span(step, tile)
        value = dot_nn(left[...], right.column_tile(step, tile))
        if residual is not None:
            value = value + residual[:, at]
        dst[:, at] = value.astype(dst.dtype)

    unrolled(columns // tile, one)


def product_t_into(dst, left, right, columns, tile=TILE):
    def one(step):
        dst[:, span(step, tile)] = dot_nt(left[...], right.row_tile(step, tile)).astype(dst.dtype)

    unrolled(columns // tile, one)


def up_into(act, slope, left, w_up, columns, tile):
    def one(step):
        at = span(step, tile)
        hidden = dot_nn(left[...], w_up.column_tile(step, tile))
        share = 0.5 * (1.0 + lax.erf(hidden * ROOT_HALF))
        act[:, at] = (hidden * share).astype(LOW)
        slope[:, at] = share + hidden * (BELL * jnp.exp(-0.5 * hidden * hidden))

    unrolled(columns // tile, one)


def down_back_into(grad_pre, branch, w_down, slope, columns, tile):
    def one(step):
        at = span(step, tile)
        grad_pre[:, at] = (dot_nt(branch[...], w_down.row_tile(step, tile)) * slope[:, at]).astype(LOW)

    unrolled(columns // tile, one)


def weight_grad(out, out_tile, left, right, turned, stage, stage_sem, slot=0, before=None):
    rows, columns = left.shape[1], right.shape[1]
    groups = columns // LANES
    high = rows // TALL
    count = high * groups

    def turn(step):
        turned[span(step, TILE), :] = left[:, span(step, TILE)].T

    loop(rows // TILE, turn)
    if before is not None:
        before()
    tiles = stage.at[slot, pl.ds(0, count)].reshape(high, groups, TALL, LANES)
    piece = columns // TILE
    unroll = next(u for u in (3, 2, 1) if piece % u == 0)

    def across(step):
        for part in range(unroll):
            tile = step * unroll + part
            value = dot_nn(turned[pl.ds(0, rows), :], right[:, span(tile, TILE)]).astype(LOW)
            for half in range(2):
                tiles[:, tile * 2 + half] = value[:, half * LANES : (half + 1) * LANES].reshape(
                    high, TALL, LANES
                )

    loop(piece // unroll, across)
    copy = lambda: pltpu.make_async_copy(
        stage.at[slot, pl.ds(0, count)], out.at[pl.ds(out_tile, count)], stage_sem.at[slot]
    )
    copy().start()
    return lambda: copy().wait()


class Emitter:
    def __init__(self, out, turned, stage, stage_sem):
        self.args = turned, stage, stage_sem
        self.out, self.tiles, self.waits = out, entry_tiles(), []

    def __call__(self, entry, left, right):
        index = len(self.waits)
        before = self.waits[index - 2] if index >= 2 else None
        self.waits.append(
            weight_grad(self.out, self.tiles[entry][0], left, right, *self.args, index % 2, before)
        )

    def finish(self):
        for wait in self.waits[-2:]:
            wait()


def head_masks(head_size, dtype):
    lane = lax.broadcasted_iota(jnp.int32, (1, LANES), 1) // head_size
    return [(lane == head).astype(dtype) for head in range(LANES // head_size)]


def stacked(rows, masks):
    return jnp.concatenate([rows * mask for mask in masks], axis=0)


def unstacked(rows, masks, size):
    total = None
    for index, mask in enumerate(masks):
        piece = rows[index * size : (index + 1) * size] * mask
        total = piece if total is None else total + piece
    return total


def soft_rows(queries, keys, allowed, scale):
    scores = jnp.where(allowed, dot_nt(queries, keys), NEG)
    scores = scores - jnp.max(scores, axis=-1, keepdims=True)
    powers = jnp.exp2(scores * (scale * LOG2_E))
    return powers * (1.0 / jnp.sum(powers, axis=-1, keepdims=True))


def attend_into(dst, qkv, rows, at, width, allowed, head_size):
    masks = head_masks(head_size, LOW)
    size = rows.size
    column = lambda part: pl.ds(pl.multiple_of(part * width + at * LANES, LANES), LANES)
    queries = stacked(qkv[rows, column(0)], masks)
    probs = soft_rows(queries, qkv[rows, column(1)], allowed, head_size**-0.5).astype(LOW)
    values = dot_nn(probs, qkv[rows, column(2)])
    dst[rows, column(0)] = unstacked(values, head_masks(head_size, FULL), size).astype(LOW)


def attend_back_into(dst, grad, qkv, rows, at, width, allowed, head_size):
    masks = head_masks(head_size, LOW)
    lanes = head_masks(head_size, FULL)
    size = rows.size
    scale = head_size**-0.5
    column = lambda part: pl.ds(pl.multiple_of(part * width + at * LANES, LANES), LANES)
    queries = stacked(qkv[rows, column(0)], masks)
    keys = qkv[rows, column(1)]
    probs = soft_rows(queries, keys, allowed, scale)
    grads = stacked(grad[rows, column(0)], masks)
    slopes = dot_nt(grads, qkv[rows, column(2)])
    slopes = probs * (slopes - jnp.sum(slopes * probs, axis=-1, keepdims=True))
    slopes = slopes.astype(LOW)
    dst[rows, column(0)] = (unstacked(dot_nn(slopes, keys), lanes, size) * scale).astype(LOW)
    dst[rows, column(1)] = (dot_tn(slopes, queries) * scale).astype(LOW)
    dst[rows, column(2)] = dot_tn(probs.astype(LOW), grads).astype(LOW)


def entry_tiles():
    tiles, offset = {}, 0
    for entry_name, (rows, columns) in layout():
        tiles[entry_name] = (offset // (TALL * LANES), rows, columns)
        offset += rows * columns
    tiles["vecs"] = (tiles["enc_vecs"][0], 4 * TALL, LANES)
    return tiles


def vec_reader(buffer, first, groups):
    rows = buffer[...].reshape(4 * TALL, LANES).astype(FULL)

    def vec(index):
        start = first + index * groups
        return jnp.concatenate([rows[start + g : start + g + 1] for g in range(groups)], axis=1)

    return vec


def fetch(flat, names, buffers, sems):
    tiles = entry_tiles()

    def build(index):
        start, rows, columns = tiles[names[index]]
        count = rows * columns // (TALL * LANES)
        return pltpu.make_async_copy(flat.at[pl.ds(start, count)], buffers[index], sems.at[index])

    for index in range(len(names)):
        build(index).start()

    def ready(index):
        build(index).wait()
        _, rows, columns = tiles[names[index]]
        return Blocked(buffers[index], rows, columns)

    return ready


def tile_buffers(names):
    tiles = entry_tiles()
    return [
        pltpu.VMEM((tiles[entry][1] * tiles[entry][2] // (TALL * LANES), TALL, LANES), LOW)
        for entry in names
    ]


def position_table(columns, padded):
    half = columns // 2
    frequency = np.exp(
        np.float32(-math.log(10000.0)) * np.arange(half, dtype=np.float32) / np.float32(half)
    ).astype(np.float32)
    angles = np.arange(PATCHES, dtype=np.float32)[:, None] * frequency
    table = np.zeros((padded, columns), np.float32)
    table[:PATCHES] = np.concatenate(
        [np.sin(angles.astype(np.float64)), np.cos(angles.astype(np.float64))], axis=-1
    )
    return table


def split_low(table):
    parts, rest = [], table.astype(np.float64)
    for _ in range(3):
        part = rest.astype(ml_dtypes.bfloat16)
        parts.append(part)
        rest = rest - part.astype(np.float64)
    return np.stack(parts)


MESH = pl.DeviceIdType.MESH
A_HALF = 1104
A_ROWS = 2 * A_HALF
B_HALF = 320
B_ROWS = 2 * B_HALF
SHARD_ROWS = 2834
PAD_ROWS = A_ROWS + B_ROWS
B_TRUE = SHARD_ROWS - A_ROWS
HALO = 384
WIDE_ROWS = SHARD_ROWS + 2 * HALO
PARTS = {
    "a1": (0, A_HALF),
    "a2": (A_HALF, A_HALF),
    "b": (A_ROWS, B_ROWS),
    "b1": (A_ROWS, B_HALF),
    "b2": (A_ROWS + B_HALF, B_HALF),
}
TRUE_PARTS = {**PARTS, "b": (A_ROWS, B_TRUE), "b2": (A_ROWS + B_HALF, B_TRUE - B_HALF)}
SLOTS = {"a1": 0, "a2": 1, "b": 2, "b1": 2, "b2": 3}
COLUMNS = "oxyd"
ARRIVALS = {
    0: (
        12, 22, 102, 10, 20, 100, 11, 21, 101, 33, 34, 112, 122, 30, 110, 202, 120, 31, 200, 121,
        111, 201, 132, 130, 210, 212, 220, 131, 222, 302, 221, 211, 300, 230, 231, 301, 320, 310,
        232, 312, 321, 311, 322, 332, 330, 331,
    ),
    1: (
        2, 112, 122, 202, 0, 110, 120, 200, 1, 111, 121, 201, 133, 134, 12, 212, 22, 222, 20, 10,
        32, 302, 130, 210, 300, 220, 11, 301, 232, 21, 131, 312, 221, 211, 322, 332, 30, 310,
        230, 311, 320, 31, 321, 231, 330, 331,
    ),
}


def item_of(code):
    return code // 100, COLUMNS[code // 10 % 10], list(PARTS)[code % 10]


def own_item(inner, part):
    return 100 * inner + list(PARTS).index(part)


class Place:
    def __init__(self):
        self.core = lax.axis_index("seq")
        self.chip = lax.axis_index("dp")
        chip = self.chip
        self.z = chip // 4
        y, x = (chip // 2) % 2, chip % 2
        self.col = chip % 4
        self.col_x = self.col + 1 - 2 * x
        self.col_y = self.col + 2 - 4 * y
        self.col_d = self.col_x + 2 - 4 * y
        self.columns = {"o": self.col, "x": self.col_x, "y": self.col_y, "d": self.col_d}
        self.side = self.z // 2
        sign = 1 - 2 * self.side
        self.inner = self.z + self.side * (3 - 2 * self.z)
        self.me = 16 * self.core + chip
        self.devices = {
            "x": (self.core, 4 * self.z + self.col_x),
            "y": (self.core, 4 * self.z + self.col_y),
            "far": (self.core, chip + 4 * sign),
            "near": (self.core, chip - 4 * sign * self.inner),
            "core": (1 - self.core, chip),
            "next": self.ring(1),
            "back": self.ring(31),
        }

    def ring(self, step):
        peer = (self.me + step) % 32
        return (peer // 16, peer % 16)

    def plane(self, mirrored):
        return mirrored + self.side * (3 - 2 * mirrored)

    def greet(self):
        barrier = pltpu.get_barrier_semaphore()
        for link in ("x", "y", "far", "core", "next", "back"):
            pl.semaphore_signal(
                barrier, inc=1, device_id=self.devices[link], device_id_type=MESH
            )

        @pl.when(self.inner == 1)
        def _():
            pl.semaphore_signal(
                barrier, inc=1, device_id=self.devices["near"], device_id_type=MESH
            )

        pl.semaphore_wait(barrier, 6 + self.inner)


class Outbox:
    def __init__(self):
        self.sent = []

    def send(self, src, dst, send_sem, recv_sem, device):
        def build():
            return pltpu.make_async_remote_copy(
                src_ref=src,
                dst_ref=dst,
                send_sem=send_sem,
                recv_sem=recv_sem,
                device_id=device,
                device_id_type=MESH,
            )

        build().start()
        self.sent.append(build)

    def finish(self):
        for build in self.sent:
            build().wait_send()


def arrived(ref, sem, device):
    pltpu.make_async_remote_copy(
        src_ref=ref, dst_ref=ref, send_sem=sem, recv_sem=sem, device_id=device, device_id_type=MESH
    ).wait_recv()


def by_place(at, body):
    for inner in (0, 1):
        pl.when(at.inner == inner)(partial(body, inner))


def onward(inner, item):
    mirrored, column, part = item_of(item)
    line = ["far", "near"][: 1 + inner]
    if mirrored != inner:
        line = [] if inner == 0 else ["far" if mirrored == 0 else "near"]
    if part[0] == "a":
        if column == "o":
            return [(link, part) for link in [*line, "x", "y"]]
        if (column, part) in (("x", "a1"), ("y", "a2")):
            return [("y" if column == "x" else "x", part)]
        return []
    links = [(link, "b") for link in line]
    if mirrored == inner:
        links = {
            "o": [("x", "b"), ("y", "b")],
            "x": [("y", "b1")],
            "y": [("x", "b2")],
            "d": [],
        }[column] + links
    return links


def gather_exchange(at, flat, source, recv, core_recv, sends, core_send):
    def block(chip, part, core):
        first, size = TRUE_PARTS[part]
        return flat.at[pl.ds((core * 16 + chip) * SHARD_ROWS + first, size)]

    def body(inner):
        out = Outbox()
        diagonal = []

        def pass_on(item):
            mirrored, column, part = item_of(item)
            chip = 4 * at.plane(mirrored) + at.columns[column]
            own = mirrored == inner and column == "o"
            links = onward(inner, item)
            if mirrored == inner and column == "d" and part[0] == "b":
                diagonal.append(part)
                links = links if len(diagonal) == 2 else []
            for link, piece in [*links, ("core", part)]:
                slot = SLOTS[piece]
                ref = block(chip, piece, at.core)
                sent, got = (core_send, core_recv) if link == "core" else (sends[link], recv)
                out.send(
                    source(piece) if own else ref,
                    ref,
                    sent.at[chip, slot],
                    got.at[chip, slot],
                    at.devices[link],
                )

        for part in ("b", "a1", "a2"):
            pass_on(own_item(inner, part))
        for item in ARRIVALS[inner]:
            mirrored, column, part = item_of(item)
            chip = 4 * at.plane(mirrored) + at.columns[column]
            arrived(block(chip, part, at.core), recv.at[chip, SLOTS[part]], at.devices["x"])
            pass_on(item)
        for part in ("b", "a1", "a2"):
            arrived(
                block(at.chip, part, 1 - at.core),
                core_recv.at[at.chip, SLOTS[part]],
                at.devices["x"],
            )
        for item in ARRIVALS[inner]:
            mirrored, column, part = item_of(item)
            chip = 4 * at.plane(mirrored) + at.columns[column]
            ref = block(chip, part, 1 - at.core)
            arrived(ref, core_recv.at[chip, SLOTS[part]], at.devices["x"])
        out.finish()

    by_place(at, body)


def entry_blocks(me, body):
    first = me * SHARD_ROWS
    offset = 0
    for _, (rows, columns) in layout()[:11]:
        groups, blocks = columns // LANES, rows // TALL
        unit = TALL * groups
        low = jnp.minimum(jnp.maximum(first - offset, 0) // unit, blocks)
        high = jnp.minimum(
            (jnp.maximum(first + SHARD_ROWS - offset, 0) + unit - 1) // unit, blocks
        )

        def one(block, carry, offset=offset, unit=unit, groups=groups):
            body(offset + block * unit, groups)
            return carry

        lax.fori_loop(low, high, one, 0)
        offset += unit * blocks
    return offset


VEC_ROWS = 64


def gather_kernel(
    master_ref, visible_ref, flat_ref, both_ref, wide, turned, own_sem, halo_send, halo_recv, *sems
):
    recv, core_recv, send_x, send_y, send_far, send_near, core_send = sems
    at = Place()
    first = at.me * SHARD_ROWS
    skew = (at.me * 2) % TALL
    own = pltpu.make_async_copy(master_ref, wide.at[pl.ds(HALO, SHARD_ROWS)], own_sem.at[0])
    own.start()
    at.greet()
    out = Outbox()
    tail = wide.at[pl.ds(HALO + SHARD_ROWS, HALO)]
    head = wide.at[pl.ds(0, HALO)]
    out.send(
        master_ref.at[pl.ds(0, HALO)],
        tail,
        halo_send.at[0],
        halo_recv.at[0],
        at.devices["back"],
    )
    out.send(
        master_ref.at[pl.ds(SHARD_ROWS - HALO, HALO)],
        head,
        halo_send.at[1],
        halo_recv.at[1],
        at.devices["next"],
    )
    half = visible_ref.shape[0]
    rows_here = both_ref.at[pl.ds(pl.multiple_of(at.core * half, half), half)]
    rows_there = both_ref.at[pl.ds(pl.multiple_of((1 - at.core) * half, half), half)]
    out.send(visible_ref, rows_here, halo_send.at[2], halo_recv.at[2], at.devices["core"])
    keep = pltpu.make_async_copy(visible_ref, rows_here, own_sem.at[2])
    keep.start()
    own.wait()
    arrived(tail, halo_recv.at[0], at.devices["x"])
    arrived(head, halo_recv.at[1], at.devices["x"])

    def turn(row, groups):
        start = row - first + HALO
        spot = row - (first - skew) + HALO
        for group in range(groups):
            turned[pl.ds(pl.multiple_of(spot + group * TALL, TALL), TALL), :] = wide[
                pl.ds(start + group, TALL, stride=groups), :
            ].astype(LOW)

    vec_start = entry_blocks(at.me, turn)

    @pl.when(at.me == 31)
    def _():
        start = vec_start - 31 * SHARD_ROWS + HALO
        spot = start + (31 * 2) % TALL
        turned[pl.ds(spot, VEC_ROWS), :] = wide[pl.ds(start, VEC_ROWS), :].astype(LOW)

    mine = pltpu.make_async_copy(
        turned.at[pl.ds(HALO + skew, SHARD_ROWS)],
        flat_ref.at[pl.ds(first, SHARD_ROWS)],
        own_sem.at[1],
    )
    mine.start()

    def source(part):
        start, size = TRUE_PARTS[part]
        return turned.at[pl.ds(HALO + skew + start, size)]

    sends = {"x": send_x, "y": send_y, "far": send_far, "near": send_near}
    gather_exchange(at, flat_ref, source, recv, core_recv, sends, core_send)
    mine.wait()
    keep.wait()
    arrived(rows_there, halo_recv.at[2], at.devices["x"])
    out.finish()


def gather_weights(master_rows, visible_rows):
    hbm = pl.BlockSpec(memory_space=pltpu.HBM)
    threes = pltpu.SemaphoreType.DMA((3,))
    half, width = visible_rows.shape
    return pl.pallas_call(
        gather_kernel,
        out_shape=[
            jax.ShapeDtypeStruct((32 * SHARD_ROWS, LANES), LOW),
            jax.ShapeDtypeStruct((2 * half, width), LOW),
        ],
        in_specs=[hbm, hbm],
        out_specs=[hbm, hbm],
        scratch_shapes=[
            pltpu.VMEM((WIDE_ROWS + 6, LANES), FULL),
            pltpu.VMEM((WIDE_ROWS + 30, LANES), LOW),
            threes,
            threes,
            threes,
        ]
        + [pltpu.SemaphoreType.DMA((16, 4))] * 7,
        compiler_params=pltpu.CompilerParams(
            collective_id=0, has_side_effects=True, vmem_limit_bytes=60 * 1024 * 1024
        ),
        name="gather_weights",
    )(master_rows, visible_rows)


def add_into(dst, start, terms, size, chunk):
    def one(step):
        row = step * chunk
        total = None
        for ref, first in terms:
            piece = ref[pl.ds(pl.multiple_of(first + row, TALL), chunk), :].astype(FULL)
            total = piece if total is None else total + piece
        dst[pl.ds(pl.multiple_of(start + row, TALL), chunk), :] = total.astype(dst.dtype)

    loop(size // chunk, one)


def reduce_kernel(
    grad_ref,
    loss_ref,
    shard_ref,
    total_ref,
    own,
    theirs,
    from_x,
    from_y,
    pass_x,
    pass_y,
    far_a,
    near_a,
    far_b,
    near_b,
    wide,
    plain,
    scalars,
    load_sem,
    core_send,
    core_recv,
    send_x,
    send_y,
    send_far,
    send_near,
    recv_x,
    recv_y,
    recv_far,
    recv_near,
    halo_send,
    halo_recv,
    tiny_send,
    tiny_recv,
):
    at = Place()
    tail = pl.ds(SHARD_ROWS - 2, TALL)
    for index in range(16):
        own[index, tail, :] = jnp.zeros((TALL, LANES), LOW)
        theirs[index, tail, :] = jnp.zeros((TALL, LANES), LOW)
    body = pl.ds(0, SHARD_ROWS)

    def shard_rows(core, chip):
        return grad_ref.at[pl.ds((core * 16 + chip) * SHARD_ROWS, SHARD_ROWS)]

    def load(chip):
        return pltpu.make_async_copy(
            shard_rows(at.core, chip), own.at[chip, body], load_sem.at[chip]
        )

    at.greet()
    pairs = Outbox()
    for mirrored in (3, 2, 1 - at.inner, at.inner):
        for column in ("d", "y", "x", "o"):
            chip = 4 * at.plane(mirrored) + at.columns[column]
            pairs.send(
                shard_rows(1 - at.core, chip),
                theirs.at[chip, body],
                core_send.at[chip],
                core_recv.at[chip],
                at.devices["core"],
            )
            load(chip).start()
    sends = {"x": send_x, "y": send_y, "far": send_far, "near": send_near}
    recvs = {"x": recv_x, "y": recv_y, "far": recv_far, "near": recv_near}
    relayed = {"x": pass_x, "y": pass_y}
    direct = {"x": from_x, "y": from_y}
    lines = {"far": (far_a, far_b), "near": (near_a, near_b)}

    def reduce_parts(inner):
        out = Outbox()
        paired, joined = set(), set()

        def pair(chip, key):
            if key in paired:
                return
            paired.add(key)
            load(chip).wait()
            arrived(theirs.at[chip, body], core_recv.at[chip], at.devices["x"])
            add_into(own.at[chip], 0, [(own.at[chip], 0), (theirs.at[chip], 0)], PAD_ROWS, 32)

        def landing(link, plane, chip, part, relay):
            first, size = PARTS[part]
            if link in lines and part == "b":
                return lines[link][1].at[chip], 0, size, (chip, SLOTS[part])
            if link in lines:
                return lines[link][0].at[plane], first, size, (chip, SLOTS[part])
            if relay:
                return relayed[link].at[plane], first, size, (plane, 3 + (part[0] == "b"))
            return direct[link].at[plane], first, size, (plane, SLOTS[part])

        def step(item):
            mirrored, column, part = item_of(item)
            plane = at.plane(mirrored)
            chip = 4 * plane + at.columns[column]
            pair(chip, (mirrored, column))
            first, size = PARTS[part]
            terms = []
            links = onward(inner, item)
            if mirrored == inner and column == "d" and part[0] == "b":
                links = [] if joined else links
                joined.add(part)
            own_item = mirrored == inner and column == "o"
            for link, piece in links:
                relay = column in ("x", "y")
                buffer, start, count, index = landing(link, plane, chip, piece, relay)
                arrived(buffer.at[pl.ds(start, count)], recvs[link].at[*index], at.devices["x"])
                terms.append((buffer, start, count))
            if own_item:
                whole = [(own.at[chip], first)] + [(buffer, start) for buffer, start, _ in terms]
                if part == "b":
                    add_into(plain, 0, whole, size, size // 4)
                    wide[pl.ds(HALO + A_ROWS, B_TRUE), :] = plain[pl.ds(0, B_TRUE), :]
                else:
                    add_into(wide, HALO + first, whole, size, size // 3)
                return
            full_size = B_ROWS if part[0] == "b" else size
            full_first = PARTS["b"][0] if part[0] == "b" else first
            whole = [(buffer, start) for buffer, start, count in terms if count == full_size]
            halves = [(buffer, start, count) for buffer, start, count in terms if count != full_size]
            if whole:
                add_into(
                    own.at[chip],
                    full_first,
                    [(own.at[chip], full_first), *whole],
                    full_size,
                    full_size // (4 if part[0] == "b" else 3),
                )
            for buffer, start, count in halves:
                add_into(
                    own.at[chip], start, [(own.at[chip], start), (buffer, start)], count, count // 2
                )
            if column == "o" or (part == "b" and mirrored != inner):
                link = "near" if inner == 1 and mirrored == 0 else "far"
                target = "near" if inner == 0 else "far"
                buffer, start, _, index = landing(target, plane, chip, part, False)
                arrive_sem = recvs[target]
            else:
                link = {"x": "x", "y": "y", "d": "y" if part in ("a1", "b1") else "x"}[column]
                buffer, start, _, index = landing(link, plane, chip, part, column == "d")
                arrive_sem = recvs[link]
            out.send(
                own.at[chip, pl.ds(first, size)],
                buffer.at[pl.ds(start, size)],
                sends[link].at[*index],
                arrive_sem.at[*index],
                at.devices[link],
            )

        for item in reversed(ARRIVALS[inner]):
            step(item)
        for part in ("a2", "a1", "b"):
            step(own_item(inner, part))
        out.finish()

    by_place(at, reduce_parts)
    pairs.finish()

    halo = Outbox()
    head, after = wide.at[pl.ds(0, HALO)], wide.at[pl.ds(HALO + SHARD_ROWS, HALO)]
    halo.send(
        wide.at[pl.ds(HALO, HALO)], after, halo_send.at[0], halo_recv.at[0], at.devices["back"]
    )
    halo.send(
        wide.at[pl.ds(SHARD_ROWS, HALO)], head, halo_send.at[1], halo_recv.at[1], at.devices["next"]
    )
    whole_steps = SHARD_ROWS // 32

    def squares(index, carry):
        piece = wide[pl.ds(pl.multiple_of(HALO + index * 32, 8), 32), :]
        piece = piece * piece
        return carry + jnp.sum(piece.reshape(4, 8, LANES), axis=0)

    square = lax.fori_loop(0, whole_steps, squares, jnp.zeros((8, LANES), FULL))
    rest = wide[pl.ds(HALO + whole_steps * 32, SHARD_ROWS - whole_steps * 32), :]
    square = square + 0.125 * jnp.sum(rest * rest, axis=0, keepdims=True)
    scalars[at.me, 0] = square
    scalars[at.me, 1] = jnp.broadcast_to(loss_ref[...], (8, LANES))
    for index in range(1, 32):
        halo.send(
            scalars.at[at.me],
            scalars.at[at.me],
            tiny_send.at[index],
            tiny_recv.at[at.me],
            at.ring(index),
        )
    arrived(after, halo_recv.at[0], at.devices["x"])
    arrived(head, halo_recv.at[1], at.devices["x"])

    def turn_back(row, groups):
        start = row - at.me * SHARD_ROWS + HALO
        for group in range(groups):
            plain[pl.ds(start + group, TALL, stride=groups), :] = wide[
                pl.ds(start + group * TALL, TALL), :
            ]

    vec_start = entry_blocks(at.me, turn_back)

    @pl.when(at.me == 31)
    def _():
        spot = pl.ds(vec_start - 31 * SHARD_ROWS + HALO, VEC_ROWS)
        plain[spot, :] = wide[spot, :]

    shard_ref[...] = plain[pl.ds(HALO, SHARD_ROWS), :]
    for index in range(1, 32):
        peer = (at.me + index) % 32
        arrived(scalars.at[peer], tiny_recv.at[peer], at.devices["x"])
    total_ref[...] = jnp.sum(scalars[...], axis=0)
    halo.finish()


def reduce_gradients(grad_rows, loss_row):
    hbm = pl.BlockSpec(memory_space=pltpu.HBM)
    vmem = pl.BlockSpec(memory_space=pltpu.VMEM)
    dma = pltpu.SemaphoreType.DMA
    shard_total, totals = pl.pallas_call(
        reduce_kernel,
        out_shape=[
            jax.ShapeDtypeStruct((SHARD_ROWS, LANES), FULL),
            jax.ShapeDtypeStruct((2, 8, LANES), FULL),
        ],
        in_specs=[hbm, vmem],
        out_specs=[vmem, vmem],
        scratch_shapes=[pltpu.VMEM((16, PAD_ROWS, LANES), LOW)] * 2
        + [pltpu.VMEM((4, PAD_ROWS, LANES), LOW)] * 4
        + [pltpu.VMEM((4, A_ROWS, LANES), LOW)] * 2
        + [pltpu.VMEM((16, B_ROWS, LANES), LOW)] * 2
        + [pltpu.VMEM((WIDE_ROWS + 6, LANES), FULL)] * 2
        + [pltpu.VMEM((32, 2, 8, LANES), FULL)]
        + [dma((16,))] * 3
        + [dma((4, 5))] * 2
        + [dma((16, 4))] * 2
        + [dma((4, 5))] * 2
        + [dma((16, 4))] * 2
        + [dma((2,))] * 2
        + [dma((32,))] * 2,
        compiler_params=pltpu.CompilerParams(
            collective_id=1, has_side_effects=True, vmem_limit_bytes=60 * 1024 * 1024
        ),
        name="reduce_gradients",
    )(grad_rows, loss_row)
    return shard_total.reshape(-1), jnp.sum(totals[0]), totals[1, 0, 0]


ROWS = 256
ENC_CHUNK = 64
FETCHED = ("vecs", "embed", "enc_qkv", "enc_out", "enc_up", "enc_down", "project")
BACKWARD_FETCHED = ("vecs", "project", "enc_down", "enc_up", "enc_out", "enc_qkv")


def encoder_forward_kernel(
    part_ref,
    visible_ref,
    segments_ref,
    patches_ref,
    table_ref,
    flat_ref,
    vis_rows,
    embedded,
    normed_a,
    qkv_rows,
    attn_out,
    after_attn,
    normed_b,
    slope,
    hidden_act,
    encoded,
    final_enc,
    projected,
    row_facts,
    column_facts,
    sems,
    *buffers,
):
    ready = fetch(flat_ref, FETCHED, buffers, sems)
    part = part_ref[0]
    total = segments_ref.shape[1]
    images = IMG_SEQ // 2
    spare = ROWS - images * VIS
    segments = segments_ref[...]
    image = segments - part * images
    inside = (image >= 0) & (image < images)
    padding = segments == IMG_SEQ
    flags = jnp.concatenate(
        [
            inside.astype(FULL),
            padding.astype(FULL),
            jnp.zeros((6, total), FULL),
        ],
        axis=0,
    ).astype(LOW)
    row = lax.broadcasted_iota(jnp.int32, (total, total), 0)
    column = lax.broadcasted_iota(jnp.int32, (total, total), 1)
    counts = dot_nn(flags, (row <= column).astype(FULL).astype(LOW)).astype(jnp.int32)
    inside_count, padding_count = counts[0:1], counts[1:2]
    padding_slot = padding_count - part * spare
    chosen = inside | (padding & (padding_slot >= 1) & (padding_slot <= spare))
    slot = inside_count + jnp.clip(padding_slot, 0, spare) - 1
    slot = jnp.where(chosen, slot, -1)
    select = (lax.broadcasted_iota(jnp.int32, (ROWS, total), 0) == slot).astype(FULL).astype(LOW)
    facts = jnp.concatenate(
        [segments.astype(FULL), patches_ref[...].astype(FULL), jnp.zeros((LANES - 2, total), FULL)],
        axis=0,
    ).astype(LOW)
    row_facts[...] = dot_nt(facts[0:16], select)
    column_facts[...] = dot_nt(select, facts)
    vis_rows[...] = dot_nn(select, visible_ref[...]).astype(LOW)
    patch = column_facts[:, 1:2].astype(jnp.int32)
    spot = (lax.broadcasted_iota(jnp.int32, (ROWS, table_ref.shape[1]), 1) == patch).astype(FULL).astype(LOW)
    embedded[...] = dot_nn(spot, table_ref[0]) + dot_nn(spot, table_ref[1]) + dot_nn(spot, table_ref[2])
    w_embed = ready(1)
    product_into(embedded, vis_rows, w_embed, D, residual=embedded)
    ready(0)
    vec = vec_reader(buffers[0], 0, D // LANES)
    norm_into(normed_a, embedded, vec(0), vec(1), ROWS, ENC_CHUNK)
    w_qkv = ready(2)
    product_into(qkv_rows, normed_a, w_qkv, 3 * D)
    allowed = column_facts[:, 0:1] == row_facts[0:1, :]
    allowed = jnp.concatenate([allowed.astype(FULL)] * 2, axis=0) > 0.5

    def attend(step):
        for part in range(2):
            attend_into(
                attn_out, qkv_rows, pl.ds(0, ROWS), 2 * step + part, D, allowed, D // HEADS
            )

    loop(D // LANES // 2, attend)
    w_out = ready(3)
    product_into(after_attn, attn_out, w_out, D, residual=embedded)
    norm_into(normed_b, after_attn, vec(2), vec(3), ROWS, ENC_CHUNK)
    w_up = ready(4)
    up_into(hidden_act, slope, normed_b, w_up, FF, 512)
    w_down = ready(5)
    product_into(encoded, hidden_act, w_down, D, residual=after_attn)
    norm_into(final_enc, encoded, vec(4), vec(5), ROWS, ENC_CHUNK)
    w_proj = ready(6)
    product_into(projected, final_enc, w_proj, DD)


def encoder_forward(part, visible_rows, segments, patch_ids, flat_weights):
    hbm = pl.BlockSpec(memory_space=pltpu.HBM)
    vmem = pl.BlockSpec(memory_space=pltpu.VMEM)
    smem = pl.BlockSpec(memory_space=pltpu.SMEM)
    table = jnp.asarray(split_low(position_table(D, 256)))
    low, full = (lambda *s: jax.ShapeDtypeStruct(s, LOW)), (lambda *s: jax.ShapeDtypeStruct(s, FULL))
    return pl.pallas_call(
        encoder_forward_kernel,
        out_shape=[
            low(ROWS, PIX),
            full(ROWS, D),
            low(ROWS, D),
            low(ROWS, 3 * D),
            low(ROWS, D),
            full(ROWS, D),
            low(ROWS, D),
            full(ROWS, FF),
            low(ROWS, FF),
            full(ROWS, D),
            low(ROWS, D),
            low(ROWS, DD),
            full(16, ROWS),
            full(ROWS, LANES),
        ],
        in_specs=[smem] + [vmem] * 4 + [hbm],
        out_specs=[vmem] * 14,
        scratch_shapes=[pltpu.SemaphoreType.DMA((7,))] + tile_buffers(FETCHED),
        compiler_params=pltpu.CompilerParams(vmem_limit_bytes=60 * 1024 * 1024),
        name="encoder_forward",
    )(part, visible_rows, segments, patch_ids, table, flat_weights)


def encoder_backward_kernel(
    vis_rows,
    embedded,
    normed_a,
    qkv_rows,
    attn_out,
    after_attn,
    normed_b,
    slope,
    hidden_act,
    encoded,
    final_enc,
    row_facts,
    column_facts,
    grad_projected,
    decoder_vecs,
    weights_ref,
    partial_ref,
    flat_ref,
    grad_rows,
    upper,
    branch,
    grad_pre,
    middle,
    grad_attn,
    grad_qkv,
    vec_grads,
    turned,
    stage,
    vec_full,
    vec_stage,
    stage_sem,
    sems,
    *buffers,
):
    del partial_ref
    ready = fetch(weights_ref, BACKWARD_FETCHED, buffers, sems)
    tiles = entry_tiles()
    ready(0)
    vec = vec_reader(buffers[0], 0, D // LANES)
    grad_of = lambda index: vec_grads.at[pl.ds(index, 1), :]

    emit = Emitter(flat_ref, turned, stage, stage_sem)

    emit("project", final_enc, grad_projected)
    w_proj = ready(1)
    product_t_into(upper, grad_projected, w_proj, D)
    norm_back(grad_rows, encoded, upper, None, vec(4), grad_of(4), grad_of(5), ROWS, ENC_CHUNK)
    branch[...] = grad_rows[...].astype(LOW)
    emit("enc_down", hidden_act, branch)
    w_down = ready(2)
    down_back_into(grad_pre, branch, w_down, slope, FF, 512)
    emit("enc_up", normed_b, grad_pre)
    w_up = ready(3)
    product_t_into(upper, grad_pre, w_up, D)
    norm_back(grad_rows, after_attn, upper, grad_rows, vec(2), grad_of(2), grad_of(3), ROWS, ENC_CHUNK)
    middle[...] = grad_rows[...].astype(LOW)
    emit("enc_out", attn_out, middle)
    w_out = ready(4)
    product_t_into(grad_attn, middle, w_out, D)
    allowed = column_facts[:, 0:1] == row_facts[0:1, :]
    allowed = jnp.concatenate([allowed.astype(FULL)] * 2, axis=0) > 0.5

    def attend_back(step):
        for part in range(2):
            attend_back_into(
                grad_qkv,
                grad_attn,
                qkv_rows,
                pl.ds(0, ROWS),
                2 * step + part,
                D,
                allowed,
                D // HEADS,
            )

    loop(D // LANES // 2, attend_back)
    emit("enc_qkv", normed_a, grad_qkv)
    w_qkv = ready(5)
    product_t_into(upper, grad_qkv, w_qkv, D)
    norm_back(grad_rows, embedded, upper, grad_rows, vec(0), grad_of(0), grad_of(1), ROWS, ENC_CHUNK)
    branch[...] = grad_rows[...].astype(LOW)
    emit("embed", vis_rows, branch)
    emit.finish()
    groups = D // LANES
    for index in range(6):
        for group in range(groups):
            vec_full[pl.ds(index * groups + group, 1), :] = vec_grads[
                pl.ds(index, 1), pl.ds(group * LANES, LANES)
            ]
    base, groups = 6 * groups, DD // LANES
    for index in range(7):
        for group in range(groups):
            vec_full[pl.ds(base + index * groups + group, 1), :] = decoder_vecs[
                pl.ds(index, 1), pl.ds(group * LANES, LANES)
            ]
    vec_stage[...] = vec_full[...].astype(LOW).reshape(4, TALL, LANES)
    copy = pltpu.make_async_copy(vec_stage, flat_ref.at[pl.ds(tiles["enc_vecs"][0], 4)], stage_sem.at[0])
    copy.start()
    copy.wait()


def encoder_backward(saved, grad_projected, flat_weights, decoder_vec_grads, flat):
    hbm = pl.BlockSpec(memory_space=pltpu.HBM)
    vmem = pl.BlockSpec(memory_space=pltpu.VMEM)
    inputs = [*saved, grad_projected, decoder_vec_grads, flat_weights, flat]
    low, full = (lambda *s: pltpu.VMEM(s, LOW)), (lambda *s: pltpu.VMEM(s, FULL))
    return pl.pallas_call(
        encoder_backward_kernel,
        out_shape=jax.ShapeDtypeStruct(flat.shape, LOW),
        in_specs=[vmem] * 15 + [hbm] * 2,
        out_specs=hbm,
        input_output_aliases={len(inputs) - 1: 0},
        scratch_shapes=[
            full(ROWS, D),
            full(ROWS, D),
            low(ROWS, D),
            low(ROWS, FF),
            low(ROWS, D),
            low(ROWS, D),
            low(ROWS, 3 * D),
            full(8, D),
            low(FF, ROWS),
            low(2, FF * D // (TALL * LANES), TALL, LANES),
            full(64, LANES),
            low(4, TALL, LANES),
            pltpu.SemaphoreType.DMA((2,)),
            pltpu.SemaphoreType.DMA((6,)),
        ]
        + tile_buffers(BACKWARD_FETCHED),
        compiler_params=pltpu.CompilerParams(vmem_limit_bytes=60 * 1024 * 1024),
        name="encoder_backward",
    )(*inputs)


IMAGES = 5
DECODER_FETCHED = ("vecs", "dec_qkv", "dec_out", "dec_up", "dec_down", "pixel")
IMG_ROWS = 208
DEC_ROWS = IMAGES * IMG_ROWS


def decoder_kernel(
    part_ref,
    projected,
    row_facts,
    targets_ref,
    table_ref,
    weights_ref,
    flat_ref,
    grad_projected,
    vec_grads,
    loss_ref,
    dec_in,
    low_rows,
    qkv_rows,
    attn_out,
    after_attn,
    normed_b,
    slope,
    hidden_act,
    decoded,
    final_dec,
    grad_pred,
    upper,
    masked,
    turned,
    stage,
    stage_sem,
    sems,
    *buffers,
    mask_total,
):
    ready = fetch(weights_ref, DECODER_FETCHED, buffers, sems)
    tiles = entry_tiles()
    ready(0)
    vec = vec_reader(buffers[0], 6 * D // LANES, DD // LANES)
    grad_of = lambda index: vec_grads.at[pl.ds(index, 1), :]
    part = part_ref[0]
    image_of = row_facts[0:1, :].astype(jnp.int32) - part * IMAGES
    patch_of = row_facts[1:2, :].astype(jnp.int32)
    patch = lax.broadcasted_iota(jnp.int32, (IMG_ROWS, ROWS), 0)

    def selector(index):
        return ((patch_of == patch) & (image_of == index)).astype(FULL)

    def place(index):
        at = span(index, IMG_ROWS)
        select = selector(index)
        real = (patch[:, 0:1] < PATCHES).astype(FULL)
        hidden = real * (1.0 - jnp.sum(select, axis=-1, keepdims=True))
        masked[at, :] = jnp.broadcast_to(hidden, (IMG_ROWS, LANES))
        dec_in[at, :] = dot_nn(select.astype(LOW), projected[...]) + hidden * vec(6) + table_ref[...]

    loop(IMAGES, place)
    norm_into(low_rows, dec_in, vec(0), vec(1), DEC_ROWS, IMG_ROWS)
    w_qkv = ready(1)
    product_into(qkv_rows, low_rows, w_qkv, 3 * DD)
    head_size = DD // DHEADS
    heads = LANES // head_size
    allowed = lax.broadcasted_iota(jnp.int32, (heads * IMG_ROWS, IMG_ROWS), 1) < PATCHES
    groups = DD // LANES

    def attend(step):
        rows = span(step, IMG_ROWS)
        for at in range(groups):
            attend_into(attn_out, qkv_rows, rows, at, DD, allowed, head_size)

    loop(IMAGES, attend)
    w_out = ready(2)
    product_into(after_attn, attn_out, w_out, DD, residual=dec_in)
    norm_into(normed_b, after_attn, vec(2), vec(3), DEC_ROWS, IMG_ROWS)
    w_up = ready(3)
    up_into(hidden_act, slope, normed_b, w_up, DFF, TILE)
    w_down = ready(4)
    product_into(decoded, hidden_act, w_down, DD, residual=after_attn)
    norm_into(final_dec, decoded, vec(4), vec(5), DEC_ROWS, IMG_ROWS)
    w_pix = ready(5)
    loss_ref[...] = jnp.zeros_like(loss_ref)

    def compare(index):
        at = span(index, IMG_ROWS)
        image = pl.ds(0, PATCHES)
        goal, _ = norm_parts(targets_ref[index].astype(FULL))
        goal = jnp.concatenate([goal, jnp.zeros((IMG_ROWS - PATCHES, PIX), FULL)], axis=0)
        error = dot_nn(final_dec[at, :], w_pix.column_tile(0, PIX)) - goal
        weight = masked[at, 0:1]
        rows = jnp.mean(error * error, axis=-1, keepdims=True) * weight
        loss_ref[...] = loss_ref[...] + jnp.sum(rows) * (1.0 / mask_total)
        grad_pred[at, :] = (weight * error * (2.0 / (PIX * mask_total))).astype(LOW)

    loop(IMAGES, compare)

    emit = Emitter(flat_ref, turned, stage, stage_sem)

    emit("pixel", final_dec, grad_pred)
    product_t_into(upper, grad_pred, w_pix, DD)
    grad_rows, branch = decoded, final_dec
    norm_back(grad_rows, decoded, upper, None, vec(4), grad_of(4), grad_of(5), DEC_ROWS, IMG_ROWS)
    branch[...] = grad_rows[...].astype(LOW)
    emit("dec_down", hidden_act, branch)
    grad_pre = hidden_act
    down_back_into(grad_pre, branch, w_down, slope, DFF, TILE)
    emit("dec_up", normed_b, grad_pre)
    product_t_into(upper, grad_pre, w_up, DD)
    norm_back(grad_rows, after_attn, upper, grad_rows, vec(2), grad_of(2), grad_of(3), DEC_ROWS, IMG_ROWS)
    branch[...] = grad_rows[...].astype(LOW)
    emit("dec_out", attn_out, branch)
    grad_attn, grad_qkv = normed_b, grad_pre.at[:, pl.ds(0, 3 * DD)]
    product_t_into(grad_attn, branch, w_out, DD)

    def attend_back(step):
        rows = span(step, IMG_ROWS)
        for at in range(groups):
            attend_back_into(grad_qkv, grad_attn, qkv_rows, rows, at, DD, allowed, head_size)

    loop(IMAGES, attend_back)
    emit("dec_qkv", low_rows, grad_qkv)
    emit.finish()
    product_t_into(upper, grad_qkv, w_qkv, DD)
    norm_back(grad_rows, dec_in, upper, grad_rows, vec(0), grad_of(0), grad_of(1), DEC_ROWS, IMG_ROWS)
    upper[pl.ds(0, ROWS), :] = jnp.zeros((ROWS, DD), FULL)

    def collect(index, token):
        at = span(index, IMG_ROWS)
        rows = grad_rows[at, :]
        token = token + jnp.sum((rows * masked[at, 0:1]).reshape(IMG_ROWS // 8, 8, DD), axis=0)
        upper[pl.ds(0, ROWS), :] = upper[pl.ds(0, ROWS), :] + dot_tn(
            selector(index).astype(LOW), rows.astype(LOW)
        )
        return token

    token = lax.fori_loop(0, IMAGES, collect, jnp.zeros((8, DD), FULL))
    grad_of(6)[...] = jnp.sum(token, axis=0, keepdims=True)
    grad_projected[...] = upper[pl.ds(0, ROWS), :].astype(LOW)


def decoder_step(part, projected, row_facts, targets, flat_weights, mask_total):
    hbm = pl.BlockSpec(memory_space=pltpu.HBM)
    vmem = pl.BlockSpec(memory_space=pltpu.VMEM)
    smem = pl.BlockSpec(memory_space=pltpu.SMEM)
    table = jnp.asarray(position_table(DD, IMG_ROWS))
    low, full = (lambda *s: pltpu.VMEM(s, LOW)), (lambda *s: pltpu.VMEM(s, FULL))
    return pl.pallas_call(
        partial(decoder_kernel, mask_total=mask_total),
        out_shape=[
            jax.ShapeDtypeStruct(flat_weights.shape, LOW),
            jax.ShapeDtypeStruct((ROWS, DD), LOW),
            jax.ShapeDtypeStruct((8, DD), FULL),
            jax.ShapeDtypeStruct((1, LANES), FULL),
        ],
        in_specs=[smem] + [vmem] * 4 + [hbm],
        out_specs=[hbm] + [vmem] * 3,
        scratch_shapes=[
            full(DEC_ROWS, DD),
            low(DEC_ROWS, DD),
            low(DEC_ROWS, 3 * DD),
            low(DEC_ROWS, DD),
            full(DEC_ROWS, DD),
            low(DEC_ROWS, DD),
            full(DEC_ROWS, DFF),
            low(DEC_ROWS, DFF),
            full(DEC_ROWS, DD),
            low(DEC_ROWS, DD),
            low(DEC_ROWS, PIX),
            full(DEC_ROWS, DD),
            full(DEC_ROWS, LANES),
            low(DFF, DEC_ROWS),
            low(2, DFF * DD // (TALL * LANES), TALL, LANES),
            pltpu.SemaphoreType.DMA((2,)),
            pltpu.SemaphoreType.DMA((6,)),
        ]
        + tile_buffers(DECODER_FETCHED),
        compiler_params=pltpu.CompilerParams(vmem_limit_bytes=62 * 1024 * 1024),
        name="decoder_step",
    )(part, projected, row_facts, targets, table, flat_weights)


def to_tiles(full_flat):
    pieces, offset = [], 0
    for _, (rows, columns) in layout()[:11]:
        piece = full_flat[offset : offset + rows * columns]
        piece = piece.reshape(rows // TALL, TALL, columns // LANES, LANES)
        pieces.append(piece.transpose(0, 2, 1, 3).reshape(-1, LANES))
        offset += rows * columns
    return jnp.concatenate([*pieces, full_flat[offset:].reshape(-1, LANES)])


def from_tiles(rows_flat):
    pieces, offset = [], 0
    for _, (rows, columns) in layout()[:11]:
        count = rows * columns // LANES
        piece = rows_flat[offset : offset + count]
        piece = piece.reshape(rows // TALL, columns // LANES, TALL, LANES)
        pieces.append(piece.transpose(0, 2, 1, 3).reshape(-1))
        offset += count
    return jnp.concatenate([*pieces, rows_flat[offset:].reshape(-1)])


def shards(visible, segments, patch_ids, targets, master, moment_one, moment_two, step_count):
    part = lax.axis_index("seq")
    in_kernels = master.shape[0] == SHARD_ROWS * LANES and lax.axis_size("dp") == 16
    if in_kernels:
        flat_weights, visible_rows = gather_weights(
            master.reshape(SHARD_ROWS, LANES), visible[0]
        )
    else:
        full_flat = lax.all_gather(master.astype(LOW), ("seq", "dp"), axis=0, tiled=True)
        flat_weights = to_tiles(full_flat)
        visible_rows = lax.all_gather(visible[0], "seq", axis=0, tiled=True)
    flat_weights = flat_weights.reshape(-1, TALL, LANES)
    part_row = part.reshape(1).astype(jnp.int32)
    mask_total = (PATCHES - VIS) * IMG_SEQ * visible.shape[0] * lax.axis_size("dp")
    *saved, projected, row_facts, column_facts = encoder_forward(
        part_row, visible_rows, segments, patch_ids, flat_weights
    )
    flat_grads, grad_projected, decoder_vec_grads, loss_row = decoder_step(
        part_row, projected, row_facts, targets[0], flat_weights, mask_total
    )
    flat_grads = encoder_backward(
        [*saved, row_facts, column_facts],
        grad_projected,
        flat_weights,
        decoder_vec_grads,
        flat_grads,
    )
    flat_grads = flat_grads.reshape(-1, LANES)
    if in_kernels:
        grad_shard, square_sum, loss_sum = reduce_gradients(flat_grads, loss_row)
    else:
        grad_flat = from_tiles(flat_grads.astype(FULL))
        grad_shard = lax.psum_scatter(grad_flat, ("seq", "dp"), scatter_dimension=0, tiled=True)
        square_sum, loss_sum = lax.psum(
            (jnp.sum(grad_shard * grad_shard), loss_row[0, 0]), ("seq", "dp")
        )
    grad_norm = jnp.sqrt(square_sum)
    clipped = grad_shard * jnp.minimum(1.0, clip_limit / (grad_norm + 1e-06))
    new_one = beta_mom * moment_one + (1.0 - beta_mom) * clipped
    new_two = beta_mom * moment_two + (1.0 - beta_mom) * clipped * clipped
    correction = 1.0 - jnp.power(jnp.float32(beta_mom), step_count[0].astype(jnp.float32))
    new_master = master - learn_rate * (
        new_one / correction / (jnp.sqrt(new_two / correction) + adam_eps) + decay_rate * master
    )
    return (new_one, new_two, new_master, new_master.astype(jnp.bfloat16), grad_norm, loss_sum)


def solution(mesh):
    in_specs = (
        P("dp", "seq", None),
        P("dp", None),
        P("dp", None),
        P("dp", "seq", None, None),
        P(("seq", "dp")),
        P(("seq", "dp")),
        P(("seq", "dp")),
        P(),
    )
    out_specs = (P(("seq", "dp")), P(("seq", "dp")), P(("seq", "dp")), P(("seq", "dp")), P(), P())
    return jax.shard_map(shards, mesh=mesh, in_specs=in_specs, out_specs=out_specs, check_vma=False)
```

```python
from functools import partial
import math

import jax
import jax.numpy as jnp
import ml_dtypes
import numpy as np
from jax import lax
from jax.experimental import pallas as pl
from jax.experimental.pallas import tpu as pltpu
from jax.sharding import PartitionSpec as P

D = 768
HEADS = 12
FF = 3072
DD = 512
DHEADS = 16
DFF = 2048
PIX = 768
PATCHES = 196
VIS = 49
IMG_SEQ = 10


norm_eps = 1e-06
neg_big = -1000000000.0
clip_limit = 0.0001
learn_rate = 0.03
decay_rate = 0.05
adam_eps = 1e-08
beta_mom = 0.5


def layout():
    return [
        ("embed", (PIX, D)),
        ("enc_qkv", (D, 3 * D)),
        ("enc_out", (D, D)),
        ("enc_up", (D, FF)),
        ("enc_down", (FF, D)),
        ("project", (D, DD)),
        ("dec_qkv", (DD, 3 * DD)),
        ("dec_out", (DD, DD)),
        ("dec_up", (DD, DFF)),
        ("dec_down", (DFF, DD)),
        ("pixel", (DD, PIX)),
        ("enc_vecs", (6, D)),
        ("dec_vecs", (7, DD)),
    ]


def unflatten(flat_vec):
    params = {}
    offset = 0
    for entry_name, entry_shape in layout():
        entry_size = entry_shape[0] * entry_shape[1]
        params[entry_name] = flat_vec[offset : offset + entry_size].reshape(entry_shape)
        offset += entry_size
    return params


LOW = jnp.bfloat16
FULL = jnp.float32
TILE = 256
TALL = 16
LANES = 128
NEG = neg_big
ROOT_HALF = math.sqrt(0.5)
LOG2_E = 1.0 / math.log(2.0)
BELL = 1.0 / math.sqrt(2.0 * math.pi)


def dot_nn(left, right):
    return lax.dot_general(left, right, (((1,), (0,)), ((), ())), preferred_element_type=FULL)


def dot_nt(left, right):
    return lax.dot_general(left, right, (((1,), (1,)), ((), ())), preferred_element_type=FULL)


def dot_tn(left, right):
    return lax.dot_general(left, right, (((0,), (0,)), ((), ())), preferred_element_type=FULL)


def loop(count, body):
    def one(step, carry):
        body(step)
        return carry

    lax.fori_loop(0, count, one, 0)


def unrolled(count, body):
    size = next(size for size in (3, 2, 1) if count % size == 0)

    def one(step):
        for part in range(size):
            body(step * size + part)

    loop(count // size, one)


def span(step, size):
    return pl.ds(pl.multiple_of(step * size, size), size)


def norm_parts(rows):
    average = jnp.mean(rows, axis=-1, keepdims=True)
    centered = rows - average
    scale = lax.rsqrt(jnp.mean(centered * centered, axis=-1, keepdims=True) + norm_eps)
    return centered * scale, scale


def norm_into(dst, src, gain, shift, rows, chunk):
    def one(step):
        at = span(step, chunk)
        unit, _ = norm_parts(src[at, :])
        dst[at, :] = (unit * gain + shift).astype(LOW)

    loop(rows // chunk, one)


def norm_back(dst, src, grad, residual, gain, gain_grad, shift_grad, rows, chunk):
    width = src.shape[1]

    def one(step, carry):
        at = span(step, chunk)
        unit, scale = norm_parts(src[at, :])
        upper = grad[at, :]
        gains = carry[0] + jnp.sum((upper * unit).reshape(chunk // 8, 8, width), axis=0)
        shifts = carry[1] + jnp.sum(upper.reshape(chunk // 8, 8, width), axis=0)
        upper = upper * gain
        lower = scale * (
            upper
            - jnp.mean(upper, axis=-1, keepdims=True)
            - unit * jnp.mean(upper * unit, axis=-1, keepdims=True)
        )
        if residual is not None:
            lower = lower + residual[at, :]
        dst[at, :] = lower
        return gains, shifts

    zero = jnp.zeros((8, width), FULL)
    gains, shifts = lax.fori_loop(0, rows // chunk, one, (zero, zero))
    gain_grad[...] = jnp.sum(gains, axis=0, keepdims=True)
    shift_grad[...] = jnp.sum(shifts, axis=0, keepdims=True)


class Blocked:
    def __init__(self, ref, rows, columns):
        self.rows, self.groups = rows, columns // LANES
        self.ref = ref.reshape(rows // TALL, self.groups, TALL, LANES)

    def piece(self, first_row, rows, first_group, groups):
        tall = pl.ds(first_row // TALL, rows // TALL)
        parts = [
            self.ref[tall, first_group + index].reshape(rows, LANES) for index in range(groups)
        ]
        return parts[0] if groups == 1 else jnp.concatenate(parts, axis=1)

    def column_tile(self, step, tile):
        count = tile // LANES
        return self.piece(0, self.rows, step * count, count)

    def row_tile(self, step, tile):
        return self.piece(step * tile, tile, 0, self.groups)


def product_into(dst, left, right, columns, tile=TILE, residual=None):
    def one(step):
        at = span(step, tile)
        value = dot_nn(left[...], right.column_tile(step, tile))
        if residual is not None:
            value = value + residual[:, at]
        dst[:, at] = value.astype(dst.dtype)

    unrolled(columns // tile, one)


def product_t_into(dst, left, right, columns, tile=TILE):
    def one(step):
        dst[:, span(step, tile)] = dot_nt(left[...], right.row_tile(step, tile)).astype(dst.dtype)

    unrolled(columns // tile, one)


def up_into(act, slope, left, w_up, columns, tile):
    def one(step):
        at = span(step, tile)
        hidden = dot_nn(left[...], w_up.column_tile(step, tile))
        share = 0.5 * (1.0 + lax.erf(hidden * ROOT_HALF))
        act[:, at] = (hidden * share).astype(LOW)
        slope[:, at] = share + hidden * (BELL * jnp.exp(-0.5 * hidden * hidden))

    unrolled(columns // tile, one)


def down_back_into(grad_pre, branch, w_down, slope, columns, tile):
    def one(step):
        at = span(step, tile)
        grad_pre[:, at] = (dot_nt(branch[...], w_down.row_tile(step, tile)) * slope[:, at]).astype(LOW)

    unrolled(columns // tile, one)


def weight_grad(out, out_tile, left, right, turned, stage, stage_sem, slot=0, before=None):
    rows, columns = left.shape[1], right.shape[1]
    groups = columns // LANES
    high = rows // TALL
    count = high * groups

    def turn(step):
        turned[span(step, TILE), :] = left[:, span(step, TILE)].T

    loop(rows // TILE, turn)
    if before is not None:
        before()
    tiles = stage.at[slot, pl.ds(0, count)].reshape(high, groups, TALL, LANES)
    piece = columns // TILE
    unroll = next(u for u in (3, 2, 1) if piece % u == 0)

    def across(step):
        for part in range(unroll):
            tile = step * unroll + part
            value = dot_nn(turned[pl.ds(0, rows), :], right[:, span(tile, TILE)]).astype(LOW)
            for half in range(2):
                tiles[:, tile * 2 + half] = value[:, half * LANES : (half + 1) * LANES].reshape(
                    high, TALL, LANES
                )

    loop(piece // unroll, across)
    copy = lambda: pltpu.make_async_copy(
        stage.at[slot, pl.ds(0, count)], out.at[pl.ds(out_tile, count)], stage_sem.at[slot]
    )
    copy().start()
    return lambda: copy().wait()


class Emitter:
    def __init__(self, out, turned, stage, stage_sem):
        self.args = turned, stage, stage_sem
        self.out, self.tiles, self.waits = out, entry_tiles(), []

    def __call__(self, entry, left, right):
        index = len(self.waits)
        before = self.waits[index - 2] if index >= 2 else None
        self.waits.append(
            weight_grad(self.out, self.tiles[entry][0], left, right, *self.args, index % 2, before)
        )

    def finish(self):
        for wait in self.waits[-2:]:
            wait()


def head_masks(head_size, dtype):
    lane = lax.broadcasted_iota(jnp.int32, (1, LANES), 1) // head_size
    return [(lane == head).astype(dtype) for head in range(LANES // head_size)]


def stacked(rows, masks):
    return jnp.concatenate([rows * mask for mask in masks], axis=0)


def unstacked(rows, masks, size):
    total = None
    for index, mask in enumerate(masks):
        piece = rows[index * size : (index + 1) * size] * mask
        total = piece if total is None else total + piece
    return total


def soft_rows(queries, keys, allowed, scale):
    scores = jnp.where(allowed, dot_nt(queries, keys), NEG)
    scores = scores - jnp.max(scores, axis=-1, keepdims=True)
    powers = jnp.exp2(scores * (scale * LOG2_E))
    return powers * (1.0 / jnp.sum(powers, axis=-1, keepdims=True))


def attend_into(dst, qkv, rows, at, width, allowed, head_size):
    masks = head_masks(head_size, LOW)
    size = rows.size
    column = lambda part: pl.ds(pl.multiple_of(part * width + at * LANES, LANES), LANES)
    queries = stacked(qkv[rows, column(0)], masks)
    probs = soft_rows(queries, qkv[rows, column(1)], allowed, head_size**-0.5).astype(LOW)
    values = dot_nn(probs, qkv[rows, column(2)])
    dst[rows, column(0)] = unstacked(values, head_masks(head_size, FULL), size).astype(LOW)


def soft_columns(keys, queries, allowed, scale, heads):
    scores = jnp.where(allowed, dot_nt(keys, queries), NEG)
    scores = scores.reshape(heads, scores.shape[0] // heads, scores.shape[1])
    scores = scores - jnp.max(scores, axis=1, keepdims=True)
    powers = jnp.exp2(scores * (scale * LOG2_E))
    return powers * (1.0 / jnp.sum(powers, axis=1, keepdims=True))


def attend_back_into(dst, grad, qkv, rows, at, width, allowed, head_size):
    masks = head_masks(head_size, LOW)
    lanes = head_masks(head_size, FULL)
    size = rows.size
    scale = head_size**-0.5
    column = lambda part: pl.ds(pl.multiple_of(part * width + at * LANES, LANES), LANES)
    queries = qkv[rows, column(0)]
    keys = stacked(qkv[rows, column(1)], masks)
    grads = grad[rows, column(0)]
    probs = soft_columns(keys, queries, allowed, scale, len(masks))
    slopes = dot_nt(stacked(qkv[rows, column(2)], masks), grads).reshape(probs.shape)
    slopes = probs * (slopes - jnp.sum(slopes * probs, axis=1, keepdims=True))
    flat = (len(masks) * size, size)
    slopes, probs = slopes.reshape(flat).astype(LOW), probs.reshape(flat).astype(LOW)
    dst[rows, column(0)] = (dot_tn(keys, slopes).T * scale).astype(LOW)
    dst[rows, column(1)] = (unstacked(dot_nn(slopes, queries), lanes, size) * scale).astype(LOW)
    dst[rows, column(2)] = unstacked(dot_nn(probs, grads), lanes, size).astype(LOW)


def entry_tiles():
    tiles, offset = {}, 0
    for entry_name, (rows, columns) in layout():
        tiles[entry_name] = (offset // (TALL * LANES), rows, columns)
        offset += rows * columns
    tiles["vecs"] = (tiles["enc_vecs"][0], 4 * TALL, LANES)
    return tiles


def vec_reader(buffer, first, groups):
    rows = buffer[...].reshape(4 * TALL, LANES).astype(FULL)

    def vec(index):
        start = first + index * groups
        return jnp.concatenate([rows[start + g : start + g + 1] for g in range(groups)], axis=1)

    return vec


def fetch(flat, names, buffers, sems):
    tiles = entry_tiles()

    def build(index):
        start, rows, columns = tiles[names[index]]
        count = rows * columns // (TALL * LANES)
        return pltpu.make_async_copy(flat.at[pl.ds(start, count)], buffers[index], sems.at[index])

    for index in range(len(names)):
        build(index).start()

    def ready(index):
        build(index).wait()
        _, rows, columns = tiles[names[index]]
        return Blocked(buffers[index], rows, columns)

    return ready


def tile_buffers(names):
    tiles = entry_tiles()
    return [
        pltpu.VMEM((tiles[entry][1] * tiles[entry][2] // (TALL * LANES), TALL, LANES), LOW)
        for entry in names
    ]


def position_table(columns, padded):
    half = columns // 2
    frequency = np.exp(
        np.float32(-math.log(10000.0)) * np.arange(half, dtype=np.float32) / np.float32(half)
    ).astype(np.float32)
    angles = np.arange(PATCHES, dtype=np.float32)[:, None] * frequency
    table = np.zeros((padded, columns), np.float32)
    table[:PATCHES] = np.concatenate(
        [np.sin(angles.astype(np.float64)), np.cos(angles.astype(np.float64))], axis=-1
    )
    return table


def split_low(table):
    parts, rest = [], table.astype(np.float64)
    for _ in range(3):
        part = rest.astype(ml_dtypes.bfloat16)
        parts.append(part)
        rest = rest - part.astype(np.float64)
    return np.stack(parts)


MESH = pl.DeviceIdType.MESH
A_HALF = 1104
A_ROWS = 2 * A_HALF
B_HALF = 320
B_ROWS = 2 * B_HALF
SHARD_ROWS = 2834
PAD_ROWS = A_ROWS + B_ROWS
B_TRUE = SHARD_ROWS - A_ROWS
HALO = 384
HALO_STEP = 64
WIDE_ROWS = SHARD_ROWS + 2 * HALO
PARTS = {
    "a1": (0, A_HALF),
    "a2": (A_HALF, A_HALF),
    "b": (A_ROWS, B_ROWS),
    "b1": (A_ROWS, B_HALF),
    "b2": (A_ROWS + B_HALF, B_HALF),
}
TRUE_PARTS = {**PARTS, "b": (A_ROWS, B_TRUE), "b2": (A_ROWS + B_HALF, B_TRUE - B_HALF)}
SLOTS = {"a1": 0, "a2": 1, "b": 2, "b1": 2, "b2": 3}
COLUMNS = "oxyd"
ARRIVALS = {
    0: (
        12, 22, 102, 10, 20, 100, 11, 21, 101, 33, 34, 112, 122, 30, 110, 202, 120, 31, 200, 121,
        111, 201, 132, 130, 210, 212, 220, 131, 222, 302, 221, 211, 300, 230, 231, 301, 320, 310,
        232, 312, 321, 311, 322, 332, 330, 331,
    ),
    1: (
        2, 112, 122, 202, 0, 110, 120, 200, 1, 111, 121, 201, 133, 134, 12, 212, 22, 222, 20, 10,
        32, 302, 130, 210, 300, 220, 11, 301, 232, 21, 131, 312, 221, 211, 322, 332, 30, 310,
        230, 311, 320, 31, 321, 231, 330, 331,
    ),
}


def item_of(code):
    return code // 100, COLUMNS[code // 10 % 10], list(PARTS)[code % 10]


def own_item(inner, part):
    return 100 * inner + list(PARTS).index(part)


class Place:
    def __init__(self):
        self.core = lax.axis_index("seq")
        self.chip = lax.axis_index("dp")
        chip = self.chip
        self.z = chip // 4
        y, x = (chip // 2) % 2, chip % 2
        self.col = chip % 4
        self.col_x = self.col + 1 - 2 * x
        self.col_y = self.col + 2 - 4 * y
        self.col_d = self.col_x + 2 - 4 * y
        self.columns = {"o": self.col, "x": self.col_x, "y": self.col_y, "d": self.col_d}
        self.side = self.z // 2
        sign = 1 - 2 * self.side
        self.inner = self.z + self.side * (3 - 2 * self.z)
        self.me = 16 * self.core + chip
        self.devices = {
            "x": (self.core, 4 * self.z + self.col_x),
            "y": (self.core, 4 * self.z + self.col_y),
            "far": (self.core, chip + 4 * sign),
            "near": (self.core, chip - 4 * sign * self.inner),
            "core": (1 - self.core, chip),
            "next": self.ring(1),
            "back": self.ring(31),
        }

    def ring(self, step):
        peer = (self.me + step) % 32
        return (peer // 16, peer % 16)

    def plane(self, mirrored):
        return mirrored + self.side * (3 - 2 * mirrored)

    def greet(self):
        barrier = pltpu.get_barrier_semaphore()
        for link in ("x", "y", "far", "core", "next", "back"):
            pl.semaphore_signal(
                barrier, inc=1, device_id=self.devices[link], device_id_type=MESH
            )

        @pl.when(self.inner == 1)
        def _():
            pl.semaphore_signal(
                barrier, inc=1, device_id=self.devices["near"], device_id_type=MESH
            )

        pl.semaphore_wait(barrier, 6 + self.inner)


class Outbox:
    def __init__(self):
        self.sent = []

    def send(self, src, dst, send_sem, recv_sem, device):
        def build():
            return pltpu.make_async_remote_copy(
                src_ref=src,
                dst_ref=dst,
                send_sem=send_sem,
                recv_sem=recv_sem,
                device_id=device,
                device_id_type=MESH,
            )

        build().start()
        self.sent.append(build)

    def finish(self):
        for build in self.sent:
            build().wait_send()


def arrived(ref, sem, device):
    pltpu.make_async_remote_copy(
        src_ref=ref, dst_ref=ref, send_sem=sem, recv_sem=sem, device_id=device, device_id_type=MESH
    ).wait_recv()


def by_place(at, body):
    for inner in (0, 1):
        pl.when(at.inner == inner)(partial(body, inner))


def onward(inner, item):
    mirrored, column, part = item_of(item)
    line = ["far", "near"][: 1 + inner]
    if mirrored != inner:
        line = [] if inner == 0 else ["far" if mirrored == 0 else "near"]
    if part[0] == "a":
        if column == "o":
            return [(link, part) for link in [*line, "x", "y"]]
        if (column, part) in (("x", "a1"), ("y", "a2")):
            return [("y" if column == "x" else "x", part)]
        return []
    links = [(link, "b") for link in line]
    if mirrored == inner:
        links = {
            "o": [("x", "b"), ("y", "b")],
            "x": [("y", "b1")],
            "y": [("x", "b2")],
            "d": [],
        }[column] + links
    return links


def gather_exchange(at, flat, source, recv, core_recv, sends, core_send):
    def block(chip, part, core):
        first, size = TRUE_PARTS[part]
        return flat.at[pl.ds((core * 16 + chip) * SHARD_ROWS + first, size)]

    def body(inner):
        out = Outbox()
        diagonal = []

        def pass_on(item):
            mirrored, column, part = item_of(item)
            chip = 4 * at.plane(mirrored) + at.columns[column]
            own = mirrored == inner and column == "o"
            links = onward(inner, item)
            if mirrored == inner and column == "d" and part[0] == "b":
                diagonal.append(part)
                links = links if len(diagonal) == 2 else []
            for link, piece in [*links, ("core", part)]:
                slot = SLOTS[piece]
                ref = block(chip, piece, at.core)
                sent, got = (core_send, core_recv) if link == "core" else (sends[link], recv)
                out.send(
                    source(piece) if own else ref,
                    ref,
                    sent.at[chip, slot],
                    got.at[chip, slot],
                    at.devices[link],
                )

        for part in ("b", "a1", "a2"):
            pass_on(own_item(inner, part))
        for item in ARRIVALS[inner]:
            mirrored, column, part = item_of(item)
            chip = 4 * at.plane(mirrored) + at.columns[column]
            arrived(block(chip, part, at.core), recv.at[chip, SLOTS[part]], at.devices["x"])
            pass_on(item)
        for part in ("b", "a1", "a2"):
            arrived(
                block(at.chip, part, 1 - at.core),
                core_recv.at[at.chip, SLOTS[part]],
                at.devices["x"],
            )
        for item in ARRIVALS[inner]:
            mirrored, column, part = item_of(item)
            chip = 4 * at.plane(mirrored) + at.columns[column]
            ref = block(chip, part, 1 - at.core)
            arrived(ref, core_recv.at[chip, SLOTS[part]], at.devices["x"])
        out.finish()

    by_place(at, body)


def entry_blocks(me, body, edges=False):
    first, stop = me * SHARD_ROWS, me * SHARD_ROWS + SHARD_ROWS
    offset = 0
    for _, (rows, columns) in layout()[:11]:
        groups, blocks = columns // LANES, rows // TALL
        unit = TALL * groups
        total = unit * blocks
        if edges:
            for cut in (first, stop):
                inside = jnp.maximum(cut - offset, 0)
                block = inside // unit

                @pl.when((inside < total) & (inside % unit > 0))
                def _(block=block, offset=offset, unit=unit, groups=groups):
                    body(offset + block * unit, groups)
        else:
            low = jnp.minimum((jnp.maximum(first - offset, 0) + unit - 1) // unit, blocks)
            high = jnp.minimum(jnp.maximum(stop - offset, 0) // unit, blocks)

            def one(block, carry, offset=offset, unit=unit, groups=groups):
                body(offset + block * unit, groups)
                return carry

            lax.fori_loop(low, jnp.maximum(high, low), one, 0)
        offset += total
    return offset


def cut_rows(cut):
    before = after = 0
    offset = 0
    for _, (rows, columns) in layout()[:11]:
        unit, total = TALL * (columns // LANES), rows * (columns // LANES)
        inside = jnp.maximum(cut - offset, 0)
        cuts = ((inside < total) & (inside % unit > 0)).astype(jnp.int32)
        before = before + cuts * (inside % unit)
        after = after + cuts * (unit - inside % unit)
        offset += total
    return before, after


class Halo:
    def __init__(self, at, here, start, wide, send_sem, recv_sem):
        self.at, self.here, self.start, self.wide = at, here, start, wide
        self.sems = send_sem, recv_sem
        first = at.me * SHARD_ROWS
        head, give_back = cut_rows(first)
        give_next, tail = cut_rows(first + SHARD_ROWS)
        self.given, self.taken = (give_back, give_next), (tail, head)

    def copies(self, side, index):
        low, high = HALO_STEP * index, HALO_STEP * (index + 1)
        src = self.start + (low if side == 0 else SHARD_ROWS - high)
        dst = HALO + SHARD_ROWS + low if side == 0 else HALO - high
        return pltpu.make_async_remote_copy(
            src_ref=self.here.at[pl.ds(src, HALO_STEP)],
            dst_ref=self.wide.at[pl.ds(dst, HALO_STEP)],
            send_sem=self.sems[0].at[side, index],
            recv_sem=self.sems[1].at[side, index],
            device_id=self.at.devices["back" if side == 0 else "next"],
            device_id_type=MESH,
        )

    def each(self, rows, action):
        for side in range(2):
            for index in range(HALO // HALO_STEP):
                pl.when(rows[side] > HALO_STEP * index)(partial(action, side, index))

    def start_all(self):
        self.each(self.given, lambda side, index: self.copies(side, index).start())

    def take(self):
        self.each(self.taken, lambda side, index: self.copies(side, index).wait_recv())

    def finish(self):
        self.each(self.given, lambda side, index: self.copies(side, index).wait_send())


VEC_ROWS = 64


def gather_kernel(
    master_ref, visible_ref, flat_ref, both_ref, wide, turned, own_sem, halo_send, halo_recv, *sems
):
    recv, core_recv, send_x, send_y, send_far, send_near, core_send = sems
    at = Place()
    first = at.me * SHARD_ROWS
    skew = (at.me * 2) % TALL
    own = pltpu.make_async_copy(master_ref, wide.at[pl.ds(HALO, SHARD_ROWS)], own_sem.at[0])
    own.start()
    at.greet()
    out = Outbox()
    halo = Halo(at, master_ref, 0, wide, halo_send, halo_recv)
    halo.start_all()
    half = visible_ref.shape[0]
    rows_here = both_ref.at[pl.ds(pl.multiple_of(at.core * half, half), half)]
    rows_there = both_ref.at[pl.ds(pl.multiple_of((1 - at.core) * half, half), half)]
    out.send(visible_ref, rows_here, own_sem.at[3], own_sem.at[4], at.devices["core"])
    keep = pltpu.make_async_copy(visible_ref, rows_here, own_sem.at[2])
    keep.start()
    own.wait()

    def turn(row, groups):
        start = row - first + HALO
        spot = row - (first - skew) + HALO
        for group in range(groups):
            turned[pl.ds(pl.multiple_of(spot + group * TALL, TALL), TALL), :] = wide[
                pl.ds(start + group, TALL, stride=groups), :
            ].astype(LOW)

    vec_start = entry_blocks(at.me, turn)
    halo.take()
    entry_blocks(at.me, turn, edges=True)

    @pl.when(at.me == 31)
    def _():
        start = vec_start - 31 * SHARD_ROWS + HALO
        spot = start + (31 * 2) % TALL
        turned[pl.ds(spot, VEC_ROWS), :] = wide[pl.ds(start, VEC_ROWS), :].astype(LOW)

    mine = pltpu.make_async_copy(
        turned.at[pl.ds(HALO + skew, SHARD_ROWS)],
        flat_ref.at[pl.ds(first, SHARD_ROWS)],
        own_sem.at[1],
    )
    mine.start()

    def source(part):
        start, size = TRUE_PARTS[part]
        return turned.at[pl.ds(HALO + skew + start, size)]

    sends = {"x": send_x, "y": send_y, "far": send_far, "near": send_near}
    gather_exchange(at, flat_ref, source, recv, core_recv, sends, core_send)
    mine.wait()
    keep.wait()
    arrived(rows_there, own_sem.at[4], at.devices["x"])
    out.finish()
    halo.finish()


def gather_weights(master_rows, visible_rows):
    hbm = pl.BlockSpec(memory_space=pltpu.HBM)
    steps = pltpu.SemaphoreType.DMA((2, HALO // HALO_STEP))
    half, width = visible_rows.shape
    return pl.pallas_call(
        gather_kernel,
        out_shape=[
            jax.ShapeDtypeStruct((32 * SHARD_ROWS, LANES), LOW),
            jax.ShapeDtypeStruct((2 * half, width), LOW),
        ],
        in_specs=[hbm, hbm],
        out_specs=[hbm, hbm],
        scratch_shapes=[
            pltpu.VMEM((WIDE_ROWS + 6, LANES), FULL),
            pltpu.VMEM((WIDE_ROWS + 30, LANES), LOW),
            pltpu.SemaphoreType.DMA((5,)),
            steps,
            steps,
        ]
        + [pltpu.SemaphoreType.DMA((16, 4))] * 7,
        compiler_params=pltpu.CompilerParams(
            collective_id=0, has_side_effects=True, vmem_limit_bytes=60 * 1024 * 1024
        ),
        name="gather_weights",
    )(master_rows, visible_rows)


def add_into(dst, start, terms, size, chunk):
    def one(step):
        row = step * chunk
        total = None
        for ref, first in terms:
            piece = ref[pl.ds(pl.multiple_of(first + row, TALL), chunk), :].astype(FULL)
            total = piece if total is None else total + piece
        dst[pl.ds(pl.multiple_of(start + row, TALL), chunk), :] = total.astype(dst.dtype)

    loop(size // chunk, one)


def reduce_kernel(
    grad_ref,
    loss_ref,
    shard_ref,
    total_ref,
    own,
    theirs,
    from_x,
    from_y,
    pass_x,
    pass_y,
    far_a,
    near_a,
    far_b,
    near_b,
    wide,
    plain,
    scalars,
    load_sem,
    core_send,
    core_recv,
    send_x,
    send_y,
    send_far,
    send_near,
    recv_x,
    recv_y,
    recv_far,
    recv_near,
    halo_send,
    halo_recv,
    tiny_send,
    tiny_recv,
):
    at = Place()
    tail = pl.ds(SHARD_ROWS - 2, TALL)
    for index in range(16):
        own[index, tail, :] = jnp.zeros((TALL, LANES), LOW)
        theirs[index, tail, :] = jnp.zeros((TALL, LANES), LOW)
    body = pl.ds(0, SHARD_ROWS)

    def shard_rows(core, chip):
        return grad_ref.at[pl.ds((core * 16 + chip) * SHARD_ROWS, SHARD_ROWS)]

    def load(chip):
        return pltpu.make_async_copy(
            shard_rows(at.core, chip), own.at[chip, body], load_sem.at[chip]
        )

    at.greet()
    pairs = Outbox()
    for mirrored in (3, 2, 1 - at.inner, at.inner):
        for column in ("d", "y", "x", "o"):
            chip = 4 * at.plane(mirrored) + at.columns[column]
            pairs.send(
                shard_rows(1 - at.core, chip),
                theirs.at[chip, body],
                core_send.at[chip],
                core_recv.at[chip],
                at.devices["core"],
            )
            load(chip).start()
    sends = {"x": send_x, "y": send_y, "far": send_far, "near": send_near}
    recvs = {"x": recv_x, "y": recv_y, "far": recv_far, "near": recv_near}
    relayed = {"x": pass_x, "y": pass_y}
    direct = {"x": from_x, "y": from_y}
    lines = {"far": (far_a, far_b), "near": (near_a, near_b)}

    def reduce_parts(inner):
        out = Outbox()
        paired, joined = set(), set()

        def pair(chip, column, part):
            if (column, "all") not in paired:
                paired.add((column, "all"))
                load(chip).wait()
                arrived(theirs.at[chip, body], core_recv.at[chip], at.devices["x"])
            name = "b" if part[0] == "b" else part
            if (column, name) not in paired:
                paired.add((column, name))
                first, size = PARTS[name]
                add_into(
                    own.at[chip],
                    first,
                    [(own.at[chip], first), (theirs.at[chip], first)],
                    size,
                    size // (4 if name == "b" else 3),
                )

        def landing(link, plane, chip, part, relay):
            first, size = PARTS[part]
            if link in lines and part == "b":
                return lines[link][1].at[chip], 0, size, (chip, SLOTS[part])
            if link in lines:
                return lines[link][0].at[plane], first, size, (chip, SLOTS[part])
            if relay:
                return relayed[link].at[plane], first, size, (plane, 3 + (part[0] == "b"))
            return direct[link].at[plane], first, size, (plane, SLOTS[part])

        def step(item):
            mirrored, column, part = item_of(item)
            plane = at.plane(mirrored)
            chip = 4 * plane + at.columns[column]
            pair(chip, (mirrored, column), part)
            first, size = PARTS[part]
            terms = []
            links = onward(inner, item)
            if mirrored == inner and column == "d" and part[0] == "b":
                links = [] if joined else links
                joined.add(part)
            own_item = mirrored == inner and column == "o"
            for link, piece in links:
                relay = column in ("x", "y")
                buffer, start, count, index = landing(link, plane, chip, piece, relay)
                arrived(buffer.at[pl.ds(start, count)], recvs[link].at[*index], at.devices["x"])
                terms.append((buffer, start, count))
            if own_item:
                whole = [(own.at[chip], first)] + [(buffer, start) for buffer, start, _ in terms]
                if part == "b":
                    add_into(plain, 0, whole, size, size // 4)
                    wide[pl.ds(HALO + A_ROWS, B_TRUE), :] = plain[pl.ds(0, B_TRUE), :]
                else:
                    add_into(wide, HALO + first, whole, size, size // 3)
                return
            full_size = B_ROWS if part[0] == "b" else size
            full_first = PARTS["b"][0] if part[0] == "b" else first
            whole = [(buffer, start) for buffer, start, count in terms if count == full_size]
            halves = [(buffer, start, count) for buffer, start, count in terms if count != full_size]
            if whole:
                add_into(
                    own.at[chip],
                    full_first,
                    [(own.at[chip], full_first), *whole],
                    full_size,
                    full_size // (4 if part[0] == "b" else 3),
                )
            for buffer, start, count in halves:
                add_into(
                    own.at[chip], start, [(own.at[chip], start), (buffer, start)], count, count // 2
                )
            if column == "o" or (part == "b" and mirrored != inner):
                link = "near" if inner == 1 and mirrored == 0 else "far"
                target = "near" if inner == 0 else "far"
                buffer, start, _, index = landing(target, plane, chip, part, False)
                arrive_sem = recvs[target]
            else:
                link = {"x": "x", "y": "y", "d": "y" if part in ("a1", "b1") else "x"}[column]
                buffer, start, _, index = landing(link, plane, chip, part, column == "d")
                arrive_sem = recvs[link]
            out.send(
                own.at[chip, pl.ds(first, size)],
                buffer.at[pl.ds(start, size)],
                sends[link].at[*index],
                arrive_sem.at[*index],
                at.devices[link],
            )

        for item in reversed(ARRIVALS[inner]):
            step(item)
        for part in ("a2", "a1", "b"):
            step(own_item(inner, part))
        out.finish()

    by_place(at, reduce_parts)
    pairs.finish()

    tiny = Outbox()
    halo = Halo(at, wide, HALO, wide, halo_send, halo_recv)
    halo.start_all()
    step_rows = 352
    whole_steps = SHARD_ROWS // step_rows

    def squares(index, carry):
        piece = wide[pl.ds(pl.multiple_of(HALO + index * step_rows, 8), step_rows), :]
        piece = piece * piece
        return carry + jnp.sum(piece.reshape(step_rows // 8, 8, LANES), axis=0)

    square = lax.fori_loop(0, whole_steps, squares, jnp.zeros((8, LANES), FULL))
    rest = wide[pl.ds(HALO + whole_steps * step_rows, SHARD_ROWS - whole_steps * step_rows), :]
    square = square + 0.125 * jnp.sum(rest * rest, axis=0, keepdims=True)
    scalars[at.me, 0] = square
    scalars[at.me, 1] = jnp.broadcast_to(loss_ref[...], (8, LANES))
    for index in range(1, 32):
        tiny.send(
            scalars.at[at.me],
            scalars.at[at.me],
            tiny_send.at[index],
            tiny_recv.at[at.me],
            at.ring(index),
        )
    def turn_back(row, groups):
        start = row - at.me * SHARD_ROWS + HALO
        for group in range(groups):
            plain[pl.ds(start + group, TALL, stride=groups), :] = wide[
                pl.ds(start + group * TALL, TALL), :
            ]

    vec_start = entry_blocks(at.me, turn_back)
    halo.take()
    entry_blocks(at.me, turn_back, edges=True)

    @pl.when(at.me == 31)
    def _():
        spot = pl.ds(vec_start - 31 * SHARD_ROWS + HALO, VEC_ROWS)
        plain[spot, :] = wide[spot, :]

    shard_ref[...] = plain[pl.ds(HALO, SHARD_ROWS), :]
    for index in range(1, 32):
        peer = (at.me + index) % 32
        arrived(scalars.at[peer], tiny_recv.at[peer], at.devices["x"])
    total_ref[...] = jnp.sum(scalars[...], axis=0)
    halo.finish()
    tiny.finish()


def reduce_gradients(grad_rows, loss_row):
    hbm = pl.BlockSpec(memory_space=pltpu.HBM)
    vmem = pl.BlockSpec(memory_space=pltpu.VMEM)
    dma = pltpu.SemaphoreType.DMA
    shard_total, totals = pl.pallas_call(
        reduce_kernel,
        out_shape=[
            jax.ShapeDtypeStruct((SHARD_ROWS, LANES), FULL),
            jax.ShapeDtypeStruct((2, 8, LANES), FULL),
        ],
        in_specs=[hbm, vmem],
        out_specs=[vmem, vmem],
        scratch_shapes=[pltpu.VMEM((16, PAD_ROWS, LANES), LOW)] * 2
        + [pltpu.VMEM((4, PAD_ROWS, LANES), LOW)] * 4
        + [pltpu.VMEM((4, A_ROWS, LANES), LOW)] * 2
        + [pltpu.VMEM((16, B_ROWS, LANES), LOW)] * 2
        + [pltpu.VMEM((WIDE_ROWS + 6, LANES), FULL)] * 2
        + [pltpu.VMEM((32, 2, 8, LANES), FULL)]
        + [dma((16,))] * 3
        + [dma((4, 5))] * 2
        + [dma((16, 4))] * 2
        + [dma((4, 5))] * 2
        + [dma((16, 4))] * 2
        + [dma((2, HALO // HALO_STEP))] * 2
        + [dma((32,))] * 2,
        compiler_params=pltpu.CompilerParams(
            collective_id=1, has_side_effects=True, vmem_limit_bytes=60 * 1024 * 1024
        ),
        name="reduce_gradients",
    )(grad_rows, loss_row)
    return shard_total.reshape(-1), jnp.sum(totals[0]), totals[1, 0, 0]


ROWS = 256
ENC_CHUNK = 64
FETCHED = ("vecs", "embed", "enc_qkv", "enc_out", "enc_up", "enc_down", "project")
BACKWARD_FETCHED = ("vecs", "project", "enc_down", "enc_up", "enc_out", "enc_qkv")


def encoder_forward_kernel(
    part_ref,
    visible_ref,
    segments_ref,
    patches_ref,
    table_ref,
    flat_ref,
    *refs,
):
    results, kept, (out_sem, sems, *buffers) = refs[:14], refs[14:28], refs[28:]
    (
        vis_rows,
        embedded,
        normed_a,
        qkv_rows,
        attn_out,
        after_attn,
        normed_b,
        slope,
        hidden_act,
        encoded,
        final_enc,
        projected,
        row_facts,
        column_facts,
    ) = kept

    def shipment(index):
        return pltpu.make_async_copy(kept[index], results[index], out_sem.at[index])

    def ship(*indices):
        for index in indices:
            shipment(index).start()

    ready = fetch(flat_ref, FETCHED, buffers, sems)
    part = part_ref[0]
    total = segments_ref.shape[1]
    images = IMG_SEQ // 2
    spare = ROWS - images * VIS
    segments = segments_ref[...]
    image = segments - part * images
    inside = (image >= 0) & (image < images)
    padding = segments == IMG_SEQ
    flags = jnp.concatenate(
        [
            inside.astype(FULL),
            padding.astype(FULL),
            jnp.zeros((6, total), FULL),
        ],
        axis=0,
    ).astype(LOW)
    row = lax.broadcasted_iota(jnp.int32, (total, total), 0)
    column = lax.broadcasted_iota(jnp.int32, (total, total), 1)
    counts = dot_nn(flags, (row <= column).astype(FULL).astype(LOW)).astype(jnp.int32)
    inside_count, padding_count = counts[0:1], counts[1:2]
    padding_slot = padding_count - part * spare
    chosen = inside | (padding & (padding_slot >= 1) & (padding_slot <= spare))
    slot = inside_count + jnp.clip(padding_slot, 0, spare) - 1
    slot = jnp.where(chosen, slot, -1)
    select = (lax.broadcasted_iota(jnp.int32, (ROWS, total), 0) == slot).astype(FULL).astype(LOW)
    facts = jnp.concatenate(
        [segments.astype(FULL), patches_ref[...].astype(FULL), jnp.zeros((LANES - 2, total), FULL)],
        axis=0,
    ).astype(LOW)
    row_facts[...] = dot_nt(facts[0:16], select)
    column_facts[...] = dot_nt(select, facts)
    vis_rows[...] = dot_nn(select, visible_ref[...]).astype(LOW)
    ship(0, 12, 13)
    patch = column_facts[:, 1:2].astype(jnp.int32)
    spot = (lax.broadcasted_iota(jnp.int32, (ROWS, table_ref.shape[1]), 1) == patch).astype(FULL).astype(LOW)
    embedded[...] = dot_nn(spot, table_ref[0]) + dot_nn(spot, table_ref[1]) + dot_nn(spot, table_ref[2])
    w_embed = ready(1)
    product_into(embedded, vis_rows, w_embed, D, residual=embedded)
    ship(1)
    ready(0)
    vec = vec_reader(buffers[0], 0, D // LANES)
    norm_into(normed_a, embedded, vec(0), vec(1), ROWS, ENC_CHUNK)
    ship(2)
    w_qkv = ready(2)
    product_into(qkv_rows, normed_a, w_qkv, 3 * D)
    ship(3)
    allowed = column_facts[:, 0:1] == row_facts[0:1, :]
    allowed = jnp.concatenate([allowed.astype(FULL)] * 2, axis=0) > 0.5

    def attend(step):
        for part in range(2):
            attend_into(
                attn_out, qkv_rows, pl.ds(0, ROWS), 2 * step + part, D, allowed, D // HEADS
            )

    loop(D // LANES // 2, attend)
    ship(4)
    w_out = ready(3)
    product_into(after_attn, attn_out, w_out, D, residual=embedded)
    ship(5)
    norm_into(normed_b, after_attn, vec(2), vec(3), ROWS, ENC_CHUNK)
    ship(6)
    w_up = ready(4)
    up_into(hidden_act, slope, normed_b, w_up, FF, 512)
    ship(7, 8)
    w_down = ready(5)
    product_into(encoded, hidden_act, w_down, D, residual=after_attn)
    ship(9)
    norm_into(final_enc, encoded, vec(4), vec(5), ROWS, ENC_CHUNK)
    ship(10)
    w_proj = ready(6)
    product_into(projected, final_enc, w_proj, DD)
    ship(11)
    for index in range(len(kept)):
        shipment(index).wait()


def encoder_forward(part, visible_rows, segments, patch_ids, flat_weights):
    hbm = pl.BlockSpec(memory_space=pltpu.HBM)
    vmem = pl.BlockSpec(memory_space=pltpu.VMEM)
    smem = pl.BlockSpec(memory_space=pltpu.SMEM)
    table = jnp.asarray(split_low(position_table(D, 256)))
    kept = [
        ((ROWS, PIX), LOW),
        ((ROWS, D), FULL),
        ((ROWS, D), LOW),
        ((ROWS, 3 * D), LOW),
        ((ROWS, D), LOW),
        ((ROWS, D), FULL),
        ((ROWS, D), LOW),
        ((ROWS, FF), FULL),
        ((ROWS, FF), LOW),
        ((ROWS, D), FULL),
        ((ROWS, D), LOW),
        ((ROWS, DD), LOW),
        ((16, ROWS), FULL),
        ((ROWS, LANES), FULL),
    ]
    return pl.pallas_call(
        encoder_forward_kernel,
        out_shape=[jax.ShapeDtypeStruct(s, d) for s, d in kept],
        in_specs=[smem] + [vmem] * 4 + [hbm],
        out_specs=[hbm] * 14,
        scratch_shapes=[pltpu.VMEM(s, d) for s, d in kept]
        + [pltpu.SemaphoreType.DMA((14,)), pltpu.SemaphoreType.DMA((7,))] + tile_buffers(FETCHED),
        compiler_params=pltpu.CompilerParams(vmem_limit_bytes=60 * 1024 * 1024),
        name="encoder_forward",
    )(part, visible_rows, segments, patch_ids, table, flat_weights)


def encoder_backward_kernel(
    grad_projected,
    decoder_vecs,
    *refs,
):
    stored, refs = refs[:13], refs[13:]
    weights_ref, partial_ref, flat_ref, refs = *refs[:3], refs[3:]
    kept, refs = refs[:13], refs[13:]
    (
        grad_rows,
        upper,
        branch,
        grad_pre,
        middle,
        grad_attn,
        grad_qkv,
        vec_grads,
        turned,
        stage,
        vec_full,
        vec_stage,
        stage_sem,
        kept_sem,
        sems,
        *buffers,
    ) = refs
    (
        vis_rows,
        embedded,
        normed_a,
        qkv_rows,
        attn_out,
        after_attn,
        normed_b,
        slope,
        hidden_act,
        encoded,
        final_enc,
        row_facts,
        column_facts,
    ) = kept

    def delivery(index):
        return pltpu.make_async_copy(stored[index], kept[index], kept_sem.at[index])

    def need(*indices):
        for index in indices:
            delivery(index).wait()

    for index in (10, 9, 8):
        delivery(index).start()
    del partial_ref
    ready = fetch(weights_ref, BACKWARD_FETCHED, buffers, sems)
    for index in (7, 6, 5, 4, 12, 11, 3, 2, 1, 0):
        delivery(index).start()
    tiles = entry_tiles()
    ready(0)
    vec = vec_reader(buffers[0], 0, D // LANES)
    grad_of = lambda index: vec_grads.at[pl.ds(index, 1), :]

    emit = Emitter(flat_ref, turned, stage, stage_sem)

    need(10)
    emit("project", final_enc, grad_projected)
    w_proj = ready(1)
    product_t_into(upper, grad_projected, w_proj, D)
    need(9)
    norm_back(grad_rows, encoded, upper, None, vec(4), grad_of(4), grad_of(5), ROWS, ENC_CHUNK)
    branch[...] = grad_rows[...].astype(LOW)
    need(8)
    emit("enc_down", hidden_act, branch)
    need(7)
    w_down = ready(2)
    down_back_into(grad_pre, branch, w_down, slope, FF, 512)
    need(6)
    emit("enc_up", normed_b, grad_pre)
    w_up = ready(3)
    product_t_into(upper, grad_pre, w_up, D)
    need(5)
    norm_back(grad_rows, after_attn, upper, grad_rows, vec(2), grad_of(2), grad_of(3), ROWS, ENC_CHUNK)
    middle[...] = grad_rows[...].astype(LOW)
    need(4)
    emit("enc_out", attn_out, middle)
    w_out = ready(4)
    product_t_into(grad_attn, middle, w_out, D)
    need(12, 11, 3)
    allowed = column_facts[:, 0:1] == row_facts[0:1, :]
    allowed = jnp.concatenate([allowed.astype(FULL)] * 2, axis=0) > 0.5

    def attend_back(step):
        for part in range(2):
            attend_back_into(
                grad_qkv,
                grad_attn,
                qkv_rows,
                pl.ds(0, ROWS),
                2 * step + part,
                D,
                allowed,
                D // HEADS,
            )

    loop(D // LANES // 2, attend_back)
    need(2)
    emit("enc_qkv", normed_a, grad_qkv)
    w_qkv = ready(5)
    product_t_into(upper, grad_qkv, w_qkv, D)
    need(1)
    norm_back(grad_rows, embedded, upper, grad_rows, vec(0), grad_of(0), grad_of(1), ROWS, ENC_CHUNK)
    branch[...] = grad_rows[...].astype(LOW)
    need(0)
    emit("embed", vis_rows, branch)
    emit.finish()
    groups = D // LANES
    for index in range(6):
        for group in range(groups):
            vec_full[pl.ds(index * groups + group, 1), :] = vec_grads[
                pl.ds(index, 1), pl.ds(group * LANES, LANES)
            ]
    base, groups = 6 * groups, DD // LANES
    for index in range(7):
        for group in range(groups):
            vec_full[pl.ds(base + index * groups + group, 1), :] = decoder_vecs[
                pl.ds(index, 1), pl.ds(group * LANES, LANES)
            ]
    vec_stage[...] = vec_full[...].astype(LOW).reshape(4, TALL, LANES)
    copy = pltpu.make_async_copy(vec_stage, flat_ref.at[pl.ds(tiles["enc_vecs"][0], 4)], stage_sem.at[0])
    copy.start()
    copy.wait()


def encoder_backward(saved, grad_projected, flat_weights, decoder_vec_grads, flat):
    hbm = pl.BlockSpec(memory_space=pltpu.HBM)
    vmem = pl.BlockSpec(memory_space=pltpu.VMEM)
    inputs = [grad_projected, decoder_vec_grads, *saved, flat_weights, flat]
    low, full = (lambda *s: pltpu.VMEM(s, LOW)), (lambda *s: pltpu.VMEM(s, FULL))
    return pl.pallas_call(
        encoder_backward_kernel,
        out_shape=jax.ShapeDtypeStruct(flat.shape, LOW),
        in_specs=[vmem] * 2 + [hbm] * 15,
        out_specs=hbm,
        input_output_aliases={len(inputs) - 1: 0},
        scratch_shapes=[pltpu.VMEM(array.shape, array.dtype) for array in saved]
        + [
            full(ROWS, D),
            full(ROWS, D),
            low(ROWS, D),
            low(ROWS, FF),
            low(ROWS, D),
            low(ROWS, D),
            low(ROWS, 3 * D),
            full(8, D),
            low(FF, ROWS),
            low(2, FF * D // (TALL * LANES), TALL, LANES),
            full(64, LANES),
            low(4, TALL, LANES),
            pltpu.SemaphoreType.DMA((2,)),
            pltpu.SemaphoreType.DMA((13,)),
            pltpu.SemaphoreType.DMA((6,)),
        ]
        + tile_buffers(BACKWARD_FETCHED),
        compiler_params=pltpu.CompilerParams(vmem_limit_bytes=60 * 1024 * 1024),
        name="encoder_backward",
    )(*inputs)


IMAGES = 5
DECODER_FETCHED = ("vecs", "dec_qkv", "dec_out", "dec_up", "dec_down", "pixel")
IMG_ROWS = 208
DEC_ROWS = IMAGES * IMG_ROWS


def decoder_kernel(
    part_ref,
    projected,
    row_facts,
    targets_ref,
    table_ref,
    weights_ref,
    flat_ref,
    grad_projected,
    vec_grads,
    loss_ref,
    dec_in,
    low_rows,
    qkv_rows,
    attn_out,
    after_attn,
    normed_b,
    slope,
    hidden_act,
    decoded,
    final_dec,
    grad_pred,
    upper,
    masked,
    turned,
    stage,
    stage_sem,
    sems,
    *buffers,
    mask_total,
):
    ready = fetch(weights_ref, DECODER_FETCHED, buffers, sems)
    tiles = entry_tiles()
    ready(0)
    vec = vec_reader(buffers[0], 6 * D // LANES, DD // LANES)
    grad_of = lambda index: vec_grads.at[pl.ds(index, 1), :]
    part = part_ref[0]
    image_of = row_facts[0:1, :].astype(jnp.int32) - part * IMAGES
    patch_of = row_facts[1:2, :].astype(jnp.int32)
    patch = lax.broadcasted_iota(jnp.int32, (IMG_ROWS, ROWS), 0)

    def selector(index):
        return ((patch_of == patch) & (image_of == index)).astype(FULL)

    def place(index):
        at = span(index, IMG_ROWS)
        select = selector(index)
        real = (patch[:, 0:1] < PATCHES).astype(FULL)
        hidden = real * (1.0 - jnp.sum(select, axis=-1, keepdims=True))
        masked[at, :] = jnp.broadcast_to(hidden, (IMG_ROWS, LANES))
        dec_in[at, :] = dot_nn(select.astype(LOW), projected[...]) + hidden * vec(6) + table_ref[...]

    loop(IMAGES, place)
    norm_into(low_rows, dec_in, vec(0), vec(1), DEC_ROWS, IMG_ROWS)
    w_qkv = ready(1)
    product_into(qkv_rows, low_rows, w_qkv, 3 * DD)
    head_size = DD // DHEADS
    heads = LANES // head_size
    allowed = lax.broadcasted_iota(jnp.int32, (heads * IMG_ROWS, IMG_ROWS), 1) < PATCHES
    groups = DD // LANES

    def attend(step):
        rows = span(step, IMG_ROWS)
        for at in range(groups):
            attend_into(attn_out, qkv_rows, rows, at, DD, allowed, head_size)

    loop(IMAGES, attend)
    w_out = ready(2)
    product_into(after_attn, attn_out, w_out, DD, residual=dec_in)
    norm_into(normed_b, after_attn, vec(2), vec(3), DEC_ROWS, IMG_ROWS)
    w_up = ready(3)
    up_into(hidden_act, slope, normed_b, w_up, DFF, TILE)
    w_down = ready(4)
    product_into(decoded, hidden_act, w_down, DD, residual=after_attn)
    norm_into(final_dec, decoded, vec(4), vec(5), DEC_ROWS, IMG_ROWS)
    w_pix = ready(5)
    loss_ref[...] = jnp.zeros_like(loss_ref)

    def compare(index):
        at = span(index, IMG_ROWS)
        image = pl.ds(0, PATCHES)
        goal, _ = norm_parts(targets_ref[index].astype(FULL))
        goal = jnp.concatenate([goal, jnp.zeros((IMG_ROWS - PATCHES, PIX), FULL)], axis=0)
        error = dot_nn(final_dec[at, :], w_pix.column_tile(0, PIX)) - goal
        weight = masked[at, 0:1]
        rows = jnp.mean(error * error, axis=-1, keepdims=True) * weight
        loss_ref[...] = loss_ref[...] + jnp.sum(rows) * (1.0 / mask_total)
        grad_pred[at, :] = (weight * error * (2.0 / (PIX * mask_total))).astype(LOW)

    loop(IMAGES, compare)

    emit = Emitter(flat_ref, turned, stage, stage_sem)

    emit("pixel", final_dec, grad_pred)
    product_t_into(upper, grad_pred, w_pix, DD)
    grad_rows, branch = decoded, final_dec
    norm_back(grad_rows, decoded, upper, None, vec(4), grad_of(4), grad_of(5), DEC_ROWS, IMG_ROWS)
    branch[...] = grad_rows[...].astype(LOW)
    emit("dec_down", hidden_act, branch)
    grad_pre = hidden_act
    down_back_into(grad_pre, branch, w_down, slope, DFF, TILE)
    emit("dec_up", normed_b, grad_pre)
    product_t_into(upper, grad_pre, w_up, DD)
    norm_back(grad_rows, after_attn, upper, grad_rows, vec(2), grad_of(2), grad_of(3), DEC_ROWS, IMG_ROWS)
    branch[...] = grad_rows[...].astype(LOW)
    emit("dec_out", attn_out, branch)
    grad_attn, grad_qkv = normed_b, grad_pre.at[:, pl.ds(0, 3 * DD)]
    product_t_into(grad_attn, branch, w_out, DD)

    key_row = lax.broadcasted_iota(jnp.int32, (heads, IMG_ROWS, IMG_ROWS), 1)
    real_keys = (key_row < PATCHES).astype(FULL).reshape(heads * IMG_ROWS, IMG_ROWS) > 0.5

    def attend_back(step):
        rows = span(step, IMG_ROWS)
        for at in range(groups):
            attend_back_into(grad_qkv, grad_attn, qkv_rows, rows, at, DD, real_keys, head_size)

    loop(IMAGES, attend_back)
    emit("dec_qkv", low_rows, grad_qkv)
    emit.finish()
    product_t_into(upper, grad_qkv, w_qkv, DD)
    norm_back(grad_rows, dec_in, upper, grad_rows, vec(0), grad_of(0), grad_of(1), DEC_ROWS, IMG_ROWS)
    upper[pl.ds(0, ROWS), :] = jnp.zeros((ROWS, DD), FULL)

    def collect(index, token):
        at = span(index, IMG_ROWS)
        rows = grad_rows[at, :]
        token = token + jnp.sum((rows * masked[at, 0:1]).reshape(IMG_ROWS // 8, 8, DD), axis=0)
        upper[pl.ds(0, ROWS), :] = upper[pl.ds(0, ROWS), :] + dot_tn(
            selector(index).astype(LOW), rows.astype(LOW)
        )
        return token

    token = lax.fori_loop(0, IMAGES, collect, jnp.zeros((8, DD), FULL))
    grad_of(6)[...] = jnp.sum(token, axis=0, keepdims=True)
    grad_projected[...] = upper[pl.ds(0, ROWS), :].astype(LOW)


def decoder_step(part, projected, row_facts, targets, flat_weights, mask_total):
    hbm = pl.BlockSpec(memory_space=pltpu.HBM)
    vmem = pl.BlockSpec(memory_space=pltpu.VMEM)
    smem = pl.BlockSpec(memory_space=pltpu.SMEM)
    table = jnp.asarray(position_table(DD, IMG_ROWS))
    low, full = (lambda *s: pltpu.VMEM(s, LOW)), (lambda *s: pltpu.VMEM(s, FULL))
    return pl.pallas_call(
        partial(decoder_kernel, mask_total=mask_total),
        out_shape=[
            jax.ShapeDtypeStruct(flat_weights.shape, LOW),
            jax.ShapeDtypeStruct((ROWS, DD), LOW),
            jax.ShapeDtypeStruct((8, DD), FULL),
            jax.ShapeDtypeStruct((1, LANES), FULL),
        ],
        in_specs=[smem] + [vmem] * 4 + [hbm],
        out_specs=[hbm] + [vmem] * 3,
        scratch_shapes=[
            full(DEC_ROWS, DD),
            low(DEC_ROWS, DD),
            low(DEC_ROWS, 3 * DD),
            low(DEC_ROWS, DD),
            full(DEC_ROWS, DD),
            low(DEC_ROWS, DD),
            full(DEC_ROWS, DFF),
            low(DEC_ROWS, DFF),
            full(DEC_ROWS, DD),
            low(DEC_ROWS, DD),
            low(DEC_ROWS, PIX),
            full(DEC_ROWS, DD),
            full(DEC_ROWS, LANES),
            low(DFF, DEC_ROWS),
            low(2, DFF * DD // (TALL * LANES), TALL, LANES),
            pltpu.SemaphoreType.DMA((2,)),
            pltpu.SemaphoreType.DMA((6,)),
        ]
        + tile_buffers(DECODER_FETCHED),
        compiler_params=pltpu.CompilerParams(vmem_limit_bytes=62 * 1024 * 1024),
        name="decoder_step",
    )(part, projected, row_facts, targets, table, flat_weights)


def to_tiles(full_flat):
    pieces, offset = [], 0
    for _, (rows, columns) in layout()[:11]:
        piece = full_flat[offset : offset + rows * columns]
        piece = piece.reshape(rows // TALL, TALL, columns // LANES, LANES)
        pieces.append(piece.transpose(0, 2, 1, 3).reshape(-1, LANES))
        offset += rows * columns
    return jnp.concatenate([*pieces, full_flat[offset:].reshape(-1, LANES)])


def from_tiles(rows_flat):
    pieces, offset = [], 0
    for _, (rows, columns) in layout()[:11]:
        count = rows * columns // LANES
        piece = rows_flat[offset : offset + count]
        piece = piece.reshape(rows // TALL, columns // LANES, TALL, LANES)
        pieces.append(piece.transpose(0, 2, 1, 3).reshape(-1))
        offset += count
    return jnp.concatenate([*pieces, rows_flat[offset:].reshape(-1)])


def shards(visible, segments, patch_ids, targets, master, moment_one, moment_two, step_count):
    part = lax.axis_index("seq")
    in_kernels = master.shape[0] == SHARD_ROWS * LANES and lax.axis_size("dp") == 16
    if in_kernels:
        flat_weights, visible_rows = gather_weights(
            master.reshape(SHARD_ROWS, LANES), visible[0]
        )
    else:
        full_flat = lax.all_gather(master.astype(LOW), ("seq", "dp"), axis=0, tiled=True)
        flat_weights = to_tiles(full_flat)
        visible_rows = lax.all_gather(visible[0], "seq", axis=0, tiled=True)
    flat_weights = flat_weights.reshape(-1, TALL, LANES)
    part_row = part.reshape(1).astype(jnp.int32)
    mask_total = (PATCHES - VIS) * IMG_SEQ * visible.shape[0] * lax.axis_size("dp")
    *saved, projected, row_facts, column_facts = encoder_forward(
        part_row, visible_rows, segments, patch_ids, flat_weights
    )
    flat_grads, grad_projected, decoder_vec_grads, loss_row = decoder_step(
        part_row, projected, row_facts, targets[0], flat_weights, mask_total
    )
    flat_grads = encoder_backward(
        [*saved, row_facts, column_facts],
        grad_projected,
        flat_weights,
        decoder_vec_grads,
        flat_grads,
    )
    flat_grads = flat_grads.reshape(-1, LANES)
    if in_kernels:
        grad_shard, square_sum, loss_sum = reduce_gradients(flat_grads, loss_row)
    else:
        grad_flat = from_tiles(flat_grads.astype(FULL))
        grad_shard = lax.psum_scatter(grad_flat, ("seq", "dp"), scatter_dimension=0, tiled=True)
        square_sum, loss_sum = lax.psum(
            (jnp.sum(grad_shard * grad_shard), loss_row[0, 0]), ("seq", "dp")
        )
    grad_norm = jnp.sqrt(square_sum)
    clipped = grad_shard * jnp.minimum(1.0, clip_limit / (grad_norm + 1e-06))
    new_one = beta_mom * moment_one + (1.0 - beta_mom) * clipped
    new_two = beta_mom * moment_two + (1.0 - beta_mom) * clipped * clipped
    correction = 1.0 - jnp.power(jnp.float32(beta_mom), step_count[0].astype(jnp.float32))
    new_master = master - learn_rate * (
        new_one / correction / (jnp.sqrt(new_two / correction) + adam_eps) + decay_rate * master
    )
    return (new_one, new_two, new_master, new_master.astype(jnp.bfloat16), grad_norm, loss_sum)


def solution(mesh):
    in_specs = (
        P("dp", "seq", None),
        P("dp", None),
        P("dp", None),
        P("dp", "seq", None, None),
        P(("seq", "dp")),
        P(("seq", "dp")),
        P(("seq", "dp")),
        P(),
    )
    out_specs = (P(("seq", "dp")), P(("seq", "dp")), P(("seq", "dp")), P(("seq", "dp")), P(), P())
    return jax.shard_map(shards, mesh=mesh, in_specs=in_specs, out_specs=out_specs, check_vma=False)
```

```python
from functools import partial
import math

import jax
import jax.numpy as jnp
import ml_dtypes
import numpy as np
from jax import lax
from jax.experimental import pallas as pl
from jax.experimental.pallas import tpu as pltpu
from jax.sharding import PartitionSpec as P

D = 768
HEADS = 12
FF = 3072
DD = 512
DHEADS = 16
DFF = 2048
PIX = 768
PATCHES = 196
VIS = 49
IMG_SEQ = 10


norm_eps = 1e-06
neg_big = -1000000000.0
clip_limit = 0.0001
learn_rate = 0.03
decay_rate = 0.05
adam_eps = 1e-08
beta_mom = 0.5


def layout():
    return [
        ("embed", (PIX, D)),
        ("enc_qkv", (D, 3 * D)),
        ("enc_out", (D, D)),
        ("enc_up", (D, FF)),
        ("enc_down", (FF, D)),
        ("project", (D, DD)),
        ("dec_qkv", (DD, 3 * DD)),
        ("dec_out", (DD, DD)),
        ("dec_up", (DD, DFF)),
        ("dec_down", (DFF, DD)),
        ("pixel", (DD, PIX)),
        ("enc_vecs", (6, D)),
        ("dec_vecs", (7, DD)),
    ]


def unflatten(flat_vec):
    params = {}
    offset = 0
    for entry_name, entry_shape in layout():
        entry_size = entry_shape[0] * entry_shape[1]
        params[entry_name] = flat_vec[offset : offset + entry_size].reshape(entry_shape)
        offset += entry_size
    return params


LOW = jnp.bfloat16
FULL = jnp.float32
TILE = 256
TALL = 16
LANES = 128
NEG = neg_big
ROOT_HALF = math.sqrt(0.5)
LOG2_E = 1.0 / math.log(2.0)
BELL = 1.0 / math.sqrt(2.0 * math.pi)


def dot_nn(left, right):
    return lax.dot_general(left, right, (((1,), (0,)), ((), ())), preferred_element_type=FULL)


def dot_nt(left, right):
    return lax.dot_general(left, right, (((1,), (1,)), ((), ())), preferred_element_type=FULL)


def dot_tn(left, right):
    return lax.dot_general(left, right, (((0,), (0,)), ((), ())), preferred_element_type=FULL)


def loop(count, body):
    def one(step, carry):
        body(step)
        return carry

    lax.fori_loop(0, count, one, 0)


def unrolled(count, body):
    size = next(size for size in (4, 3, 2, 1) if count % size == 0)

    def one(step):
        for part in range(size):
            body(step * size + part)

    loop(count // size, one)


def span(step, size):
    return pl.ds(pl.multiple_of(step * size, size), size)


def norm_parts(rows):
    average = jnp.mean(rows, axis=-1, keepdims=True)
    centered = rows - average
    scale = lax.rsqrt(jnp.mean(centered * centered, axis=-1, keepdims=True) + norm_eps)
    return centered * scale, scale


def norm_into(dst, src, gain, shift, rows, chunk):
    def one(step):
        at = span(step, chunk)
        unit, _ = norm_parts(src[at, :])
        dst[at, :] = (unit * gain + shift).astype(LOW)

    loop(rows // chunk, one)


def norm_back(dst, src, grad, residual, gain, gain_grad, shift_grad, rows, chunk):
    width = src.shape[1]

    def one(step, carry):
        at = span(step, chunk)
        unit, scale = norm_parts(src[at, :])
        upper = grad[at, :]
        gains = carry[0] + jnp.sum((upper * unit).reshape(chunk // 8, 8, width), axis=0)
        shifts = carry[1] + jnp.sum(upper.reshape(chunk // 8, 8, width), axis=0)
        upper = upper * gain
        lower = scale * (
            upper
            - jnp.mean(upper, axis=-1, keepdims=True)
            - unit * jnp.mean(upper * unit, axis=-1, keepdims=True)
        )
        if residual is not None:
            lower = lower + residual[at, :]
        dst[at, :] = lower
        return gains, shifts

    zero = jnp.zeros((8, width), FULL)
    gains, shifts = lax.fori_loop(0, rows // chunk, one, (zero, zero))
    gain_grad[...] = jnp.sum(gains, axis=0, keepdims=True)
    shift_grad[...] = jnp.sum(shifts, axis=0, keepdims=True)


class Blocked:
    def __init__(self, ref, rows, columns):
        self.rows, self.groups = rows, columns // LANES
        self.ref = ref.reshape(rows // TALL, self.groups, TALL, LANES)

    def piece(self, first_row, rows, first_group, groups):
        tall = pl.ds(first_row // TALL, rows // TALL)
        parts = [
            self.ref[tall, first_group + index].reshape(rows, LANES) for index in range(groups)
        ]
        return parts[0] if groups == 1 else jnp.concatenate(parts, axis=1)

    def column_tile(self, step, tile):
        count = tile // LANES
        return self.piece(0, self.rows, step * count, count)

    def row_tile(self, step, tile):
        return self.piece(step * tile, tile, 0, self.groups)


def product_into(dst, left, right, columns, tile=TILE, residual=None):
    def one(step):
        at = span(step, tile)
        value = dot_nn(left[...], right.column_tile(step, tile))
        if residual is not None:
            value = value + residual[:, at]
        dst[:, at] = value.astype(dst.dtype)

    unrolled(columns // tile, one)


def product_t_into(dst, left, right, columns, tile=TILE):
    def one(step):
        dst[:, span(step, tile)] = dot_nt(left[...], right.row_tile(step, tile)).astype(dst.dtype)

    unrolled(columns // tile, one)


def up_into(act, slope, left, w_up, columns, tile):
    def one(step):
        at = span(step, tile)
        hidden = dot_nn(left[...], w_up.column_tile(step, tile))
        share = 0.5 * (1.0 + lax.erf(hidden * ROOT_HALF))
        act[:, at] = (hidden * share).astype(LOW)
        slope[:, at] = share + hidden * (BELL * jnp.exp(-0.5 * hidden * hidden))

    unrolled(columns // tile, one)


def down_back_into(grad_pre, branch, w_down, slope, columns, tile):
    def one(step):
        at = span(step, tile)
        grad_pre[:, at] = (dot_nt(branch[...], w_down.row_tile(step, tile)) * slope[:, at]).astype(LOW)

    unrolled(columns // tile, one)


def weight_grad(out, out_tile, left, right, turned, stage, stage_sem, slot=0, before=None):
    rows, columns = left.shape[1], right.shape[1]
    groups = columns // LANES
    high = rows // TALL
    count = high * groups

    def turn(step):
        turned[span(step, TILE), :] = left[:, span(step, TILE)].T

    loop(rows // TILE, turn)
    if before is not None:
        before()
    tiles = stage.at[slot, pl.ds(0, count)].reshape(high, groups, TALL, LANES)
    piece = columns // TILE
    unroll = next(u for u in (6, 4, 3, 2, 1) if piece % u == 0)

    def across(step):
        for part in range(unroll):
            tile = step * unroll + part
            value = dot_nn(turned[pl.ds(0, rows), :], right[:, span(tile, TILE)]).astype(LOW)
            for half in range(2):
                tiles[:, tile * 2 + half] = value[:, half * LANES : (half + 1) * LANES].reshape(
                    high, TALL, LANES
                )

    loop(piece // unroll, across)
    copy = lambda: pltpu.make_async_copy(
        stage.at[slot, pl.ds(0, count)], out.at[pl.ds(out_tile, count)], stage_sem.at[slot]
    )
    copy().start()
    return lambda: copy().wait()


class Emitter:
    def __init__(self, out, turned, stage, stage_sem):
        self.args = turned, stage, stage_sem
        self.out, self.tiles, self.waits = out, entry_tiles(), []

    def __call__(self, entry, left, right):
        index = len(self.waits)
        before = self.waits[index - 2] if index >= 2 else None
        self.waits.append(
            weight_grad(self.out, self.tiles[entry][0], left, right, *self.args, index % 2, before)
        )

    def finish(self):
        for wait in self.waits[-2:]:
            wait()


def head_masks(head_size, dtype):
    lane = lax.broadcasted_iota(jnp.int32, (1, LANES), 1) // head_size
    return [(lane == head).astype(dtype) for head in range(LANES // head_size)]


def stacked(rows, masks):
    return jnp.concatenate([rows * mask for mask in masks], axis=0)


def unstacked(rows, masks, size):
    total = None
    for index, mask in enumerate(masks):
        piece = rows[index * size : (index + 1) * size] * mask
        total = piece if total is None else total + piece
    return total


def soft_rows(queries, keys, allowed, scale):
    scores = jnp.where(allowed, dot_nt(queries, keys), NEG)
    scores = scores - jnp.max(scores, axis=-1, keepdims=True)
    powers = jnp.exp2(scores * (scale * LOG2_E))
    return powers * (1.0 / jnp.sum(powers, axis=-1, keepdims=True))


def attend_into(dst, qkv, rows, at, width, allowed, head_size):
    masks = head_masks(head_size, LOW)
    size = rows.size
    column = lambda part: pl.ds(pl.multiple_of(part * width + at * LANES, LANES), LANES)
    queries = stacked(qkv[rows, column(0)], masks)
    probs = soft_rows(queries, qkv[rows, column(1)], allowed, head_size**-0.5).astype(LOW)
    values = dot_nn(probs, qkv[rows, column(2)])
    dst[rows, column(0)] = unstacked(values, head_masks(head_size, FULL), size).astype(LOW)


def only_real(scores, real, allowed):
    if real is None:
        return jnp.where(allowed, scores, NEG)
    whole = real // 8 * 8
    key = whole + lax.broadcasted_iota(jnp.int32, (1, scores.shape[1] - whole, 1), 1)
    return jnp.concatenate(
        [scores[:, :whole], jnp.where(key < real, scores[:, whole:], NEG)], axis=1
    )


def column_scores(keys, queries, heads, real, allowed):
    scores = dot_nt(keys, queries)
    return only_real(scores.reshape(heads, scores.shape[0] // heads, scores.shape[1]), real, allowed)


def attend_columns_into(dst, qkv, rows, at, width, real, head_size, logs):
    masks = head_masks(head_size, LOW)
    heads, size, scale = len(masks), rows.size, head_size**-0.5 * LOG2_E
    column = lambda part: pl.ds(pl.multiple_of(part * width + at * LANES, LANES), LANES)
    keys = stacked(qkv[rows, column(1)], masks)
    scores = column_scores(keys, qkv[rows, column(0)], heads, real, None)
    top = jnp.max(scores, axis=1, keepdims=True)
    powers = jnp.exp2((scores - top) * scale)
    total = jnp.sum(powers, axis=1, keepdims=True)
    logs[...] = top * scale + jnp.log2(total)
    probs = (powers * (1.0 / total)).reshape(heads * size, size).astype(LOW)
    dst[rows, column(0)] = dot_tn(stacked(qkv[rows, column(2)], masks), probs).T.astype(LOW)


def attend_back_into(dst, grad, qkv, rows, at, width, head_size, real=None, allowed=None, logs=None):
    masks = head_masks(head_size, LOW)
    lanes = head_masks(head_size, FULL)
    heads, size, scale = len(masks), rows.size, head_size**-0.5
    column = lambda part: pl.ds(pl.multiple_of(part * width + at * LANES, LANES), LANES)
    queries = qkv[rows, column(0)]
    keys = stacked(qkv[rows, column(1)], masks)
    grads = grad[rows, column(0)]
    scores = column_scores(keys, queries, heads, real, allowed)
    if logs is None:
        scores = scores - jnp.max(scores, axis=1, keepdims=True)
        powers = jnp.exp2(scores * (scale * LOG2_E))
        probs = powers * (1.0 / jnp.sum(powers, axis=1, keepdims=True))
    else:
        probs = jnp.exp2(scores * (scale * LOG2_E) - logs[...])
    slopes = dot_nt(stacked(qkv[rows, column(2)], masks), grads).reshape(probs.shape)
    slopes = probs * (slopes - jnp.sum(slopes * probs, axis=1, keepdims=True))
    flat = (heads * size, size)
    slopes, probs = slopes.reshape(flat).astype(LOW), probs.reshape(flat).astype(LOW)
    dst[rows, column(0)] = (dot_tn(keys, slopes).T * scale).astype(LOW)
    dst[rows, column(1)] = (unstacked(dot_nn(slopes, queries), lanes, size) * scale).astype(LOW)
    dst[rows, column(2)] = unstacked(dot_nn(probs, grads), lanes, size).astype(LOW)


def entry_tiles():
    tiles, offset = {}, 0
    for entry_name, (rows, columns) in layout():
        tiles[entry_name] = (offset // (TALL * LANES), rows, columns)
        offset += rows * columns
    tiles["vecs"] = (tiles["enc_vecs"][0], 4 * TALL, LANES)
    return tiles


def vec_reader(buffer, first, groups):
    rows = buffer[...].reshape(4 * TALL, LANES).astype(FULL)

    def vec(index):
        start = first + index * groups
        return jnp.concatenate([rows[start + g : start + g + 1] for g in range(groups)], axis=1)

    return vec


def fetch(flat, names, buffers, sems):
    tiles = entry_tiles()

    def build(index):
        start, rows, columns = tiles[names[index]]
        count = rows * columns // (TALL * LANES)
        return pltpu.make_async_copy(flat.at[pl.ds(start, count)], buffers[index], sems.at[index])

    for index in range(len(names)):
        build(index).start()

    def ready(index):
        build(index).wait()
        _, rows, columns = tiles[names[index]]
        return Blocked(buffers[index], rows, columns)

    return ready


def tile_buffers(names):
    tiles = entry_tiles()
    return [
        pltpu.VMEM((tiles[entry][1] * tiles[entry][2] // (TALL * LANES), TALL, LANES), LOW)
        for entry in names
    ]


def position_table(columns, padded):
    half = columns // 2
    frequency = np.exp(
        np.float32(-math.log(10000.0)) * np.arange(half, dtype=np.float32) / np.float32(half)
    ).astype(np.float32)
    angles = np.arange(PATCHES, dtype=np.float32)[:, None] * frequency
    table = np.zeros((padded, columns), np.float32)
    table[:PATCHES] = np.concatenate(
        [np.sin(angles.astype(np.float64)), np.cos(angles.astype(np.float64))], axis=-1
    )
    return table


def split_low(table):
    parts, rest = [], table.astype(np.float64)
    for _ in range(3):
        part = rest.astype(ml_dtypes.bfloat16)
        parts.append(part)
        rest = rest - part.astype(np.float64)
    return np.stack(parts)


MESH = pl.DeviceIdType.MESH
A_HALF = 1104
A_ROWS = 2 * A_HALF
B_HALF = 320
B_ROWS = 2 * B_HALF
SHARD_ROWS = 2834
PAD_ROWS = A_ROWS + B_ROWS
B_TRUE = SHARD_ROWS - A_ROWS
HALO = 384
HALO_STEP = 64
WIDE_ROWS = SHARD_ROWS + 2 * HALO
PARTS = {
    "a1": (0, A_HALF),
    "a2": (A_HALF, A_HALF),
    "b": (A_ROWS, B_ROWS),
    "b1": (A_ROWS, B_HALF),
    "b2": (A_ROWS + B_HALF, B_HALF),
}
TRUE_PARTS = {**PARTS, "b": (A_ROWS, B_TRUE), "b2": (A_ROWS + B_HALF, B_TRUE - B_HALF)}
SLOTS = {"a1": 0, "a2": 1, "b": 2, "b1": 2, "b2": 3}
COLUMNS = "oxyd"
ARRIVALS = {
    0: (
        12, 22, 102, 10, 20, 100, 11, 21, 101, 33, 34, 112, 122, 30, 110, 202, 120, 31, 200, 121,
        111, 201, 132, 130, 210, 212, 220, 131, 222, 302, 221, 211, 300, 230, 231, 301, 320, 310,
        232, 312, 321, 311, 322, 332, 330, 331,
    ),
    1: (
        2, 112, 122, 202, 0, 110, 120, 200, 1, 111, 121, 201, 133, 134, 12, 212, 22, 222, 20, 10,
        32, 302, 130, 210, 300, 220, 11, 301, 232, 21, 131, 312, 221, 211, 322, 332, 30, 310,
        230, 311, 320, 31, 321, 231, 330, 331,
    ),
}


def item_of(code):
    return code // 100, COLUMNS[code // 10 % 10], list(PARTS)[code % 10]


def own_item(inner, part):
    return 100 * inner + list(PARTS).index(part)


class Place:
    def __init__(self):
        self.core = lax.axis_index("seq")
        self.chip = lax.axis_index("dp")
        chip = self.chip
        self.z = chip // 4
        y, x = (chip // 2) % 2, chip % 2
        self.col = chip % 4
        self.col_x = self.col + 1 - 2 * x
        self.col_y = self.col + 2 - 4 * y
        self.col_d = self.col_x + 2 - 4 * y
        self.columns = {"o": self.col, "x": self.col_x, "y": self.col_y, "d": self.col_d}
        self.side = self.z // 2
        sign = 1 - 2 * self.side
        self.inner = self.z + self.side * (3 - 2 * self.z)
        self.me = 16 * self.core + chip
        self.devices = {
            "x": (self.core, 4 * self.z + self.col_x),
            "y": (self.core, 4 * self.z + self.col_y),
            "far": (self.core, chip + 4 * sign),
            "near": (self.core, chip - 4 * sign * self.inner),
            "core": (1 - self.core, chip),
            "next": self.ring(1),
            "back": self.ring(31),
        }

    def ring(self, step):
        peer = (self.me + step) % 32
        return (peer // 16, peer % 16)

    def plane(self, mirrored):
        return mirrored + self.side * (3 - 2 * mirrored)

    def greet(self):
        barrier = pltpu.get_barrier_semaphore()
        for link in ("x", "y", "far", "core", "next", "back"):
            pl.semaphore_signal(
                barrier, inc=1, device_id=self.devices[link], device_id_type=MESH
            )

        @pl.when(self.inner == 1)
        def _():
            pl.semaphore_signal(
                barrier, inc=1, device_id=self.devices["near"], device_id_type=MESH
            )

        pl.semaphore_wait(barrier, 6 + self.inner)


class Outbox:
    def __init__(self):
        self.sent = []

    def send(self, src, dst, send_sem, recv_sem, device):
        def build():
            return pltpu.make_async_remote_copy(
                src_ref=src,
                dst_ref=dst,
                send_sem=send_sem,
                recv_sem=recv_sem,
                device_id=device,
                device_id_type=MESH,
            )

        build().start()
        self.sent.append(build)

    def finish(self):
        for build in self.sent:
            build().wait_send()


def arrived(ref, sem, device):
    pltpu.make_async_remote_copy(
        src_ref=ref, dst_ref=ref, send_sem=sem, recv_sem=sem, device_id=device, device_id_type=MESH
    ).wait_recv()


def by_place(at, body):
    for inner in (0, 1):
        pl.when(at.inner == inner)(partial(body, inner))


def onward(inner, item):
    mirrored, column, part = item_of(item)
    line = ["far", "near"][: 1 + inner]
    if mirrored != inner:
        line = [] if inner == 0 else ["far" if mirrored == 0 else "near"]
    if part[0] == "a":
        if column == "o":
            return [(link, part) for link in [*line, "x", "y"]]
        if (column, part) in (("x", "a1"), ("y", "a2")):
            return [("y" if column == "x" else "x", part)]
        return []
    links = [(link, "b") for link in line]
    if mirrored == inner:
        links = {
            "o": [("x", "b"), ("y", "b")],
            "x": [("y", "b1")],
            "y": [("x", "b2")],
            "d": [],
        }[column] + links
    return links


def gather_exchange(at, flat, source, recv, core_recv, sends, core_send):
    def block(chip, part, core):
        first, size = TRUE_PARTS[part]
        return flat.at[pl.ds((core * 16 + chip) * SHARD_ROWS + first, size)]

    def body(inner):
        out = Outbox()
        diagonal = []

        def pass_on(item):
            mirrored, column, part = item_of(item)
            chip = 4 * at.plane(mirrored) + at.columns[column]
            own = mirrored == inner and column == "o"
            links = onward(inner, item)
            if mirrored == inner and column == "d" and part[0] == "b":
                diagonal.append(part)
                links = links if len(diagonal) == 2 else []
            for link, piece in [*links, ("core", part)]:
                slot = SLOTS[piece]
                ref = block(chip, piece, at.core)
                sent, got = (core_send, core_recv) if link == "core" else (sends[link], recv)
                out.send(
                    source(piece) if own else ref,
                    ref,
                    sent.at[chip, slot],
                    got.at[chip, slot],
                    at.devices[link],
                )

        for part in ("b", "a1", "a2"):
            pass_on(own_item(inner, part))
        for item in ARRIVALS[inner]:
            mirrored, column, part = item_of(item)
            chip = 4 * at.plane(mirrored) + at.columns[column]
            arrived(block(chip, part, at.core), recv.at[chip, SLOTS[part]], at.devices["x"])
            pass_on(item)
        for part in ("b", "a1", "a2"):
            arrived(
                block(at.chip, part, 1 - at.core),
                core_recv.at[at.chip, SLOTS[part]],
                at.devices["x"],
            )
        for item in ARRIVALS[inner]:
            mirrored, column, part = item_of(item)
            chip = 4 * at.plane(mirrored) + at.columns[column]
            ref = block(chip, part, 1 - at.core)
            arrived(ref, core_recv.at[chip, SLOTS[part]], at.devices["x"])
        out.finish()

    by_place(at, body)


def entry_blocks(me, body, edges=False):
    first, stop = me * SHARD_ROWS, me * SHARD_ROWS + SHARD_ROWS
    offset = 0
    for _, (rows, columns) in layout()[:11]:
        groups, blocks = columns // LANES, rows // TALL
        unit = TALL * groups
        total = unit * blocks
        if edges:
            for cut in (first, stop):
                inside = jnp.maximum(cut - offset, 0)
                block = inside // unit

                @pl.when((inside < total) & (inside % unit > 0))
                def _(block=block, offset=offset, unit=unit, groups=groups):
                    body(offset + block * unit, groups)
        else:
            low = jnp.minimum((jnp.maximum(first - offset, 0) + unit - 1) // unit, blocks)
            high = jnp.minimum(jnp.maximum(stop - offset, 0) // unit, blocks)

            def one(block, carry, offset=offset, unit=unit, groups=groups):
                body(offset + block * unit, groups)
                return carry

            lax.fori_loop(low, jnp.maximum(high, low), one, 0)
        offset += total
    return offset


def cut_rows(cut):
    before = after = 0
    offset = 0
    for _, (rows, columns) in layout()[:11]:
        unit, total = TALL * (columns // LANES), rows * (columns // LANES)
        inside = jnp.maximum(cut - offset, 0)
        cuts = ((inside < total) & (inside % unit > 0)).astype(jnp.int32)
        before = before + cuts * (inside % unit)
        after = after + cuts * (unit - inside % unit)
        offset += total
    return before, after


class Halo:
    def __init__(self, at, here, start, wide, send_sem, recv_sem):
        self.at, self.here, self.start, self.wide = at, here, start, wide
        self.sems = send_sem, recv_sem
        first = at.me * SHARD_ROWS
        head, give_back = cut_rows(first)
        give_next, tail = cut_rows(first + SHARD_ROWS)
        self.given, self.taken = (give_back, give_next), (tail, head)

    def copies(self, side, index):
        low, high = HALO_STEP * index, HALO_STEP * (index + 1)
        src = self.start + (low if side == 0 else SHARD_ROWS - high)
        dst = HALO + SHARD_ROWS + low if side == 0 else HALO - high
        return pltpu.make_async_remote_copy(
            src_ref=self.here.at[pl.ds(src, HALO_STEP)],
            dst_ref=self.wide.at[pl.ds(dst, HALO_STEP)],
            send_sem=self.sems[0].at[side, index],
            recv_sem=self.sems[1].at[side, index],
            device_id=self.at.devices["back" if side == 0 else "next"],
            device_id_type=MESH,
        )

    def each(self, rows, action):
        for side in range(2):
            for index in range(HALO // HALO_STEP):
                pl.when(rows[side] > HALO_STEP * index)(partial(action, side, index))

    def start_all(self):
        self.each(self.given, lambda side, index: self.copies(side, index).start())

    def take(self):
        self.each(self.taken, lambda side, index: self.copies(side, index).wait_recv())

    def finish(self):
        self.each(self.given, lambda side, index: self.copies(side, index).wait_send())


VEC_ROWS = 64


def gather_kernel(
    master_ref, visible_ref, flat_ref, both_ref, wide, turned, own_sem, halo_send, halo_recv, *sems
):
    recv, core_recv, send_x, send_y, send_far, send_near, core_send = sems
    at = Place()
    first = at.me * SHARD_ROWS
    skew = (at.me * 2) % TALL
    own = pltpu.make_async_copy(master_ref, wide.at[pl.ds(HALO, SHARD_ROWS)], own_sem.at[0])
    own.start()
    at.greet()
    out = Outbox()
    halo = Halo(at, master_ref, 0, wide, halo_send, halo_recv)
    halo.start_all()
    half = visible_ref.shape[0]
    rows_here = both_ref.at[pl.ds(pl.multiple_of(at.core * half, half), half)]
    rows_there = both_ref.at[pl.ds(pl.multiple_of((1 - at.core) * half, half), half)]
    out.send(visible_ref, rows_here, own_sem.at[3], own_sem.at[4], at.devices["core"])
    keep = pltpu.make_async_copy(visible_ref, rows_here, own_sem.at[2])
    keep.start()
    own.wait()

    def turn(row, groups):
        start = row - first + HALO
        spot = row - (first - skew) + HALO
        for group in range(groups):
            turned[pl.ds(pl.multiple_of(spot + group * TALL, TALL), TALL), :] = wide[
                pl.ds(start + group, TALL, stride=groups), :
            ].astype(LOW)

    vec_start = entry_blocks(at.me, turn)
    halo.take()
    entry_blocks(at.me, turn, edges=True)

    @pl.when(at.me == 31)
    def _():
        start = vec_start - 31 * SHARD_ROWS + HALO
        spot = start + (31 * 2) % TALL
        turned[pl.ds(spot, VEC_ROWS), :] = wide[pl.ds(start, VEC_ROWS), :].astype(LOW)

    mine = pltpu.make_async_copy(
        turned.at[pl.ds(HALO + skew, SHARD_ROWS)],
        flat_ref.at[pl.ds(first, SHARD_ROWS)],
        own_sem.at[1],
    )
    mine.start()

    def source(part):
        start, size = TRUE_PARTS[part]
        return turned.at[pl.ds(HALO + skew + start, size)]

    sends = {"x": send_x, "y": send_y, "far": send_far, "near": send_near}
    gather_exchange(at, flat_ref, source, recv, core_recv, sends, core_send)
    mine.wait()
    keep.wait()
    arrived(rows_there, own_sem.at[4], at.devices["x"])
    out.finish()
    halo.finish()


def gather_weights(master_rows, visible_rows):
    hbm = pl.BlockSpec(memory_space=pltpu.HBM)
    steps = pltpu.SemaphoreType.DMA((2, HALO // HALO_STEP))
    half, width = visible_rows.shape
    return pl.pallas_call(
        gather_kernel,
        out_shape=[
            jax.ShapeDtypeStruct((32 * SHARD_ROWS, LANES), LOW),
            jax.ShapeDtypeStruct((2 * half, width), LOW),
        ],
        in_specs=[hbm, hbm],
        out_specs=[hbm, hbm],
        scratch_shapes=[
            pltpu.VMEM((WIDE_ROWS + 6, LANES), FULL),
            pltpu.VMEM((WIDE_ROWS + 30, LANES), LOW),
            pltpu.SemaphoreType.DMA((5,)),
            steps,
            steps,
        ]
        + [pltpu.SemaphoreType.DMA((16, 4))] * 7,
        compiler_params=pltpu.CompilerParams(
            collective_id=0, has_side_effects=True, vmem_limit_bytes=60 * 1024 * 1024
        ),
        name="gather_weights",
    )(master_rows, visible_rows)


def add_into(dst, start, terms, size, chunk):
    def one(step):
        row = step * chunk
        total = None
        for ref, first in terms:
            piece = ref[pl.ds(pl.multiple_of(first + row, TALL), chunk), :].astype(FULL)
            total = piece if total is None else total + piece
        dst[pl.ds(pl.multiple_of(start + row, TALL), chunk), :] = total.astype(dst.dtype)

    loop(size // chunk, one)


def reduce_kernel(
    grad_ref,
    loss_ref,
    shard_ref,
    square_ref,
    loss_total_ref,
    own,
    theirs,
    from_x,
    from_y,
    pass_x,
    pass_y,
    far_a,
    near_a,
    far_b,
    near_b,
    wide,
    plain,
    scalars,
    load_sem,
    core_send,
    core_recv,
    send_x,
    send_y,
    send_far,
    send_near,
    recv_x,
    recv_y,
    recv_far,
    recv_near,
    halo_send,
    halo_recv,
    tiny_send,
    tiny_recv,
):
    at = Place()
    tail = pl.ds(SHARD_ROWS - 2, TALL)
    for index in range(16):
        own[index, tail, :] = jnp.zeros((TALL, LANES), LOW)
        theirs[index, tail, :] = jnp.zeros((TALL, LANES), LOW)
    body = pl.ds(0, SHARD_ROWS)

    def shard_rows(core, chip):
        return grad_ref.at[pl.ds((core * 16 + chip) * SHARD_ROWS, SHARD_ROWS)]

    def load(chip):
        return pltpu.make_async_copy(
            shard_rows(at.core, chip), own.at[chip, body], load_sem.at[chip]
        )

    at.greet()
    pairs = Outbox()
    for mirrored in (3, 2, 1 - at.inner, at.inner):
        for column in ("d", "y", "x", "o"):
            chip = 4 * at.plane(mirrored) + at.columns[column]
            pairs.send(
                shard_rows(1 - at.core, chip),
                theirs.at[chip, body],
                core_send.at[chip],
                core_recv.at[chip],
                at.devices["core"],
            )
            load(chip).start()
    sends = {"x": send_x, "y": send_y, "far": send_far, "near": send_near}
    recvs = {"x": recv_x, "y": recv_y, "far": recv_far, "near": recv_near}
    relayed = {"x": pass_x, "y": pass_y}
    direct = {"x": from_x, "y": from_y}
    lines = {"far": (far_a, far_b), "near": (near_a, near_b)}

    def reduce_parts(inner):
        out = Outbox()
        paired, joined = set(), set()

        def pair(chip, column, part):
            if (column, "all") not in paired:
                paired.add((column, "all"))
                load(chip).wait()
                arrived(theirs.at[chip, body], core_recv.at[chip], at.devices["x"])
            name = "b" if part[0] == "b" else part
            if (column, name) not in paired:
                paired.add((column, name))
                first, size = PARTS[name]
                add_into(
                    own.at[chip],
                    first,
                    [(own.at[chip], first), (theirs.at[chip], first)],
                    size,
                    size // (4 if name == "b" else 3),
                )

        def landing(link, plane, chip, part, relay):
            first, size = PARTS[part]
            if link in lines and part == "b":
                return lines[link][1].at[chip], 0, size, (chip, SLOTS[part])
            if link in lines:
                return lines[link][0].at[plane], first, size, (chip, SLOTS[part])
            if relay:
                return relayed[link].at[plane], first, size, (plane, 3 + (part[0] == "b"))
            return direct[link].at[plane], first, size, (plane, SLOTS[part])

        def step(item):
            mirrored, column, part = item_of(item)
            plane = at.plane(mirrored)
            chip = 4 * plane + at.columns[column]
            pair(chip, (mirrored, column), part)
            first, size = PARTS[part]
            terms = []
            links = onward(inner, item)
            if mirrored == inner and column == "d" and part[0] == "b":
                links = [] if joined else links
                joined.add(part)
            own_item = mirrored == inner and column == "o"
            for link, piece in links:
                relay = column in ("x", "y")
                buffer, start, count, index = landing(link, plane, chip, piece, relay)
                arrived(buffer.at[pl.ds(start, count)], recvs[link].at[*index], at.devices["x"])
                terms.append((buffer, start, count))
            if own_item:
                whole = [(own.at[chip], first)] + [(buffer, start) for buffer, start, _ in terms]
                if part == "b":
                    add_into(plain, 0, whole, size, size // 4)
                    wide[pl.ds(HALO + A_ROWS, B_TRUE), :] = plain[pl.ds(0, B_TRUE), :]
                else:
                    add_into(wide, HALO + first, whole, size, size // 3)
                return
            full_size = B_ROWS if part[0] == "b" else size
            full_first = PARTS["b"][0] if part[0] == "b" else first
            whole = [(buffer, start) for buffer, start, count in terms if count == full_size]
            halves = [(buffer, start, count) for buffer, start, count in terms if count != full_size]
            if whole:
                add_into(
                    own.at[chip],
                    full_first,
                    [(own.at[chip], full_first), *whole],
                    full_size,
                    full_size // (4 if part[0] == "b" else 3),
                )
            for buffer, start, count in halves:
                add_into(
                    own.at[chip], start, [(own.at[chip], start), (buffer, start)], count, count // 2
                )
            if column == "o" or (part == "b" and mirrored != inner):
                link = "near" if inner == 1 and mirrored == 0 else "far"
                target = "near" if inner == 0 else "far"
                buffer, start, _, index = landing(target, plane, chip, part, False)
                arrive_sem = recvs[target]
            else:
                link = {"x": "x", "y": "y", "d": "y" if part in ("a1", "b1") else "x"}[column]
                buffer, start, _, index = landing(link, plane, chip, part, column == "d")
                arrive_sem = recvs[link]
            out.send(
                own.at[chip, pl.ds(first, size)],
                buffer.at[pl.ds(start, size)],
                sends[link].at[*index],
                arrive_sem.at[*index],
                at.devices[link],
            )

        for item in reversed(ARRIVALS[inner]):
            step(item)
        for part in ("a2", "a1", "b"):
            step(own_item(inner, part))
        out.finish()

    by_place(at, reduce_parts)
    pairs.finish()

    tiny = Outbox()
    halo = Halo(at, wide, HALO, wide, halo_send, halo_recv)
    halo.start_all()
    step_rows = 352
    whole_steps = SHARD_ROWS // step_rows

    def squares(index, carry):
        piece = wide[pl.ds(pl.multiple_of(HALO + index * step_rows, 8), step_rows), :]
        piece = piece * piece
        return carry + jnp.sum(piece.reshape(step_rows // 8, 8, LANES), axis=0)

    square = lax.fori_loop(0, whole_steps, squares, jnp.zeros((8, LANES), FULL))
    rest = wide[pl.ds(HALO + whole_steps * step_rows, SHARD_ROWS - whole_steps * step_rows), :]
    square = square + 0.125 * jnp.sum(rest * rest, axis=0, keepdims=True)
    scalars[at.me, 0] = square
    scalars[at.me, 1] = jnp.broadcast_to(loss_ref[...], (8, LANES))
    for index in range(1, 32):
        tiny.send(
            scalars.at[at.me],
            scalars.at[at.me],
            tiny_send.at[index],
            tiny_recv.at[at.me],
            at.ring(index),
        )
    def turn_back(row, groups):
        start = row - at.me * SHARD_ROWS + HALO
        for group in range(groups):
            plain[pl.ds(start + group, TALL, stride=groups), :] = wide[
                pl.ds(start + group * TALL, TALL), :
            ]

    vec_start = entry_blocks(at.me, turn_back)
    halo.take()
    entry_blocks(at.me, turn_back, edges=True)

    @pl.when(at.me == 31)
    def _():
        spot = pl.ds(vec_start - 31 * SHARD_ROWS + HALO, VEC_ROWS)
        plain[spot, :] = wide[spot, :]

    shard_ref[...] = plain[pl.ds(HALO, SHARD_ROWS), :]
    for index in range(1, 32):
        peer = (at.me + index) % 32
        arrived(scalars.at[peer], tiny_recv.at[peer], at.devices["x"])
    totals = jnp.sum(scalars[...], axis=0)
    square_ref[...] = jnp.sum(
        jnp.sum(totals[0], axis=0, keepdims=True), axis=1, keepdims=True
    )
    loss_total_ref[...] = totals[1, 0:1, 0:1]
    halo.finish()
    tiny.finish()


def reduce_gradients(grad_rows, loss_row):
    hbm = pl.BlockSpec(memory_space=pltpu.HBM)
    vmem = pl.BlockSpec(memory_space=pltpu.VMEM)
    dma = pltpu.SemaphoreType.DMA
    shard_total, square, loss = pl.pallas_call(
        reduce_kernel,
        out_shape=[
            jax.ShapeDtypeStruct((SHARD_ROWS, LANES), FULL),
            jax.ShapeDtypeStruct((1, 1), FULL),
            jax.ShapeDtypeStruct((1, 1), FULL),
        ],
        in_specs=[hbm, vmem],
        out_specs=[vmem, vmem, vmem],
        scratch_shapes=[pltpu.VMEM((16, PAD_ROWS, LANES), LOW)] * 2
        + [pltpu.VMEM((4, PAD_ROWS, LANES), LOW)] * 4
        + [pltpu.VMEM((4, A_ROWS, LANES), LOW)] * 2
        + [pltpu.VMEM((16, B_ROWS, LANES), LOW)] * 2
        + [pltpu.VMEM((WIDE_ROWS + 6, LANES), FULL)] * 2
        + [pltpu.VMEM((32, 2, 8, LANES), FULL)]
        + [dma((16,))] * 3
        + [dma((4, 5))] * 2
        + [dma((16, 4))] * 2
        + [dma((4, 5))] * 2
        + [dma((16, 4))] * 2
        + [dma((2, HALO // HALO_STEP))] * 2
        + [dma((32,))] * 2,
        compiler_params=pltpu.CompilerParams(
            collective_id=1, has_side_effects=True, vmem_limit_bytes=60 * 1024 * 1024
        ),
        name="reduce_gradients",
    )(grad_rows, loss_row)
    return shard_total.reshape(-1), square.reshape(()), loss.reshape(())


ROWS = 256
ENC_CHUNK = 256
FETCHED = ("vecs", "embed", "enc_qkv", "enc_out", "enc_up", "enc_down", "project")
BACKWARD_FETCHED = ("vecs", "project", "enc_down", "enc_up", "enc_out", "enc_qkv")


def encoder_forward_kernel(
    part_ref,
    visible_ref,
    segments_ref,
    patches_ref,
    table_ref,
    flat_ref,
    *refs,
):
    results, kept, (out_sem, sems, *buffers) = refs[:14], refs[14:28], refs[28:]
    (
        vis_rows,
        embedded,
        normed_a,
        qkv_rows,
        attn_out,
        after_attn,
        normed_b,
        slope,
        hidden_act,
        encoded,
        final_enc,
        projected,
        row_facts,
        column_facts,
    ) = kept

    def shipment(index):
        return pltpu.make_async_copy(kept[index], results[index], out_sem.at[index])

    def ship(*indices):
        for index in indices:
            shipment(index).start()

    ready = fetch(flat_ref, FETCHED, buffers, sems)
    part = part_ref[0]
    total = segments_ref.shape[1]
    images = IMG_SEQ // 2
    spare = ROWS - images * VIS
    segments = segments_ref[...]
    image = segments - part * images
    inside = (image >= 0) & (image < images)
    padding = segments == IMG_SEQ
    flags = jnp.concatenate(
        [
            inside.astype(FULL),
            padding.astype(FULL),
            jnp.zeros((6, total), FULL),
        ],
        axis=0,
    ).astype(LOW)
    row = lax.broadcasted_iota(jnp.int32, (total, total), 0)
    column = lax.broadcasted_iota(jnp.int32, (total, total), 1)
    counts = dot_nn(flags, (row <= column).astype(FULL).astype(LOW)).astype(jnp.int32)
    inside_count, padding_count = counts[0:1], counts[1:2]
    padding_slot = padding_count - part * spare
    chosen = inside | (padding & (padding_slot >= 1) & (padding_slot <= spare))
    slot = inside_count + jnp.clip(padding_slot, 0, spare) - 1
    slot = jnp.where(chosen, slot, -1)
    select = (lax.broadcasted_iota(jnp.int32, (ROWS, total), 0) == slot).astype(FULL).astype(LOW)
    facts = jnp.concatenate(
        [segments.astype(FULL), patches_ref[...].astype(FULL), jnp.zeros((LANES - 2, total), FULL)],
        axis=0,
    ).astype(LOW)
    row_facts[...] = dot_nt(facts[0:16], select)
    column_facts[...] = dot_nt(select, facts)
    vis_rows[...] = dot_nn(select, visible_ref[...]).astype(LOW)
    ship(0, 12, 13)
    patch = column_facts[:, 1:2].astype(jnp.int32)
    spot = (lax.broadcasted_iota(jnp.int32, (ROWS, table_ref.shape[1]), 1) == patch).astype(FULL).astype(LOW)
    embedded[...] = dot_nn(spot, table_ref[0]) + dot_nn(spot, table_ref[1]) + dot_nn(spot, table_ref[2])
    w_embed = ready(1)
    product_into(embedded, vis_rows, w_embed, D, residual=embedded)
    ship(1)
    ready(0)
    vec = vec_reader(buffers[0], 0, D // LANES)
    norm_into(normed_a, embedded, vec(0), vec(1), ROWS, ENC_CHUNK)
    ship(2)
    w_qkv = ready(2)
    product_into(qkv_rows, normed_a, w_qkv, 3 * D)
    ship(3)
    allowed = column_facts[:, 0:1] == row_facts[0:1, :]
    allowed = jnp.concatenate([allowed.astype(FULL)] * 2, axis=0) > 0.5

    def attend(step):
        for part in range(2):
            attend_into(
                attn_out, qkv_rows, pl.ds(0, ROWS), 2 * step + part, D, allowed, D // HEADS
            )

    loop(D // LANES // 2, attend)
    ship(4)
    w_out = ready(3)
    product_into(after_attn, attn_out, w_out, D, residual=embedded)
    ship(5)
    norm_into(normed_b, after_attn, vec(2), vec(3), ROWS, ENC_CHUNK)
    ship(6)
    w_up = ready(4)
    up_into(hidden_act, slope, normed_b, w_up, FF, 512)
    ship(7, 8)
    w_down = ready(5)
    product_into(encoded, hidden_act, w_down, D, residual=after_attn)
    ship(9)
    norm_into(final_enc, encoded, vec(4), vec(5), ROWS, ENC_CHUNK)
    ship(10)
    w_proj = ready(6)
    product_into(projected, final_enc, w_proj, DD)
    ship(11)
    for index in range(len(kept)):
        shipment(index).wait()


def encoder_forward(part, visible_rows, segments, patch_ids, flat_weights):
    hbm = pl.BlockSpec(memory_space=pltpu.HBM)
    vmem = pl.BlockSpec(memory_space=pltpu.VMEM)
    smem = pl.BlockSpec(memory_space=pltpu.SMEM)
    table = jnp.asarray(split_low(position_table(D, 256)))
    kept = [
        ((ROWS, PIX), LOW),
        ((ROWS, D), FULL),
        ((ROWS, D), LOW),
        ((ROWS, 3 * D), LOW),
        ((ROWS, D), LOW),
        ((ROWS, D), FULL),
        ((ROWS, D), LOW),
        ((ROWS, FF), FULL),
        ((ROWS, FF), LOW),
        ((ROWS, D), FULL),
        ((ROWS, D), LOW),
        ((ROWS, DD), LOW),
        ((16, ROWS), FULL),
        ((ROWS, LANES), FULL),
    ]
    return pl.pallas_call(
        encoder_forward_kernel,
        out_shape=[jax.ShapeDtypeStruct(s, d) for s, d in kept],
        in_specs=[smem] + [vmem] * 4 + [hbm],
        out_specs=[hbm] * 14,
        scratch_shapes=[pltpu.VMEM(s, d) for s, d in kept]
        + [pltpu.SemaphoreType.DMA((14,)), pltpu.SemaphoreType.DMA((7,))] + tile_buffers(FETCHED),
        compiler_params=pltpu.CompilerParams(vmem_limit_bytes=60 * 1024 * 1024),
        name="encoder_forward",
    )(part, visible_rows, segments, patch_ids, table, flat_weights)


def encoder_backward_kernel(
    grad_projected,
    decoder_vecs,
    *refs,
):
    stored, refs = refs[:13], refs[13:]
    weights_ref, partial_ref, flat_ref, refs = *refs[:3], refs[3:]
    kept, refs = refs[:13], refs[13:]
    (
        grad_rows,
        upper,
        branch,
        grad_pre,
        middle,
        grad_attn,
        grad_qkv,
        vec_grads,
        turned,
        stage,
        vec_full,
        vec_stage,
        stage_sem,
        kept_sem,
        sems,
        *buffers,
    ) = refs
    (
        vis_rows,
        embedded,
        normed_a,
        qkv_rows,
        attn_out,
        after_attn,
        normed_b,
        slope,
        hidden_act,
        encoded,
        final_enc,
        row_facts,
        column_facts,
    ) = kept

    def delivery(index):
        return pltpu.make_async_copy(stored[index], kept[index], kept_sem.at[index])

    def need(*indices):
        for index in indices:
            delivery(index).wait()

    for index in (10, 9, 8):
        delivery(index).start()
    del partial_ref
    ready = fetch(weights_ref, BACKWARD_FETCHED, buffers, sems)
    for index in (7, 6, 5, 4, 12, 11, 3, 2, 1, 0):
        delivery(index).start()
    tiles = entry_tiles()
    ready(0)
    vec = vec_reader(buffers[0], 0, D // LANES)
    grad_of = lambda index: vec_grads.at[pl.ds(index, 1), :]

    emit = Emitter(flat_ref, turned, stage, stage_sem)

    need(10)
    emit("project", final_enc, grad_projected)
    w_proj = ready(1)
    product_t_into(upper, grad_projected, w_proj, D)
    need(9)
    norm_back(grad_rows, encoded, upper, None, vec(4), grad_of(4), grad_of(5), ROWS, ENC_CHUNK)
    branch[...] = grad_rows[...].astype(LOW)
    need(8)
    emit("enc_down", hidden_act, branch)
    need(7)
    w_down = ready(2)
    down_back_into(grad_pre, branch, w_down, slope, FF, 512)
    need(6)
    emit("enc_up", normed_b, grad_pre)
    w_up = ready(3)
    product_t_into(upper, grad_pre, w_up, D)
    need(5)
    norm_back(grad_rows, after_attn, upper, grad_rows, vec(2), grad_of(2), grad_of(3), ROWS, ENC_CHUNK)
    middle[...] = grad_rows[...].astype(LOW)
    need(4)
    emit("enc_out", attn_out, middle)
    w_out = ready(4)
    product_t_into(grad_attn, middle, w_out, D)
    need(12, 11, 3)
    allowed = column_facts[:, 0:1] == row_facts[0:1, :]

    def attend_back(step):
        for part in range(2):
            attend_back_into(
                grad_qkv,
                grad_attn,
                qkv_rows,
                pl.ds(0, ROWS),
                2 * step + part,
                D,
                D // HEADS,
                allowed=allowed,
            )

    loop(D // LANES // 2, attend_back)
    need(2)
    emit("enc_qkv", normed_a, grad_qkv)
    w_qkv = ready(5)
    product_t_into(upper, grad_qkv, w_qkv, D)
    need(1)
    norm_back(grad_rows, embedded, upper, grad_rows, vec(0), grad_of(0), grad_of(1), ROWS, ENC_CHUNK)
    branch[...] = grad_rows[...].astype(LOW)
    need(0)
    emit("embed", vis_rows, branch)
    emit.finish()
    groups = D // LANES
    for index in range(6):
        for group in range(groups):
            vec_full[pl.ds(index * groups + group, 1), :] = vec_grads[
                pl.ds(index, 1), pl.ds(group * LANES, LANES)
            ]
    base, groups = 6 * groups, DD // LANES
    for index in range(7):
        for group in range(groups):
            vec_full[pl.ds(base + index * groups + group, 1), :] = decoder_vecs[
                pl.ds(index, 1), pl.ds(group * LANES, LANES)
            ]
    vec_stage[...] = vec_full[...].astype(LOW).reshape(4, TALL, LANES)
    copy = pltpu.make_async_copy(vec_stage, flat_ref.at[pl.ds(tiles["enc_vecs"][0], 4)], stage_sem.at[0])
    copy.start()
    copy.wait()


def encoder_backward(saved, grad_projected, flat_weights, decoder_vec_grads, flat):
    hbm = pl.BlockSpec(memory_space=pltpu.HBM)
    vmem = pl.BlockSpec(memory_space=pltpu.VMEM)
    inputs = [grad_projected, decoder_vec_grads, *saved, flat_weights, flat]
    low, full = (lambda *s: pltpu.VMEM(s, LOW)), (lambda *s: pltpu.VMEM(s, FULL))
    return pl.pallas_call(
        encoder_backward_kernel,
        out_shape=jax.ShapeDtypeStruct(flat.shape, LOW),
        in_specs=[vmem] * 2 + [hbm] * 15,
        out_specs=hbm,
        input_output_aliases={len(inputs) - 1: 0},
        scratch_shapes=[pltpu.VMEM(array.shape, array.dtype) for array in saved]
        + [
            full(ROWS, D),
            full(ROWS, D),
            low(ROWS, D),
            low(ROWS, FF),
            low(ROWS, D),
            low(ROWS, D),
            low(ROWS, 3 * D),
            full(8, D),
            low(FF, ROWS),
            low(2, FF * D // (TALL * LANES), TALL, LANES),
            full(64, LANES),
            low(4, TALL, LANES),
            pltpu.SemaphoreType.DMA((2,)),
            pltpu.SemaphoreType.DMA((13,)),
            pltpu.SemaphoreType.DMA((6,)),
        ]
        + tile_buffers(BACKWARD_FETCHED),
        compiler_params=pltpu.CompilerParams(vmem_limit_bytes=60 * 1024 * 1024),
        name="encoder_backward",
    )(*inputs)


IMAGES = 5
DECODER_FETCHED = ("vecs", "dec_qkv", "dec_out", "dec_up", "dec_down", "pixel")
IMG_ROWS = 200
DEC_ROWS = IMAGES * IMG_ROWS


def decoder_kernel(
    part_ref,
    projected,
    row_facts,
    targets_ref,
    table_ref,
    weights_ref,
    flat_ref,
    grad_projected,
    vec_grads,
    loss_ref,
    dec_in,
    low_rows,
    qkv_rows,
    attn_out,
    after_attn,
    normed_b,
    slope,
    hidden_act,
    decoded,
    final_dec,
    grad_pred,
    upper,
    masked,
    score_logs,
    turned,
    stage,
    stage_sem,
    sems,
    *buffers,
    mask_total,
):
    ready = fetch(weights_ref, DECODER_FETCHED, buffers, sems)
    tiles = entry_tiles()
    ready(0)
    vec = vec_reader(buffers[0], 6 * D // LANES, DD // LANES)
    grad_of = lambda index: vec_grads.at[pl.ds(index, 1), :]
    part = part_ref[0]
    image_of = row_facts[0:1, :].astype(jnp.int32) - part * IMAGES
    patch_of = row_facts[1:2, :].astype(jnp.int32)
    patch = lax.broadcasted_iota(jnp.int32, (IMG_ROWS, ROWS), 0)

    def selector(index):
        return ((patch_of == patch) & (image_of == index)).astype(FULL)

    def place(index):
        at = span(index, IMG_ROWS)
        select = selector(index)
        real = (patch[:, 0:1] < PATCHES).astype(FULL)
        hidden = real * (1.0 - jnp.sum(select, axis=-1, keepdims=True))
        masked[at, :] = jnp.broadcast_to(hidden, (IMG_ROWS, LANES))
        dec_in[at, :] = dot_nn(select.astype(LOW), projected[...]) + hidden * vec(6) + table_ref[...]

    for index in range(IMAGES):
        place(index)
    norm_into(low_rows, dec_in, vec(0), vec(1), DEC_ROWS, DEC_ROWS)
    w_qkv = ready(1)
    product_into(qkv_rows, low_rows, w_qkv, 3 * DD)
    head_size = DD // DHEADS
    heads = LANES // head_size
    groups = DD // LANES

    def attend(step):
        rows = span(step, IMG_ROWS)
        for at in range(groups):
            logs = score_logs.at[pl.ds((step * groups + at) * heads, heads)]
            attend_columns_into(attn_out, qkv_rows, rows, at, DD, PATCHES, head_size, logs)

    loop(IMAGES, attend)
    w_out = ready(2)
    product_into(after_attn, attn_out, w_out, DD, residual=dec_in)
    norm_into(normed_b, after_attn, vec(2), vec(3), DEC_ROWS, DEC_ROWS)
    w_up = ready(3)
    up_into(hidden_act, slope, normed_b, w_up, DFF, TILE)
    w_down = ready(4)
    product_into(decoded, hidden_act, w_down, DD, residual=after_attn)
    norm_into(final_dec, decoded, vec(4), vec(5), DEC_ROWS, DEC_ROWS)
    w_pix = ready(5)
    loss_ref[...] = jnp.zeros_like(loss_ref)

    def compare(index):
        at = span(index, IMG_ROWS)
        image = pl.ds(0, PATCHES)
        goal, _ = norm_parts(targets_ref[index].astype(FULL))
        goal = jnp.concatenate([goal, jnp.zeros((IMG_ROWS - PATCHES, PIX), FULL)], axis=0)
        error = dot_nn(final_dec[at, :], w_pix.column_tile(0, PIX)) - goal
        weight = masked[at, 0:1]
        rows = jnp.mean(error * error, axis=-1, keepdims=True) * weight
        loss_ref[...] = loss_ref[...] + jnp.sum(rows) * (1.0 / mask_total)
        grad_pred[at, :] = (weight * error * (2.0 / (PIX * mask_total))).astype(LOW)

    for index in range(IMAGES):
        compare(index)

    emit = Emitter(flat_ref, turned, stage, stage_sem)

    emit("pixel", final_dec, grad_pred)
    product_t_into(upper, grad_pred, w_pix, DD)
    grad_rows, branch = decoded, final_dec
    norm_back(grad_rows, decoded, upper, None, vec(4), grad_of(4), grad_of(5), DEC_ROWS, DEC_ROWS)
    branch[...] = grad_rows[...].astype(LOW)
    emit("dec_down", hidden_act, branch)
    grad_pre = hidden_act
    down_back_into(grad_pre, branch, w_down, slope, DFF, TILE)
    emit("dec_up", normed_b, grad_pre)
    product_t_into(upper, grad_pre, w_up, DD)
    norm_back(grad_rows, after_attn, upper, grad_rows, vec(2), grad_of(2), grad_of(3), DEC_ROWS, DEC_ROWS)
    branch[...] = grad_rows[...].astype(LOW)
    emit("dec_out", attn_out, branch)
    grad_attn, grad_qkv = normed_b, grad_pre.at[:, pl.ds(0, 3 * DD)]
    product_t_into(grad_attn, branch, w_out, DD)

    def attend_back(step):
        rows = span(step, IMG_ROWS)
        for at in range(groups):
            logs = score_logs.at[pl.ds((step * groups + at) * heads, heads)]
            attend_back_into(
                grad_qkv, grad_attn, qkv_rows, rows, at, DD, head_size, real=PATCHES, logs=logs
            )

    loop(IMAGES, attend_back)
    emit("dec_qkv", low_rows, grad_qkv)
    emit.finish()
    product_t_into(upper, grad_qkv, w_qkv, DD)
    norm_back(grad_rows, dec_in, upper, grad_rows, vec(0), grad_of(0), grad_of(1), DEC_ROWS, DEC_ROWS)
    upper[pl.ds(0, ROWS), :] = jnp.zeros((ROWS, DD), FULL)

    def collect(index, token):
        at = span(index, IMG_ROWS)
        rows = grad_rows[at, :]
        token = token + jnp.sum((rows * masked[at, 0:1]).reshape(IMG_ROWS // 8, 8, DD), axis=0)
        upper[pl.ds(0, ROWS), :] = upper[pl.ds(0, ROWS), :] + dot_tn(
            selector(index).astype(LOW), rows.astype(LOW)
        )
        return token

    token = lax.fori_loop(0, IMAGES, collect, jnp.zeros((8, DD), FULL))
    grad_of(6)[...] = jnp.sum(token, axis=0, keepdims=True)
    grad_projected[...] = upper[pl.ds(0, ROWS), :].astype(LOW)


def decoder_step(part, projected, row_facts, targets, flat_weights, mask_total):
    hbm = pl.BlockSpec(memory_space=pltpu.HBM)
    vmem = pl.BlockSpec(memory_space=pltpu.VMEM)
    smem = pl.BlockSpec(memory_space=pltpu.SMEM)
    table = jnp.asarray(position_table(DD, IMG_ROWS))
    low, full = (lambda *s: pltpu.VMEM(s, LOW)), (lambda *s: pltpu.VMEM(s, FULL))
    return pl.pallas_call(
        partial(decoder_kernel, mask_total=mask_total),
        out_shape=[
            jax.ShapeDtypeStruct(flat_weights.shape, LOW),
            jax.ShapeDtypeStruct((ROWS, DD), LOW),
            jax.ShapeDtypeStruct((8, DD), FULL),
            jax.ShapeDtypeStruct((1, LANES), FULL),
        ],
        in_specs=[smem] + [vmem] * 4 + [hbm],
        out_specs=[hbm] + [vmem] * 3,
        scratch_shapes=[
            full(DEC_ROWS, DD),
            low(DEC_ROWS, DD),
            low(DEC_ROWS, 3 * DD),
            low(DEC_ROWS, DD),
            full(DEC_ROWS, DD),
            low(DEC_ROWS, DD),
            full(DEC_ROWS, DFF),
            low(DEC_ROWS, DFF),
            full(DEC_ROWS, DD),
            low(DEC_ROWS, DD),
            low(DEC_ROWS, PIX),
            full(DEC_ROWS, DD),
            full(DEC_ROWS, LANES),
            full(IMAGES * DHEADS, 1, IMG_ROWS),
            low(DFF, DEC_ROWS),
            low(2, DFF * DD // (TALL * LANES), TALL, LANES),
            pltpu.SemaphoreType.DMA((2,)),
            pltpu.SemaphoreType.DMA((6,)),
        ]
        + tile_buffers(DECODER_FETCHED),
        compiler_params=pltpu.CompilerParams(vmem_limit_bytes=62 * 1024 * 1024),
        name="decoder_step",
    )(part, projected, row_facts, targets, table, flat_weights)


def to_tiles(full_flat):
    pieces, offset = [], 0
    for _, (rows, columns) in layout()[:11]:
        piece = full_flat[offset : offset + rows * columns]
        piece = piece.reshape(rows // TALL, TALL, columns // LANES, LANES)
        pieces.append(piece.transpose(0, 2, 1, 3).reshape(-1, LANES))
        offset += rows * columns
    return jnp.concatenate([*pieces, full_flat[offset:].reshape(-1, LANES)])


def from_tiles(rows_flat):
    pieces, offset = [], 0
    for _, (rows, columns) in layout()[:11]:
        count = rows * columns // LANES
        piece = rows_flat[offset : offset + count]
        piece = piece.reshape(rows // TALL, columns // LANES, TALL, LANES)
        pieces.append(piece.transpose(0, 2, 1, 3).reshape(-1))
        offset += count
    return jnp.concatenate([*pieces, rows_flat[offset:].reshape(-1)])


def shards(visible, segments, patch_ids, targets, master, moment_one, moment_two, step_count):
    part = lax.axis_index("seq")
    in_kernels = master.shape[0] == SHARD_ROWS * LANES and lax.axis_size("dp") == 16
    if in_kernels:
        flat_weights, visible_rows = gather_weights(
            master.reshape(SHARD_ROWS, LANES), visible[0]
        )
    else:
        full_flat = lax.all_gather(master.astype(LOW), ("seq", "dp"), axis=0, tiled=True)
        flat_weights = to_tiles(full_flat)
        visible_rows = lax.all_gather(visible[0], "seq", axis=0, tiled=True)
    flat_weights = flat_weights.reshape(-1, TALL, LANES)
    part_row = part.reshape(1).astype(jnp.int32)
    mask_total = (PATCHES - VIS) * IMG_SEQ * visible.shape[0] * lax.axis_size("dp")
    *saved, projected, row_facts, column_facts = encoder_forward(
        part_row, visible_rows, segments, patch_ids, flat_weights
    )
    flat_grads, grad_projected, decoder_vec_grads, loss_row = decoder_step(
        part_row, projected, row_facts, targets[0], flat_weights, mask_total
    )
    flat_grads = encoder_backward(
        [*saved, row_facts, column_facts],
        grad_projected,
        flat_weights,
        decoder_vec_grads,
        flat_grads,
    )
    flat_grads = flat_grads.reshape(-1, LANES)
    if in_kernels:
        grad_shard, square_sum, loss_sum = reduce_gradients(flat_grads, loss_row)
    else:
        grad_flat = from_tiles(flat_grads.astype(FULL))
        grad_shard = lax.psum_scatter(grad_flat, ("seq", "dp"), scatter_dimension=0, tiled=True)
        square_sum, loss_sum = lax.psum(
            (jnp.sum(grad_shard * grad_shard), loss_row[0, 0]), ("seq", "dp")
        )
    grad_norm = jnp.sqrt(square_sum)
    clipped = grad_shard * jnp.minimum(1.0, clip_limit / (grad_norm + 1e-06))
    new_one = beta_mom * moment_one + (1.0 - beta_mom) * clipped
    new_two = beta_mom * moment_two + (1.0 - beta_mom) * clipped * clipped
    correction = 1.0 - jnp.power(jnp.float32(beta_mom), step_count[0].astype(jnp.float32))
    new_master = master - learn_rate * (
        new_one / correction / (jnp.sqrt(new_two / correction) + adam_eps) + decay_rate * master
    )
    return (new_one, new_two, new_master, new_master.astype(jnp.bfloat16), grad_norm, loss_sum)


def solution(mesh):
    in_specs = (
        P("dp", "seq", None),
        P("dp", None),
        P("dp", None),
        P("dp", "seq", None, None),
        P(("seq", "dp")),
        P(("seq", "dp")),
        P(("seq", "dp")),
        P(),
    )
    out_specs = (P(("seq", "dp")), P(("seq", "dp")), P(("seq", "dp")), P(("seq", "dp")), P(), P())
    return jax.shard_map(shards, mesh=mesh, in_specs=in_specs, out_specs=out_specs, check_vma=False)
```

```python
from functools import partial
import math

import jax
import jax.numpy as jnp
import ml_dtypes
import numpy as np
from jax import lax
from jax.experimental import pallas as pl
from jax.experimental.pallas import tpu as pltpu
from jax.sharding import PartitionSpec as P

D = 768
HEADS = 12
FF = 3072
DD = 512
DHEADS = 16
DFF = 2048
PIX = 768
PATCHES = 196
VIS = 49
IMG_SEQ = 10


norm_eps = 1e-06
neg_big = -1000000000.0
clip_limit = 0.0001
learn_rate = 0.03
decay_rate = 0.05
adam_eps = 1e-08
beta_mom = 0.5


def layout():
    return [
        ("embed", (PIX, D)),
        ("enc_qkv", (D, 3 * D)),
        ("enc_out", (D, D)),
        ("enc_up", (D, FF)),
        ("enc_down", (FF, D)),
        ("project", (D, DD)),
        ("dec_qkv", (DD, 3 * DD)),
        ("dec_out", (DD, DD)),
        ("dec_up", (DD, DFF)),
        ("dec_down", (DFF, DD)),
        ("pixel", (DD, PIX)),
        ("enc_vecs", (6, D)),
        ("dec_vecs", (7, DD)),
    ]


def unflatten(flat_vec):
    params = {}
    offset = 0
    for entry_name, entry_shape in layout():
        entry_size = entry_shape[0] * entry_shape[1]
        params[entry_name] = flat_vec[offset : offset + entry_size].reshape(entry_shape)
        offset += entry_size
    return params


LOW = jnp.bfloat16
FULL = jnp.float32
TILE = 256
TALL = 16
LANES = 128
NEG = neg_big
ROOT_HALF = math.sqrt(0.5)
LOG2_E = 1.0 / math.log(2.0)
BELL = 1.0 / math.sqrt(2.0 * math.pi)


def dot_nn(left, right):
    return lax.dot_general(left, right, (((1,), (0,)), ((), ())), preferred_element_type=FULL)


def dot_nt(left, right):
    return lax.dot_general(left, right, (((1,), (1,)), ((), ())), preferred_element_type=FULL)


def dot_tn(left, right):
    return lax.dot_general(left, right, (((0,), (0,)), ((), ())), preferred_element_type=FULL)


def loop(count, body):
    def one(step, carry):
        body(step)
        return carry

    lax.fori_loop(0, count, one, 0)


def unrolled(count, body):
    size = next(size for size in (4, 3, 2, 1) if count % size == 0)

    def one(step):
        for part in range(size):
            body(step * size + part)

    loop(count // size, one)


def span(step, size):
    if isinstance(step, int):
        return pl.ds(step * size, size)
    return pl.ds(pl.multiple_of(step * size, size), size)


def norm_parts(rows):
    average = jnp.mean(rows, axis=-1, keepdims=True)
    centered = rows - average
    scale = lax.rsqrt(jnp.mean(centered * centered, axis=-1, keepdims=True) + norm_eps)
    return centered * scale, scale


def norm_into(dst, src, gain, shift, rows, chunk):
    def one(step):
        at = span(step, chunk)
        unit, _ = norm_parts(src[at, :])
        dst[at, :] = (unit * gain + shift).astype(LOW)

    loop(rows // chunk, one)


def norm_back(dst, src, grad, residual, gain, gain_grad, shift_grad, rows, chunk):
    width = src.shape[1]

    def one(step, carry):
        at = span(step, chunk)
        unit, scale = norm_parts(src[at, :])
        upper = grad[at, :]
        gains = carry[0] + jnp.sum((upper * unit).reshape(chunk // 8, 8, width), axis=0)
        shifts = carry[1] + jnp.sum(upper.reshape(chunk // 8, 8, width), axis=0)
        upper = upper * gain
        lower = scale * (
            upper
            - jnp.mean(upper, axis=-1, keepdims=True)
            - unit * jnp.mean(upper * unit, axis=-1, keepdims=True)
        )
        if residual is not None:
            lower = lower + residual[at, :]
        dst[at, :] = lower
        return gains, shifts

    zero = jnp.zeros((8, width), FULL)
    gains, shifts = lax.fori_loop(0, rows // chunk, one, (zero, zero))
    gain_grad[...] = jnp.sum(gains, axis=0, keepdims=True)
    shift_grad[...] = jnp.sum(shifts, axis=0, keepdims=True)


class Blocked:
    def __init__(self, ref, rows, columns):
        self.rows, self.groups = rows, columns // LANES
        self.ref = ref.reshape(rows // TALL, self.groups, TALL, LANES)

    def piece(self, first_row, rows, first_group, groups):
        tall = pl.ds(first_row // TALL, rows // TALL)
        parts = [
            self.ref[tall, first_group + index].reshape(rows, LANES) for index in range(groups)
        ]
        return parts[0] if groups == 1 else jnp.concatenate(parts, axis=1)

    def column_tile(self, step, tile):
        count = tile // LANES
        return self.piece(0, self.rows, step * count, count)

    def row_tile(self, step, tile):
        return self.piece(step * tile, tile, 0, self.groups)


def product_into(dst, left, right, columns, tile=TILE, residual=None):
    def one(step):
        at = span(step, tile)
        value = dot_nn(left[...], right.column_tile(step, tile))
        if residual is not None:
            value = value + residual[:, at]
        dst[:, at] = value.astype(dst.dtype)

    unrolled(columns // tile, one)


def product_t_into(dst, left, right, columns, tile=TILE):
    def one(step):
        dst[:, span(step, tile)] = dot_nt(left[...], right.row_tile(step, tile)).astype(dst.dtype)

    unrolled(columns // tile, one)


def up_into(act, slope, left, w_up, columns, tile):
    def one(step):
        at = span(step, tile)
        hidden = dot_nn(left[...], w_up.column_tile(step, tile))
        share = 0.5 * (1.0 + lax.erf(hidden * ROOT_HALF))
        act[:, at] = (hidden * share).astype(LOW)
        slope[:, at] = share + hidden * (BELL * jnp.exp(-0.5 * hidden * hidden))

    unrolled(columns // tile, one)


def down_back_into(grad_pre, branch, w_down, slope, columns, tile):
    def one(step):
        at = span(step, tile)
        grad_pre[:, at] = (dot_nt(branch[...], w_down.row_tile(step, tile)) * slope[:, at]).astype(LOW)

    unrolled(columns // tile, one)


def weight_grad(out, out_tile, left, right, turned, stage, stage_sem, slot=0, before=None):
    rows, columns = left.shape[1], right.shape[1]
    groups = columns // LANES
    high = rows // TALL
    count = high * groups

    def turn(step):
        turned[span(step, TILE), :] = left[:, span(step, TILE)].T

    for index in range(rows // TILE):
        turn(index)
    if before is not None:
        before()
    tiles = stage.at[slot, pl.ds(0, count)].reshape(high, groups, TALL, LANES)
    piece = columns // TILE
    unroll = next(u for u in (6, 4, 3, 2, 1) if piece % u == 0)

    def across(step):
        for part in range(unroll):
            tile = step * unroll + part
            value = dot_nn(turned[pl.ds(0, rows), :], right[:, span(tile, TILE)]).astype(LOW)
            for half in range(2):
                tiles[:, tile * 2 + half] = value[:, half * LANES : (half + 1) * LANES].reshape(
                    high, TALL, LANES
                )

    loop(piece // unroll, across)
    copy = lambda: pltpu.make_async_copy(
        stage.at[slot, pl.ds(0, count)], out.at[pl.ds(out_tile, count)], stage_sem.at[slot]
    )
    copy().start()
    return lambda: copy().wait()


class Emitter:
    def __init__(self, out, turned, stage, stage_sem):
        self.args = turned, stage, stage_sem
        self.out, self.tiles, self.waits = out, entry_tiles(), []

    def __call__(self, entry, left, right):
        index = len(self.waits)
        before = self.waits[index - 2] if index >= 2 else None
        self.waits.append(
            weight_grad(self.out, self.tiles[entry][0], left, right, *self.args, index % 2, before)
        )

    def finish(self):
        for wait in self.waits[-2:]:
            wait()


def head_masks(head_size, dtype):
    lane = lax.broadcasted_iota(jnp.int32, (1, LANES), 1) // head_size
    return [(lane == head).astype(dtype) for head in range(LANES // head_size)]


def stacked(rows, masks):
    return jnp.concatenate([rows * mask for mask in masks], axis=0)


def unstacked(rows, masks, size):
    total = None
    for index, mask in enumerate(masks):
        piece = rows[index * size : (index + 1) * size] * mask
        total = piece if total is None else total + piece
    return total


def soft_rows(queries, keys, allowed, scale):
    scores = jnp.where(allowed, dot_nt(queries, keys), NEG)
    scores = scores - jnp.max(scores, axis=-1, keepdims=True)
    powers = jnp.exp2(scores * (scale * LOG2_E))
    return powers * (1.0 / jnp.sum(powers, axis=-1, keepdims=True))


def attend_into(dst, qkv, rows, at, width, allowed, head_size):
    masks = head_masks(head_size, LOW)
    size = rows.size
    column = lambda part: pl.ds(pl.multiple_of(part * width + at * LANES, LANES), LANES)
    queries = stacked(qkv[rows, column(0)], masks)
    probs = soft_rows(queries, qkv[rows, column(1)], allowed, head_size**-0.5).astype(LOW)
    values = dot_nn(probs, qkv[rows, column(2)])
    dst[rows, column(0)] = unstacked(values, head_masks(head_size, FULL), size).astype(LOW)


def only_real(scores, real, allowed):
    if real is None:
        return jnp.where(allowed, scores, NEG)
    whole = real // 8 * 8
    key = whole + lax.broadcasted_iota(jnp.int32, (1, scores.shape[1] - whole, 1), 1)
    return jnp.concatenate(
        [scores[:, :whole], jnp.where(key < real, scores[:, whole:], NEG)], axis=1
    )


def column_scores(keys, queries, heads, real, allowed):
    scores = dot_nt(keys, queries)
    return only_real(scores.reshape(heads, scores.shape[0] // heads, scores.shape[1]), real, allowed)


def attend_columns_into(dst, qkv, rows, at, width, real, head_size, logs):
    masks = head_masks(head_size, LOW)
    heads, size, scale = len(masks), rows.size, head_size**-0.5 * LOG2_E
    column = lambda part: pl.ds(pl.multiple_of(part * width + at * LANES, LANES), LANES)
    keys = stacked(qkv[rows, column(1)], masks)
    scores = column_scores(keys, qkv[rows, column(0)], heads, real, None)
    top = jnp.max(scores, axis=1, keepdims=True)
    powers = jnp.exp2((scores - top) * scale)
    total = jnp.sum(powers, axis=1, keepdims=True)
    logs[...] = top * scale + jnp.log2(total)
    probs = (powers * (1.0 / total)).reshape(heads * size, size).astype(LOW)
    dst[rows, column(0)] = dot_tn(stacked(qkv[rows, column(2)], masks), probs).T.astype(LOW)


def attend_back_into(dst, grad, qkv, rows, at, width, head_size, real=None, allowed=None, logs=None):
    masks = head_masks(head_size, LOW)
    lanes = head_masks(head_size, FULL)
    heads, size, scale = len(masks), rows.size, head_size**-0.5
    column = lambda part: pl.ds(pl.multiple_of(part * width + at * LANES, LANES), LANES)
    queries = qkv[rows, column(0)]
    keys = stacked(qkv[rows, column(1)], masks)
    grads = grad[rows, column(0)]
    scores = column_scores(keys, queries, heads, real, allowed)
    if logs is None:
        scores = scores - jnp.max(scores, axis=1, keepdims=True)
        powers = jnp.exp2(scores * (scale * LOG2_E))
        probs = powers * (1.0 / jnp.sum(powers, axis=1, keepdims=True))
    else:
        probs = jnp.exp2(scores * (scale * LOG2_E) - logs[...])
    slopes = dot_nt(stacked(qkv[rows, column(2)], masks), grads).reshape(probs.shape)
    slopes = probs * (slopes - jnp.sum(slopes * probs, axis=1, keepdims=True))
    flat = (heads * size, size)
    slopes, probs = slopes.reshape(flat).astype(LOW), probs.reshape(flat).astype(LOW)
    dst[rows, column(0)] = (dot_tn(keys, slopes).T * scale).astype(LOW)
    dst[rows, column(1)] = (unstacked(dot_nn(slopes, queries), lanes, size) * scale).astype(LOW)
    dst[rows, column(2)] = unstacked(dot_nn(probs, grads), lanes, size).astype(LOW)


def entry_tiles():
    tiles, offset = {}, 0
    for entry_name, (rows, columns) in layout():
        tiles[entry_name] = (offset // (TALL * LANES), rows, columns)
        offset += rows * columns
    tiles["vecs"] = (tiles["enc_vecs"][0], 4 * TALL, LANES)
    return tiles


def vec_reader(buffer, first, groups):
    rows = buffer[...].reshape(4 * TALL, LANES).astype(FULL)

    def vec(index):
        start = first + index * groups
        return jnp.concatenate([rows[start + g : start + g + 1] for g in range(groups)], axis=1)

    return vec


def fetch(flat, names, buffers, sems):
    tiles = entry_tiles()

    def build(index):
        start, rows, columns = tiles[names[index]]
        count = rows * columns // (TALL * LANES)
        return pltpu.make_async_copy(flat.at[pl.ds(start, count)], buffers[index], sems.at[index])

    for index in range(len(names)):
        build(index).start()

    def ready(index):
        build(index).wait()
        _, rows, columns = tiles[names[index]]
        return Blocked(buffers[index], rows, columns)

    return ready


def tile_buffers(names):
    tiles = entry_tiles()
    return [
        pltpu.VMEM((tiles[entry][1] * tiles[entry][2] // (TALL * LANES), TALL, LANES), LOW)
        for entry in names
    ]


def position_table(columns, padded):
    half = columns // 2
    frequency = np.exp(
        np.float32(-math.log(10000.0)) * np.arange(half, dtype=np.float32) / np.float32(half)
    ).astype(np.float32)
    angles = np.arange(PATCHES, dtype=np.float32)[:, None] * frequency
    table = np.zeros((padded, columns), np.float32)
    table[:PATCHES] = np.concatenate(
        [np.sin(angles.astype(np.float64)), np.cos(angles.astype(np.float64))], axis=-1
    )
    return table


def split_low(table):
    parts, rest = [], table.astype(np.float64)
    for _ in range(3):
        part = rest.astype(ml_dtypes.bfloat16)
        parts.append(part)
        rest = rest - part.astype(np.float64)
    return np.stack(parts)


MESH = pl.DeviceIdType.MESH
A_HALF = 1104
A_ROWS = 2 * A_HALF
B_HALF = 320
B_ROWS = 2 * B_HALF
SHARD_ROWS = 2834
PAD_ROWS = A_ROWS + B_ROWS
B_TRUE = SHARD_ROWS - A_ROWS
HALO = 384
HALO_STEP = 64
WIDE_ROWS = SHARD_ROWS + 2 * HALO
PARTS = {
    "a1": (0, A_HALF),
    "a2": (A_HALF, A_HALF),
    "b": (A_ROWS, B_ROWS),
    "b1": (A_ROWS, B_HALF),
    "b2": (A_ROWS + B_HALF, B_HALF),
}
TRUE_PARTS = {**PARTS, "b": (A_ROWS, B_TRUE), "b2": (A_ROWS + B_HALF, B_TRUE - B_HALF)}
SLOTS = {"a1": 0, "a2": 1, "b": 2, "b1": 2, "b2": 3}
COLUMNS = "oxyd"
ARRIVALS = {
    0: (
        12, 22, 102, 10, 20, 100, 11, 21, 101, 33, 34, 112, 122, 30, 110, 202, 120, 31, 200, 121,
        111, 201, 132, 130, 210, 212, 220, 131, 222, 302, 221, 211, 300, 230, 231, 301, 320, 310,
        232, 312, 321, 311, 322, 332, 330, 331,
    ),
    1: (
        2, 112, 122, 202, 0, 110, 120, 200, 1, 111, 121, 201, 133, 134, 12, 212, 22, 222, 20, 10,
        32, 302, 130, 210, 300, 220, 11, 301, 232, 21, 131, 312, 221, 211, 322, 332, 30, 310,
        230, 311, 320, 31, 321, 231, 330, 331,
    ),
}


def item_of(code):
    return code // 100, COLUMNS[code // 10 % 10], list(PARTS)[code % 10]


def own_item(inner, part):
    return 100 * inner + list(PARTS).index(part)


class Place:
    def __init__(self):
        self.core = lax.axis_index("seq")
        self.chip = lax.axis_index("dp")
        chip = self.chip
        self.z = chip // 4
        y, x = (chip // 2) % 2, chip % 2
        self.col = chip % 4
        self.col_x = self.col + 1 - 2 * x
        self.col_y = self.col + 2 - 4 * y
        self.col_d = self.col_x + 2 - 4 * y
        self.columns = {"o": self.col, "x": self.col_x, "y": self.col_y, "d": self.col_d}
        self.side = self.z // 2
        sign = 1 - 2 * self.side
        self.inner = self.z + self.side * (3 - 2 * self.z)
        self.me = 16 * self.core + chip
        self.devices = {
            "x": (self.core, 4 * self.z + self.col_x),
            "y": (self.core, 4 * self.z + self.col_y),
            "far": (self.core, chip + 4 * sign),
            "near": (self.core, chip - 4 * sign * self.inner),
            "core": (1 - self.core, chip),
            "next": self.ring(1),
            "back": self.ring(31),
        }

    def ring(self, step):
        peer = (self.me + step) % 32
        return (peer // 16, peer % 16)

    def plane(self, mirrored):
        return mirrored + self.side * (3 - 2 * mirrored)

    def greet(self):
        barrier = pltpu.get_barrier_semaphore()
        for link in ("x", "y", "far", "core", "next", "back"):
            pl.semaphore_signal(
                barrier, inc=1, device_id=self.devices[link], device_id_type=MESH
            )

        @pl.when(self.inner == 1)
        def _():
            pl.semaphore_signal(
                barrier, inc=1, device_id=self.devices["near"], device_id_type=MESH
            )

        pl.semaphore_wait(barrier, 6 + self.inner)


class Outbox:
    def __init__(self):
        self.sent = []

    def send(self, src, dst, send_sem, recv_sem, device):
        def build():
            return pltpu.make_async_remote_copy(
                src_ref=src,
                dst_ref=dst,
                send_sem=send_sem,
                recv_sem=recv_sem,
                device_id=device,
                device_id_type=MESH,
            )

        build().start()
        self.sent.append(build)

    def finish(self):
        for build in self.sent:
            build().wait_send()


def arrived(ref, sem, device):
    pltpu.make_async_remote_copy(
        src_ref=ref, dst_ref=ref, send_sem=sem, recv_sem=sem, device_id=device, device_id_type=MESH
    ).wait_recv()


def by_place(at, body):
    for inner in (0, 1):
        pl.when(at.inner == inner)(partial(body, inner))


def onward(inner, item):
    mirrored, column, part = item_of(item)
    line = ["far", "near"][: 1 + inner]
    if mirrored != inner:
        line = [] if inner == 0 else ["far" if mirrored == 0 else "near"]
    if part[0] == "a":
        if column == "o":
            return [(link, part) for link in [*line, "x", "y"]]
        if (column, part) in (("x", "a1"), ("y", "a2")):
            return [("y" if column == "x" else "x", part)]
        return []
    links = [(link, "b") for link in line]
    if mirrored == inner:
        links = {
            "o": [("x", "b"), ("y", "b")],
            "x": [("y", "b1")],
            "y": [("x", "b2")],
            "d": [],
        }[column] + links
    return links


def gather_exchange(at, flat, source, recv, core_recv, sends, core_send):
    def block(chip, part, core):
        first, size = TRUE_PARTS[part]
        return flat.at[pl.ds((core * 16 + chip) * SHARD_ROWS + first, size)]

    def body(inner):
        out = Outbox()
        diagonal = []

        def pass_on(item):
            mirrored, column, part = item_of(item)
            chip = 4 * at.plane(mirrored) + at.columns[column]
            own = mirrored == inner and column == "o"
            links = onward(inner, item)
            if mirrored == inner and column == "d" and part[0] == "b":
                diagonal.append(part)
                links = links if len(diagonal) == 2 else []
            for link, piece in [*links, ("core", part)]:
                slot = SLOTS[piece]
                ref = block(chip, piece, at.core)
                sent, got = (core_send, core_recv) if link == "core" else (sends[link], recv)
                out.send(
                    source(piece) if own else ref,
                    ref,
                    sent.at[chip, slot],
                    got.at[chip, slot],
                    at.devices[link],
                )

        for part in ("b", "a1", "a2"):
            pass_on(own_item(inner, part))
        for item in ARRIVALS[inner]:
            mirrored, column, part = item_of(item)
            chip = 4 * at.plane(mirrored) + at.columns[column]
            arrived(block(chip, part, at.core), recv.at[chip, SLOTS[part]], at.devices["x"])
            pass_on(item)
        for part in ("b", "a1", "a2"):
            arrived(
                block(at.chip, part, 1 - at.core),
                core_recv.at[at.chip, SLOTS[part]],
                at.devices["x"],
            )
        for item in ARRIVALS[inner]:
            mirrored, column, part = item_of(item)
            chip = 4 * at.plane(mirrored) + at.columns[column]
            ref = block(chip, part, 1 - at.core)
            arrived(ref, core_recv.at[chip, SLOTS[part]], at.devices["x"])
        out.finish()

    by_place(at, body)


def entry_blocks(me, body, edges=False):
    first, stop = me * SHARD_ROWS, me * SHARD_ROWS + SHARD_ROWS
    offset = 0
    for _, (rows, columns) in layout()[:11]:
        groups, blocks = columns // LANES, rows // TALL
        unit = TALL * groups
        total = unit * blocks
        if edges:
            for cut in (first, stop):
                inside = jnp.maximum(cut - offset, 0)
                block = inside // unit

                @pl.when((inside < total) & (inside % unit > 0))
                def _(block=block, offset=offset, unit=unit, groups=groups):
                    body(offset + block * unit, groups)
        else:
            low = jnp.minimum((jnp.maximum(first - offset, 0) + unit - 1) // unit, blocks)
            high = jnp.minimum(jnp.maximum(stop - offset, 0) // unit, blocks)

            def one(block, carry, offset=offset, unit=unit, groups=groups):
                body(offset + block * unit, groups)
                return carry

            lax.fori_loop(low, jnp.maximum(high, low), one, 0)
        offset += total
    return offset


def cut_rows(cut):
    before = after = 0
    offset = 0
    for _, (rows, columns) in layout()[:11]:
        unit, total = TALL * (columns // LANES), rows * (columns // LANES)
        inside = jnp.maximum(cut - offset, 0)
        cuts = ((inside < total) & (inside % unit > 0)).astype(jnp.int32)
        before = before + cuts * (inside % unit)
        after = after + cuts * (unit - inside % unit)
        offset += total
    return before, after


class Halo:
    def __init__(self, at, here, start, wide, send_sem, recv_sem):
        self.at, self.here, self.start, self.wide = at, here, start, wide
        self.sems = send_sem, recv_sem
        first = at.me * SHARD_ROWS
        head, give_back = cut_rows(first)
        give_next, tail = cut_rows(first + SHARD_ROWS)
        self.given, self.taken = (give_back, give_next), (tail, head)

    def copies(self, side, index):
        low, high = HALO_STEP * index, HALO_STEP * (index + 1)
        src = self.start + (low if side == 0 else SHARD_ROWS - high)
        dst = HALO + SHARD_ROWS + low if side == 0 else HALO - high
        return pltpu.make_async_remote_copy(
            src_ref=self.here.at[pl.ds(src, HALO_STEP)],
            dst_ref=self.wide.at[pl.ds(dst, HALO_STEP)],
            send_sem=self.sems[0].at[side, index],
            recv_sem=self.sems[1].at[side, index],
            device_id=self.at.devices["back" if side == 0 else "next"],
            device_id_type=MESH,
        )

    def each(self, rows, action):
        for side in range(2):
            for index in range(HALO // HALO_STEP):
                pl.when(rows[side] > HALO_STEP * index)(partial(action, side, index))

    def start_all(self):
        self.each(self.given, lambda side, index: self.copies(side, index).start())

    def take(self):
        self.each(self.taken, lambda side, index: self.copies(side, index).wait_recv())

    def finish(self):
        self.each(self.given, lambda side, index: self.copies(side, index).wait_send())


VEC_ROWS = 64


def gather_kernel(
    master_ref, visible_ref, flat_ref, both_ref, wide, turned, own_sem, halo_send, halo_recv, *sems
):
    recv, core_recv, send_x, send_y, send_far, send_near, core_send = sems
    at = Place()
    first = at.me * SHARD_ROWS
    skew = (at.me * 2) % TALL
    own = pltpu.make_async_copy(master_ref, wide.at[pl.ds(HALO, SHARD_ROWS)], own_sem.at[0])
    own.start()
    at.greet()
    out = Outbox()
    halo = Halo(at, master_ref, 0, wide, halo_send, halo_recv)
    halo.start_all()
    half = visible_ref.shape[0]
    rows_here = both_ref.at[pl.ds(pl.multiple_of(at.core * half, half), half)]
    rows_there = both_ref.at[pl.ds(pl.multiple_of((1 - at.core) * half, half), half)]
    out.send(visible_ref, rows_here, own_sem.at[3], own_sem.at[4], at.devices["core"])
    keep = pltpu.make_async_copy(visible_ref, rows_here, own_sem.at[2])
    keep.start()
    own.wait()

    def turn(row, groups):
        start = row - first + HALO
        spot = row - (first - skew) + HALO
        for group in range(groups):
            turned[pl.ds(pl.multiple_of(spot + group * TALL, TALL), TALL), :] = wide[
                pl.ds(start + group, TALL, stride=groups), :
            ].astype(LOW)

    vec_start = entry_blocks(at.me, turn)
    halo.take()
    entry_blocks(at.me, turn, edges=True)

    @pl.when(at.me == 31)
    def _():
        start = vec_start - 31 * SHARD_ROWS + HALO
        spot = start + (31 * 2) % TALL
        turned[pl.ds(spot, VEC_ROWS), :] = wide[pl.ds(start, VEC_ROWS), :].astype(LOW)

    mine = pltpu.make_async_copy(
        turned.at[pl.ds(HALO + skew, SHARD_ROWS)],
        flat_ref.at[pl.ds(first, SHARD_ROWS)],
        own_sem.at[1],
    )
    mine.start()

    def source(part):
        start, size = TRUE_PARTS[part]
        return turned.at[pl.ds(HALO + skew + start, size)]

    sends = {"x": send_x, "y": send_y, "far": send_far, "near": send_near}
    gather_exchange(at, flat_ref, source, recv, core_recv, sends, core_send)
    mine.wait()
    keep.wait()
    arrived(rows_there, own_sem.at[4], at.devices["x"])
    out.finish()
    halo.finish()


def gather_weights(master_rows, visible_rows):
    hbm = pl.BlockSpec(memory_space=pltpu.HBM)
    steps = pltpu.SemaphoreType.DMA((2, HALO // HALO_STEP))
    half, width = visible_rows.shape
    return pl.pallas_call(
        gather_kernel,
        out_shape=[
            jax.ShapeDtypeStruct((32 * SHARD_ROWS, LANES), LOW),
            jax.ShapeDtypeStruct((2 * half, width), LOW),
        ],
        in_specs=[hbm, hbm],
        out_specs=[hbm, hbm],
        scratch_shapes=[
            pltpu.VMEM((WIDE_ROWS + 6, LANES), FULL),
            pltpu.VMEM((WIDE_ROWS + 30, LANES), LOW),
            pltpu.SemaphoreType.DMA((5,)),
            steps,
            steps,
        ]
        + [pltpu.SemaphoreType.DMA((16, 4))] * 7,
        compiler_params=pltpu.CompilerParams(
            collective_id=0, has_side_effects=True, vmem_limit_bytes=60 * 1024 * 1024
        ),
        name="gather_weights",
    )(master_rows, visible_rows)


def add_into(dst, start, terms, size, chunk):
    def one(step):
        row = step * chunk
        total = None
        for ref, first in terms:
            piece = ref[pl.ds(pl.multiple_of(first + row, TALL), chunk), :].astype(FULL)
            total = piece if total is None else total + piece
        dst[pl.ds(pl.multiple_of(start + row, TALL), chunk), :] = total.astype(dst.dtype)

    loop(size // chunk, one)


def reduce_kernel(
    grad_ref,
    loss_ref,
    shard_ref,
    square_ref,
    loss_total_ref,
    own,
    theirs,
    from_x,
    from_y,
    pass_x,
    pass_y,
    far_a,
    near_a,
    far_b,
    near_b,
    wide,
    plain,
    scalars,
    load_sem,
    core_send,
    core_recv,
    send_x,
    send_y,
    send_far,
    send_near,
    recv_x,
    recv_y,
    recv_far,
    recv_near,
    halo_send,
    halo_recv,
    tiny_send,
    tiny_recv,
):
    at = Place()
    tail = pl.ds(SHARD_ROWS - 2, TALL)
    for index in range(16):
        own[index, tail, :] = jnp.zeros((TALL, LANES), LOW)
        theirs[index, tail, :] = jnp.zeros((TALL, LANES), LOW)
    body = pl.ds(0, SHARD_ROWS)

    def shard_rows(core, chip):
        return grad_ref.at[pl.ds((core * 16 + chip) * SHARD_ROWS, SHARD_ROWS)]

    def load(chip):
        return pltpu.make_async_copy(
            shard_rows(at.core, chip), own.at[chip, body], load_sem.at[chip]
        )

    at.greet()
    pairs = Outbox()
    for mirrored in (3, 2, 1 - at.inner, at.inner):
        for column in ("d", "y", "x", "o"):
            chip = 4 * at.plane(mirrored) + at.columns[column]
            pairs.send(
                shard_rows(1 - at.core, chip),
                theirs.at[chip, body],
                core_send.at[chip],
                core_recv.at[chip],
                at.devices["core"],
            )
            load(chip).start()
    sends = {"x": send_x, "y": send_y, "far": send_far, "near": send_near}
    recvs = {"x": recv_x, "y": recv_y, "far": recv_far, "near": recv_near}
    relayed = {"x": pass_x, "y": pass_y}
    direct = {"x": from_x, "y": from_y}
    lines = {"far": (far_a, far_b), "near": (near_a, near_b)}

    def reduce_parts(inner):
        out = Outbox()
        paired, joined = set(), set()

        def pair(chip, column, part):
            if (column, "all") not in paired:
                paired.add((column, "all"))
                load(chip).wait()
                arrived(theirs.at[chip, body], core_recv.at[chip], at.devices["x"])
            name = "b" if part[0] == "b" else part
            if (column, name) not in paired:
                paired.add((column, name))
                first, size = PARTS[name]
                add_into(
                    own.at[chip],
                    first,
                    [(own.at[chip], first), (theirs.at[chip], first)],
                    size,
                    size // (4 if name == "b" else 3),
                )

        def landing(link, plane, chip, part, relay):
            first, size = PARTS[part]
            if link in lines and part == "b":
                return lines[link][1].at[chip], 0, size, (chip, SLOTS[part])
            if link in lines:
                return lines[link][0].at[plane], first, size, (chip, SLOTS[part])
            if relay:
                return relayed[link].at[plane], first, size, (plane, 3 + (part[0] == "b"))
            return direct[link].at[plane], first, size, (plane, SLOTS[part])

        def step(item):
            mirrored, column, part = item_of(item)
            plane = at.plane(mirrored)
            chip = 4 * plane + at.columns[column]
            pair(chip, (mirrored, column), part)
            first, size = PARTS[part]
            terms = []
            links = onward(inner, item)
            if mirrored == inner and column == "d" and part[0] == "b":
                links = [] if joined else links
                joined.add(part)
            own_item = mirrored == inner and column == "o"
            for link, piece in links:
                relay = column in ("x", "y")
                buffer, start, count, index = landing(link, plane, chip, piece, relay)
                arrived(buffer.at[pl.ds(start, count)], recvs[link].at[*index], at.devices["x"])
                terms.append((buffer, start, count))
            if own_item:
                whole = [(own.at[chip], first)] + [(buffer, start) for buffer, start, _ in terms]
                if part == "b":
                    add_into(plain, 0, whole, size, size // 4)
                    wide[pl.ds(HALO + A_ROWS, B_TRUE), :] = plain[pl.ds(0, B_TRUE), :]
                else:
                    add_into(wide, HALO + first, whole, size, size // 3)
                return
            full_size = B_ROWS if part[0] == "b" else size
            full_first = PARTS["b"][0] if part[0] == "b" else first
            whole = [(buffer, start) for buffer, start, count in terms if count == full_size]
            halves = [(buffer, start, count) for buffer, start, count in terms if count != full_size]
            if whole:
                add_into(
                    own.at[chip],
                    full_first,
                    [(own.at[chip], full_first), *whole],
                    full_size,
                    full_size // (4 if part[0] == "b" else 3),
                )
            for buffer, start, count in halves:
                add_into(
                    own.at[chip], start, [(own.at[chip], start), (buffer, start)], count, count // 2
                )
            if column == "o" or (part == "b" and mirrored != inner):
                link = "near" if inner == 1 and mirrored == 0 else "far"
                target = "near" if inner == 0 else "far"
                buffer, start, _, index = landing(target, plane, chip, part, False)
                arrive_sem = recvs[target]
            else:
                link = {"x": "x", "y": "y", "d": "y" if part in ("a1", "b1") else "x"}[column]
                buffer, start, _, index = landing(link, plane, chip, part, column == "d")
                arrive_sem = recvs[link]
            out.send(
                own.at[chip, pl.ds(first, size)],
                buffer.at[pl.ds(start, size)],
                sends[link].at[*index],
                arrive_sem.at[*index],
                at.devices[link],
            )

        for item in reversed(ARRIVALS[inner]):
            step(item)
        for part in ("a2", "a1", "b"):
            step(own_item(inner, part))
        out.finish()

    by_place(at, reduce_parts)
    pairs.finish()

    tiny = Outbox()
    halo = Halo(at, wide, HALO, wide, halo_send, halo_recv)
    halo.start_all()
    step_rows = 352
    whole_steps = SHARD_ROWS // step_rows

    def squares(index, carry):
        piece = wide[pl.ds(pl.multiple_of(HALO + index * step_rows, 8), step_rows), :]
        piece = piece * piece
        return carry + jnp.sum(piece.reshape(step_rows // 8, 8, LANES), axis=0)

    square = lax.fori_loop(0, whole_steps, squares, jnp.zeros((8, LANES), FULL))
    rest = wide[pl.ds(HALO + whole_steps * step_rows, SHARD_ROWS - whole_steps * step_rows), :]
    square = square + 0.125 * jnp.sum(rest * rest, axis=0, keepdims=True)
    scalars[at.me, 0] = square
    scalars[at.me, 1] = jnp.broadcast_to(loss_ref[...], (8, LANES))
    for index in range(1, 32):
        tiny.send(
            scalars.at[at.me],
            scalars.at[at.me],
            tiny_send.at[index],
            tiny_recv.at[at.me],
            at.ring(index),
        )
    def turn_back(row, groups):
        start = row - at.me * SHARD_ROWS + HALO
        for group in range(groups):
            plain[pl.ds(start + group, TALL, stride=groups), :] = wide[
                pl.ds(start + group * TALL, TALL), :
            ]

    vec_start = entry_blocks(at.me, turn_back)
    halo.take()
    entry_blocks(at.me, turn_back, edges=True)

    @pl.when(at.me == 31)
    def _():
        spot = pl.ds(vec_start - 31 * SHARD_ROWS + HALO, VEC_ROWS)
        plain[spot, :] = wide[spot, :]

    shard_ref[...] = plain[pl.ds(HALO, SHARD_ROWS), :]
    for index in range(1, 32):
        peer = (at.me + index) % 32
        arrived(scalars.at[peer], tiny_recv.at[peer], at.devices["x"])
    totals = jnp.sum(scalars[...], axis=0)
    square_ref[...] = jnp.sum(
        jnp.sum(totals[0], axis=0, keepdims=True), axis=1, keepdims=True
    )
    loss_total_ref[...] = totals[1, 0:1, 0:1]
    halo.finish()
    tiny.finish()


def reduce_gradients(grad_rows, loss_row):
    hbm = pl.BlockSpec(memory_space=pltpu.HBM)
    vmem = pl.BlockSpec(memory_space=pltpu.VMEM)
    dma = pltpu.SemaphoreType.DMA
    shard_total, square, loss = pl.pallas_call(
        reduce_kernel,
        out_shape=[
            jax.ShapeDtypeStruct((SHARD_ROWS, LANES), FULL),
            jax.ShapeDtypeStruct((1, 1), FULL),
            jax.ShapeDtypeStruct((1, 1), FULL),
        ],
        in_specs=[hbm, vmem],
        out_specs=[vmem, vmem, vmem],
        scratch_shapes=[pltpu.VMEM((16, PAD_ROWS, LANES), LOW)] * 2
        + [pltpu.VMEM((4, PAD_ROWS, LANES), LOW)] * 4
        + [pltpu.VMEM((4, A_ROWS, LANES), LOW)] * 2
        + [pltpu.VMEM((16, B_ROWS, LANES), LOW)] * 2
        + [pltpu.VMEM((WIDE_ROWS + 6, LANES), FULL)] * 2
        + [pltpu.VMEM((32, 2, 8, LANES), FULL)]
        + [dma((16,))] * 3
        + [dma((4, 5))] * 2
        + [dma((16, 4))] * 2
        + [dma((4, 5))] * 2
        + [dma((16, 4))] * 2
        + [dma((2, HALO // HALO_STEP))] * 2
        + [dma((32,))] * 2,
        compiler_params=pltpu.CompilerParams(
            collective_id=1, has_side_effects=True, vmem_limit_bytes=60 * 1024 * 1024
        ),
        name="reduce_gradients",
    )(grad_rows, loss_row)
    return shard_total.reshape(-1), square.reshape(()), loss.reshape(())


ROWS = 256
ENC_CHUNK = 256
FETCHED = ("vecs", "embed", "enc_qkv", "enc_out", "enc_up", "enc_down", "project")
BACKWARD_FETCHED = ("vecs", "project", "enc_down", "enc_up", "enc_out", "enc_qkv")


def encoder_forward_kernel(
    part_ref,
    visible_ref,
    segments_ref,
    patches_ref,
    table_ref,
    flat_ref,
    *refs,
):
    results, kept, (out_sem, sems, *buffers) = refs[:14], refs[14:28], refs[28:]
    (
        vis_rows,
        embedded,
        normed_a,
        qkv_rows,
        attn_out,
        after_attn,
        normed_b,
        slope,
        hidden_act,
        encoded,
        final_enc,
        projected,
        row_facts,
        column_facts,
    ) = kept

    def shipment(index):
        return pltpu.make_async_copy(kept[index], results[index], out_sem.at[index])

    def ship(*indices):
        for index in indices:
            shipment(index).start()

    ready = fetch(flat_ref, FETCHED, buffers, sems)
    part = part_ref[0]
    total = segments_ref.shape[1]
    images = IMG_SEQ // 2
    spare = ROWS - images * VIS
    segments = segments_ref[...]
    image = segments - part * images
    inside = (image >= 0) & (image < images)
    padding = segments == IMG_SEQ
    flags = jnp.concatenate(
        [
            inside.astype(FULL),
            padding.astype(FULL),
            jnp.zeros((6, total), FULL),
        ],
        axis=0,
    ).astype(LOW)
    row = lax.broadcasted_iota(jnp.int32, (total, total), 0)
    column = lax.broadcasted_iota(jnp.int32, (total, total), 1)
    counts = dot_nn(flags, (row <= column).astype(FULL).astype(LOW)).astype(jnp.int32)
    inside_count, padding_count = counts[0:1], counts[1:2]
    padding_slot = padding_count - part * spare
    chosen = inside | (padding & (padding_slot >= 1) & (padding_slot <= spare))
    slot = inside_count + jnp.clip(padding_slot, 0, spare) - 1
    slot = jnp.where(chosen, slot, -1)
    select = (lax.broadcasted_iota(jnp.int32, (ROWS, total), 0) == slot).astype(FULL).astype(LOW)
    facts = jnp.concatenate(
        [segments.astype(FULL), patches_ref[...].astype(FULL), jnp.zeros((LANES - 2, total), FULL)],
        axis=0,
    ).astype(LOW)
    row_facts[...] = dot_nt(facts[0:16], select)
    column_facts[...] = dot_nt(select, facts)
    vis_rows[...] = dot_nn(select, visible_ref[...]).astype(LOW)
    ship(0, 12, 13)
    patch = column_facts[:, 1:2].astype(jnp.int32)
    spot = (lax.broadcasted_iota(jnp.int32, (ROWS, table_ref.shape[1]), 1) == patch).astype(FULL).astype(LOW)
    embedded[...] = dot_nn(spot, table_ref[0]) + dot_nn(spot, table_ref[1]) + dot_nn(spot, table_ref[2])
    w_embed = ready(1)
    product_into(embedded, vis_rows, w_embed, D, residual=embedded)
    ship(1)
    ready(0)
    vec = vec_reader(buffers[0], 0, D // LANES)
    norm_into(normed_a, embedded, vec(0), vec(1), ROWS, ENC_CHUNK)
    ship(2)
    w_qkv = ready(2)
    product_into(qkv_rows, normed_a, w_qkv, 3 * D)
    ship(3)
    allowed = column_facts[:, 0:1] == row_facts[0:1, :]
    allowed = jnp.concatenate([allowed.astype(FULL)] * 2, axis=0) > 0.5

    def attend(step):
        for part in range(2):
            attend_into(
                attn_out, qkv_rows, pl.ds(0, ROWS), 2 * step + part, D, allowed, D // HEADS
            )

    for index in range(D // LANES // 2):
        attend(index)
    ship(4)
    w_out = ready(3)
    product_into(after_attn, attn_out, w_out, D, residual=embedded)
    ship(5)
    norm_into(normed_b, after_attn, vec(2), vec(3), ROWS, ENC_CHUNK)
    ship(6)
    w_up = ready(4)
    up_into(hidden_act, slope, normed_b, w_up, FF, 512)
    ship(7, 8)
    w_down = ready(5)
    product_into(encoded, hidden_act, w_down, D, residual=after_attn)
    ship(9)
    norm_into(final_enc, encoded, vec(4), vec(5), ROWS, ENC_CHUNK)
    ship(10)
    w_proj = ready(6)
    product_into(projected, final_enc, w_proj, DD)
    ship(11)
    for index in range(len(kept)):
        shipment(index).wait()


def encoder_forward(part, visible_rows, segments, patch_ids, flat_weights):
    hbm = pl.BlockSpec(memory_space=pltpu.HBM)
    vmem = pl.BlockSpec(memory_space=pltpu.VMEM)
    smem = pl.BlockSpec(memory_space=pltpu.SMEM)
    table = jnp.asarray(split_low(position_table(D, 256)))
    kept = [
        ((ROWS, PIX), LOW),
        ((ROWS, D), FULL),
        ((ROWS, D), LOW),
        ((ROWS, 3 * D), LOW),
        ((ROWS, D), LOW),
        ((ROWS, D), FULL),
        ((ROWS, D), LOW),
        ((ROWS, FF), FULL),
        ((ROWS, FF), LOW),
        ((ROWS, D), FULL),
        ((ROWS, D), LOW),
        ((ROWS, DD), LOW),
        ((16, ROWS), FULL),
        ((ROWS, LANES), FULL),
    ]
    return pl.pallas_call(
        encoder_forward_kernel,
        out_shape=[jax.ShapeDtypeStruct(s, d) for s, d in kept],
        in_specs=[smem] + [vmem] * 4 + [hbm],
        out_specs=[hbm] * 14,
        scratch_shapes=[pltpu.VMEM(s, d) for s, d in kept]
        + [pltpu.SemaphoreType.DMA((14,)), pltpu.SemaphoreType.DMA((7,))] + tile_buffers(FETCHED),
        compiler_params=pltpu.CompilerParams(vmem_limit_bytes=60 * 1024 * 1024),
        name="encoder_forward",
    )(part, visible_rows, segments, patch_ids, table, flat_weights)


def encoder_backward_kernel(
    grad_projected,
    decoder_vecs,
    *refs,
):
    stored, refs = refs[:13], refs[13:]
    weights_ref, partial_ref, flat_ref, refs = *refs[:3], refs[3:]
    kept, refs = refs[:13], refs[13:]
    (
        grad_rows,
        upper,
        branch,
        grad_pre,
        middle,
        grad_attn,
        grad_qkv,
        vec_grads,
        turned,
        stage,
        vec_full,
        vec_stage,
        stage_sem,
        kept_sem,
        sems,
        *buffers,
    ) = refs
    (
        vis_rows,
        embedded,
        normed_a,
        qkv_rows,
        attn_out,
        after_attn,
        normed_b,
        slope,
        hidden_act,
        encoded,
        final_enc,
        row_facts,
        column_facts,
    ) = kept

    def delivery(index):
        return pltpu.make_async_copy(stored[index], kept[index], kept_sem.at[index])

    def need(*indices):
        for index in indices:
            delivery(index).wait()

    for index in (10, 9, 8):
        delivery(index).start()
    del partial_ref
    ready = fetch(weights_ref, BACKWARD_FETCHED, buffers, sems)
    for index in (7, 6, 5, 4, 12, 11, 3, 2, 1, 0):
        delivery(index).start()
    tiles = entry_tiles()
    ready(0)
    vec = vec_reader(buffers[0], 0, D // LANES)
    grad_of = lambda index: vec_grads.at[pl.ds(index, 1), :]

    emit = Emitter(flat_ref, turned, stage, stage_sem)

    need(10)
    emit("project", final_enc, grad_projected)
    w_proj = ready(1)
    product_t_into(upper, grad_projected, w_proj, D)
    need(9)
    norm_back(grad_rows, encoded, upper, None, vec(4), grad_of(4), grad_of(5), ROWS, ENC_CHUNK)
    branch[...] = grad_rows[...].astype(LOW)
    need(8)
    emit("enc_down", hidden_act, branch)
    need(7)
    w_down = ready(2)
    down_back_into(grad_pre, branch, w_down, slope, FF, 512)
    need(6)
    emit("enc_up", normed_b, grad_pre)
    w_up = ready(3)
    product_t_into(upper, grad_pre, w_up, D)
    need(5)
    norm_back(grad_rows, after_attn, upper, grad_rows, vec(2), grad_of(2), grad_of(3), ROWS, ENC_CHUNK)
    middle[...] = grad_rows[...].astype(LOW)
    need(4)
    emit("enc_out", attn_out, middle)
    w_out = ready(4)
    product_t_into(grad_attn, middle, w_out, D)
    need(12, 11, 3)
    allowed = column_facts[:, 0:1] == row_facts[0:1, :]

    def attend_back(step):
        for part in range(2):
            attend_back_into(
                grad_qkv,
                grad_attn,
                qkv_rows,
                pl.ds(0, ROWS),
                2 * step + part,
                D,
                D // HEADS,
                allowed=allowed,
            )

    for index in range(D // LANES // 2):
        attend_back(index)
    need(2)
    emit("enc_qkv", normed_a, grad_qkv)
    w_qkv = ready(5)
    product_t_into(upper, grad_qkv, w_qkv, D)
    need(1)
    norm_back(grad_rows, embedded, upper, grad_rows, vec(0), grad_of(0), grad_of(1), ROWS, ENC_CHUNK)
    branch[...] = grad_rows[...].astype(LOW)
    need(0)
    emit("embed", vis_rows, branch)
    emit.finish()
    groups = D // LANES
    for index in range(6):
        for group in range(groups):
            vec_full[pl.ds(index * groups + group, 1), :] = vec_grads[
                pl.ds(index, 1), pl.ds(group * LANES, LANES)
            ]
    base, groups = 6 * groups, DD // LANES
    for index in range(7):
        for group in range(groups):
            vec_full[pl.ds(base + index * groups + group, 1), :] = decoder_vecs[
                pl.ds(index, 1), pl.ds(group * LANES, LANES)
            ]
    vec_stage[...] = vec_full[...].astype(LOW).reshape(4, TALL, LANES)
    copy = pltpu.make_async_copy(vec_stage, flat_ref.at[pl.ds(tiles["enc_vecs"][0], 4)], stage_sem.at[0])
    copy.start()
    copy.wait()


def encoder_backward(saved, grad_projected, flat_weights, decoder_vec_grads, flat):
    hbm = pl.BlockSpec(memory_space=pltpu.HBM)
    vmem = pl.BlockSpec(memory_space=pltpu.VMEM)
    inputs = [grad_projected, decoder_vec_grads, *saved, flat_weights, flat]
    low, full = (lambda *s: pltpu.VMEM(s, LOW)), (lambda *s: pltpu.VMEM(s, FULL))
    return pl.pallas_call(
        encoder_backward_kernel,
        out_shape=jax.ShapeDtypeStruct(flat.shape, LOW),
        in_specs=[vmem] * 2 + [hbm] * 15,
        out_specs=hbm,
        input_output_aliases={len(inputs) - 1: 0},
        scratch_shapes=[pltpu.VMEM(array.shape, array.dtype) for array in saved]
        + [
            full(ROWS, D),
            full(ROWS, D),
            low(ROWS, D),
            low(ROWS, FF),
            low(ROWS, D),
            low(ROWS, D),
            low(ROWS, 3 * D),
            full(8, D),
            low(FF, ROWS),
            low(2, FF * D // (TALL * LANES), TALL, LANES),
            full(64, LANES),
            low(4, TALL, LANES),
            pltpu.SemaphoreType.DMA((2,)),
            pltpu.SemaphoreType.DMA((13,)),
            pltpu.SemaphoreType.DMA((6,)),
        ]
        + tile_buffers(BACKWARD_FETCHED),
        compiler_params=pltpu.CompilerParams(vmem_limit_bytes=60 * 1024 * 1024),
        name="encoder_backward",
    )(*inputs)


IMAGES = 5
DECODER_FETCHED = ("vecs", "dec_qkv", "dec_out", "dec_up", "dec_down", "pixel")
IMG_ROWS = 200
DEC_ROWS = IMAGES * IMG_ROWS


def decoder_kernel(
    part_ref,
    projected,
    row_facts,
    targets_ref,
    table_ref,
    weights_ref,
    flat_ref,
    grad_projected,
    vec_grads,
    loss_ref,
    dec_in,
    low_rows,
    qkv_rows,
    attn_out,
    after_attn,
    normed_b,
    slope,
    hidden_act,
    decoded,
    final_dec,
    grad_pred,
    upper,
    masked,
    score_logs,
    turned,
    stage,
    stage_sem,
    sems,
    *buffers,
    mask_total,
):
    ready = fetch(weights_ref, DECODER_FETCHED, buffers, sems)
    tiles = entry_tiles()
    ready(0)
    vec = vec_reader(buffers[0], 6 * D // LANES, DD // LANES)
    grad_of = lambda index: vec_grads.at[pl.ds(index, 1), :]
    part = part_ref[0]
    image_of = row_facts[0:1, :].astype(jnp.int32) - part * IMAGES
    patch_of = row_facts[1:2, :].astype(jnp.int32)
    patch = lax.broadcasted_iota(jnp.int32, (IMG_ROWS, ROWS), 0)

    def selector(index):
        return ((patch_of == patch) & (image_of == index)).astype(FULL)

    def place(index):
        at = span(index, IMG_ROWS)
        select = selector(index)
        real = (patch[:, 0:1] < PATCHES).astype(FULL)
        hidden = real * (1.0 - jnp.sum(select, axis=-1, keepdims=True))
        masked[at, :] = jnp.broadcast_to(hidden, (IMG_ROWS, LANES))
        dec_in[at, :] = dot_nn(select.astype(LOW), projected[...]) + hidden * vec(6) + table_ref[...]

    for index in range(IMAGES):
        place(index)
    norm_into(low_rows, dec_in, vec(0), vec(1), DEC_ROWS, DEC_ROWS)
    w_qkv = ready(1)
    product_into(qkv_rows, low_rows, w_qkv, 3 * DD)
    head_size = DD // DHEADS
    heads = LANES // head_size
    groups = DD // LANES

    def attend(step):
        rows = span(step, IMG_ROWS)
        for at in range(groups):
            logs = score_logs.at[pl.ds((step * groups + at) * heads, heads)]
            attend_columns_into(attn_out, qkv_rows, rows, at, DD, PATCHES, head_size, logs)

    for index in range(IMAGES):
        attend(index)
    w_out = ready(2)
    product_into(after_attn, attn_out, w_out, DD, residual=dec_in)
    norm_into(normed_b, after_attn, vec(2), vec(3), DEC_ROWS, DEC_ROWS)
    w_up = ready(3)
    up_into(hidden_act, slope, normed_b, w_up, DFF, TILE)
    w_down = ready(4)
    product_into(decoded, hidden_act, w_down, DD, residual=after_attn)
    norm_into(final_dec, decoded, vec(4), vec(5), DEC_ROWS, DEC_ROWS)
    w_pix = ready(5)
    loss_ref[...] = jnp.zeros_like(loss_ref)

    def compare(index):
        at = span(index, IMG_ROWS)
        image = pl.ds(0, PATCHES)
        goal, _ = norm_parts(targets_ref[index].astype(FULL))
        goal = jnp.concatenate([goal, jnp.zeros((IMG_ROWS - PATCHES, PIX), FULL)], axis=0)
        error = dot_nn(final_dec[at, :], w_pix.column_tile(0, PIX)) - goal
        weight = masked[at, 0:1]
        rows = jnp.mean(error * error, axis=-1, keepdims=True) * weight
        loss_ref[...] = loss_ref[...] + jnp.sum(rows) * (1.0 / mask_total)
        grad_pred[at, :] = (weight * error * (2.0 / (PIX * mask_total))).astype(LOW)

    for index in range(IMAGES):
        compare(index)

    emit = Emitter(flat_ref, turned, stage, stage_sem)

    emit("pixel", final_dec, grad_pred)
    product_t_into(upper, grad_pred, w_pix, DD)
    grad_rows, branch = decoded, final_dec
    norm_back(grad_rows, decoded, upper, None, vec(4), grad_of(4), grad_of(5), DEC_ROWS, DEC_ROWS)
    branch[...] = grad_rows[...].astype(LOW)
    emit("dec_down", hidden_act, branch)
    grad_pre = hidden_act
    down_back_into(grad_pre, branch, w_down, slope, DFF, TILE)
    emit("dec_up", normed_b, grad_pre)
    product_t_into(upper, grad_pre, w_up, DD)
    norm_back(grad_rows, after_attn, upper, grad_rows, vec(2), grad_of(2), grad_of(3), DEC_ROWS, DEC_ROWS)
    branch[...] = grad_rows[...].astype(LOW)
    emit("dec_out", attn_out, branch)
    grad_attn, grad_qkv = normed_b, grad_pre.at[:, pl.ds(0, 3 * DD)]
    product_t_into(grad_attn, branch, w_out, DD)

    def attend_back(step):
        rows = span(step, IMG_ROWS)
        for at in range(groups):
            logs = score_logs.at[pl.ds((step * groups + at) * heads, heads)]
            attend_back_into(
                grad_qkv, grad_attn, qkv_rows, rows, at, DD, head_size, real=PATCHES, logs=logs
            )

    for index in range(IMAGES):
        attend_back(index)
    emit("dec_qkv", low_rows, grad_qkv)
    emit.finish()
    product_t_into(upper, grad_qkv, w_qkv, DD)
    norm_back(grad_rows, dec_in, upper, grad_rows, vec(0), grad_of(0), grad_of(1), DEC_ROWS, DEC_ROWS)
    upper[pl.ds(0, ROWS), :] = jnp.zeros((ROWS, DD), FULL)

    def collect(index, token):
        at = span(index, IMG_ROWS)
        rows = grad_rows[at, :]
        token = token + jnp.sum((rows * masked[at, 0:1]).reshape(IMG_ROWS // 8, 8, DD), axis=0)
        upper[pl.ds(0, ROWS), :] = upper[pl.ds(0, ROWS), :] + dot_tn(
            selector(index).astype(LOW), rows.astype(LOW)
        )
        return token

    token = jnp.zeros((8, DD), FULL)
    for index in range(IMAGES):
        token = collect(index, token)
    grad_of(6)[...] = jnp.sum(token, axis=0, keepdims=True)
    grad_projected[...] = upper[pl.ds(0, ROWS), :].astype(LOW)


def decoder_step(part, projected, row_facts, targets, flat_weights, mask_total):
    hbm = pl.BlockSpec(memory_space=pltpu.HBM)
    vmem = pl.BlockSpec(memory_space=pltpu.VMEM)
    smem = pl.BlockSpec(memory_space=pltpu.SMEM)
    table = jnp.asarray(position_table(DD, IMG_ROWS))
    low, full = (lambda *s: pltpu.VMEM(s, LOW)), (lambda *s: pltpu.VMEM(s, FULL))
    return pl.pallas_call(
        partial(decoder_kernel, mask_total=mask_total),
        out_shape=[
            jax.ShapeDtypeStruct(flat_weights.shape, LOW),
            jax.ShapeDtypeStruct((ROWS, DD), LOW),
            jax.ShapeDtypeStruct((8, DD), FULL),
            jax.ShapeDtypeStruct((1, LANES), FULL),
        ],
        in_specs=[smem] + [vmem] * 4 + [hbm],
        out_specs=[hbm] + [vmem] * 3,
        scratch_shapes=[
            full(DEC_ROWS, DD),
            low(DEC_ROWS, DD),
            low(DEC_ROWS, 3 * DD),
            low(DEC_ROWS, DD),
            full(DEC_ROWS, DD),
            low(DEC_ROWS, DD),
            full(DEC_ROWS, DFF),
            low(DEC_ROWS, DFF),
            full(DEC_ROWS, DD),
            low(DEC_ROWS, DD),
            low(DEC_ROWS, PIX),
            full(DEC_ROWS, DD),
            full(DEC_ROWS, LANES),
            full(IMAGES * DHEADS, 1, IMG_ROWS),
            low(DFF, DEC_ROWS),
            low(2, DFF * DD // (TALL * LANES), TALL, LANES),
            pltpu.SemaphoreType.DMA((2,)),
            pltpu.SemaphoreType.DMA((6,)),
        ]
        + tile_buffers(DECODER_FETCHED),
        compiler_params=pltpu.CompilerParams(vmem_limit_bytes=62 * 1024 * 1024),
        name="decoder_step",
    )(part, projected, row_facts, targets, table, flat_weights)


def to_tiles(full_flat):
    pieces, offset = [], 0
    for _, (rows, columns) in layout()[:11]:
        piece = full_flat[offset : offset + rows * columns]
        piece = piece.reshape(rows // TALL, TALL, columns // LANES, LANES)
        pieces.append(piece.transpose(0, 2, 1, 3).reshape(-1, LANES))
        offset += rows * columns
    return jnp.concatenate([*pieces, full_flat[offset:].reshape(-1, LANES)])


def from_tiles(rows_flat):
    pieces, offset = [], 0
    for _, (rows, columns) in layout()[:11]:
        count = rows * columns // LANES
        piece = rows_flat[offset : offset + count]
        piece = piece.reshape(rows // TALL, columns // LANES, TALL, LANES)
        pieces.append(piece.transpose(0, 2, 1, 3).reshape(-1))
        offset += count
    return jnp.concatenate([*pieces, rows_flat[offset:].reshape(-1)])


def shards(visible, segments, patch_ids, targets, master, moment_one, moment_two, step_count):
    part = lax.axis_index("seq")
    in_kernels = master.shape[0] == SHARD_ROWS * LANES and lax.axis_size("dp") == 16
    if in_kernels:
        flat_weights, visible_rows = gather_weights(
            master.reshape(SHARD_ROWS, LANES), visible[0]
        )
    else:
        full_flat = lax.all_gather(master.astype(LOW), ("seq", "dp"), axis=0, tiled=True)
        flat_weights = to_tiles(full_flat)
        visible_rows = lax.all_gather(visible[0], "seq", axis=0, tiled=True)
    flat_weights = flat_weights.reshape(-1, TALL, LANES)
    part_row = part.reshape(1).astype(jnp.int32)
    mask_total = (PATCHES - VIS) * IMG_SEQ * visible.shape[0] * lax.axis_size("dp")
    *saved, projected, row_facts, column_facts = encoder_forward(
        part_row, visible_rows, segments, patch_ids, flat_weights
    )
    flat_grads, grad_projected, decoder_vec_grads, loss_row = decoder_step(
        part_row, projected, row_facts, targets[0], flat_weights, mask_total
    )
    flat_grads = encoder_backward(
        [*saved, row_facts, column_facts],
        grad_projected,
        flat_weights,
        decoder_vec_grads,
        flat_grads,
    )
    flat_grads = flat_grads.reshape(-1, LANES)
    if in_kernels:
        grad_shard, square_sum, loss_sum = reduce_gradients(flat_grads, loss_row)
    else:
        grad_flat = from_tiles(flat_grads.astype(FULL))
        grad_shard = lax.psum_scatter(grad_flat, ("seq", "dp"), scatter_dimension=0, tiled=True)
        square_sum, loss_sum = lax.psum(
            (jnp.sum(grad_shard * grad_shard), loss_row[0, 0]), ("seq", "dp")
        )
    grad_norm = jnp.sqrt(square_sum)
    clipped = grad_shard * jnp.minimum(1.0, clip_limit / (grad_norm + 1e-06))
    new_one = beta_mom * moment_one + (1.0 - beta_mom) * clipped
    new_two = beta_mom * moment_two + (1.0 - beta_mom) * clipped * clipped
    correction = 1.0 - jnp.power(jnp.float32(beta_mom), step_count[0].astype(jnp.float32))
    new_master = master - learn_rate * (
        new_one / correction / (jnp.sqrt(new_two / correction) + adam_eps) + decay_rate * master
    )
    return (new_one, new_two, new_master, new_master.astype(jnp.bfloat16), grad_norm, loss_sum)


def solution(mesh):
    in_specs = (
        P("dp", "seq", None),
        P("dp", None),
        P("dp", None),
        P("dp", "seq", None, None),
        P(("seq", "dp")),
        P(("seq", "dp")),
        P(("seq", "dp")),
        P(),
    )
    out_specs = (P(("seq", "dp")), P(("seq", "dp")), P(("seq", "dp")), P(("seq", "dp")), P(), P())
    return jax.shard_map(shards, mesh=mesh, in_specs=in_specs, out_specs=out_specs, check_vma=False)
```

```python
from functools import partial
import math

import jax
import jax.numpy as jnp
import ml_dtypes
import numpy as np
from jax import lax
from jax.experimental import pallas as pl
from jax.experimental.pallas import tpu as pltpu
from jax.sharding import PartitionSpec as P

D = 768
HEADS = 12
FF = 3072
DD = 512
DHEADS = 16
DFF = 2048
PIX = 768
PATCHES = 196
VIS = 49
IMG_SEQ = 10


norm_eps = 1e-06
neg_big = -1000000000.0
clip_limit = 0.0001
learn_rate = 0.03
decay_rate = 0.05
adam_eps = 1e-08
beta_mom = 0.5


def layout():
    return [
        ("embed", (PIX, D)),
        ("enc_qkv", (D, 3 * D)),
        ("enc_out", (D, D)),
        ("enc_up", (D, FF)),
        ("enc_down", (FF, D)),
        ("project", (D, DD)),
        ("dec_qkv", (DD, 3 * DD)),
        ("dec_out", (DD, DD)),
        ("dec_up", (DD, DFF)),
        ("dec_down", (DFF, DD)),
        ("pixel", (DD, PIX)),
        ("enc_vecs", (6, D)),
        ("dec_vecs", (7, DD)),
    ]


def unflatten(flat_vec):
    params = {}
    offset = 0
    for entry_name, entry_shape in layout():
        entry_size = entry_shape[0] * entry_shape[1]
        params[entry_name] = flat_vec[offset : offset + entry_size].reshape(entry_shape)
        offset += entry_size
    return params


LOW = jnp.bfloat16
FULL = jnp.float32
TILE = 256
TALL = 16
LANES = 128
NEG = neg_big
ROOT_HALF = math.sqrt(0.5)
LOG2_E = 1.0 / math.log(2.0)
BELL = 1.0 / math.sqrt(2.0 * math.pi)


def dot_nn(left, right):
    return lax.dot_general(left, right, (((1,), (0,)), ((), ())), preferred_element_type=FULL)


def dot_nt(left, right):
    return lax.dot_general(left, right, (((1,), (1,)), ((), ())), preferred_element_type=FULL)


def dot_tn(left, right):
    return lax.dot_general(left, right, (((0,), (0,)), ((), ())), preferred_element_type=FULL)


def loop(count, body):
    def one(step, carry):
        body(step)
        return carry

    lax.fori_loop(0, count, one, 0)


def unrolled(count, body):
    size = next(size for size in (4, 3, 2, 1) if count % size == 0)

    def one(step):
        for part in range(size):
            body(step * size + part)

    loop(count // size, one)


def span(step, size):
    if isinstance(step, int):
        return pl.ds(step * size, size)
    return pl.ds(pl.multiple_of(step * size, size), size)


def norm_parts(rows):
    average = jnp.mean(rows, axis=-1, keepdims=True)
    centered = rows - average
    scale = lax.rsqrt(jnp.mean(centered * centered, axis=-1, keepdims=True) + norm_eps)
    return centered * scale, scale


def norm_into(dst, src, gain, shift, rows, chunk):
    def one(step):
        at = span(step, chunk)
        unit, _ = norm_parts(src[at, :])
        dst[at, :] = (unit * gain + shift).astype(LOW)

    loop(rows // chunk, one)


def norm_back(dst, src, grad, residual, gain, gain_grad, shift_grad, rows, chunk):
    width = src.shape[1]

    def one(step, carry):
        at = span(step, chunk)
        unit, scale = norm_parts(src[at, :])
        upper = grad[at, :]
        gains = carry[0] + jnp.sum((upper * unit).reshape(chunk // 8, 8, width), axis=0)
        shifts = carry[1] + jnp.sum(upper.reshape(chunk // 8, 8, width), axis=0)
        upper = upper * gain
        lower = scale * (
            upper
            - jnp.mean(upper, axis=-1, keepdims=True)
            - unit * jnp.mean(upper * unit, axis=-1, keepdims=True)
        )
        if residual is not None:
            lower = lower + residual[at, :]
        dst[at, :] = lower
        return gains, shifts

    zero = jnp.zeros((8, width), FULL)
    gains, shifts = lax.fori_loop(0, rows // chunk, one, (zero, zero))
    gain_grad[...] = jnp.sum(gains, axis=0, keepdims=True)
    shift_grad[...] = jnp.sum(shifts, axis=0, keepdims=True)


class Blocked:
    def __init__(self, ref, rows, columns):
        self.rows, self.groups = rows, columns // LANES
        self.ref = ref.reshape(rows // TALL, self.groups, TALL, LANES)

    def piece(self, first_row, rows, first_group, groups):
        tall = pl.ds(first_row // TALL, rows // TALL)
        parts = [
            self.ref[tall, first_group + index].reshape(rows, LANES) for index in range(groups)
        ]
        return parts[0] if groups == 1 else jnp.concatenate(parts, axis=1)

    def column_tile(self, step, tile):
        count = tile // LANES
        return self.piece(0, self.rows, step * count, count)

    def row_tile(self, step, tile):
        return self.piece(step * tile, tile, 0, self.groups)


def product_into(dst, left, right, columns, tile=TILE, residual=None):
    def one(step):
        at = span(step, tile)
        value = dot_nn(left[...], right.column_tile(step, tile))
        if residual is not None:
            value = value + residual[:, at]
        dst[:, at] = value.astype(dst.dtype)

    unrolled(columns // tile, one)


def product_t_into(dst, left, right, columns, tile=TILE):
    def one(step):
        dst[:, span(step, tile)] = dot_nt(left[...], right.row_tile(step, tile)).astype(dst.dtype)

    unrolled(columns // tile, one)


def up_into(act, slope, left, w_up, columns, tile):
    def one(step):
        at = span(step, tile)
        hidden = dot_nn(left[...], w_up.column_tile(step, tile))
        share = 0.5 * (1.0 + lax.erf(hidden * ROOT_HALF))
        act[:, at] = (hidden * share).astype(LOW)
        slope[:, at] = share + hidden * (BELL * jnp.exp(-0.5 * hidden * hidden))

    unrolled(columns // tile, one)


def down_back_into(grad_pre, branch, w_down, slope, columns, tile):
    def one(step):
        at = span(step, tile)
        grad_pre[:, at] = (dot_nt(branch[...], w_down.row_tile(step, tile)) * slope[:, at]).astype(LOW)

    unrolled(columns // tile, one)


def weight_grad(out, out_tile, left, right, turned, stage, stage_sem, slot=0, before=None):
    rows, columns = left.shape[1], right.shape[1]
    groups = columns // LANES
    high = rows // TALL
    count = high * groups

    def turn(step):
        turned[span(step, TILE), :] = left[:, span(step, TILE)].T

    for index in range(rows // TILE):
        turn(index)
    if before is not None:
        before()
    tiles = stage.at[slot, pl.ds(0, count)].reshape(high, groups, TALL, LANES)
    piece = columns // TILE
    unroll = next(u for u in (6, 4, 3, 2, 1) if piece % u == 0)

    def across(step):
        for part in range(unroll):
            tile = step * unroll + part
            value = dot_nn(turned[pl.ds(0, rows), :], right[:, span(tile, TILE)]).astype(LOW)
            for half in range(2):
                tiles[:, tile * 2 + half] = value[:, half * LANES : (half + 1) * LANES].reshape(
                    high, TALL, LANES
                )

    loop(piece // unroll, across)
    copy = lambda: pltpu.make_async_copy(
        stage.at[slot, pl.ds(0, count)], out.at[pl.ds(out_tile, count)], stage_sem.at[slot]
    )
    copy().start()
    return lambda: copy().wait()


class Emitter:
    def __init__(self, out, turned, stage, stage_sem):
        self.args = turned, stage, stage_sem
        self.out, self.tiles, self.waits = out, entry_tiles(), []

    def __call__(self, entry, left, right):
        index = len(self.waits)
        before = self.waits[index - 2] if index >= 2 else None
        self.waits.append(
            weight_grad(self.out, self.tiles[entry][0], left, right, *self.args, index % 2, before)
        )

    def finish(self):
        for wait in self.waits[-2:]:
            wait()


def head_masks(head_size, dtype):
    lane = lax.broadcasted_iota(jnp.int32, (1, LANES), 1) // head_size
    return [(lane == head).astype(dtype) for head in range(LANES // head_size)]


def stacked(rows, masks):
    return jnp.concatenate([rows * mask for mask in masks], axis=0)


def unstacked(rows, masks, size):
    total = None
    for index, mask in enumerate(masks):
        piece = rows[index * size : (index + 1) * size] * mask
        total = piece if total is None else total + piece
    return total


def soft_rows(queries, keys, allowed, scale):
    scores = jnp.where(allowed, dot_nt(queries, keys), NEG)
    scores = scores - jnp.max(scores, axis=-1, keepdims=True)
    powers = jnp.exp2(scores * (scale * LOG2_E))
    return powers * (1.0 / jnp.sum(powers, axis=-1, keepdims=True))


def attend_into(dst, qkv, rows, at, width, allowed, head_size):
    masks = head_masks(head_size, LOW)
    size = rows.size
    column = lambda part: pl.ds(pl.multiple_of(part * width + at * LANES, LANES), LANES)
    queries = stacked(qkv[rows, column(0)], masks)
    probs = soft_rows(queries, qkv[rows, column(1)], allowed, head_size**-0.5).astype(LOW)
    values = dot_nn(probs, qkv[rows, column(2)])
    dst[rows, column(0)] = unstacked(values, head_masks(head_size, FULL), size).astype(LOW)


def only_real(scores, real, allowed):
    if real is None:
        return jnp.where(allowed, scores, NEG)
    whole = real // 8 * 8
    key = whole + lax.broadcasted_iota(jnp.int32, (1, scores.shape[1] - whole, 1), 1)
    return jnp.concatenate(
        [scores[:, :whole], jnp.where(key < real, scores[:, whole:], NEG)], axis=1
    )


def column_scores(keys, queries, heads, real, allowed):
    scores = dot_nt(keys, queries)
    return only_real(scores.reshape(heads, scores.shape[0] // heads, scores.shape[1]), real, allowed)


def attend_columns_into(dst, qkv, rows, at, width, real, head_size, logs):
    masks = head_masks(head_size, LOW)
    heads, size, scale = len(masks), rows.size, head_size**-0.5 * LOG2_E
    column = lambda part: pl.ds(pl.multiple_of(part * width + at * LANES, LANES), LANES)
    keys = stacked(qkv[rows, column(1)], masks)
    scores = column_scores(keys, qkv[rows, column(0)], heads, real, None)
    top = jnp.max(scores, axis=1, keepdims=True)
    powers = jnp.exp2((scores - top) * scale)
    total = jnp.sum(powers, axis=1, keepdims=True)
    logs[...] = top * scale + jnp.log2(total)
    probs = (powers * (1.0 / total)).reshape(heads * size, size).astype(LOW)
    dst[rows, column(0)] = dot_tn(stacked(qkv[rows, column(2)], masks), probs).T.astype(LOW)


def attend_back_into(dst, grad, qkv, rows, at, width, head_size, real=None, allowed=None, logs=None):
    masks = head_masks(head_size, LOW)
    lanes = head_masks(head_size, FULL)
    heads, size, scale = len(masks), rows.size, head_size**-0.5
    column = lambda part: pl.ds(pl.multiple_of(part * width + at * LANES, LANES), LANES)
    queries = qkv[rows, column(0)]
    keys = stacked(qkv[rows, column(1)], masks)
    grads = grad[rows, column(0)]
    scores = column_scores(keys, queries, heads, real, allowed)
    if logs is None:
        scores = scores - jnp.max(scores, axis=1, keepdims=True)
        powers = jnp.exp2(scores * (scale * LOG2_E))
        probs = powers * (1.0 / jnp.sum(powers, axis=1, keepdims=True))
    else:
        probs = jnp.exp2(scores * (scale * LOG2_E) - logs[...])
    slopes = dot_nt(stacked(qkv[rows, column(2)], masks), grads).reshape(probs.shape)
    slopes = probs * (slopes - jnp.sum(slopes * probs, axis=1, keepdims=True))
    flat = (heads * size, size)
    slopes, probs = slopes.reshape(flat).astype(LOW), probs.reshape(flat).astype(LOW)
    dst[rows, column(0)] = (dot_tn(keys, slopes).T * scale).astype(LOW)
    dst[rows, column(1)] = (unstacked(dot_nn(slopes, queries), lanes, size) * scale).astype(LOW)
    dst[rows, column(2)] = unstacked(dot_nn(probs, grads), lanes, size).astype(LOW)


def entry_tiles():
    tiles, offset = {}, 0
    for entry_name, (rows, columns) in layout():
        tiles[entry_name] = (offset // (TALL * LANES), rows, columns)
        offset += rows * columns
    tiles["vecs"] = (tiles["enc_vecs"][0], 4 * TALL, LANES)
    return tiles


def vec_reader(buffer, first, groups):
    rows = buffer[...].reshape(4 * TALL, LANES).astype(FULL)

    def vec(index):
        start = first + index * groups
        return jnp.concatenate([rows[start + g : start + g + 1] for g in range(groups)], axis=1)

    return vec


def fetch(flat, names, buffers, sems):
    tiles = entry_tiles()

    def build(index):
        start, rows, columns = tiles[names[index]]
        count = rows * columns // (TALL * LANES)
        return pltpu.make_async_copy(flat.at[pl.ds(start, count)], buffers[index], sems.at[index])

    for index in range(len(names)):
        build(index).start()

    def ready(index):
        build(index).wait()
        _, rows, columns = tiles[names[index]]
        return Blocked(buffers[index], rows, columns)

    return ready


def tile_buffers(names):
    tiles = entry_tiles()
    return [
        pltpu.VMEM((tiles[entry][1] * tiles[entry][2] // (TALL * LANES), TALL, LANES), LOW)
        for entry in names
    ]


def position_table(columns, padded):
    half = columns // 2
    frequency = np.exp(
        np.float32(-math.log(10000.0)) * np.arange(half, dtype=np.float32) / np.float32(half)
    ).astype(np.float32)
    angles = np.arange(PATCHES, dtype=np.float32)[:, None] * frequency
    table = np.zeros((padded, columns), np.float32)
    table[:PATCHES] = np.concatenate(
        [np.sin(angles.astype(np.float64)), np.cos(angles.astype(np.float64))], axis=-1
    )
    return table


def split_low(table):
    parts, rest = [], table.astype(np.float64)
    for _ in range(3):
        part = rest.astype(ml_dtypes.bfloat16)
        parts.append(part)
        rest = rest - part.astype(np.float64)
    return np.stack(parts)


MESH = pl.DeviceIdType.MESH
A_HALF = 1104
A_ROWS = 2 * A_HALF
B_HALF = 320
B_ROWS = 2 * B_HALF
SHARD_ROWS = 2834
PAD_ROWS = A_ROWS + B_ROWS
B_TRUE = SHARD_ROWS - A_ROWS
HALO = 384
HALO_STEP = 64
WIDE_ROWS = SHARD_ROWS + 2 * HALO
PARTS = {
    "a1": (0, A_HALF),
    "a2": (A_HALF, A_HALF),
    "b": (A_ROWS, B_ROWS),
    "b1": (A_ROWS, B_HALF),
    "b2": (A_ROWS + B_HALF, B_HALF),
}
TRUE_PARTS = {**PARTS, "b": (A_ROWS, B_TRUE), "b2": (A_ROWS + B_HALF, B_TRUE - B_HALF)}
SLOTS = {"a1": 0, "a2": 1, "b": 2, "b1": 2, "b2": 3}
COLUMNS = "oxyd"
ARRIVALS = {
    0: (
        12, 22, 102, 10, 20, 100, 11, 21, 101, 33, 34, 112, 122, 30, 110, 202, 120, 31, 200, 121,
        111, 201, 132, 130, 210, 212, 220, 131, 222, 302, 221, 211, 300, 230, 231, 301, 320, 310,
        232, 312, 321, 311, 322, 332, 330, 331,
    ),
    1: (
        2, 112, 122, 202, 0, 110, 120, 200, 1, 111, 121, 201, 133, 134, 12, 212, 22, 222, 20, 10,
        32, 302, 130, 210, 300, 220, 11, 301, 232, 21, 131, 312, 221, 211, 322, 332, 30, 310,
        230, 311, 320, 31, 321, 231, 330, 331,
    ),
}


def item_of(code):
    return code // 100, COLUMNS[code // 10 % 10], list(PARTS)[code % 10]


def own_item(inner, part):
    return 100 * inner + list(PARTS).index(part)


class Place:
    def __init__(self):
        self.core = lax.axis_index("seq")
        self.chip = lax.axis_index("dp")
        chip = self.chip
        self.z = chip // 4
        y, x = (chip // 2) % 2, chip % 2
        self.col = chip % 4
        self.col_x = self.col + 1 - 2 * x
        self.col_y = self.col + 2 - 4 * y
        self.col_d = self.col_x + 2 - 4 * y
        self.columns = {"o": self.col, "x": self.col_x, "y": self.col_y, "d": self.col_d}
        self.side = self.z // 2
        sign = 1 - 2 * self.side
        self.inner = self.z + self.side * (3 - 2 * self.z)
        self.me = 16 * self.core + chip
        self.devices = {
            "x": (self.core, 4 * self.z + self.col_x),
            "y": (self.core, 4 * self.z + self.col_y),
            "far": (self.core, chip + 4 * sign),
            "near": (self.core, chip - 4 * sign * self.inner),
            "core": (1 - self.core, chip),
            "next": self.ring(1),
            "back": self.ring(31),
        }

    def ring(self, step):
        peer = (self.me + step) % 32
        return (peer // 16, peer % 16)

    def plane(self, mirrored):
        return mirrored + self.side * (3 - 2 * mirrored)

    def greet(self):
        barrier = pltpu.get_barrier_semaphore()
        for link in ("x", "y", "far", "core", "next", "back"):
            pl.semaphore_signal(
                barrier, inc=1, device_id=self.devices[link], device_id_type=MESH
            )

        @pl.when(self.inner == 1)
        def _():
            pl.semaphore_signal(
                barrier, inc=1, device_id=self.devices["near"], device_id_type=MESH
            )

        pl.semaphore_wait(barrier, 6 + self.inner)


class Outbox:
    def __init__(self):
        self.sent = []

    def send(self, src, dst, send_sem, recv_sem, device):
        def build():
            return pltpu.make_async_remote_copy(
                src_ref=src,
                dst_ref=dst,
                send_sem=send_sem,
                recv_sem=recv_sem,
                device_id=device,
                device_id_type=MESH,
            )

        build().start()
        self.sent.append(build)

    def finish(self):
        for build in self.sent:
            build().wait_send()


def arrived(ref, sem, device):
    pltpu.make_async_remote_copy(
        src_ref=ref, dst_ref=ref, send_sem=sem, recv_sem=sem, device_id=device, device_id_type=MESH
    ).wait_recv()


def by_place(at, body):
    for inner in (0, 1):
        pl.when(at.inner == inner)(partial(body, inner))


def onward(inner, item):
    mirrored, column, part = item_of(item)
    line = ["far", "near"][: 1 + inner]
    if mirrored != inner:
        line = [] if inner == 0 else ["far" if mirrored == 0 else "near"]
    if part[0] == "a":
        if column == "o":
            return [(link, part) for link in [*line, "x", "y"]]
        if (column, part) in (("x", "a1"), ("y", "a2")):
            return [("y" if column == "x" else "x", part)]
        return []
    links = [(link, "b") for link in line]
    if mirrored == inner:
        links = {
            "o": [("x", "b"), ("y", "b")],
            "x": [("y", "b1")],
            "y": [("x", "b2")],
            "d": [],
        }[column] + links
    return links


def gather_exchange(at, flat, source, recv, core_recv, sends, core_send):
    def block(chip, part, core):
        first, size = TRUE_PARTS[part]
        return flat.at[pl.ds((core * 16 + chip) * SHARD_ROWS + first, size)]

    def body(inner):
        out = Outbox()
        diagonal = []

        def pass_on(item):
            mirrored, column, part = item_of(item)
            chip = 4 * at.plane(mirrored) + at.columns[column]
            own = mirrored == inner and column == "o"
            links = onward(inner, item)
            if mirrored == inner and column == "d" and part[0] == "b":
                diagonal.append(part)
                links = links if len(diagonal) == 2 else []
            for link, piece in [*links, ("core", part)]:
                slot = SLOTS[piece]
                ref = block(chip, piece, at.core)
                sent, got = (core_send, core_recv) if link == "core" else (sends[link], recv)
                out.send(
                    source(piece) if own else ref,
                    ref,
                    sent.at[chip, slot],
                    got.at[chip, slot],
                    at.devices[link],
                )

        for part in ("b", "a1", "a2"):
            pass_on(own_item(inner, part))
        for item in ARRIVALS[inner]:
            mirrored, column, part = item_of(item)
            chip = 4 * at.plane(mirrored) + at.columns[column]
            arrived(block(chip, part, at.core), recv.at[chip, SLOTS[part]], at.devices["x"])
            pass_on(item)
        for part in ("b", "a1", "a2"):
            arrived(
                block(at.chip, part, 1 - at.core),
                core_recv.at[at.chip, SLOTS[part]],
                at.devices["x"],
            )
        for item in ARRIVALS[inner]:
            mirrored, column, part = item_of(item)
            chip = 4 * at.plane(mirrored) + at.columns[column]
            ref = block(chip, part, 1 - at.core)
            arrived(ref, core_recv.at[chip, SLOTS[part]], at.devices["x"])
        out.finish()

    by_place(at, body)


def entry_blocks(me, body, edges=False):
    first, stop = me * SHARD_ROWS, me * SHARD_ROWS + SHARD_ROWS
    offset = 0
    for _, (rows, columns) in layout()[:11]:
        groups, blocks = columns // LANES, rows // TALL
        unit = TALL * groups
        total = unit * blocks
        if edges:
            for cut in (first, stop):
                inside = jnp.maximum(cut - offset, 0)
                block = inside // unit

                @pl.when((inside < total) & (inside % unit > 0))
                def _(block=block, offset=offset, unit=unit, groups=groups):
                    body(offset + block * unit, groups)
        else:
            low = jnp.minimum((jnp.maximum(first - offset, 0) + unit - 1) // unit, blocks)
            high = jnp.minimum(jnp.maximum(stop - offset, 0) // unit, blocks)

            def one(block, carry, offset=offset, unit=unit, groups=groups):
                body(offset + block * unit, groups)
                return carry

            lax.fori_loop(low, jnp.maximum(high, low), one, 0)
        offset += total
    return offset


def cut_rows(cut):
    before = after = 0
    offset = 0
    for _, (rows, columns) in layout()[:11]:
        unit, total = TALL * (columns // LANES), rows * (columns // LANES)
        inside = jnp.maximum(cut - offset, 0)
        cuts = ((inside < total) & (inside % unit > 0)).astype(jnp.int32)
        before = before + cuts * (inside % unit)
        after = after + cuts * (unit - inside % unit)
        offset += total
    return before, after


class Halo:
    def __init__(self, at, here, start, wide, send_sem, recv_sem):
        self.at, self.here, self.start, self.wide = at, here, start, wide
        self.sems = send_sem, recv_sem
        first = at.me * SHARD_ROWS
        head, give_back = cut_rows(first)
        give_next, tail = cut_rows(first + SHARD_ROWS)
        self.given, self.taken = (give_back, give_next), (tail, head)

    def copies(self, side, index):
        low, high = HALO_STEP * index, HALO_STEP * (index + 1)
        src = self.start + (low if side == 0 else SHARD_ROWS - high)
        dst = HALO + SHARD_ROWS + low if side == 0 else HALO - high
        return pltpu.make_async_remote_copy(
            src_ref=self.here.at[pl.ds(src, HALO_STEP)],
            dst_ref=self.wide.at[pl.ds(dst, HALO_STEP)],
            send_sem=self.sems[0].at[side, index],
            recv_sem=self.sems[1].at[side, index],
            device_id=self.at.devices["back" if side == 0 else "next"],
            device_id_type=MESH,
        )

    def each(self, rows, action):
        for side in range(2):
            for index in range(HALO // HALO_STEP):
                pl.when(rows[side] > HALO_STEP * index)(partial(action, side, index))

    def start_all(self):
        self.each(self.given, lambda side, index: self.copies(side, index).start())

    def take(self):
        self.each(self.taken, lambda side, index: self.copies(side, index).wait_recv())

    def finish(self):
        self.each(self.given, lambda side, index: self.copies(side, index).wait_send())


VEC_ROWS = 64


def gather_kernel(
    master_ref, visible_ref, flat_ref, both_ref, wide, turned, own_sem, halo_send, halo_recv, *sems
):
    recv, core_recv, send_x, send_y, send_far, send_near, core_send = sems
    at = Place()
    first = at.me * SHARD_ROWS
    skew = (at.me * 2) % TALL
    own = pltpu.make_async_copy(master_ref, wide.at[pl.ds(HALO, SHARD_ROWS)], own_sem.at[0])
    own.start()
    at.greet()
    out = Outbox()
    halo = Halo(at, master_ref, 0, wide, halo_send, halo_recv)
    halo.start_all()
    half = visible_ref.shape[0]
    rows_here = both_ref.at[pl.ds(pl.multiple_of(at.core * half, half), half)]
    rows_there = both_ref.at[pl.ds(pl.multiple_of((1 - at.core) * half, half), half)]
    out.send(visible_ref, rows_here, own_sem.at[3], own_sem.at[4], at.devices["core"])
    keep = pltpu.make_async_copy(visible_ref, rows_here, own_sem.at[2])
    keep.start()
    own.wait()

    def turn(row, groups):
        start = row - first + HALO
        spot = row - (first - skew) + HALO
        for group in range(groups):
            turned[pl.ds(pl.multiple_of(spot + group * TALL, TALL), TALL), :] = wide[
                pl.ds(start + group, TALL, stride=groups), :
            ].astype(LOW)

    vec_start = entry_blocks(at.me, turn)
    halo.take()
    entry_blocks(at.me, turn, edges=True)

    @pl.when(at.me == 31)
    def _():
        start = vec_start - 31 * SHARD_ROWS + HALO
        spot = start + (31 * 2) % TALL
        turned[pl.ds(spot, VEC_ROWS), :] = wide[pl.ds(start, VEC_ROWS), :].astype(LOW)

    mine = pltpu.make_async_copy(
        turned.at[pl.ds(HALO + skew, SHARD_ROWS)],
        flat_ref.at[pl.ds(first, SHARD_ROWS)],
        own_sem.at[1],
    )
    mine.start()

    def source(part):
        start, size = TRUE_PARTS[part]
        return turned.at[pl.ds(HALO + skew + start, size)]

    sends = {"x": send_x, "y": send_y, "far": send_far, "near": send_near}
    gather_exchange(at, flat_ref, source, recv, core_recv, sends, core_send)
    mine.wait()
    keep.wait()
    arrived(rows_there, own_sem.at[4], at.devices["x"])
    out.finish()
    halo.finish()


def gather_weights(master_rows, visible_rows):
    hbm = pl.BlockSpec(memory_space=pltpu.HBM)
    steps = pltpu.SemaphoreType.DMA((2, HALO // HALO_STEP))
    half, width = visible_rows.shape
    return pl.pallas_call(
        gather_kernel,
        out_shape=[
            jax.ShapeDtypeStruct((32 * SHARD_ROWS, LANES), LOW),
            jax.ShapeDtypeStruct((2 * half, width), LOW),
        ],
        in_specs=[hbm, hbm],
        out_specs=[hbm, hbm],
        scratch_shapes=[
            pltpu.VMEM((WIDE_ROWS + 6, LANES), FULL),
            pltpu.VMEM((WIDE_ROWS + 30, LANES), LOW),
            pltpu.SemaphoreType.DMA((5,)),
            steps,
            steps,
        ]
        + [pltpu.SemaphoreType.DMA((16, 4))] * 7,
        compiler_params=pltpu.CompilerParams(
            collective_id=0, has_side_effects=True, vmem_limit_bytes=60 * 1024 * 1024
        ),
        name="gather_weights",
    )(master_rows, visible_rows)


def add_into(dst, start, terms, size, chunk):
    def one(step):
        row = step * chunk
        total = None
        for ref, first in terms:
            piece = ref[pl.ds(pl.multiple_of(first + row, TALL), chunk), :].astype(FULL)
            total = piece if total is None else total + piece
        dst[pl.ds(pl.multiple_of(start + row, TALL), chunk), :] = total.astype(dst.dtype)

    loop(size // chunk, one)


def reduce_kernel(
    grad_ref,
    loss_ref,
    shard_ref,
    square_ref,
    loss_total_ref,
    own,
    theirs,
    from_x,
    from_y,
    pass_x,
    pass_y,
    far_a,
    near_a,
    far_b,
    near_b,
    wide,
    plain,
    scalars,
    load_sem,
    core_send,
    core_recv,
    send_x,
    send_y,
    send_far,
    send_near,
    recv_x,
    recv_y,
    recv_far,
    recv_near,
    halo_send,
    halo_recv,
    tiny_send,
    tiny_recv,
):
    at = Place()
    tail = pl.ds(SHARD_ROWS - 2, TALL)
    for index in range(16):
        own[index, tail, :] = jnp.zeros((TALL, LANES), LOW)
        theirs[index, tail, :] = jnp.zeros((TALL, LANES), LOW)
    body = pl.ds(0, SHARD_ROWS)

    def shard_rows(core, chip):
        return grad_ref.at[pl.ds((core * 16 + chip) * SHARD_ROWS, SHARD_ROWS)]

    def load(chip):
        return pltpu.make_async_copy(
            shard_rows(at.core, chip), own.at[chip, body], load_sem.at[chip]
        )

    at.greet()
    pairs = Outbox()
    for mirrored in (3, 2, 1 - at.inner, at.inner):
        for column in ("d", "y", "x", "o"):
            chip = 4 * at.plane(mirrored) + at.columns[column]
            pairs.send(
                shard_rows(1 - at.core, chip),
                theirs.at[chip, body],
                core_send.at[chip],
                core_recv.at[chip],
                at.devices["core"],
            )
            load(chip).start()
    sends = {"x": send_x, "y": send_y, "far": send_far, "near": send_near}
    recvs = {"x": recv_x, "y": recv_y, "far": recv_far, "near": recv_near}
    relayed = {"x": pass_x, "y": pass_y}
    direct = {"x": from_x, "y": from_y}
    lines = {"far": (far_a, far_b), "near": (near_a, near_b)}

    def reduce_parts(inner):
        out = Outbox()
        paired, joined = set(), set()

        def pair(chip, column, part):
            if (column, "all") not in paired:
                paired.add((column, "all"))
                load(chip).wait()
                arrived(theirs.at[chip, body], core_recv.at[chip], at.devices["x"])
            name = "b" if part[0] == "b" else part
            if (column, name) not in paired:
                paired.add((column, name))
                first, size = PARTS[name]
                add_into(
                    own.at[chip],
                    first,
                    [(own.at[chip], first), (theirs.at[chip], first)],
                    size,
                    size // (4 if name == "b" else 3),
                )

        def landing(link, plane, chip, part, relay):
            first, size = PARTS[part]
            if link in lines and part == "b":
                return lines[link][1].at[chip], 0, size, (chip, SLOTS[part])
            if link in lines:
                return lines[link][0].at[plane], first, size, (chip, SLOTS[part])
            if relay:
                return relayed[link].at[plane], first, size, (plane, 3 + (part[0] == "b"))
            return direct[link].at[plane], first, size, (plane, SLOTS[part])

        def step(item):
            mirrored, column, part = item_of(item)
            plane = at.plane(mirrored)
            chip = 4 * plane + at.columns[column]
            pair(chip, (mirrored, column), part)
            first, size = PARTS[part]
            terms = []
            links = onward(inner, item)
            if mirrored == inner and column == "d" and part[0] == "b":
                links = [] if joined else links
                joined.add(part)
            own_item = mirrored == inner and column == "o"
            for link, piece in links:
                relay = column in ("x", "y")
                buffer, start, count, index = landing(link, plane, chip, piece, relay)
                arrived(buffer.at[pl.ds(start, count)], recvs[link].at[*index], at.devices["x"])
                terms.append((buffer, start, count))
            if own_item:
                whole = [(own.at[chip], first)] + [(buffer, start) for buffer, start, _ in terms]
                if part == "b":
                    add_into(plain, 0, whole, size, size // 4)
                    wide[pl.ds(HALO + A_ROWS, B_TRUE), :] = plain[pl.ds(0, B_TRUE), :]
                else:
                    add_into(wide, HALO + first, whole, size, size // 3)
                return
            full_size = B_ROWS if part[0] == "b" else size
            full_first = PARTS["b"][0] if part[0] == "b" else first
            whole = [(buffer, start) for buffer, start, count in terms if count == full_size]
            halves = [(buffer, start, count) for buffer, start, count in terms if count != full_size]
            if whole:
                add_into(
                    own.at[chip],
                    full_first,
                    [(own.at[chip], full_first), *whole],
                    full_size,
                    full_size // (4 if part[0] == "b" else 3),
                )
            for buffer, start, count in halves:
                add_into(
                    own.at[chip], start, [(own.at[chip], start), (buffer, start)], count, count // 2
                )
            if column == "o" or (part == "b" and mirrored != inner):
                link = "near" if inner == 1 and mirrored == 0 else "far"
                target = "near" if inner == 0 else "far"
                buffer, start, _, index = landing(target, plane, chip, part, False)
                arrive_sem = recvs[target]
            else:
                link = {"x": "x", "y": "y", "d": "y" if part in ("a1", "b1") else "x"}[column]
                buffer, start, _, index = landing(link, plane, chip, part, column == "d")
                arrive_sem = recvs[link]
            out.send(
                own.at[chip, pl.ds(first, size)],
                buffer.at[pl.ds(start, size)],
                sends[link].at[*index],
                arrive_sem.at[*index],
                at.devices[link],
            )

        for item in reversed(ARRIVALS[inner]):
            step(item)
        for part in ("a2", "a1", "b"):
            step(own_item(inner, part))
        out.finish()

    by_place(at, reduce_parts)
    pairs.finish()

    tiny = Outbox()
    halo = Halo(at, wide, HALO, wide, halo_send, halo_recv)
    halo.start_all()
    step_rows = 352
    whole_steps = SHARD_ROWS // step_rows

    def squares(index, carry):
        piece = wide[pl.ds(pl.multiple_of(HALO + index * step_rows, 8), step_rows), :]
        piece = piece * piece
        return carry + jnp.sum(piece.reshape(step_rows // 8, 8, LANES), axis=0)

    square = lax.fori_loop(0, whole_steps, squares, jnp.zeros((8, LANES), FULL))
    rest = wide[pl.ds(HALO + whole_steps * step_rows, SHARD_ROWS - whole_steps * step_rows), :]
    square = square + 0.125 * jnp.sum(rest * rest, axis=0, keepdims=True)
    scalars[at.me, 0] = square
    scalars[at.me, 1] = jnp.broadcast_to(loss_ref[...], (8, LANES))
    for index in range(1, 32):
        tiny.send(
            scalars.at[at.me],
            scalars.at[at.me],
            tiny_send.at[index],
            tiny_recv.at[at.me],
            at.ring(index),
        )
    def turn_back(row, groups):
        start = row - at.me * SHARD_ROWS + HALO
        for group in range(groups):
            plain[pl.ds(start + group, TALL, stride=groups), :] = wide[
                pl.ds(start + group * TALL, TALL), :
            ]

    vec_start = entry_blocks(at.me, turn_back)
    halo.take()
    entry_blocks(at.me, turn_back, edges=True)

    @pl.when(at.me == 31)
    def _():
        spot = pl.ds(vec_start - 31 * SHARD_ROWS + HALO, VEC_ROWS)
        plain[spot, :] = wide[spot, :]

    shard_ref[...] = plain[pl.ds(HALO, SHARD_ROWS), :]
    for index in range(1, 32):
        peer = (at.me + index) % 32
        arrived(scalars.at[peer], tiny_recv.at[peer], at.devices["x"])
    totals = jnp.sum(scalars[...], axis=0)
    square_ref[...] = jnp.sum(
        jnp.sum(totals[0], axis=0, keepdims=True), axis=1, keepdims=True
    )
    loss_total_ref[...] = totals[1, 0:1, 0:1]
    halo.finish()
    tiny.finish()


def reduce_gradients(grad_rows, loss_row):
    hbm = pl.BlockSpec(memory_space=pltpu.HBM)
    vmem = pl.BlockSpec(memory_space=pltpu.VMEM)
    dma = pltpu.SemaphoreType.DMA
    shard_total, square, loss = pl.pallas_call(
        reduce_kernel,
        out_shape=[
            jax.ShapeDtypeStruct((SHARD_ROWS, LANES), FULL),
            jax.ShapeDtypeStruct((1, 1), FULL),
            jax.ShapeDtypeStruct((1, 1), FULL),
        ],
        in_specs=[hbm, vmem],
        out_specs=[vmem, vmem, vmem],
        scratch_shapes=[pltpu.VMEM((16, PAD_ROWS, LANES), LOW)] * 2
        + [pltpu.VMEM((4, PAD_ROWS, LANES), LOW)] * 4
        + [pltpu.VMEM((4, A_ROWS, LANES), LOW)] * 2
        + [pltpu.VMEM((16, B_ROWS, LANES), LOW)] * 2
        + [pltpu.VMEM((WIDE_ROWS + 6, LANES), FULL)] * 2
        + [pltpu.VMEM((32, 2, 8, LANES), FULL)]
        + [dma((16,))] * 3
        + [dma((4, 5))] * 2
        + [dma((16, 4))] * 2
        + [dma((4, 5))] * 2
        + [dma((16, 4))] * 2
        + [dma((2, HALO // HALO_STEP))] * 2
        + [dma((32,))] * 2,
        compiler_params=pltpu.CompilerParams(
            collective_id=1, has_side_effects=True, vmem_limit_bytes=60 * 1024 * 1024
        ),
        name="reduce_gradients",
    )(grad_rows, loss_row)
    return shard_total.reshape(-1), square.reshape(()), loss.reshape(())


ROWS = 256
ENC_CHUNK = 256
FETCHED = ("vecs", "embed", "enc_qkv", "enc_out", "enc_up", "enc_down", "project")
BACKWARD_FETCHED = ("vecs", "project", "enc_down", "enc_up", "enc_out", "enc_qkv")


def encoder_forward_kernel(
    part_ref,
    visible_ref,
    segments_ref,
    patches_ref,
    table_ref,
    flat_ref,
    *refs,
):
    results, kept, (out_sem, sems, *buffers) = refs[:14], refs[14:28], refs[28:]
    (
        vis_rows,
        embedded,
        normed_a,
        qkv_rows,
        attn_out,
        after_attn,
        normed_b,
        slope,
        hidden_act,
        encoded,
        final_enc,
        projected,
        row_facts,
        column_facts,
    ) = kept

    def shipment(index):
        return pltpu.make_async_copy(kept[index], results[index], out_sem.at[index])

    def ship(*indices):
        for index in indices:
            shipment(index).start()

    ready = fetch(flat_ref, FETCHED, buffers, sems)
    part = part_ref[0]
    total = segments_ref.shape[1]
    images = IMG_SEQ // 2
    spare = ROWS - images * VIS
    segments = segments_ref[...]
    image = segments - part * images
    inside = (image >= 0) & (image < images)
    padding = segments == IMG_SEQ
    flags = jnp.concatenate(
        [
            inside.astype(FULL),
            padding.astype(FULL),
            jnp.zeros((6, total), FULL),
        ],
        axis=0,
    ).astype(LOW)
    row = lax.broadcasted_iota(jnp.int32, (total, total), 0)
    column = lax.broadcasted_iota(jnp.int32, (total, total), 1)
    counts = dot_nn(flags, (row <= column).astype(FULL).astype(LOW)).astype(jnp.int32)
    inside_count, padding_count = counts[0:1], counts[1:2]
    padding_slot = padding_count - part * spare
    chosen = inside | (padding & (padding_slot >= 1) & (padding_slot <= spare))
    slot = inside_count + jnp.clip(padding_slot, 0, spare) - 1
    slot = jnp.where(chosen, slot, -1)
    select = (lax.broadcasted_iota(jnp.int32, (ROWS, total), 0) == slot).astype(FULL).astype(LOW)
    facts = jnp.concatenate(
        [segments.astype(FULL), patches_ref[...].astype(FULL), jnp.zeros((LANES - 2, total), FULL)],
        axis=0,
    ).astype(LOW)
    row_facts[...] = dot_nt(facts[0:16], select)
    column_facts[...] = dot_nt(select, facts)
    vis_rows[...] = dot_nn(select, visible_ref[...]).astype(LOW)
    ship(0, 12, 13)
    patch = column_facts[:, 1:2].astype(jnp.int32)
    spot = (lax.broadcasted_iota(jnp.int32, (ROWS, table_ref.shape[1]), 1) == patch).astype(FULL).astype(LOW)
    embedded[...] = dot_nn(spot, table_ref[0]) + dot_nn(spot, table_ref[1]) + dot_nn(spot, table_ref[2])
    w_embed = ready(1)
    product_into(embedded, vis_rows, w_embed, D, residual=embedded)
    ship(1)
    ready(0)
    vec = vec_reader(buffers[0], 0, D // LANES)
    norm_into(normed_a, embedded, vec(0), vec(1), ROWS, ENC_CHUNK)
    ship(2)
    w_qkv = ready(2)
    product_into(qkv_rows, normed_a, w_qkv, 3 * D)
    ship(3)
    allowed = column_facts[:, 0:1] == row_facts[0:1, :]
    allowed = jnp.concatenate([allowed.astype(FULL)] * 2, axis=0) > 0.5

    def attend(step):
        for part in range(2):
            attend_into(
                attn_out, qkv_rows, pl.ds(0, ROWS), 2 * step + part, D, allowed, D // HEADS
            )

    for index in range(D // LANES // 2):
        attend(index)
    ship(4)
    w_out = ready(3)
    product_into(after_attn, attn_out, w_out, D, residual=embedded)
    ship(5)
    norm_into(normed_b, after_attn, vec(2), vec(3), ROWS, ENC_CHUNK)
    ship(6)
    w_up = ready(4)
    up_into(hidden_act, slope, normed_b, w_up, FF, 512)
    ship(7, 8)
    w_down = ready(5)
    product_into(encoded, hidden_act, w_down, D, residual=after_attn)
    ship(9)
    norm_into(final_enc, encoded, vec(4), vec(5), ROWS, ENC_CHUNK)
    ship(10)
    w_proj = ready(6)
    product_into(projected, final_enc, w_proj, DD)
    ship(11)
    for index in range(len(kept)):
        shipment(index).wait()


def encoder_forward(part, visible_rows, segments, patch_ids, flat_weights):
    hbm = pl.BlockSpec(memory_space=pltpu.HBM)
    vmem = pl.BlockSpec(memory_space=pltpu.VMEM)
    smem = pl.BlockSpec(memory_space=pltpu.SMEM)
    table = jnp.asarray(split_low(position_table(D, 256)))
    kept = [
        ((ROWS, PIX), LOW),
        ((ROWS, D), FULL),
        ((ROWS, D), LOW),
        ((ROWS, 3 * D), LOW),
        ((ROWS, D), LOW),
        ((ROWS, D), FULL),
        ((ROWS, D), LOW),
        ((ROWS, FF), FULL),
        ((ROWS, FF), LOW),
        ((ROWS, D), FULL),
        ((ROWS, D), LOW),
        ((ROWS, DD), LOW),
        ((16, ROWS), FULL),
        ((ROWS, LANES), FULL),
    ]
    return pl.pallas_call(
        encoder_forward_kernel,
        out_shape=[jax.ShapeDtypeStruct(s, d) for s, d in kept],
        in_specs=[smem] + [vmem] * 4 + [hbm],
        out_specs=[hbm] * 14,
        scratch_shapes=[pltpu.VMEM(s, d) for s, d in kept]
        + [pltpu.SemaphoreType.DMA((14,)), pltpu.SemaphoreType.DMA((7,))] + tile_buffers(FETCHED),
        compiler_params=pltpu.CompilerParams(vmem_limit_bytes=60 * 1024 * 1024),
        name="encoder_forward",
    )(part, visible_rows, segments, patch_ids, table, flat_weights)


def encoder_backward_kernel(
    grad_projected,
    decoder_vecs,
    *refs,
):
    stored, refs = refs[:13], refs[13:]
    weights_ref, partial_ref, flat_ref, refs = *refs[:3], refs[3:]
    kept, refs = refs[:13], refs[13:]
    (
        grad_rows,
        upper,
        branch,
        grad_pre,
        middle,
        grad_attn,
        grad_qkv,
        vec_grads,
        turned,
        stage,
        vec_full,
        vec_stage,
        stage_sem,
        kept_sem,
        sems,
        *buffers,
    ) = refs
    (
        vis_rows,
        embedded,
        normed_a,
        qkv_rows,
        attn_out,
        after_attn,
        normed_b,
        slope,
        hidden_act,
        encoded,
        final_enc,
        row_facts,
        column_facts,
    ) = kept

    def delivery(index):
        return pltpu.make_async_copy(stored[index], kept[index], kept_sem.at[index])

    def need(*indices):
        for index in indices:
            delivery(index).wait()

    for index in (10, 9, 8):
        delivery(index).start()
    del partial_ref
    ready = fetch(weights_ref, BACKWARD_FETCHED, buffers, sems)
    for index in (7, 6, 5, 4, 12, 11, 3, 2, 1, 0):
        delivery(index).start()
    tiles = entry_tiles()
    ready(0)
    vec = vec_reader(buffers[0], 0, D // LANES)
    grad_of = lambda index: vec_grads.at[pl.ds(index, 1), :]

    emit = Emitter(flat_ref, turned, stage, stage_sem)

    need(10)
    emit("project", final_enc, grad_projected)
    w_proj = ready(1)
    product_t_into(upper, grad_projected, w_proj, D)
    need(9)
    norm_back(grad_rows, encoded, upper, None, vec(4), grad_of(4), grad_of(5), ROWS, ENC_CHUNK)
    branch[...] = grad_rows[...].astype(LOW)
    need(8)
    emit("enc_down", hidden_act, branch)
    need(7)
    w_down = ready(2)
    down_back_into(grad_pre, branch, w_down, slope, FF, 512)
    need(6)
    emit("enc_up", normed_b, grad_pre)
    w_up = ready(3)
    product_t_into(upper, grad_pre, w_up, D)
    need(5)
    norm_back(grad_rows, after_attn, upper, grad_rows, vec(2), grad_of(2), grad_of(3), ROWS, ENC_CHUNK)
    middle[...] = grad_rows[...].astype(LOW)
    need(4)
    emit("enc_out", attn_out, middle)
    w_out = ready(4)
    product_t_into(grad_attn, middle, w_out, D)
    need(12, 11, 3)
    allowed = column_facts[:, 0:1] == row_facts[0:1, :]

    def attend_back(step):
        for part in range(2):
            attend_back_into(
                grad_qkv,
                grad_attn,
                qkv_rows,
                pl.ds(0, ROWS),
                2 * step + part,
                D,
                D // HEADS,
                allowed=allowed,
            )

    for index in range(D // LANES // 2):
        attend_back(index)
    need(2)
    emit("enc_qkv", normed_a, grad_qkv)
    w_qkv = ready(5)
    product_t_into(upper, grad_qkv, w_qkv, D)
    need(1)
    norm_back(grad_rows, embedded, upper, grad_rows, vec(0), grad_of(0), grad_of(1), ROWS, ENC_CHUNK)
    branch[...] = grad_rows[...].astype(LOW)
    need(0)
    emit("embed", vis_rows, branch)
    emit.finish()
    groups = D // LANES
    for index in range(6):
        for group in range(groups):
            vec_full[pl.ds(index * groups + group, 1), :] = vec_grads[
                pl.ds(index, 1), pl.ds(group * LANES, LANES)
            ]
    base, groups = 6 * groups, DD // LANES
    for index in range(7):
        for group in range(groups):
            vec_full[pl.ds(base + index * groups + group, 1), :] = decoder_vecs[
                pl.ds(index, 1), pl.ds(group * LANES, LANES)
            ]
    vec_stage[...] = vec_full[...].astype(LOW).reshape(4, TALL, LANES)
    copy = pltpu.make_async_copy(vec_stage, flat_ref.at[pl.ds(tiles["enc_vecs"][0], 4)], stage_sem.at[0])
    copy.start()
    copy.wait()


def encoder_backward(saved, grad_projected, flat_weights, decoder_vec_grads, flat):
    hbm = pl.BlockSpec(memory_space=pltpu.HBM)
    vmem = pl.BlockSpec(memory_space=pltpu.VMEM)
    inputs = [grad_projected, decoder_vec_grads, *saved, flat_weights, flat]
    low, full = (lambda *s: pltpu.VMEM(s, LOW)), (lambda *s: pltpu.VMEM(s, FULL))
    return pl.pallas_call(
        encoder_backward_kernel,
        out_shape=jax.ShapeDtypeStruct(flat.shape, LOW),
        in_specs=[vmem] * 2 + [hbm] * 15,
        out_specs=hbm,
        input_output_aliases={len(inputs) - 1: 0},
        scratch_shapes=[pltpu.VMEM(array.shape, array.dtype) for array in saved]
        + [
            full(ROWS, D),
            full(ROWS, D),
            low(ROWS, D),
            low(ROWS, FF),
            low(ROWS, D),
            low(ROWS, D),
            low(ROWS, 3 * D),
            full(8, D),
            low(FF, ROWS),
            low(2, FF * D // (TALL * LANES), TALL, LANES),
            full(64, LANES),
            low(4, TALL, LANES),
            pltpu.SemaphoreType.DMA((2,)),
            pltpu.SemaphoreType.DMA((13,)),
            pltpu.SemaphoreType.DMA((6,)),
        ]
        + tile_buffers(BACKWARD_FETCHED),
        compiler_params=pltpu.CompilerParams(vmem_limit_bytes=60 * 1024 * 1024),
        name="encoder_backward",
    )(*inputs)


IMAGES = 5
DECODER_FETCHED = ("vecs", "dec_qkv", "dec_out", "dec_up", "dec_down", "pixel")
IMG_ROWS = 200
DEC_ROWS = IMAGES * IMG_ROWS


def decoder_kernel(
    part_ref,
    projected,
    row_facts,
    targets_ref,
    table_ref,
    weights_ref,
    flat_ref,
    grad_projected,
    vec_grads,
    loss_ref,
    dec_in,
    low_rows,
    qkv_rows,
    attn_out,
    after_attn,
    normed_b,
    slope,
    hidden_act,
    decoded,
    final_dec,
    grad_pred,
    upper,
    masked,
    score_logs,
    turned,
    stage,
    stage_sem,
    sems,
    *buffers,
    mask_total,
):
    ready = fetch(weights_ref, DECODER_FETCHED, buffers, sems)
    tiles = entry_tiles()
    ready(0)
    vec = vec_reader(buffers[0], 6 * D // LANES, DD // LANES)
    grad_of = lambda index: vec_grads.at[pl.ds(index, 1), :]
    part = part_ref[0]
    image_of = row_facts[0:1, :].astype(jnp.int32) - part * IMAGES
    patch_of = row_facts[1:2, :].astype(jnp.int32)
    patch = lax.broadcasted_iota(jnp.int32, (IMG_ROWS, ROWS), 0)

    def selector(index):
        return ((patch_of == patch) & (image_of == index)).astype(FULL)

    def place(index):
        at = span(index, IMG_ROWS)
        select = selector(index)
        real = (patch[:, 0:1] < PATCHES).astype(FULL)
        hidden = real * (1.0 - jnp.sum(select, axis=-1, keepdims=True))
        masked[at, :] = jnp.broadcast_to(hidden, (IMG_ROWS, LANES))
        dec_in[at, :] = dot_nn(select.astype(LOW), projected[...]) + hidden * vec(6) + table_ref[...]

    for index in range(IMAGES):
        place(index)
    norm_into(low_rows, dec_in, vec(0), vec(1), DEC_ROWS, DEC_ROWS)
    w_qkv = ready(1)
    product_into(qkv_rows, low_rows, w_qkv, 3 * DD)
    head_size = DD // DHEADS
    heads = LANES // head_size
    groups = DD // LANES

    def attend(step):
        rows = span(step, IMG_ROWS)
        for at in range(groups):
            logs = score_logs.at[pl.ds((step * groups + at) * heads, heads)]
            attend_columns_into(attn_out, qkv_rows, rows, at, DD, PATCHES, head_size, logs)

    for index in range(IMAGES):
        attend(index)
    w_out = ready(2)
    product_into(after_attn, attn_out, w_out, DD, residual=dec_in)
    norm_into(normed_b, after_attn, vec(2), vec(3), DEC_ROWS, DEC_ROWS)
    w_up = ready(3)
    up_into(hidden_act, slope, normed_b, w_up, DFF, 512)
    w_down = ready(4)
    product_into(decoded, hidden_act, w_down, DD, residual=after_attn)
    norm_into(final_dec, decoded, vec(4), vec(5), DEC_ROWS, DEC_ROWS)
    w_pix = ready(5)
    loss_ref[...] = jnp.zeros_like(loss_ref)

    def compare(index):
        at = span(index, IMG_ROWS)
        image = pl.ds(0, PATCHES)
        goal, _ = norm_parts(targets_ref[index].astype(FULL))
        goal = jnp.concatenate([goal, jnp.zeros((IMG_ROWS - PATCHES, PIX), FULL)], axis=0)
        error = dot_nn(final_dec[at, :], w_pix.column_tile(0, PIX)) - goal
        weight = masked[at, 0:1]
        rows = jnp.mean(error * error, axis=-1, keepdims=True) * weight
        loss_ref[...] = loss_ref[...] + jnp.sum(rows) * (1.0 / mask_total)
        grad_pred[at, :] = (weight * error * (2.0 / (PIX * mask_total))).astype(LOW)

    for index in range(IMAGES):
        compare(index)

    emit = Emitter(flat_ref, turned, stage, stage_sem)

    emit("pixel", final_dec, grad_pred)
    product_t_into(upper, grad_pred, w_pix, DD)
    grad_rows, branch = decoded, final_dec
    norm_back(grad_rows, decoded, upper, None, vec(4), grad_of(4), grad_of(5), DEC_ROWS, DEC_ROWS)
    branch[...] = grad_rows[...].astype(LOW)
    emit("dec_down", hidden_act, branch)
    grad_pre = hidden_act
    down_back_into(grad_pre, branch, w_down, slope, DFF, 512)
    emit("dec_up", normed_b, grad_pre)
    product_t_into(upper, grad_pre, w_up, DD)
    norm_back(grad_rows, after_attn, upper, grad_rows, vec(2), grad_of(2), grad_of(3), DEC_ROWS, DEC_ROWS)
    branch[...] = grad_rows[...].astype(LOW)
    emit("dec_out", attn_out, branch)
    grad_attn, grad_qkv = normed_b, grad_pre.at[:, pl.ds(0, 3 * DD)]
    product_t_into(grad_attn, branch, w_out, DD)

    def attend_back(step):
        rows = span(step, IMG_ROWS)
        for at in range(groups):
            logs = score_logs.at[pl.ds((step * groups + at) * heads, heads)]
            attend_back_into(
                grad_qkv, grad_attn, qkv_rows, rows, at, DD, head_size, real=PATCHES, logs=logs
            )

    for index in range(IMAGES):
        attend_back(index)
    emit("dec_qkv", low_rows, grad_qkv)
    emit.finish()
    product_t_into(upper, grad_qkv, w_qkv, DD)
    norm_back(grad_rows, dec_in, upper, grad_rows, vec(0), grad_of(0), grad_of(1), DEC_ROWS, DEC_ROWS)
    upper[pl.ds(0, ROWS), :] = jnp.zeros((ROWS, DD), FULL)

    def collect(index, token):
        at = span(index, IMG_ROWS)
        rows = grad_rows[at, :]
        token = token + jnp.sum((rows * masked[at, 0:1]).reshape(IMG_ROWS // 8, 8, DD), axis=0)
        upper[pl.ds(0, ROWS), :] = upper[pl.ds(0, ROWS), :] + dot_tn(
            selector(index).astype(LOW), rows.astype(LOW)
        )
        return token

    token = jnp.zeros((8, DD), FULL)
    for index in range(IMAGES):
        token = collect(index, token)
    grad_of(6)[...] = jnp.sum(token, axis=0, keepdims=True)
    grad_projected[...] = upper[pl.ds(0, ROWS), :].astype(LOW)


def decoder_step(part, projected, row_facts, targets, flat_weights, mask_total):
    hbm = pl.BlockSpec(memory_space=pltpu.HBM)
    vmem = pl.BlockSpec(memory_space=pltpu.VMEM)
    smem = pl.BlockSpec(memory_space=pltpu.SMEM)
    table = jnp.asarray(position_table(DD, IMG_ROWS))
    low, full = (lambda *s: pltpu.VMEM(s, LOW)), (lambda *s: pltpu.VMEM(s, FULL))
    return pl.pallas_call(
        partial(decoder_kernel, mask_total=mask_total),
        out_shape=[
            jax.ShapeDtypeStruct(flat_weights.shape, LOW),
            jax.ShapeDtypeStruct((ROWS, DD), LOW),
            jax.ShapeDtypeStruct((8, DD), FULL),
            jax.ShapeDtypeStruct((1, LANES), FULL),
        ],
        in_specs=[smem] + [vmem] * 4 + [hbm],
        out_specs=[hbm] + [vmem] * 3,
        scratch_shapes=[
            full(DEC_ROWS, DD),
            low(DEC_ROWS, DD),
            low(DEC_ROWS, 3 * DD),
            low(DEC_ROWS, DD),
            full(DEC_ROWS, DD),
            low(DEC_ROWS, DD),
            full(DEC_ROWS, DFF),
            low(DEC_ROWS, DFF),
            full(DEC_ROWS, DD),
            low(DEC_ROWS, DD),
            low(DEC_ROWS, PIX),
            full(DEC_ROWS, DD),
            full(DEC_ROWS, LANES),
            full(IMAGES * DHEADS, 1, IMG_ROWS),
            low(DFF, DEC_ROWS),
            low(2, DFF * DD // (TALL * LANES), TALL, LANES),
            pltpu.SemaphoreType.DMA((2,)),
            pltpu.SemaphoreType.DMA((6,)),
        ]
        + tile_buffers(DECODER_FETCHED),
        compiler_params=pltpu.CompilerParams(vmem_limit_bytes=62 * 1024 * 1024),
        name="decoder_step",
    )(part, projected, row_facts, targets, table, flat_weights)


def to_tiles(full_flat):
    pieces, offset = [], 0
    for _, (rows, columns) in layout()[:11]:
        piece = full_flat[offset : offset + rows * columns]
        piece = piece.reshape(rows // TALL, TALL, columns // LANES, LANES)
        pieces.append(piece.transpose(0, 2, 1, 3).reshape(-1, LANES))
        offset += rows * columns
    return jnp.concatenate([*pieces, full_flat[offset:].reshape(-1, LANES)])


def from_tiles(rows_flat):
    pieces, offset = [], 0
    for _, (rows, columns) in layout()[:11]:
        count = rows * columns // LANES
        piece = rows_flat[offset : offset + count]
        piece = piece.reshape(rows // TALL, columns // LANES, TALL, LANES)
        pieces.append(piece.transpose(0, 2, 1, 3).reshape(-1))
        offset += count
    return jnp.concatenate([*pieces, rows_flat[offset:].reshape(-1)])


def shards(visible, segments, patch_ids, targets, master, moment_one, moment_two, step_count):
    part = lax.axis_index("seq")
    in_kernels = master.shape[0] == SHARD_ROWS * LANES and lax.axis_size("dp") == 16
    if in_kernels:
        flat_weights, visible_rows = gather_weights(
            master.reshape(SHARD_ROWS, LANES), visible[0]
        )
    else:
        full_flat = lax.all_gather(master.astype(LOW), ("seq", "dp"), axis=0, tiled=True)
        flat_weights = to_tiles(full_flat)
        visible_rows = lax.all_gather(visible[0], "seq", axis=0, tiled=True)
    flat_weights = flat_weights.reshape(-1, TALL, LANES)
    part_row = part.reshape(1).astype(jnp.int32)
    mask_total = (PATCHES - VIS) * IMG_SEQ * visible.shape[0] * lax.axis_size("dp")
    *saved, projected, row_facts, column_facts = encoder_forward(
        part_row, visible_rows, segments, patch_ids, flat_weights
    )
    flat_grads, grad_projected, decoder_vec_grads, loss_row = decoder_step(
        part_row, projected, row_facts, targets[0], flat_weights, mask_total
    )
    flat_grads = encoder_backward(
        [*saved, row_facts, column_facts],
        grad_projected,
        flat_weights,
        decoder_vec_grads,
        flat_grads,
    )
    flat_grads = flat_grads.reshape(-1, LANES)
    if in_kernels:
        grad_shard, square_sum, loss_sum = reduce_gradients(flat_grads, loss_row)
    else:
        grad_flat = from_tiles(flat_grads.astype(FULL))
        grad_shard = lax.psum_scatter(grad_flat, ("seq", "dp"), scatter_dimension=0, tiled=True)
        square_sum, loss_sum = lax.psum(
            (jnp.sum(grad_shard * grad_shard), loss_row[0, 0]), ("seq", "dp")
        )
    grad_norm = jnp.sqrt(square_sum)
    clipped = grad_shard * jnp.minimum(1.0, clip_limit / (grad_norm + 1e-06))
    new_one = beta_mom * moment_one + (1.0 - beta_mom) * clipped
    new_two = beta_mom * moment_two + (1.0 - beta_mom) * clipped * clipped
    correction = 1.0 - jnp.power(jnp.float32(beta_mom), step_count[0].astype(jnp.float32))
    new_master = master - learn_rate * (
        new_one / correction / (jnp.sqrt(new_two / correction) + adam_eps) + decay_rate * master
    )
    return (new_one, new_two, new_master, new_master.astype(jnp.bfloat16), grad_norm, loss_sum)


def solution(mesh):
    in_specs = (
        P("dp", "seq", None),
        P("dp", None),
        P("dp", None),
        P("dp", "seq", None, None),
        P(("seq", "dp")),
        P(("seq", "dp")),
        P(("seq", "dp")),
        P(),
    )
    out_specs = (P(("seq", "dp")), P(("seq", "dp")), P(("seq", "dp")), P(("seq", "dp")), P(), P())
    return jax.shard_map(shards, mesh=mesh, in_specs=in_specs, out_specs=out_specs, check_vma=False)
```
